512 devices in a mesh: ctx: 32 (over z, y_hi), exp: 8 (over x, y_lo), rep: 2 (over core).
Axes of the slice: x: 4, y: 8 (y_hi: 4, y_lo: 2; y = y_hi * 2 + y_lo), z: 8, core: 2. Of those that a mesh axis runs over, the one named last changes fastest.
Arguments:
- queries: bfloat16 [4096, 4096], P(('rep', 'ctx'), 'exp'), parts along dimension 0, may hold values from -8 to 8
- key_rows: bfloat16 [4096, 256], P(('rep', 'ctx')), parts along dimension 0, may hold values from -8 to 8
- value_head_rows: bfloat16 [4096, 256], P(('rep', 'ctx')), parts along dimension 0, may hold values from -6 to 6
- block_order: int32 [64], P('rep'), parts along dimension 0, may hold values from 0 to 31, each once
- residual: bfloat16 [4096, 4096], P(('rep', 'ctx'), 'exp'), parts along dimension 0, may hold values from -8 to 8
- norm_gain: float32 [4096], P('exp'), may hold values from 0.25 to 1.75
- expert_ids: int32 [4096, 8], P(('rep', 'ctx')), parts along dimension 0, may hold values from 0 to 63, all different within a row; in each aligned block of 64 rows (0 to 63, 64 to 127, ...) at most 16 rows name the same one
- route_weight: float32 [4096, 8], P(('rep', 'ctx')), parts along dimension 0, may hold values from 0.02 to 0.5
- gate_weight: bfloat16 [64, 4096, 768], P('ctx', 'exp'), may hold values from -0.09375 to 0.09375
- up_weight: bfloat16 [64, 4096, 768], P('ctx', 'exp'), may hold values from -0.09375 to 0.09375
- down_weight: bfloat16 [64, 768, 4096], P('ctx', None, 'exp'), may hold values from -0.21875 to 0.21875
Outputs:
- layer_out: bfloat16 [4096, 4096], P(('rep', 'ctx'), 'exp'), parts along dimension 0
The draws below stay inside these ranges and needn't reach their ends.
There are 2 independent parts, one for each index of `rep`. The reference program is written for one: setup_inputs(seed, part) draws one part's arguments, and reference() takes and returns one part's arrays. A program takes and returns all parts, laid end to end along the dimension named above; an argument that names none is the same for every part. Nothing has to cross between parts.
Inputs may be any that keep to these rules, and one draw needn't show every extreme that they name: `expert_ids`: each row names 8 different experts. In each aligned block of 64 rows no expert is named by more than 16 rows, a bound that some block reaches. `block_order`: each block index appears once.
All inputs are finite; a program needn't handle non-finite values.
Results may differ from the reference program's by a relative error of at most 0.011.
Values may be sent and summed in bfloat16 or wider, within the bound.
A program may use at most 64 MiB of HBM per device.

```python
import math
import jax
import jax.numpy as jnp
import numpy as np
from jax import lax

D = 4096
QUERY_HEADS = 32
KEY_VALUE_HEADS = 2
HEAD_SIZE = 128
HID = 768
TOPK = 8
TOKC = 64
PROMPT_LENGTH = 2048
EXPERTS = 64
CAP = 16
N_CTX = 32
N_EXP = 8


def draw_queries(key, part):
    value_tensor = jnp.clip(jax.random.normal(jax.random.fold_in(key, 1), (PROMPT_LENGTH, QUERY_HEADS * HEAD_SIZE), jnp.float32), -6.0, 6.0)
    return value_tensor.astype(jnp.bfloat16)


def draw_key_rows(key, part):
    value_tensor = jnp.clip(jax.random.normal(jax.random.fold_in(key, 4), (PROMPT_LENGTH, KEY_VALUE_HEADS * HEAD_SIZE), jnp.float32), -6.0, 6.0)
    return value_tensor.astype(jnp.bfloat16)


def draw_residual(key, part):
    column = jnp.arange(D, dtype=jnp.float32)
    rising = 0.5 * jnp.exp(math.log(3.0) * column / D)
    jitter = jnp.exp(jax.random.uniform(jax.random.fold_in(key, 11), (1, D), jnp.float32, -0.4, 0.4))
    value_tensor = jax.random.normal(jax.random.fold_in(key, 12), (PROMPT_LENGTH, D), jnp.float32)
    return jnp.clip(value_tensor * rising[None, :] * jitter, -8.0, 8.0).astype(jnp.bfloat16)


def block_levels(rng, shape, shards, low, top_value):
    def one(dim, parts):
        heights = jax.random.uniform(jax.random.fold_in(jax.random.fold_in(rng, 6), dim), (parts,), jnp.float32, low / len(shards), top_value / len(shards))
        return jnp.repeat(jnp.exp(heights), shape[dim] // parts).reshape((-1,) + (1,) * (len(shape) - dim - 1))

    level = one(*shards[0])
    for cut in shards[1:]:
        level = level * one(*cut)
    return level


def shared_out(rng, own, number, rows, count, top, limit, slope):
    sequence = jax.random.permutation(rng, count)
    packed, usual = portions_of(count, rows * top, limit, slope, True), portions_of(count, rows * top, limit, slope, False)
    places = jnp.arange(count)

    def named(lengths, offset_by):
        used = int((lengths > 0).sum())
        fixed = max(1, used // 4)
        moved = fixed + (places - fixed + offset_by * (used - fixed)) % max(1, count - fixed)
        return jnp.zeros((count,), jnp.int32).at[sequence[jnp.where(places < fixed, places, moved)]].set(jnp.asarray(lengths, jnp.int32))

    lengths = jnp.where(number % 4 == 0, named(packed, number // 4), named(usual, number - number // 4 - 1))
    mixed = jax.random.permutation(jax.random.fold_in(own, 3), count)
    source_of, sink = mixed[0:count // 2 * 2:2], mixed[1:count // 2 * 2:2]
    room = jnp.minimum(lengths[source_of] - 1, limit - lengths[sink]) // 2
    room = jnp.where((source_of == sequence[0]) | (sink == sequence[0]) | (lengths[sink] == 0), 0, jnp.maximum(room, 0))
    moved = jax.random.randint(jax.random.fold_in(own, 4), (count // 2,), 0, 1 << 20) % (room + 1)
    lengths = lengths.at[source_of].add(-moved).at[sink].add(moved)
    members = jnp.searchsorted(jnp.cumsum(lengths), jnp.arange(rows * top), side="right").astype(jnp.int32)
    grid = members.reshape(top, rows).T
    grid = grid[jax.random.permutation(jax.random.fold_in(own, 1), rows)]
    offset_by = jax.random.randint(jax.random.fold_in(own, 2), (rows, 1), 0, top)
    return jnp.take_along_axis(grid, (jnp.arange(top)[None, :] + offset_by) % top, axis=1)


def portions_of(amount, total, bound, slope, full):
    weights = [(1 << 20) // math.isqrt(standing ** slope) + 1 for standing in range(1, amount + 1)]
    largest = bound if full else min(bound, max(-(-total // amount), total * weights[0] // sum(weights)))
    least = 1 if total - largest >= amount - 1 else 0
    holding, spare = [largest] + [least] * (amount - 1), total - largest - least * (amount - 1)
    while spare > 0:
        movable = [i for i in range(1, amount) if holding[i] < largest] or [i for i in range(1, amount) if holding[i] < bound]
        mass, remaining = sum([weights[i] for i in movable]), spare
        for i in movable:
            extra = min(bound - holding[i], max(1, remaining * weights[i] // mass), spare)
            holding[i] = holding[i] + extra
            spare = spare - extra
    return np.array(holding)


def scatter_about(key, extent, scale, limit, cuts=(), held_as=jnp.bfloat16):
    factor_of = block_levels(key, extent, cuts, -0.22, 0.18) if cuts else 1.0
    entries = jax.random.normal(key, extent, jnp.float32) * scale * factor_of
    return jnp.minimum(jnp.maximum(entries, -limit), limit).astype(held_as)


def setup_inputs(seed: int = 0, part: int = 0) -> dict:
    key_of = jax.random.split(jax.random.key(seed), 12)
    own_keys = jax.random.split(jax.random.fold_in(key_of[11], part), 12)
    queries = draw_queries(jax.random.fold_in(jax.random.fold_in(key_of[11], part), 71), part)
    key_rows = draw_key_rows(jax.random.fold_in(jax.random.fold_in(key_of[11], part), 71), part)
    value_head_rows = scatter_about(own_keys[2], (PROMPT_LENGTH, KEY_VALUE_HEADS * HEAD_SIZE), 1.0, 6.0, ((0, 32),))
    block_order = jax.random.permutation(own_keys[3], N_CTX).astype(jnp.int32)
    residual = draw_residual(jax.random.fold_in(jax.random.fold_in(key_of[11], part), 71), part)
    norm_gain = jnp.clip(1.0 + 0.15 * jax.random.normal(key_of[5], (D,), jnp.float32), 0.25, 1.75)
    expert_ids_keys = jax.random.split(jax.random.fold_in(own_keys[6], 1), PROMPT_LENGTH // TOKC)
    expert_ids_turns = jax.random.permutation(jax.random.fold_in(own_keys[6], 3), PROMPT_LENGTH // TOKC)
    expert_ids = jax.vmap(lambda own, number: shared_out(jax.random.fold_in(own_keys[6], 2), own, number, TOKC, EXPERTS, TOPK, CAP, 2))(expert_ids_keys, expert_ids_turns).reshape((PROMPT_LENGTH, TOPK))
    route_weight = jnp.clip(jnp.exp(math.log(0.5) - 3.218876 * jax.random.uniform(own_keys[7], (PROMPT_LENGTH, TOPK), jnp.float32) ** block_levels(own_keys[7], (PROMPT_LENGTH, TOPK), ((0, 32),), -0.2, 0.2)), 0.02, 0.5)
    gate_weight = scatter_about(key_of[8], (EXPERTS, D, HID), D ** -0.5, 0.09375, ((0, 32), (1, 8)))
    up_weight = scatter_about(key_of[9], (EXPERTS, D, HID), D ** -0.5, 0.09375, ((0, 32), (1, 8)))
    down_weight = scatter_about(key_of[10], (EXPERTS, HID, D), HID ** -0.5, 0.21875, ((0, 32), (2, 8)))
    return dict(queries=queries, key_rows=key_rows, value_head_rows=value_head_rows, block_order=block_order, residual=residual, norm_gain=norm_gain, expert_ids=expert_ids, route_weight=route_weight, gate_weight=gate_weight, up_weight=up_weight, down_weight=down_weight)


MASKED_SCORE = -1e+30
NORM_EPS = 1e-06

def reference(queries, key_rows, value_head_rows, block_order, residual, norm_gain, expert_ids, route_weight, gate_weight, up_weight, down_weight):
    row_index = jnp.arange(PROMPT_LENGTH, dtype=jnp.int32)
    positions = block_order[row_index // TOKC] * TOKC + row_index % TOKC
    query_group_size = QUERY_HEADS // KEY_VALUE_HEADS
    inv_scale = 1.0 / math.sqrt(HEAD_SIZE)
    visible = positions[None, :] <= positions[:, None]

    def one_head(head_id):
        query_head = lax.dynamic_slice_in_dim(queries, (head_id * HEAD_SIZE).astype(jnp.int32), HEAD_SIZE, 1)
        kv_start = (head_id // query_group_size * HEAD_SIZE).astype(jnp.int32)
        key_head = lax.dynamic_slice_in_dim(key_rows, kv_start, HEAD_SIZE, 1)
        value_head = lax.dynamic_slice_in_dim(value_head_rows, kv_start, HEAD_SIZE, 1)
        scores = jnp.dot(query_head, key_head.T, preferred_element_type=jnp.float32) * inv_scale
        scores = jnp.where(visible, scores, MASKED_SCORE)
        row_max = lax.optimization_barrier(jnp.max(scores, axis=1, keepdims=True))
        weights = jnp.where(visible, jnp.exp(scores - row_max), 0.0)
        weight_sum = lax.optimization_barrier(jnp.sum(weights, axis=1, keepdims=True))
        return jnp.dot(weights.astype(jnp.bfloat16), value_head, preferred_element_type=jnp.float32) / weight_sum
    per_head = lax.map(one_head, jnp.arange(QUERY_HEADS, dtype=jnp.int32))
    attention = jnp.transpose(per_head, (1, 0, 2)).reshape(PROMPT_LENGTH, QUERY_HEADS * HEAD_SIZE).astype(jnp.bfloat16)
    mixed_rows = (residual.astype(jnp.float32) + attention.astype(jnp.float32)).astype(jnp.bfloat16)
    mixed_f = mixed_rows.astype(jnp.float32)
    mean_square = lax.optimization_barrier(jnp.mean(mixed_f * mixed_f, axis=1, keepdims=True))
    normed = (mixed_f * lax.rsqrt(mean_square + NORM_EPS) * norm_gain.astype(jnp.float32)[None, :]).astype(jnp.bfloat16)
    flat_ids = expert_ids.reshape(N_CTX, TOKC * TOPK)
    onehot = (flat_ids[:, :, None] == jnp.arange(EXPERTS, dtype=jnp.int32)[None, None, :]).astype(jnp.int32)
    slot_rank = lax.optimization_barrier(jnp.sum((jnp.cumsum(onehot, axis=1) - onehot) * onehot, axis=2))
    shard_index = jnp.arange(N_CTX, dtype=jnp.int32)[:, None]
    slot_index = (flat_ids * (N_CTX * CAP) + shard_index * CAP + slot_rank).reshape(-1).astype(jnp.int32)
    token_index = (shard_index * TOKC + jnp.arange(TOKC * TOPK, dtype=jnp.int32)[None, :] // TOPK).reshape(-1).astype(jnp.int32)
    slot_total = EXPERTS * N_CTX * CAP
    slot_token = jnp.zeros((slot_total,), jnp.int32).at[slot_index].set(token_index).reshape(EXPERTS, N_CTX * CAP)
    slot_live = jnp.zeros((slot_total,), jnp.float32).at[slot_index].set(1.0).reshape(EXPERTS, N_CTX * CAP)
    slot_scale = jnp.zeros((slot_total,), jnp.float32).at[slot_index].set(route_weight.reshape(-1).astype(jnp.float32)).reshape(EXPERTS, N_CTX * CAP)
    feature_slice = D // N_EXP

    def expert_step(combined, expert):
        rows_of = slot_token[expert]
        inputs = jnp.where(slot_live[expert][:, None] > 0, normed[rows_of], jnp.zeros((), jnp.bfloat16))
        inputs = inputs.astype(jnp.float32).reshape(-1, N_EXP, feature_slice)
        gate_mat = gate_weight[expert].astype(jnp.float32).reshape(N_EXP, feature_slice, HID)
        up_mat = up_weight[expert].astype(jnp.float32).reshape(N_EXP, feature_slice, HID)
        gate_part = jnp.einsum('njd,jdh->jnh', inputs, gate_mat, precision=lax.Precision.HIGHEST)
        up_part = jnp.einsum('njd,jdh->jnh', inputs, up_mat, precision=lax.Precision.HIGHEST)
        gate_sum = lax.optimization_barrier(jnp.sum(lax.optimization_barrier(gate_part.astype(jnp.bfloat16)).astype(jnp.float32), axis=0))
        up_sum = lax.optimization_barrier(jnp.sum(lax.optimization_barrier(up_part.astype(jnp.bfloat16)).astype(jnp.float32), axis=0))
        hidden = (jax.nn.silu(gate_sum) * up_sum).astype(jnp.bfloat16)
        expert_out = jnp.dot(hidden, down_weight[expert], preferred_element_type=jnp.float32).astype(jnp.bfloat16)
        contrib = slot_scale[expert][:, None] * expert_out.astype(jnp.float32)
        return (combined.at[rows_of].add(contrib), None)
    routed_sum, _ = lax.scan(expert_step, jnp.zeros((PROMPT_LENGTH, D), jnp.float32), jnp.arange(EXPERTS, dtype=jnp.int32))
    return (mixed_f + routed_sum).astype(jnp.bfloat16)
```

```python
import functools
import math

import jax
import jax.numpy as jnp
from jax import lax
from jax.experimental import pallas as pl
from jax.experimental.pallas import tpu as pltpu
from jax.sharding import PartitionSpec as P

D = 4096
QUERY_HEADS = 32
KEY_VALUE_HEADS = 2
HEAD_SIZE = 128
TOPK = 8
EXP_ROW = 2

MASKED_SCORE = -1e30
NORM_EPS = 1e-06
MESH = pl.DeviceIdType.MESH


def exchange_kernel(axis, n, gather, n_in, *refs):
    ins, outs = refs[:n_in], refs[n_in : 2 * n_in]
    send_sem, recv_sem = refs[2 * n_in], refs[2 * n_in + 1]
    me = lax.axis_index(axis)
    barrier = pltpu.get_barrier_semaphore()
    for k in range(1, n):
        pl.semaphore_signal(
            barrier, inc=1, device_id={axis: lax.rem(me + k, n)}, device_id_type=MESH
        )
    pl.semaphore_wait(barrier, n - 1)
    copies = []
    for k in range(1, n):
        peer = lax.rem(me + k, n)
        for i in range(n_in):
            copy = pltpu.make_async_remote_copy(
                src_ref=ins[i] if gather else ins[i].at[peer],
                dst_ref=outs[i].at[me],
                send_sem=send_sem.at[i, k],
                recv_sem=recv_sem.at[i, k],
                device_id={axis: peer},
                device_id_type=MESH,
            )
            copy.start()
            copies.append(copy)
    for i in range(n_in):
        outs[i][me] = ins[i][...] if gather else ins[i][me]
    for copy in copies:
        copy.wait()


def exchange(xs, axis, n, gather, collective_id):
    n_in = len(xs)
    out_shape = [
        jax.ShapeDtypeStruct((n,) + (x.shape if gather else x.shape[1:]), x.dtype) for x in xs
    ]
    nbytes = sum(x.size * x.dtype.itemsize for x in xs) * (n if gather else 1)
    return pl.pallas_call(
        functools.partial(exchange_kernel, axis, n, gather, n_in),
        out_shape=out_shape,
        in_specs=[pl.BlockSpec(memory_space=pltpu.VMEM)] * n_in,
        out_specs=[pl.BlockSpec(memory_space=pltpu.VMEM)] * n_in,
        scratch_shapes=[
            pltpu.SemaphoreType.DMA((n_in, n)),
            pltpu.SemaphoreType.DMA((n_in, n)),
        ],
        compiler_params=pltpu.CompilerParams(collective_id=collective_id, has_side_effects=True),
        cost_estimate=pl.CostEstimate(flops=0, bytes_accessed=2 * nbytes, transcendentals=0),
    )(*xs)


def local(
    queries,
    key_rows,
    value_head_rows,
    block_order,
    residual,
    norm_gain,
    expert_ids,
    route_weight,
    gate_weight,
    up_weight,
    down_weight,
):
    shard_rows = queries.shape[0]
    ctx_count = lax.axis_size("ctx")
    exp_count = lax.axis_size("exp")
    local_head = queries.shape[1] // HEAD_SIZE
    expert_index = lax.axis_index("exp")
    ctx_index = lax.axis_index("ctx")
    key_value_head = expert_index * local_head // (QUERY_HEADS // KEY_VALUE_HEADS)
    my_keys = lax.dynamic_slice_in_dim(key_rows, key_value_head * HEAD_SIZE, HEAD_SIZE, 1)
    my_values = lax.dynamic_slice_in_dim(value_head_rows, key_value_head * HEAD_SIZE, HEAD_SIZE, 1)
    block_ids = jnp.arange(ctx_count, dtype=jnp.int32)
    own_block = jnp.sum(jnp.where(block_ids == ctx_index, block_order, 0))
    local_rows = jnp.arange(shard_rows, dtype=jnp.int32)
    query_pos = jnp.tile(own_block * shard_rows + local_rows, local_head)
    query_flat = (
        queries.reshape(shard_rows, local_head, HEAD_SIZE)
        .transpose(1, 0, 2)
        .reshape(local_head * shard_rows, HEAD_SIZE)
    )
    inv_scale = 1.0 / math.sqrt(HEAD_SIZE)
    (key_value_all,) = exchange(
        [jnp.concatenate([my_keys, my_values], axis=1)], "ctx", ctx_count, True, 0
    )
    key_value_all = key_value_all.reshape(ctx_count * shard_rows, 2 * HEAD_SIZE)
    piece_keys = key_value_all[:, :HEAD_SIZE]
    piece_values = key_value_all[:, HEAD_SIZE:]
    key_index = jnp.arange(piece_keys.shape[0], dtype=jnp.int32)
    owner_shard = key_index // shard_rows
    key_block = jnp.sum(
        jnp.where(owner_shard[:, None] == block_ids[None, :], block_order[None, :], 0), axis=1
    )
    key_pos = key_block * shard_rows + key_index % shard_rows
    visible = key_pos[None, :] <= query_pos[:, None]
    scores = (
        lax.dot_general(
            query_flat, piece_keys, (((1,), (1,)), ((), ())), preferred_element_type=jnp.float32
        )
        * inv_scale
    )
    scores = jnp.where(visible, scores, MASKED_SCORE)
    newest = jnp.max(scores, axis=1)
    weights = jnp.where(visible, jnp.exp(scores - newest[:, None]), 0.0)
    running_sum = jnp.sum(weights, axis=1)
    weighted = jnp.dot(
        weights.astype(jnp.bfloat16), piece_values, preferred_element_type=jnp.float32
    )
    attention = (
        (weighted / running_sum[:, None])
        .reshape(local_head, shard_rows, HEAD_SIZE)
        .transpose(1, 0, 2)
        .reshape(shard_rows, local_head * HEAD_SIZE)
        .astype(jnp.bfloat16)
    )
    mixed_rows = (residual.astype(jnp.float32) + attention.astype(jnp.float32)).astype(jnp.bfloat16)
    mixed_f = mixed_rows.astype(jnp.float32)
    square_part = jnp.sum(mixed_f * mixed_f, axis=1)
    square_block = jnp.pad(square_part.reshape(1, shard_rows), ((0, 7), (0, 128 - shard_rows)))
    (square_all,) = exchange([square_block], "exp", exp_count, True, 1)
    square_sum = jnp.sum(square_all, axis=0)[0, :shard_rows]
    normed = (mixed_f * lax.rsqrt(square_sum[:, None] / D + NORM_EPS) * norm_gain[None, :]).astype(
        jnp.bfloat16
    )
    expert_count = ctx_count * EXP_ROW
    capacity = 2 * shard_rows * TOPK // expert_count
    flat_ids = expert_ids.reshape(-1)
    onehot = (flat_ids[:, None] == jnp.arange(expert_count, dtype=jnp.int32)[None, :]).astype(
        jnp.int32
    )
    slot_rank = jnp.sum((jnp.cumsum(onehot, axis=0) - onehot) * onehot, axis=1)
    slot_index = flat_ids * capacity + slot_rank
    source_rows = jnp.arange(shard_rows * TOPK, dtype=jnp.int32) // TOPK
    outgoing = (
        jnp.zeros((expert_count * capacity, normed.shape[1]), jnp.bfloat16)
        .at[slot_index]
        .set(normed[source_rows])
    )
    outgoing = outgoing.reshape(ctx_count, EXP_ROW, capacity, normed.shape[1])
    (incoming,) = exchange([outgoing], "ctx", ctx_count, False, 2)
    gate_part = jnp.einsum(
        "skcd,kdh->skch", incoming, gate_weight, preferred_element_type=jnp.float32
    ).astype(jnp.bfloat16)
    up_part = jnp.einsum(
        "skcd,kdh->skch", incoming, up_weight, preferred_element_type=jnp.float32
    ).astype(jnp.bfloat16)
    slot_count = ctx_count * EXP_ROW * capacity
    hid = gate_part.shape[-1]
    chunk = slot_count // exp_count
    gate_recv, up_recv = exchange(
        [gate_part.reshape(exp_count, chunk, hid), up_part.reshape(exp_count, chunk, hid)],
        "exp",
        exp_count,
        False,
        3,
    )
    gate_full = jnp.sum(gate_recv.astype(jnp.float32), axis=0)
    up_full = jnp.sum(up_recv.astype(jnp.float32), axis=0)
    hidden_mine = (jax.nn.silu(gate_full) * up_full).astype(jnp.bfloat16)
    (hidden,) = exchange([hidden_mine], "exp", exp_count, True, 4)
    hidden = hidden.reshape(ctx_count, EXP_ROW, capacity, hid)
    expert_out = jnp.einsum(
        "skch,khd->skcd", hidden, down_weight, preferred_element_type=jnp.float32
    ).astype(jnp.bfloat16)
    (returned,) = exchange([expert_out], "ctx", ctx_count, False, 5)
    flat_back = returned.reshape(expert_count * capacity, normed.shape[1])
    picked = flat_back[slot_index].astype(jnp.float32).reshape(shard_rows, TOPK, normed.shape[1])
    routed_sum = jnp.sum(route_weight[:, :, None] * picked, axis=1)
    return (mixed_f + routed_sum).astype(jnp.bfloat16)


def solution(mesh):
    placed = (
        P(("rep", "ctx"), "exp"),
        P(("rep", "ctx"), None),
        P(("rep", "ctx"), None),
        P("rep"),
        P(("rep", "ctx"), "exp"),
        P("exp"),
        P(("rep", "ctx"), None),
        P(("rep", "ctx"), None),
        P("ctx", "exp", None),
        P("ctx", "exp", None),
        P("ctx", None, "exp"),
    )
    return jax.shard_map(
        local, mesh=mesh, in_specs=placed, out_specs=P(("rep", "ctx"), "exp"), check_vma=False
    )
```

```python
import functools
import math

import jax
import jax.numpy as jnp
from jax import lax
from jax.experimental import pallas as pl
from jax.experimental.pallas import tpu as pltpu
from jax.sharding import PartitionSpec as P

D = 4096
QUERY_HEADS = 32
KEY_VALUE_HEADS = 2
HEAD_SIZE = 128
TOPK = 8
EXP_ROW = 2

MASKED_SCORE = -1e30
NORM_EPS = 1e-06
MESH = pl.DeviceIdType.MESH


def exchange_kernel(axis, n, gather, n_in, *refs):
    ins, outs = refs[:n_in], refs[n_in : 2 * n_in]
    send_sem, recv_sem = refs[2 * n_in], refs[2 * n_in + 1]
    me = lax.axis_index(axis)
    barrier = pltpu.get_barrier_semaphore()
    for k in range(1, n):
        pl.semaphore_signal(
            barrier, inc=1, device_id={axis: lax.rem(me + k, n)}, device_id_type=MESH
        )
    pl.semaphore_wait(barrier, n - 1)
    copies = []
    for k in range(1, n):
        peer = lax.rem(me + k, n)
        for i in range(n_in):
            copy = pltpu.make_async_remote_copy(
                src_ref=ins[i] if gather else ins[i].at[peer],
                dst_ref=outs[i].at[me],
                send_sem=send_sem.at[i, k],
                recv_sem=recv_sem.at[i, k],
                device_id={axis: peer},
                device_id_type=MESH,
            )
            copy.start()
            copies.append(copy)
    for i in range(n_in):
        outs[i][me] = ins[i][...] if gather else ins[i][me]
    for copy in copies:
        copy.wait()


def exchange(xs, axis, n, gather, collective_id):
    n_in = len(xs)
    out_shape = [
        jax.ShapeDtypeStruct((n,) + (x.shape if gather else x.shape[1:]), x.dtype) for x in xs
    ]
    nbytes = sum(x.size * x.dtype.itemsize for x in xs) * (n if gather else 1)
    return pl.pallas_call(
        functools.partial(exchange_kernel, axis, n, gather, n_in),
        out_shape=out_shape,
        in_specs=[pl.BlockSpec(memory_space=pltpu.VMEM)] * n_in,
        out_specs=[pl.BlockSpec(memory_space=pltpu.VMEM)] * n_in,
        scratch_shapes=[
            pltpu.SemaphoreType.DMA((n_in, n)),
            pltpu.SemaphoreType.DMA((n_in, n)),
        ],
        compiler_params=pltpu.CompilerParams(collective_id=collective_id, has_side_effects=True),
        cost_estimate=pl.CostEstimate(flops=0, bytes_accessed=2 * nbytes, transcendentals=0),
    )(*xs)


def dispatch_reduce_kernel(n_ctx, n_exp, *refs):
    (outgoing, gate_w, up_w, gate_recv, up_recv, incoming, gate_stage, up_stage,
     d_send, d_recv, r_send, r_recv) = refs
    per_chunk = n_ctx // n_exp
    me_c = lax.axis_index("ctx")
    me_e = lax.axis_index("exp")
    plane = me_c // per_chunk
    barrier = pltpu.get_barrier_semaphore()
    for k in range(1, n_ctx):
        pl.semaphore_signal(
            barrier, inc=1, device_id={"ctx": lax.rem(me_c + k, n_ctx)}, device_id_type=MESH
        )
    for k in range(1, n_exp):
        pl.semaphore_signal(
            barrier, inc=1, device_id={"exp": lax.rem(me_e + k, n_exp)}, device_id_type=MESH
        )
    pl.semaphore_wait(barrier, n_ctx + n_exp - 2)

    def dispatch_copy(p):
        return pltpu.make_async_remote_copy(
            src_ref=outgoing.at[p],
            dst_ref=incoming.at[me_c],
            send_sem=d_send.at[p],
            recv_sem=d_recv.at[me_c],
            device_id={"ctx": p},
            device_id_type=MESH,
        )

    for t in range(n_exp):
        z_r = lax.rem(plane + 2 * n_exp - me_e - t, n_exp)
        for y in range(per_chunk):
            p = z_r * per_chunk + y

            @pl.when(p != me_c)
            def _():
                dispatch_copy(p).start()

            @pl.when(p == me_c)
            def _():
                pltpu.make_async_copy(outgoing.at[p], incoming.at[p], d_recv.at[p]).start()

    parts = ((gate_w, gate_stage, gate_recv), (up_w, up_stage, up_recv))

    def reduce_copy(j, which):
        _, stage, recv = parts[which]
        return pltpu.make_async_remote_copy(
            src_ref=stage.at[j],
            dst_ref=recv.at[me_e],
            send_sem=r_send.at[j, which],
            recv_sem=r_recv.at[me_e, which],
            device_id={"exp": j},
            device_id_type=MESH,
        )

    rows = gate_stage.shape[2]
    for t in range(n_exp):
        j = lax.rem(plane + me_e + t, n_exp)
        for y in range(per_chunk):
            s = j * per_chunk + y
            pltpu.make_async_copy(incoming.at[s], incoming.at[s], d_recv.at[s]).wait()
        first = pl.multiple_of(j * per_chunk, per_chunk)
        for k in range(EXP_ROW):
            x = incoming[pl.ds(first, per_chunk), k].reshape(rows, incoming.shape[-1])
            for w, stage, _ in parts:
                stage[j, k] = jnp.dot(x, w[k], preferred_element_type=jnp.float32).astype(
                    stage.dtype
                )

        @pl.when(j != me_e)
        def _():
            for which in range(2):
                reduce_copy(j, which).start()

        @pl.when(j == me_e)
        def _():
            for which, (_, stage, recv) in enumerate(parts):
                pltpu.make_async_copy(stage.at[j], recv.at[j], r_recv.at[j, which]).start()

    for s in range(n_exp):
        for which, (_, _, recv) in enumerate(parts):
            pltpu.make_async_copy(recv.at[s], recv.at[s], r_recv.at[s, which]).wait()
    for j in range(n_exp):

        @pl.when(j != me_e)
        def _():
            for which in range(2):
                reduce_copy(j, which).wait_send()

    for p in range(n_ctx):

        @pl.when(p != me_c)
        def _():
            dispatch_copy(p).wait_send()


def dispatch_reduce(outgoing, gate_weight, up_weight, n_ctx, n_exp, collective_id):
    hid = gate_weight.shape[-1]
    slots = outgoing.shape[0] * outgoing.shape[2] // n_exp
    recv_shape = jax.ShapeDtypeStruct((n_exp, EXP_ROW, slots, hid), jnp.bfloat16)
    flops = 2 * 2 * outgoing.size * hid
    nbytes = 2 * outgoing.size * 2 + 4 * gate_weight.size * 2 + 4 * n_exp * EXP_ROW * slots * hid * 2
    return pl.pallas_call(
        functools.partial(dispatch_reduce_kernel, n_ctx, n_exp),
        out_shape=[recv_shape, recv_shape],
        in_specs=[pl.BlockSpec(memory_space=pltpu.VMEM)] * 3,
        out_specs=[pl.BlockSpec(memory_space=pltpu.VMEM)] * 2,
        scratch_shapes=[
            pltpu.VMEM(outgoing.shape, outgoing.dtype),
            pltpu.VMEM(recv_shape.shape, jnp.bfloat16),
            pltpu.VMEM(recv_shape.shape, jnp.bfloat16),
            pltpu.SemaphoreType.DMA((n_ctx,)),
            pltpu.SemaphoreType.DMA((n_ctx,)),
            pltpu.SemaphoreType.DMA((n_exp, 2)),
            pltpu.SemaphoreType.DMA((n_exp, 2)),
        ],
        compiler_params=pltpu.CompilerParams(collective_id=collective_id, has_side_effects=True),
        cost_estimate=pl.CostEstimate(flops=flops, bytes_accessed=nbytes, transcendentals=0),
    )(outgoing, gate_weight, up_weight)


def local(
    queries,
    key_rows,
    value_head_rows,
    block_order,
    residual,
    norm_gain,
    expert_ids,
    route_weight,
    gate_weight,
    up_weight,
    down_weight,
):
    shard_rows = queries.shape[0]
    ctx_count = lax.axis_size("ctx")
    exp_count = lax.axis_size("exp")
    local_head = queries.shape[1] // HEAD_SIZE
    expert_index = lax.axis_index("exp")
    ctx_index = lax.axis_index("ctx")
    key_value_head = expert_index * local_head // (QUERY_HEADS // KEY_VALUE_HEADS)
    my_keys = lax.dynamic_slice_in_dim(key_rows, key_value_head * HEAD_SIZE, HEAD_SIZE, 1)
    my_values = lax.dynamic_slice_in_dim(value_head_rows, key_value_head * HEAD_SIZE, HEAD_SIZE, 1)
    block_ids = jnp.arange(ctx_count, dtype=jnp.int32)
    own_block = jnp.sum(jnp.where(block_ids == ctx_index, block_order, 0))
    local_rows = jnp.arange(shard_rows, dtype=jnp.int32)
    query_pos = jnp.tile(own_block * shard_rows + local_rows, local_head)
    query_flat = (
        queries.reshape(shard_rows, local_head, HEAD_SIZE)
        .transpose(1, 0, 2)
        .reshape(local_head * shard_rows, HEAD_SIZE)
    )
    inv_scale = 1.0 / math.sqrt(HEAD_SIZE)
    (key_value_all,) = exchange(
        [jnp.concatenate([my_keys, my_values], axis=1)], "ctx", ctx_count, True, 0
    )
    key_value_all = key_value_all.reshape(ctx_count * shard_rows, 2 * HEAD_SIZE)
    piece_keys = key_value_all[:, :HEAD_SIZE]
    piece_values = key_value_all[:, HEAD_SIZE:]
    key_index = jnp.arange(piece_keys.shape[0], dtype=jnp.int32)
    owner_shard = key_index // shard_rows
    key_block = jnp.sum(
        jnp.where(owner_shard[:, None] == block_ids[None, :], block_order[None, :], 0), axis=1
    )
    key_pos = key_block * shard_rows + key_index % shard_rows
    visible = key_pos[None, :] <= query_pos[:, None]
    scores = (
        lax.dot_general(
            query_flat, piece_keys, (((1,), (1,)), ((), ())), preferred_element_type=jnp.float32
        )
        * inv_scale
    )
    scores = jnp.where(visible, scores, MASKED_SCORE)
    newest = jnp.max(scores, axis=1)
    weights = jnp.where(visible, jnp.exp(scores - newest[:, None]), 0.0)
    running_sum = jnp.sum(weights, axis=1)
    weighted = jnp.dot(
        weights.astype(jnp.bfloat16), piece_values, preferred_element_type=jnp.float32
    )
    attention = (
        (weighted / running_sum[:, None])
        .reshape(local_head, shard_rows, HEAD_SIZE)
        .transpose(1, 0, 2)
        .reshape(shard_rows, local_head * HEAD_SIZE)
        .astype(jnp.bfloat16)
    )
    mixed_rows = (residual.astype(jnp.float32) + attention.astype(jnp.float32)).astype(jnp.bfloat16)
    mixed_f = mixed_rows.astype(jnp.float32)
    square_part = jnp.sum(mixed_f * mixed_f, axis=1)
    square_block = jnp.pad(square_part.reshape(1, shard_rows), ((0, 7), (0, 128 - shard_rows)))
    (square_all,) = exchange([square_block], "exp", exp_count, True, 1)
    square_sum = jnp.sum(square_all, axis=0)[0, :shard_rows]
    normed = (mixed_f * lax.rsqrt(square_sum[:, None] / D + NORM_EPS) * norm_gain[None, :]).astype(
        jnp.bfloat16
    )
    expert_count = ctx_count * EXP_ROW
    capacity = 2 * shard_rows * TOPK // expert_count
    flat_ids = expert_ids.reshape(-1)
    onehot = (flat_ids[:, None] == jnp.arange(expert_count, dtype=jnp.int32)[None, :]).astype(
        jnp.int32
    )
    slot_rank = jnp.sum((jnp.cumsum(onehot, axis=0) - onehot) * onehot, axis=1)
    slot_index = flat_ids * capacity + slot_rank
    source_rows = jnp.arange(shard_rows * TOPK, dtype=jnp.int32) // TOPK
    outgoing = (
        jnp.zeros((expert_count * capacity, normed.shape[1]), jnp.bfloat16)
        .at[slot_index]
        .set(normed[source_rows])
    )
    outgoing = outgoing.reshape(ctx_count, EXP_ROW, capacity, normed.shape[1])
    gate_recv, up_recv = dispatch_reduce(outgoing, gate_weight, up_weight, ctx_count, exp_count, 2)
    gate_full = jnp.sum(gate_recv.astype(jnp.float32), axis=0)
    up_full = jnp.sum(up_recv.astype(jnp.float32), axis=0)
    hidden_mine = (jax.nn.silu(gate_full) * up_full).astype(jnp.bfloat16)
    (hidden,) = exchange([hidden_mine], "exp", exp_count, True, 4)
    expert_out = jnp.einsum(
        "jksh,khd->jksd", hidden, down_weight, preferred_element_type=jnp.float32
    ).astype(jnp.bfloat16)
    per_chunk = ctx_count // exp_count
    expert_out = (
        expert_out.reshape(exp_count, EXP_ROW, per_chunk, capacity, normed.shape[1])
        .transpose(0, 2, 1, 3, 4)
        .reshape(ctx_count, EXP_ROW, capacity, normed.shape[1])
    )
    (returned,) = exchange([expert_out], "ctx", ctx_count, False, 5)
    flat_back = returned.reshape(expert_count * capacity, normed.shape[1])
    picked = flat_back[slot_index].astype(jnp.float32).reshape(shard_rows, TOPK, normed.shape[1])
    routed_sum = jnp.sum(route_weight[:, :, None] * picked, axis=1)
    return (mixed_f + routed_sum).astype(jnp.bfloat16)


def solution(mesh):
    placed = (
        P(("rep", "ctx"), "exp"),
        P(("rep", "ctx"), None),
        P(("rep", "ctx"), None),
        P("rep"),
        P(("rep", "ctx"), "exp"),
        P("exp"),
        P(("rep", "ctx"), None),
        P(("rep", "ctx"), None),
        P("ctx", "exp", None),
        P("ctx", "exp", None),
        P("ctx", None, "exp"),
    )
    return jax.shard_map(
        local, mesh=mesh, in_specs=placed, out_specs=P(("rep", "ctx"), "exp"), check_vma=False
    )
```

```python
import functools
import math

import jax
import jax.numpy as jnp
from jax import lax
from jax.experimental import pallas as pl
from jax.experimental.pallas import tpu as pltpu
from jax.sharding import PartitionSpec as P

D = 4096
QUERY_HEADS = 32
KEY_VALUE_HEADS = 2
HEAD_SIZE = 128
TOPK = 8
EXP_ROW = 2

MASKED_SCORE = -1e30
NORM_EPS = 1e-06
MESH = pl.DeviceIdType.MESH


def exchange_kernel(axis, n, gather, n_in, *refs):
    ins, outs = refs[:n_in], refs[n_in : 2 * n_in]
    send_sem, recv_sem = refs[2 * n_in], refs[2 * n_in + 1]
    me = lax.axis_index(axis)
    barrier = pltpu.get_barrier_semaphore()
    for k in range(1, n):
        pl.semaphore_signal(
            barrier, inc=1, device_id={axis: lax.rem(me + k, n)}, device_id_type=MESH
        )
    pl.semaphore_wait(barrier, n - 1)
    copies = []
    for k in range(1, n):
        peer = lax.rem(me + k, n)
        for i in range(n_in):
            copy = pltpu.make_async_remote_copy(
                src_ref=ins[i] if gather else ins[i].at[peer],
                dst_ref=outs[i].at[me],
                send_sem=send_sem.at[i, k],
                recv_sem=recv_sem.at[i, k],
                device_id={axis: peer},
                device_id_type=MESH,
            )
            copy.start()
            copies.append(copy)
    for i in range(n_in):
        outs[i][me] = ins[i][...] if gather else ins[i][me]
    for copy in copies:
        copy.wait()


def exchange(xs, axis, n, gather, collective_id):
    n_in = len(xs)
    out_shape = [
        jax.ShapeDtypeStruct((n,) + (x.shape if gather else x.shape[1:]), x.dtype) for x in xs
    ]
    nbytes = sum(x.size * x.dtype.itemsize for x in xs) * (n if gather else 1)
    return pl.pallas_call(
        functools.partial(exchange_kernel, axis, n, gather, n_in),
        out_shape=out_shape,
        in_specs=[pl.BlockSpec(memory_space=pltpu.VMEM)] * n_in,
        out_specs=[pl.BlockSpec(memory_space=pltpu.VMEM)] * n_in,
        scratch_shapes=[
            pltpu.SemaphoreType.DMA((n_in, n)),
            pltpu.SemaphoreType.DMA((n_in, n)),
        ],
        compiler_params=pltpu.CompilerParams(collective_id=collective_id, has_side_effects=True),
        cost_estimate=pl.CostEstimate(flops=0, bytes_accessed=2 * nbytes, transcendentals=0),
    )(*xs)


def dispatch_reduce_kernel(n_ctx, n_exp, *refs):
    (outgoing, gate_w, up_w, gate_recv, up_recv, incoming, gate_stage, up_stage,
     d_send, d_recv, r_send, r_recv) = refs
    per_chunk = n_ctx // n_exp
    me_c = lax.axis_index("ctx")
    me_e = lax.axis_index("exp")
    plane = me_c // per_chunk
    barrier = pltpu.get_barrier_semaphore()
    for k in range(1, n_ctx):
        pl.semaphore_signal(
            barrier, inc=1, device_id={"ctx": lax.rem(me_c + k, n_ctx)}, device_id_type=MESH
        )
    for k in range(1, n_exp):
        pl.semaphore_signal(
            barrier, inc=1, device_id={"exp": lax.rem(me_e + k, n_exp)}, device_id_type=MESH
        )
    pl.semaphore_wait(barrier, n_ctx + n_exp - 2)

    def dispatch_copy(p):
        return pltpu.make_async_remote_copy(
            src_ref=outgoing.at[p],
            dst_ref=incoming.at[me_c],
            send_sem=d_send.at[p],
            recv_sem=d_recv.at[me_c],
            device_id={"ctx": p},
            device_id_type=MESH,
        )

    for t in range(n_exp):
        z_r = lax.rem(plane + 2 * n_exp - me_e - t, n_exp)
        for y in range(per_chunk):
            p = z_r * per_chunk + y

            @pl.when(p != me_c)
            def _():
                dispatch_copy(p).start()

            @pl.when(p == me_c)
            def _():
                pltpu.make_async_copy(outgoing.at[p], incoming.at[p], d_recv.at[p]).start()

    parts = ((gate_w, gate_stage, gate_recv), (up_w, up_stage, up_recv))

    def reduce_copy(j, which):
        _, stage, recv = parts[which]
        return pltpu.make_async_remote_copy(
            src_ref=stage.at[j],
            dst_ref=recv.at[me_e],
            send_sem=r_send.at[j, which],
            recv_sem=r_recv.at[me_e, which],
            device_id={"exp": j},
            device_id_type=MESH,
        )

    rows = gate_stage.shape[2]
    for t in range(n_exp):
        j = lax.rem(plane + me_e + t, n_exp)
        for y in range(per_chunk):
            s = j * per_chunk + y
            pltpu.make_async_copy(incoming.at[s], incoming.at[s], d_recv.at[s]).wait()
        first = pl.multiple_of(j * per_chunk, per_chunk)
        for k in range(EXP_ROW):
            x = incoming[pl.ds(first, per_chunk), k].reshape(rows, incoming.shape[-1])
            for w, stage, _ in parts:
                stage[j, k] = jnp.dot(x, w[k], preferred_element_type=jnp.float32).astype(
                    stage.dtype
                )

        @pl.when(j != me_e)
        def _():
            for which in range(2):
                reduce_copy(j, which).start()

        @pl.when(j == me_e)
        def _():
            for which, (_, stage, recv) in enumerate(parts):
                pltpu.make_async_copy(stage.at[j], recv.at[j], r_recv.at[j, which]).start()

    for s in range(n_exp):
        for which, (_, _, recv) in enumerate(parts):
            pltpu.make_async_copy(recv.at[s], recv.at[s], r_recv.at[s, which]).wait()
    for j in range(n_exp):

        @pl.when(j != me_e)
        def _():
            for which in range(2):
                reduce_copy(j, which).wait_send()

    for p in range(n_ctx):

        @pl.when(p != me_c)
        def _():
            dispatch_copy(p).wait_send()


def dispatch_reduce(outgoing, gate_weight, up_weight, n_ctx, n_exp, collective_id):
    hid = gate_weight.shape[-1]
    slots = outgoing.shape[0] * outgoing.shape[2] // n_exp
    recv_shape = jax.ShapeDtypeStruct((n_exp, EXP_ROW, slots, hid), jnp.bfloat16)
    flops = 2 * 2 * outgoing.size * hid
    nbytes = 2 * outgoing.size * 2 + 4 * gate_weight.size * 2 + 4 * n_exp * EXP_ROW * slots * hid * 2
    return pl.pallas_call(
        functools.partial(dispatch_reduce_kernel, n_ctx, n_exp),
        out_shape=[recv_shape, recv_shape],
        in_specs=[pl.BlockSpec(memory_space=pltpu.VMEM)] * 3,
        out_specs=[pl.BlockSpec(memory_space=pltpu.VMEM)] * 2,
        scratch_shapes=[
            pltpu.VMEM(outgoing.shape, outgoing.dtype),
            pltpu.VMEM(recv_shape.shape, jnp.bfloat16),
            pltpu.VMEM(recv_shape.shape, jnp.bfloat16),
            pltpu.SemaphoreType.DMA((n_ctx,)),
            pltpu.SemaphoreType.DMA((n_ctx,)),
            pltpu.SemaphoreType.DMA((n_exp, 2)),
            pltpu.SemaphoreType.DMA((n_exp, 2)),
        ],
        compiler_params=pltpu.CompilerParams(collective_id=collective_id, has_side_effects=True),
        cost_estimate=pl.CostEstimate(flops=flops, bytes_accessed=nbytes, transcendentals=0),
    )(outgoing, gate_weight, up_weight)


def kv_gather_kernel(n_ctx, n_exp, group, *refs):
    block, kv_all, s1_send, s1_recv, s2_send, s2_recv = refs
    per_plane = n_ctx // n_exp
    planes = n_ctx // per_plane
    me_c = lax.axis_index("ctx")
    me_e = lax.axis_index("exp")
    q = lax.rem(me_e, group)
    head_base = me_e - q
    plane = me_c // per_plane
    barrier = pltpu.get_barrier_semaphore()
    for k in range(1, n_ctx):
        pl.semaphore_signal(
            barrier, inc=1, device_id={"ctx": lax.rem(me_c + k, n_ctx)}, device_id_type=MESH
        )
    for k in range(1, group):
        pl.semaphore_signal(
            barrier, inc=1, device_id={"exp": head_base + lax.rem(q + k, group)}, device_id_type=MESH
        )
    pl.semaphore_wait(barrier, n_ctx + group - 2)

    def first_copy(p):
        return pltpu.make_async_remote_copy(
            src_ref=block,
            dst_ref=kv_all.at[me_c],
            send_sem=s1_send.at[p],
            recv_sem=s1_recv.at[me_c],
            device_id={"ctx": p},
            device_id_type=MESH,
        )

    halves = 2
    for h in range(halves):
        z_r = lax.rem(plane + 2 * planes - q - h * (planes // halves), planes)
        for y in range(per_plane):
            p = z_r * per_plane + y

            @pl.when(p != me_c)
            def _():
                first_copy(p).start()

            @pl.when(p == me_c)
            def _():
                pltpu.make_async_copy(block, kv_all.at[p], s1_recv.at[p]).start()

    def second_copy(h, r):
        first = pl.multiple_of(lax.rem(plane + q + h * (planes // halves), planes) * per_plane, per_plane)
        return pltpu.make_async_remote_copy(
            src_ref=kv_all.at[pl.ds(first, per_plane)],
            dst_ref=kv_all.at[pl.ds(first, per_plane)],
            send_sem=s2_send.at[r, h],
            recv_sem=s2_recv.at[r, h],
            device_id={"exp": head_base + lax.rem(q + r, group)},
            device_id_type=MESH,
        )

    for h in range(halves):
        z_s = lax.rem(plane + q + h * (planes // halves), planes)
        for y in range(per_plane):
            s = z_s * per_plane + y
            pltpu.make_async_copy(kv_all.at[s], kv_all.at[s], s1_recv.at[s]).wait()
        for r in range(1, group):
            second_copy(h, r).start()
    for h in range(halves):
        for r in range(1, group):
            second_copy(h, r).wait_recv()
    for h in range(halves):
        for r in range(1, group):
            second_copy(h, r).wait_send()
    for h in range(halves):
        z_r = lax.rem(plane + 2 * planes - q - h * (planes // halves), planes)
        for y in range(per_plane):
            p = z_r * per_plane + y

            @pl.when(p != me_c)
            def _():
                first_copy(p).wait_send()


def kv_gather(block, n_ctx, n_exp, group, collective_id):
    nbytes = block.size * block.dtype.itemsize * n_ctx
    return pl.pallas_call(
        functools.partial(kv_gather_kernel, n_ctx, n_exp, group),
        out_shape=jax.ShapeDtypeStruct((n_ctx,) + block.shape, block.dtype),
        in_specs=[pl.BlockSpec(memory_space=pltpu.VMEM)],
        out_specs=pl.BlockSpec(memory_space=pltpu.VMEM),
        scratch_shapes=[
            pltpu.SemaphoreType.DMA((n_ctx,)),
            pltpu.SemaphoreType.DMA((n_ctx,)),
            pltpu.SemaphoreType.DMA((group, 2)),
            pltpu.SemaphoreType.DMA((group, 2)),
        ],
        compiler_params=pltpu.CompilerParams(collective_id=collective_id, has_side_effects=True),
        cost_estimate=pl.CostEstimate(flops=0, bytes_accessed=2 * nbytes, transcendentals=0),
    )(block)


def local(
    queries,
    key_rows,
    value_head_rows,
    block_order,
    residual,
    norm_gain,
    expert_ids,
    route_weight,
    gate_weight,
    up_weight,
    down_weight,
):
    shard_rows = queries.shape[0]
    ctx_count = lax.axis_size("ctx")
    exp_count = lax.axis_size("exp")
    local_head = queries.shape[1] // HEAD_SIZE
    expert_index = lax.axis_index("exp")
    ctx_index = lax.axis_index("ctx")
    key_value_head = expert_index * local_head // (QUERY_HEADS // KEY_VALUE_HEADS)
    my_keys = lax.dynamic_slice_in_dim(key_rows, key_value_head * HEAD_SIZE, HEAD_SIZE, 1)
    my_values = lax.dynamic_slice_in_dim(value_head_rows, key_value_head * HEAD_SIZE, HEAD_SIZE, 1)
    block_ids = jnp.arange(ctx_count, dtype=jnp.int32)
    own_block = jnp.sum(jnp.where(block_ids == ctx_index, block_order, 0))
    local_rows = jnp.arange(shard_rows, dtype=jnp.int32)
    query_pos = jnp.tile(own_block * shard_rows + local_rows, local_head)
    query_flat = (
        queries.reshape(shard_rows, local_head, HEAD_SIZE)
        .transpose(1, 0, 2)
        .reshape(local_head * shard_rows, HEAD_SIZE)
    )
    inv_scale = 1.0 / math.sqrt(HEAD_SIZE)
    key_value_all = kv_gather(
        jnp.concatenate([my_keys, my_values], axis=1),
        ctx_count,
        exp_count,
        QUERY_HEADS // KEY_VALUE_HEADS // local_head,
        0,
    )
    key_value_all = key_value_all.reshape(ctx_count * shard_rows, 2 * HEAD_SIZE)
    piece_keys = key_value_all[:, :HEAD_SIZE]
    piece_values = key_value_all[:, HEAD_SIZE:]
    key_index = jnp.arange(piece_keys.shape[0], dtype=jnp.int32)
    owner_shard = key_index // shard_rows
    key_block = jnp.sum(
        jnp.where(owner_shard[:, None] == block_ids[None, :], block_order[None, :], 0), axis=1
    )
    key_pos = key_block * shard_rows + key_index % shard_rows
    visible = key_pos[None, :] <= query_pos[:, None]
    scores = (
        lax.dot_general(
            query_flat, piece_keys, (((1,), (1,)), ((), ())), preferred_element_type=jnp.float32
        )
        * inv_scale
    )
    scores = jnp.where(visible, scores, MASKED_SCORE)
    newest = jnp.max(scores, axis=1)
    weights = jnp.where(visible, jnp.exp(scores - newest[:, None]), 0.0)
    running_sum = jnp.sum(weights, axis=1)
    weighted = jnp.dot(
        weights.astype(jnp.bfloat16), piece_values, preferred_element_type=jnp.float32
    )
    attention = (
        (weighted / running_sum[:, None])
        .reshape(local_head, shard_rows, HEAD_SIZE)
        .transpose(1, 0, 2)
        .reshape(shard_rows, local_head * HEAD_SIZE)
        .astype(jnp.bfloat16)
    )
    mixed_rows = (residual.astype(jnp.float32) + attention.astype(jnp.float32)).astype(jnp.bfloat16)
    mixed_f = mixed_rows.astype(jnp.float32)
    square_part = jnp.sum(mixed_f * mixed_f, axis=1)
    square_block = jnp.pad(square_part.reshape(1, shard_rows), ((0, 7), (0, 128 - shard_rows)))
    (square_all,) = exchange([square_block], "exp", exp_count, True, 1)
    square_sum = jnp.sum(square_all, axis=0)[0, :shard_rows]
    normed = (mixed_f * lax.rsqrt(square_sum[:, None] / D + NORM_EPS) * norm_gain[None, :]).astype(
        jnp.bfloat16
    )
    expert_count = ctx_count * EXP_ROW
    capacity = 2 * shard_rows * TOPK // expert_count
    flat_ids = expert_ids.reshape(-1)
    onehot = (flat_ids[:, None] == jnp.arange(expert_count, dtype=jnp.int32)[None, :]).astype(
        jnp.int32
    )
    slot_rank = jnp.sum((jnp.cumsum(onehot, axis=0) - onehot) * onehot, axis=1)
    slot_index = flat_ids * capacity + slot_rank
    source_rows = jnp.arange(shard_rows * TOPK, dtype=jnp.int32) // TOPK
    outgoing = (
        jnp.zeros((expert_count * capacity, normed.shape[1]), jnp.bfloat16)
        .at[slot_index]
        .set(normed[source_rows])
    )
    outgoing = outgoing.reshape(ctx_count, EXP_ROW, capacity, normed.shape[1])
    gate_recv, up_recv = dispatch_reduce(outgoing, gate_weight, up_weight, ctx_count, exp_count, 2)
    gate_full = jnp.sum(gate_recv.astype(jnp.float32), axis=0)
    up_full = jnp.sum(up_recv.astype(jnp.float32), axis=0)
    hidden_mine = (jax.nn.silu(gate_full) * up_full).astype(jnp.bfloat16)
    (hidden,) = exchange([hidden_mine], "exp", exp_count, True, 4)
    expert_out = jnp.einsum(
        "jksh,khd->jksd", hidden, down_weight, preferred_element_type=jnp.float32
    ).astype(jnp.bfloat16)
    per_chunk = ctx_count // exp_count
    expert_out = (
        expert_out.reshape(exp_count, EXP_ROW, per_chunk, capacity, normed.shape[1])
        .transpose(0, 2, 1, 3, 4)
        .reshape(ctx_count, EXP_ROW, capacity, normed.shape[1])
    )
    (returned,) = exchange([expert_out], "ctx", ctx_count, False, 5)
    flat_back = returned.reshape(expert_count * capacity, normed.shape[1])
    picked = flat_back[slot_index].astype(jnp.float32).reshape(shard_rows, TOPK, normed.shape[1])
    routed_sum = jnp.sum(route_weight[:, :, None] * picked, axis=1)
    return (mixed_f + routed_sum).astype(jnp.bfloat16)


def solution(mesh):
    placed = (
        P(("rep", "ctx"), "exp"),
        P(("rep", "ctx"), None),
        P(("rep", "ctx"), None),
        P("rep"),
        P(("rep", "ctx"), "exp"),
        P("exp"),
        P(("rep", "ctx"), None),
        P(("rep", "ctx"), None),
        P("ctx", "exp", None),
        P("ctx", "exp", None),
        P("ctx", None, "exp"),
    )
    return jax.shard_map(
        local, mesh=mesh, in_specs=placed, out_specs=P(("rep", "ctx"), "exp"), check_vma=False
    )
```

```python
import functools
import math

import jax
import jax.numpy as jnp
from jax import lax
from jax.experimental import pallas as pl
from jax.experimental.pallas import tpu as pltpu
from jax.sharding import PartitionSpec as P

D = 4096
QUERY_HEADS = 32
KEY_VALUE_HEADS = 2
HEAD_SIZE = 128
TOPK = 8
EXP_ROW = 2

MASKED_SCORE = -1e30
NORM_EPS = 1e-06
MESH = pl.DeviceIdType.MESH


def exchange_kernel(axis, n, gather, n_in, *refs):
    ins, outs = refs[:n_in], refs[n_in : 2 * n_in]
    send_sem, recv_sem = refs[2 * n_in], refs[2 * n_in + 1]
    me = lax.axis_index(axis)
    barrier = pltpu.get_barrier_semaphore()
    for k in range(1, n):
        pl.semaphore_signal(
            barrier, inc=1, device_id={axis: lax.rem(me + k, n)}, device_id_type=MESH
        )
    pl.semaphore_wait(barrier, n - 1)
    copies = []
    for k in range(1, n):
        peer = lax.rem(me + k, n)
        for i in range(n_in):
            copy = pltpu.make_async_remote_copy(
                src_ref=ins[i] if gather else ins[i].at[peer],
                dst_ref=outs[i].at[me],
                send_sem=send_sem.at[i, k],
                recv_sem=recv_sem.at[i, k],
                device_id={axis: peer},
                device_id_type=MESH,
            )
            copy.start()
            copies.append(copy)
    for i in range(n_in):
        outs[i][me] = ins[i][...] if gather else ins[i][me]
    for copy in copies:
        copy.wait()


def exchange(xs, axis, n, gather, collective_id):
    n_in = len(xs)
    out_shape = [
        jax.ShapeDtypeStruct((n,) + (x.shape if gather else x.shape[1:]), x.dtype) for x in xs
    ]
    nbytes = sum(x.size * x.dtype.itemsize for x in xs) * (n if gather else 1)
    return pl.pallas_call(
        functools.partial(exchange_kernel, axis, n, gather, n_in),
        out_shape=out_shape,
        in_specs=[pl.BlockSpec(memory_space=pltpu.VMEM)] * n_in,
        out_specs=[pl.BlockSpec(memory_space=pltpu.VMEM)] * n_in,
        scratch_shapes=[
            pltpu.SemaphoreType.DMA((n_in, n)),
            pltpu.SemaphoreType.DMA((n_in, n)),
        ],
        compiler_params=pltpu.CompilerParams(collective_id=collective_id, has_side_effects=True),
        cost_estimate=pl.CostEstimate(flops=0, bytes_accessed=2 * nbytes, transcendentals=0),
    )(*xs)


def dispatch_reduce_kernel(n_ctx, n_exp, *refs):
    (outgoing, gate_w, up_w, gate_recv, up_recv, incoming, gate_stage, up_stage,
     d_send, d_recv, r_send, r_recv) = refs
    per_chunk = n_ctx // n_exp
    me_c = lax.axis_index("ctx")
    me_e = lax.axis_index("exp")
    plane = me_c // per_chunk
    barrier = pltpu.get_barrier_semaphore()
    for k in range(1, n_ctx):
        pl.semaphore_signal(
            barrier, inc=1, device_id={"ctx": lax.rem(me_c + k, n_ctx)}, device_id_type=MESH
        )
    for k in range(1, n_exp):
        pl.semaphore_signal(
            barrier, inc=1, device_id={"exp": lax.rem(me_e + k, n_exp)}, device_id_type=MESH
        )
    pl.semaphore_wait(barrier, n_ctx + n_exp - 2)

    def dispatch_copy(p):
        return pltpu.make_async_remote_copy(
            src_ref=outgoing.at[p],
            dst_ref=incoming.at[me_c],
            send_sem=d_send.at[p],
            recv_sem=d_recv.at[me_c],
            device_id={"ctx": p},
            device_id_type=MESH,
        )

    for t in range(n_exp):
        z_r = lax.rem(plane + 2 * n_exp - me_e - t, n_exp)
        for y in range(per_chunk):
            p = z_r * per_chunk + y

            @pl.when(p != me_c)
            def _():
                dispatch_copy(p).start()

            @pl.when(p == me_c)
            def _():
                pltpu.make_async_copy(outgoing.at[p], incoming.at[p], d_recv.at[p]).start()

    parts = ((gate_w, gate_stage, gate_recv), (up_w, up_stage, up_recv))

    def reduce_copy(j, which):
        _, stage, recv = parts[which]
        return pltpu.make_async_remote_copy(
            src_ref=stage.at[j],
            dst_ref=recv.at[me_e],
            send_sem=r_send.at[j, which],
            recv_sem=r_recv.at[me_e, which],
            device_id={"exp": j},
            device_id_type=MESH,
        )

    rows = gate_stage.shape[2]
    for t in range(n_exp):
        j = lax.rem(plane + me_e + t, n_exp)
        for y in range(per_chunk):
            s = j * per_chunk + y
            pltpu.make_async_copy(incoming.at[s], incoming.at[s], d_recv.at[s]).wait()
        first = pl.multiple_of(j * per_chunk, per_chunk)
        for k in range(EXP_ROW):
            x = incoming[pl.ds(first, per_chunk), k].reshape(rows, incoming.shape[-1])
            for w, stage, _ in parts:
                stage[j, k] = jnp.dot(x, w[k], preferred_element_type=jnp.float32).astype(
                    stage.dtype
                )

        @pl.when(j != me_e)
        def _():
            for which in range(2):
                reduce_copy(j, which).start()

        @pl.when(j == me_e)
        def _():
            for which, (_, stage, recv) in enumerate(parts):
                pltpu.make_async_copy(stage.at[j], recv.at[j], r_recv.at[j, which]).start()

    for s in range(n_exp):
        for which, (_, _, recv) in enumerate(parts):
            pltpu.make_async_copy(recv.at[s], recv.at[s], r_recv.at[s, which]).wait()
    for j in range(n_exp):

        @pl.when(j != me_e)
        def _():
            for which in range(2):
                reduce_copy(j, which).wait_send()

    for p in range(n_ctx):

        @pl.when(p != me_c)
        def _():
            dispatch_copy(p).wait_send()


def dispatch_reduce(outgoing, gate_weight, up_weight, n_ctx, n_exp, collective_id):
    hid = gate_weight.shape[-1]
    slots = outgoing.shape[0] * outgoing.shape[2] // n_exp
    recv_shape = jax.ShapeDtypeStruct((n_exp, EXP_ROW, slots, hid), jnp.bfloat16)
    flops = 2 * 2 * outgoing.size * hid
    nbytes = 2 * outgoing.size * 2 + 4 * gate_weight.size * 2 + 4 * n_exp * EXP_ROW * slots * hid * 2
    return pl.pallas_call(
        functools.partial(dispatch_reduce_kernel, n_ctx, n_exp),
        out_shape=[recv_shape, recv_shape],
        in_specs=[pl.BlockSpec(memory_space=pltpu.VMEM)] * 3,
        out_specs=[pl.BlockSpec(memory_space=pltpu.VMEM)] * 2,
        scratch_shapes=[
            pltpu.VMEM(outgoing.shape, outgoing.dtype),
            pltpu.VMEM(recv_shape.shape, jnp.bfloat16),
            pltpu.VMEM(recv_shape.shape, jnp.bfloat16),
            pltpu.SemaphoreType.DMA((n_ctx,)),
            pltpu.SemaphoreType.DMA((n_ctx,)),
            pltpu.SemaphoreType.DMA((n_exp, 2)),
            pltpu.SemaphoreType.DMA((n_exp, 2)),
        ],
        compiler_params=pltpu.CompilerParams(collective_id=collective_id, has_side_effects=True),
        cost_estimate=pl.CostEstimate(flops=flops, bytes_accessed=nbytes, transcendentals=0),
    )(outgoing, gate_weight, up_weight)


def kv_gather_kernel(n_ctx, n_exp, group, *refs):
    block, kv_all, s1_send, s1_recv, s2_send, s2_recv = refs
    per_plane = n_ctx // n_exp
    planes = n_ctx // per_plane
    me_c = lax.axis_index("ctx")
    me_e = lax.axis_index("exp")
    q = lax.rem(me_e, group)
    head_base = me_e - q
    plane = me_c // per_plane
    barrier = pltpu.get_barrier_semaphore()
    for k in range(1, n_ctx):
        pl.semaphore_signal(
            barrier, inc=1, device_id={"ctx": lax.rem(me_c + k, n_ctx)}, device_id_type=MESH
        )
    for k in range(1, group):
        pl.semaphore_signal(
            barrier, inc=1, device_id={"exp": head_base + lax.rem(q + k, group)}, device_id_type=MESH
        )
    pl.semaphore_wait(barrier, n_ctx + group - 2)

    def first_copy(p):
        return pltpu.make_async_remote_copy(
            src_ref=block,
            dst_ref=kv_all.at[me_c],
            send_sem=s1_send.at[p],
            recv_sem=s1_recv.at[me_c],
            device_id={"ctx": p},
            device_id_type=MESH,
        )

    halves = 2
    for h in range(halves):
        z_r = lax.rem(plane + 2 * planes - q - h * (planes // halves), planes)
        for y in range(per_plane):
            p = z_r * per_plane + y

            @pl.when(p != me_c)
            def _():
                first_copy(p).start()

            @pl.when(p == me_c)
            def _():
                pltpu.make_async_copy(block, kv_all.at[p], s1_recv.at[p]).start()

    def second_copy(h, r):
        first = pl.multiple_of(lax.rem(plane + q + h * (planes // halves), planes) * per_plane, per_plane)
        return pltpu.make_async_remote_copy(
            src_ref=kv_all.at[pl.ds(first, per_plane)],
            dst_ref=kv_all.at[pl.ds(first, per_plane)],
            send_sem=s2_send.at[r, h],
            recv_sem=s2_recv.at[r, h],
            device_id={"exp": head_base + lax.rem(q + r, group)},
            device_id_type=MESH,
        )

    for h in range(halves):
        z_s = lax.rem(plane + q + h * (planes // halves), planes)
        for y in range(per_plane):
            s = z_s * per_plane + y
            pltpu.make_async_copy(kv_all.at[s], kv_all.at[s], s1_recv.at[s]).wait()
        for r in range(1, group):
            second_copy(h, r).start()
    for h in range(halves):
        for r in range(1, group):
            second_copy(h, r).wait_recv()
    for h in range(halves):
        for r in range(1, group):
            second_copy(h, r).wait_send()
    for h in range(halves):
        z_r = lax.rem(plane + 2 * planes - q - h * (planes // halves), planes)
        for y in range(per_plane):
            p = z_r * per_plane + y

            @pl.when(p != me_c)
            def _():
                first_copy(p).wait_send()


def kv_gather(block, n_ctx, n_exp, group, collective_id):
    nbytes = block.size * block.dtype.itemsize * n_ctx
    return pl.pallas_call(
        functools.partial(kv_gather_kernel, n_ctx, n_exp, group),
        out_shape=jax.ShapeDtypeStruct((n_ctx,) + block.shape, block.dtype),
        in_specs=[pl.BlockSpec(memory_space=pltpu.VMEM)],
        out_specs=pl.BlockSpec(memory_space=pltpu.VMEM),
        scratch_shapes=[
            pltpu.SemaphoreType.DMA((n_ctx,)),
            pltpu.SemaphoreType.DMA((n_ctx,)),
            pltpu.SemaphoreType.DMA((group, 2)),
            pltpu.SemaphoreType.DMA((group, 2)),
        ],
        compiler_params=pltpu.CompilerParams(collective_id=collective_id, has_side_effects=True),
        cost_estimate=pl.CostEstimate(flops=0, bytes_accessed=2 * nbytes, transcendentals=0),
    )(block)


def gather_return_kernel(n_ctx, n_exp, *refs):
    hidden_mine, down_w, returned, hidden_all, ret_stage, a_send, a_recv, b_send, b_recv = refs
    per_chunk = n_ctx // n_exp
    me_c = lax.axis_index("ctx")
    me_e = lax.axis_index("exp")
    plane = me_c // per_chunk
    barrier = pltpu.get_barrier_semaphore()
    for k in range(1, n_ctx):
        pl.semaphore_signal(
            barrier, inc=1, device_id={"ctx": lax.rem(me_c + k, n_ctx)}, device_id_type=MESH
        )
    for k in range(1, n_exp):
        pl.semaphore_signal(
            barrier, inc=1, device_id={"exp": lax.rem(me_e + k, n_exp)}, device_id_type=MESH
        )
    pl.semaphore_wait(barrier, n_ctx + n_exp - 2)

    def gather_copy(r):
        return pltpu.make_async_remote_copy(
            src_ref=hidden_mine,
            dst_ref=hidden_all.at[me_e],
            send_sem=a_send.at[r],
            recv_sem=a_recv.at[me_e],
            device_id={"exp": r},
            device_id_type=MESH,
        )

    for t in range(n_exp):
        r = lax.rem(me_e + 2 * n_exp - plane - t, n_exp)

        @pl.when(r != me_e)
        def _():
            gather_copy(r).start()

        @pl.when(r == me_e)
        def _():
            pltpu.make_async_copy(hidden_mine, hidden_all.at[r], a_recv.at[r]).start()

    def return_copy(s):
        return pltpu.make_async_remote_copy(
            src_ref=ret_stage.at[s],
            dst_ref=returned.at[me_c],
            send_sem=b_send.at[s],
            recv_sem=b_recv.at[me_c],
            device_id={"ctx": s},
            device_id_type=MESH,
        )

    rows = hidden_all.shape[2]
    for t in range(n_exp):
        j = lax.rem(me_e + plane + t, n_exp)
        pltpu.make_async_copy(hidden_all.at[j], hidden_all.at[j], a_recv.at[j]).wait()
        first = pl.multiple_of(j * per_chunk, per_chunk)
        for k in range(EXP_ROW):
            out = jnp.dot(hidden_all[j, k], down_w[k], preferred_element_type=jnp.float32)
            ret_stage[pl.ds(first, per_chunk), k] = out.astype(ret_stage.dtype).reshape(
                per_chunk, rows // per_chunk, out.shape[-1]
            )
        for y in range(per_chunk):
            s = j * per_chunk + y

            @pl.when(s != me_c)
            def _():
                return_copy(s).start()

            @pl.when(s == me_c)
            def _():
                pltpu.make_async_copy(ret_stage.at[s], returned.at[s], b_recv.at[s]).start()

    for s in range(n_ctx):
        pltpu.make_async_copy(returned.at[s], returned.at[s], b_recv.at[s]).wait()
    for r in range(n_exp):

        @pl.when(r != me_e)
        def _():
            gather_copy(r).wait_send()

    for s in range(n_ctx):

        @pl.when(s != me_c)
        def _():
            return_copy(s).wait_send()


def gather_return(hidden_mine, down_weight, n_ctx, n_exp, collective_id):
    hid, width = down_weight.shape[1:]
    slots = hidden_mine.shape[1]
    ret_shape = (n_ctx, EXP_ROW, slots * n_exp // n_ctx, width)
    flops = 2 * n_exp * hidden_mine.size * width
    nbytes = 2 * n_exp * hidden_mine.size * 2 + down_weight.size * 2 + 4 * n_ctx * EXP_ROW * slots * width * 2 // n_exp
    return pl.pallas_call(
        functools.partial(gather_return_kernel, n_ctx, n_exp),
        out_shape=jax.ShapeDtypeStruct(ret_shape, jnp.bfloat16),
        in_specs=[pl.BlockSpec(memory_space=pltpu.VMEM)] * 2,
        out_specs=pl.BlockSpec(memory_space=pltpu.VMEM),
        scratch_shapes=[
            pltpu.VMEM((n_exp,) + hidden_mine.shape, jnp.bfloat16),
            pltpu.VMEM(ret_shape, jnp.bfloat16),
            pltpu.SemaphoreType.DMA((n_exp,)),
            pltpu.SemaphoreType.DMA((n_exp,)),
            pltpu.SemaphoreType.DMA((n_ctx,)),
            pltpu.SemaphoreType.DMA((n_ctx,)),
        ],
        compiler_params=pltpu.CompilerParams(collective_id=collective_id, has_side_effects=True),
        cost_estimate=pl.CostEstimate(flops=flops, bytes_accessed=nbytes, transcendentals=0),
    )(hidden_mine, down_weight)


def local(
    queries,
    key_rows,
    value_head_rows,
    block_order,
    residual,
    norm_gain,
    expert_ids,
    route_weight,
    gate_weight,
    up_weight,
    down_weight,
):
    shard_rows = queries.shape[0]
    ctx_count = lax.axis_size("ctx")
    exp_count = lax.axis_size("exp")
    local_head = queries.shape[1] // HEAD_SIZE
    expert_index = lax.axis_index("exp")
    ctx_index = lax.axis_index("ctx")
    key_value_head = expert_index * local_head // (QUERY_HEADS // KEY_VALUE_HEADS)
    my_keys = lax.dynamic_slice_in_dim(key_rows, key_value_head * HEAD_SIZE, HEAD_SIZE, 1)
    my_values = lax.dynamic_slice_in_dim(value_head_rows, key_value_head * HEAD_SIZE, HEAD_SIZE, 1)
    block_ids = jnp.arange(ctx_count, dtype=jnp.int32)
    own_block = jnp.sum(jnp.where(block_ids == ctx_index, block_order, 0))
    local_rows = jnp.arange(shard_rows, dtype=jnp.int32)
    query_pos = jnp.tile(own_block * shard_rows + local_rows, local_head)
    query_flat = (
        queries.reshape(shard_rows, local_head, HEAD_SIZE)
        .transpose(1, 0, 2)
        .reshape(local_head * shard_rows, HEAD_SIZE)
    )
    inv_scale = 1.0 / math.sqrt(HEAD_SIZE)
    key_value_all = kv_gather(
        jnp.concatenate([my_keys, my_values], axis=1),
        ctx_count,
        exp_count,
        QUERY_HEADS // KEY_VALUE_HEADS // local_head,
        0,
    )
    key_value_all = key_value_all.reshape(ctx_count * shard_rows, 2 * HEAD_SIZE)
    piece_keys = key_value_all[:, :HEAD_SIZE]
    piece_values = key_value_all[:, HEAD_SIZE:]
    key_index = jnp.arange(piece_keys.shape[0], dtype=jnp.int32)
    owner_shard = key_index // shard_rows
    key_block = jnp.sum(
        jnp.where(owner_shard[:, None] == block_ids[None, :], block_order[None, :], 0), axis=1
    )
    key_pos = key_block * shard_rows + key_index % shard_rows
    visible = key_pos[None, :] <= query_pos[:, None]
    scores = (
        lax.dot_general(
            query_flat, piece_keys, (((1,), (1,)), ((), ())), preferred_element_type=jnp.float32
        )
        * inv_scale
    )
    scores = jnp.where(visible, scores, MASKED_SCORE)
    newest = jnp.max(scores, axis=1)
    weights = jnp.where(visible, jnp.exp(scores - newest[:, None]), 0.0)
    running_sum = jnp.sum(weights, axis=1)
    weighted = jnp.dot(
        weights.astype(jnp.bfloat16), piece_values, preferred_element_type=jnp.float32
    )
    attention = (
        (weighted / running_sum[:, None])
        .reshape(local_head, shard_rows, HEAD_SIZE)
        .transpose(1, 0, 2)
        .reshape(shard_rows, local_head * HEAD_SIZE)
        .astype(jnp.bfloat16)
    )
    mixed_rows = (residual.astype(jnp.float32) + attention.astype(jnp.float32)).astype(jnp.bfloat16)
    mixed_f = mixed_rows.astype(jnp.float32)
    square_part = jnp.sum(mixed_f * mixed_f, axis=1)
    square_block = jnp.pad(square_part.reshape(1, shard_rows), ((0, 7), (0, 128 - shard_rows)))
    (square_all,) = exchange([square_block], "exp", exp_count, True, 1)
    square_sum = jnp.sum(square_all, axis=0)[0, :shard_rows]
    normed = (mixed_f * lax.rsqrt(square_sum[:, None] / D + NORM_EPS) * norm_gain[None, :]).astype(
        jnp.bfloat16
    )
    expert_count = ctx_count * EXP_ROW
    capacity = 2 * shard_rows * TOPK // expert_count
    flat_ids = expert_ids.reshape(-1)
    onehot = (flat_ids[:, None] == jnp.arange(expert_count, dtype=jnp.int32)[None, :]).astype(
        jnp.int32
    )
    slot_rank = jnp.sum((jnp.cumsum(onehot, axis=0) - onehot) * onehot, axis=1)
    slot_index = flat_ids * capacity + slot_rank
    source_rows = jnp.arange(shard_rows * TOPK, dtype=jnp.int32) // TOPK
    outgoing = (
        jnp.zeros((expert_count * capacity, normed.shape[1]), jnp.bfloat16)
        .at[slot_index]
        .set(normed[source_rows])
    )
    outgoing = outgoing.reshape(ctx_count, EXP_ROW, capacity, normed.shape[1])
    gate_recv, up_recv = dispatch_reduce(outgoing, gate_weight, up_weight, ctx_count, exp_count, 2)
    gate_full = jnp.sum(gate_recv.astype(jnp.float32), axis=0)
    up_full = jnp.sum(up_recv.astype(jnp.float32), axis=0)
    hidden_mine = (jax.nn.silu(gate_full) * up_full).astype(jnp.bfloat16)
    returned = gather_return(hidden_mine, down_weight, ctx_count, exp_count, 4)
    flat_back = returned.reshape(expert_count * capacity, normed.shape[1])
    picked = flat_back[slot_index].astype(jnp.float32).reshape(shard_rows, TOPK, normed.shape[1])
    routed_sum = jnp.sum(route_weight[:, :, None] * picked, axis=1)
    return (mixed_f + routed_sum).astype(jnp.bfloat16)


def solution(mesh):
    placed = (
        P(("rep", "ctx"), "exp"),
        P(("rep", "ctx"), None),
        P(("rep", "ctx"), None),
        P("rep"),
        P(("rep", "ctx"), "exp"),
        P("exp"),
        P(("rep", "ctx"), None),
        P(("rep", "ctx"), None),
        P("ctx", "exp", None),
        P("ctx", "exp", None),
        P("ctx", None, "exp"),
    )
    return jax.shard_map(
        local, mesh=mesh, in_specs=placed, out_specs=P(("rep", "ctx"), "exp"), check_vma=False
    )
```

```python
import functools
import math

import jax
import jax.numpy as jnp
from jax import lax
from jax.experimental import pallas as pl
from jax.experimental.pallas import tpu as pltpu
from jax.sharding import PartitionSpec as P

D = 4096
QUERY_HEADS = 32
KEY_VALUE_HEADS = 2
HEAD_SIZE = 128
TOPK = 8
EXP_ROW = 2

MASKED_SCORE = -1e30
NORM_EPS = 1e-06
MESH = pl.DeviceIdType.MESH


def exchange_kernel(axis, n, gather, n_in, *refs):
    ins, outs = refs[:n_in], refs[n_in : 2 * n_in]
    send_sem, recv_sem = refs[2 * n_in], refs[2 * n_in + 1]
    me = lax.axis_index(axis)
    barrier = pltpu.get_barrier_semaphore()
    for k in range(1, n):
        pl.semaphore_signal(
            barrier, inc=1, device_id={axis: lax.rem(me + k, n)}, device_id_type=MESH
        )
    pl.semaphore_wait(barrier, n - 1)
    copies = []
    for k in range(1, n):
        peer = lax.rem(me + k, n)
        for i in range(n_in):
            copy = pltpu.make_async_remote_copy(
                src_ref=ins[i] if gather else ins[i].at[peer],
                dst_ref=outs[i].at[me],
                send_sem=send_sem.at[i, k],
                recv_sem=recv_sem.at[i, k],
                device_id={axis: peer},
                device_id_type=MESH,
            )
            copy.start()
            copies.append(copy)
    for i in range(n_in):
        outs[i][me] = ins[i][...] if gather else ins[i][me]
    for copy in copies:
        copy.wait()


def exchange(xs, axis, n, gather, collective_id):
    n_in = len(xs)
    out_shape = [
        jax.ShapeDtypeStruct((n,) + (x.shape if gather else x.shape[1:]), x.dtype) for x in xs
    ]
    nbytes = sum(x.size * x.dtype.itemsize for x in xs) * (n if gather else 1)
    return pl.pallas_call(
        functools.partial(exchange_kernel, axis, n, gather, n_in),
        out_shape=out_shape,
        in_specs=[pl.BlockSpec(memory_space=pltpu.VMEM)] * n_in,
        out_specs=[pl.BlockSpec(memory_space=pltpu.VMEM)] * n_in,
        scratch_shapes=[
            pltpu.SemaphoreType.DMA((n_in, n)),
            pltpu.SemaphoreType.DMA((n_in, n)),
        ],
        compiler_params=pltpu.CompilerParams(collective_id=collective_id, has_side_effects=True),
        cost_estimate=pl.CostEstimate(flops=0, bytes_accessed=2 * nbytes, transcendentals=0),
    )(*xs)


def dispatch_reduce_kernel(n_ctx, n_exp, *refs):
    (mixed, square_block, gain, slot_rows, gate_w, up_w, gate_recv, up_recv, square_all, outgoing, incoming,
     gate_stage, up_stage, q_send, q_recv, d_send, d_recv, r_send, r_recv) = refs
    per_chunk = n_ctx // n_exp
    me_c = lax.axis_index("ctx")
    me_e = lax.axis_index("exp")
    plane = me_c // per_chunk
    barrier = pltpu.get_barrier_semaphore()
    for k in range(1, n_ctx):
        pl.semaphore_signal(
            barrier, inc=1, device_id={"ctx": lax.rem(me_c + k, n_ctx)}, device_id_type=MESH
        )
    for k in range(1, n_exp):
        pl.semaphore_signal(
            barrier, inc=1, device_id={"exp": lax.rem(me_e + k, n_exp)}, device_id_type=MESH
        )
    pl.semaphore_wait(barrier, n_ctx + n_exp - 2)

    def square_copy(r):
        return pltpu.make_async_remote_copy(
            src_ref=square_block,
            dst_ref=square_all.at[me_e],
            send_sem=q_send.at[r],
            recv_sem=q_recv.at[me_e],
            device_id={"exp": r},
            device_id_type=MESH,
        )

    for k in range(1, n_exp):
        square_copy(lax.rem(me_e + k, n_exp)).start()
    pltpu.make_async_copy(square_block, square_all.at[me_e], q_recv.at[me_e]).start()
    for s in range(n_exp):
        pltpu.make_async_copy(square_all.at[s], square_all.at[s], q_recv.at[s]).wait()
    square_sum = square_all[0]
    for s in range(1, n_exp):
        square_sum = square_sum + square_all[s]
    scale = lax.rsqrt(square_sum[:, :1] / D + NORM_EPS)
    normed = (mixed[...].astype(jnp.float32) * scale * gain[...]).astype(jnp.bfloat16)
    filled = jnp.dot(slot_rows[...], normed, preferred_element_type=jnp.float32)
    outgoing[...] = filled.astype(outgoing.dtype).reshape(outgoing.shape)

    def dispatch_copy(p):
        return pltpu.make_async_remote_copy(
            src_ref=outgoing.at[p],
            dst_ref=incoming.at[me_c],
            send_sem=d_send.at[p],
            recv_sem=d_recv.at[me_c],
            device_id={"ctx": p},
            device_id_type=MESH,
        )

    for t in range(n_exp):
        z_r = lax.rem(plane + 2 * n_exp - me_e - t, n_exp)
        for y in range(per_chunk):
            p = z_r * per_chunk + y

            @pl.when(p != me_c)
            def _():
                dispatch_copy(p).start()

            @pl.when(p == me_c)
            def _():
                pltpu.make_async_copy(outgoing.at[p], incoming.at[p], d_recv.at[p]).start()

    parts = ((gate_w, gate_stage, gate_recv), (up_w, up_stage, up_recv))

    def reduce_copy(j, which):
        _, stage, recv = parts[which]
        return pltpu.make_async_remote_copy(
            src_ref=stage.at[j],
            dst_ref=recv.at[me_e],
            send_sem=r_send.at[j, which],
            recv_sem=r_recv.at[me_e, which],
            device_id={"exp": j},
            device_id_type=MESH,
        )

    rows = gate_stage.shape[2]
    for t in range(n_exp):
        j = lax.rem(plane + me_e + t, n_exp)
        for y in range(per_chunk):
            s = j * per_chunk + y
            pltpu.make_async_copy(incoming.at[s], incoming.at[s], d_recv.at[s]).wait()
        first = pl.multiple_of(j * per_chunk, per_chunk)
        for k in range(EXP_ROW):
            x = incoming[pl.ds(first, per_chunk), k].reshape(rows, incoming.shape[-1])
            for w, stage, _ in parts:
                stage[j, k] = jnp.dot(x, w[k], preferred_element_type=jnp.float32).astype(
                    stage.dtype
                )

        @pl.when(j != me_e)
        def _():
            for which in range(2):
                reduce_copy(j, which).start()

        @pl.when(j == me_e)
        def _():
            for which, (_, stage, recv) in enumerate(parts):
                pltpu.make_async_copy(stage.at[j], recv.at[j], r_recv.at[j, which]).start()

    for s in range(n_exp):
        for which, (_, _, recv) in enumerate(parts):
            pltpu.make_async_copy(recv.at[s], recv.at[s], r_recv.at[s, which]).wait()
    for j in range(n_exp):

        @pl.when(j != me_e)
        def _():
            for which in range(2):
                reduce_copy(j, which).wait_send()

    for p in range(n_ctx):

        @pl.when(p != me_c)
        def _():
            dispatch_copy(p).wait_send()
    for r in range(n_exp):

        @pl.when(r != me_e)
        def _():
            square_copy(r).wait_send()


def dispatch_reduce(
    mixed, square_block, gain, slot_rows, out_shape, gate_weight, up_weight, n_ctx, n_exp, collective_id
):
    hid = gate_weight.shape[-1]
    size = math.prod(out_shape)
    slots = out_shape[0] * out_shape[2] // n_exp
    recv_shape = jax.ShapeDtypeStruct((n_exp, EXP_ROW, slots, hid), jnp.bfloat16)
    flops = 2 * 2 * size * hid + 2 * size * mixed.shape[0]
    nbytes = 2 * size * 2 + 4 * gate_weight.size * 2 + 4 * n_exp * EXP_ROW * slots * hid * 2
    return pl.pallas_call(
        functools.partial(dispatch_reduce_kernel, n_ctx, n_exp),
        out_shape=[recv_shape, recv_shape],
        in_specs=[pl.BlockSpec(memory_space=pltpu.VMEM)] * 6,
        out_specs=[pl.BlockSpec(memory_space=pltpu.VMEM)] * 2,
        scratch_shapes=[
            pltpu.VMEM((n_exp,) + square_block.shape, jnp.float32),
            pltpu.VMEM(out_shape, jnp.bfloat16),
            pltpu.VMEM(out_shape, jnp.bfloat16),
            pltpu.VMEM(recv_shape.shape, jnp.bfloat16),
            pltpu.VMEM(recv_shape.shape, jnp.bfloat16),
            pltpu.SemaphoreType.DMA((n_exp,)),
            pltpu.SemaphoreType.DMA((n_exp,)),
            pltpu.SemaphoreType.DMA((n_ctx,)),
            pltpu.SemaphoreType.DMA((n_ctx,)),
            pltpu.SemaphoreType.DMA((n_exp, 2)),
            pltpu.SemaphoreType.DMA((n_exp, 2)),
        ],
        compiler_params=pltpu.CompilerParams(collective_id=collective_id, has_side_effects=True),
        cost_estimate=pl.CostEstimate(flops=flops, bytes_accessed=nbytes, transcendentals=0),
    )(mixed, square_block, gain, slot_rows, gate_weight, up_weight)


def kv_gather_kernel(n_ctx, n_exp, group, *refs):
    block, kv_all, s1_send, s1_recv, s2_send, s2_recv = refs
    per_plane = n_ctx // n_exp
    planes = n_ctx // per_plane
    me_c = lax.axis_index("ctx")
    me_e = lax.axis_index("exp")
    q = lax.rem(me_e, group)
    head_base = me_e - q
    plane = me_c // per_plane
    barrier = pltpu.get_barrier_semaphore()
    for k in range(1, n_ctx):
        pl.semaphore_signal(
            barrier, inc=1, device_id={"ctx": lax.rem(me_c + k, n_ctx)}, device_id_type=MESH
        )
    for k in range(1, group):
        pl.semaphore_signal(
            barrier, inc=1, device_id={"exp": head_base + lax.rem(q + k, group)}, device_id_type=MESH
        )
    pl.semaphore_wait(barrier, n_ctx + group - 2)

    def first_copy(p):
        return pltpu.make_async_remote_copy(
            src_ref=block,
            dst_ref=kv_all.at[me_c],
            send_sem=s1_send.at[p],
            recv_sem=s1_recv.at[me_c],
            device_id={"ctx": p},
            device_id_type=MESH,
        )

    halves = 2
    for h in range(halves):
        z_r = lax.rem(plane + 2 * planes - q - h * (planes // halves), planes)
        for y in range(per_plane):
            p = z_r * per_plane + y

            @pl.when(p != me_c)
            def _():
                first_copy(p).start()

            @pl.when(p == me_c)
            def _():
                pltpu.make_async_copy(block, kv_all.at[p], s1_recv.at[p]).start()

    def second_copy(h, r):
        first = pl.multiple_of(lax.rem(plane + q + h * (planes // halves), planes) * per_plane, per_plane)
        return pltpu.make_async_remote_copy(
            src_ref=kv_all.at[pl.ds(first, per_plane)],
            dst_ref=kv_all.at[pl.ds(first, per_plane)],
            send_sem=s2_send.at[r, h],
            recv_sem=s2_recv.at[r, h],
            device_id={"exp": head_base + lax.rem(q + r, group)},
            device_id_type=MESH,
        )

    for h in range(halves):
        z_s = lax.rem(plane + q + h * (planes // halves), planes)
        for y in range(per_plane):
            s = z_s * per_plane + y
            pltpu.make_async_copy(kv_all.at[s], kv_all.at[s], s1_recv.at[s]).wait()
        for r in range(1, group):
            second_copy(h, r).start()
    for h in range(halves):
        for r in range(1, group):
            second_copy(h, r).wait_recv()
    for h in range(halves):
        for r in range(1, group):
            second_copy(h, r).wait_send()
    for h in range(halves):
        z_r = lax.rem(plane + 2 * planes - q - h * (planes // halves), planes)
        for y in range(per_plane):
            p = z_r * per_plane + y

            @pl.when(p != me_c)
            def _():
                first_copy(p).wait_send()


def kv_gather(block, n_ctx, n_exp, group, collective_id):
    nbytes = block.size * block.dtype.itemsize * n_ctx
    return pl.pallas_call(
        functools.partial(kv_gather_kernel, n_ctx, n_exp, group),
        out_shape=jax.ShapeDtypeStruct((n_ctx,) + block.shape, block.dtype),
        in_specs=[pl.BlockSpec(memory_space=pltpu.VMEM)],
        out_specs=pl.BlockSpec(memory_space=pltpu.VMEM),
        scratch_shapes=[
            pltpu.SemaphoreType.DMA((n_ctx,)),
            pltpu.SemaphoreType.DMA((n_ctx,)),
            pltpu.SemaphoreType.DMA((group, 2)),
            pltpu.SemaphoreType.DMA((group, 2)),
        ],
        compiler_params=pltpu.CompilerParams(collective_id=collective_id, has_side_effects=True),
        cost_estimate=pl.CostEstimate(flops=0, bytes_accessed=2 * nbytes, transcendentals=0),
    )(block)


def gather_return_kernel(n_ctx, n_exp, *refs):
    hidden_mine, down_w, returned, hidden_all, ret_stage, a_send, a_recv, b_send, b_recv = refs
    per_chunk = n_ctx // n_exp
    me_c = lax.axis_index("ctx")
    me_e = lax.axis_index("exp")
    plane = me_c // per_chunk
    barrier = pltpu.get_barrier_semaphore()
    for k in range(1, n_ctx):
        pl.semaphore_signal(
            barrier, inc=1, device_id={"ctx": lax.rem(me_c + k, n_ctx)}, device_id_type=MESH
        )
    for k in range(1, n_exp):
        pl.semaphore_signal(
            barrier, inc=1, device_id={"exp": lax.rem(me_e + k, n_exp)}, device_id_type=MESH
        )
    pl.semaphore_wait(barrier, n_ctx + n_exp - 2)

    def gather_copy(r):
        return pltpu.make_async_remote_copy(
            src_ref=hidden_mine,
            dst_ref=hidden_all.at[me_e],
            send_sem=a_send.at[r],
            recv_sem=a_recv.at[me_e],
            device_id={"exp": r},
            device_id_type=MESH,
        )

    for t in range(n_exp):
        r = lax.rem(me_e + 2 * n_exp - plane - t, n_exp)

        @pl.when(r != me_e)
        def _():
            gather_copy(r).start()

        @pl.when(r == me_e)
        def _():
            pltpu.make_async_copy(hidden_mine, hidden_all.at[r], a_recv.at[r]).start()

    def return_copy(s):
        return pltpu.make_async_remote_copy(
            src_ref=ret_stage.at[s],
            dst_ref=returned.at[me_c],
            send_sem=b_send.at[s],
            recv_sem=b_recv.at[me_c],
            device_id={"ctx": s},
            device_id_type=MESH,
        )

    rows = hidden_all.shape[2]
    for t in range(n_exp):
        j = lax.rem(me_e + plane + t, n_exp)
        pltpu.make_async_copy(hidden_all.at[j], hidden_all.at[j], a_recv.at[j]).wait()
        first = pl.multiple_of(j * per_chunk, per_chunk)
        for k in range(EXP_ROW):
            out = jnp.dot(hidden_all[j, k], down_w[k], preferred_element_type=jnp.float32)
            ret_stage[pl.ds(first, per_chunk), k] = out.astype(ret_stage.dtype).reshape(
                per_chunk, rows // per_chunk, out.shape[-1]
            )
        for y in range(per_chunk):
            s = j * per_chunk + y

            @pl.when(s != me_c)
            def _():
                return_copy(s).start()

            @pl.when(s == me_c)
            def _():
                pltpu.make_async_copy(ret_stage.at[s], returned.at[s], b_recv.at[s]).start()

    for s in range(n_ctx):
        pltpu.make_async_copy(returned.at[s], returned.at[s], b_recv.at[s]).wait()
    for r in range(n_exp):

        @pl.when(r != me_e)
        def _():
            gather_copy(r).wait_send()

    for s in range(n_ctx):

        @pl.when(s != me_c)
        def _():
            return_copy(s).wait_send()


def gather_return(hidden_mine, down_weight, n_ctx, n_exp, collective_id):
    hid, width = down_weight.shape[1:]
    slots = hidden_mine.shape[1]
    ret_shape = (n_ctx, EXP_ROW, slots * n_exp // n_ctx, width)
    flops = 2 * n_exp * hidden_mine.size * width
    nbytes = 2 * n_exp * hidden_mine.size * 2 + down_weight.size * 2 + 4 * n_ctx * EXP_ROW * slots * width * 2 // n_exp
    return pl.pallas_call(
        functools.partial(gather_return_kernel, n_ctx, n_exp),
        out_shape=jax.ShapeDtypeStruct(ret_shape, jnp.bfloat16),
        in_specs=[pl.BlockSpec(memory_space=pltpu.VMEM)] * 2,
        out_specs=pl.BlockSpec(memory_space=pltpu.VMEM),
        scratch_shapes=[
            pltpu.VMEM((n_exp,) + hidden_mine.shape, jnp.bfloat16),
            pltpu.VMEM(ret_shape, jnp.bfloat16),
            pltpu.SemaphoreType.DMA((n_exp,)),
            pltpu.SemaphoreType.DMA((n_exp,)),
            pltpu.SemaphoreType.DMA((n_ctx,)),
            pltpu.SemaphoreType.DMA((n_ctx,)),
        ],
        compiler_params=pltpu.CompilerParams(collective_id=collective_id, has_side_effects=True),
        cost_estimate=pl.CostEstimate(flops=flops, bytes_accessed=nbytes, transcendentals=0),
    )(hidden_mine, down_weight)


def local(
    queries,
    key_rows,
    value_head_rows,
    block_order,
    residual,
    norm_gain,
    expert_ids,
    route_weight,
    gate_weight,
    up_weight,
    down_weight,
):
    shard_rows = queries.shape[0]
    ctx_count = lax.axis_size("ctx")
    exp_count = lax.axis_size("exp")
    local_head = queries.shape[1] // HEAD_SIZE
    expert_index = lax.axis_index("exp")
    ctx_index = lax.axis_index("ctx")
    key_value_head = expert_index * local_head // (QUERY_HEADS // KEY_VALUE_HEADS)
    my_keys = lax.dynamic_slice_in_dim(key_rows, key_value_head * HEAD_SIZE, HEAD_SIZE, 1)
    my_values = lax.dynamic_slice_in_dim(value_head_rows, key_value_head * HEAD_SIZE, HEAD_SIZE, 1)
    block_ids = jnp.arange(ctx_count, dtype=jnp.int32)
    own_block = jnp.sum(jnp.where(block_ids == ctx_index, block_order, 0))
    local_rows = jnp.arange(shard_rows, dtype=jnp.int32)
    query_pos = jnp.tile(own_block * shard_rows + local_rows, local_head)
    query_flat = (
        queries.reshape(shard_rows, local_head, HEAD_SIZE)
        .transpose(1, 0, 2)
        .reshape(local_head * shard_rows, HEAD_SIZE)
    )
    inv_scale = 1.0 / math.sqrt(HEAD_SIZE)
    key_value_all = kv_gather(
        jnp.concatenate([my_keys, my_values], axis=1),
        ctx_count,
        exp_count,
        QUERY_HEADS // KEY_VALUE_HEADS // local_head,
        0,
    )
    key_value_all = key_value_all.reshape(ctx_count * shard_rows, 2 * HEAD_SIZE)
    piece_keys = key_value_all[:, :HEAD_SIZE]
    piece_values = key_value_all[:, HEAD_SIZE:]
    key_index = jnp.arange(piece_keys.shape[0], dtype=jnp.int32)
    owner_shard = key_index // shard_rows
    key_block = jnp.sum(
        jnp.where(owner_shard[:, None] == block_ids[None, :], block_order[None, :], 0), axis=1
    )
    key_pos = key_block * shard_rows + key_index % shard_rows
    visible = key_pos[None, :] <= query_pos[:, None]
    scores = (
        lax.dot_general(
            query_flat, piece_keys, (((1,), (1,)), ((), ())), preferred_element_type=jnp.float32
        )
        * inv_scale
    )
    scores = jnp.where(visible, scores, MASKED_SCORE)
    newest = jnp.max(scores, axis=1)
    weights = jnp.where(visible, jnp.exp(scores - newest[:, None]), 0.0)
    running_sum = jnp.sum(weights, axis=1)
    weighted = jnp.dot(
        weights.astype(jnp.bfloat16), piece_values, preferred_element_type=jnp.float32
    )
    attention = (
        (weighted / running_sum[:, None])
        .reshape(local_head, shard_rows, HEAD_SIZE)
        .transpose(1, 0, 2)
        .reshape(shard_rows, local_head * HEAD_SIZE)
        .astype(jnp.bfloat16)
    )
    mixed_rows = (residual.astype(jnp.float32) + attention.astype(jnp.float32)).astype(jnp.bfloat16)
    mixed_f = mixed_rows.astype(jnp.float32)
    square_part = jnp.sum(mixed_f * mixed_f, axis=1)
    square_block = jnp.broadcast_to(square_part[:, None], (shard_rows, 128))
    expert_count = ctx_count * EXP_ROW
    capacity = 2 * shard_rows * TOPK // expert_count
    flat_ids = expert_ids.reshape(-1)
    onehot = (flat_ids[:, None] == jnp.arange(expert_count, dtype=jnp.int32)[None, :]).astype(
        jnp.int32
    )
    slot_rank = jnp.sum((jnp.cumsum(onehot, axis=0) - onehot) * onehot, axis=1)
    slot_index = flat_ids * capacity + slot_rank
    slot_total = expert_count * capacity
    slot_rows = jnp.any(
        slot_index.reshape(shard_rows, TOPK)[None, :, :]
        == jnp.arange(slot_total, dtype=jnp.int32)[:, None, None],
        axis=2,
    ).astype(jnp.bfloat16)
    gate_recv, up_recv = dispatch_reduce(
        mixed_rows,
        square_block,
        norm_gain.reshape(1, -1),
        slot_rows,
        (ctx_count, EXP_ROW, capacity, mixed_rows.shape[1]),
        gate_weight,
        up_weight,
        ctx_count,
        exp_count,
        2,
    )
    gate_full = jnp.sum(gate_recv.astype(jnp.float32), axis=0)
    up_full = jnp.sum(up_recv.astype(jnp.float32), axis=0)
    hidden_mine = (jax.nn.silu(gate_full) * up_full).astype(jnp.bfloat16)
    returned = gather_return(hidden_mine, down_weight, ctx_count, exp_count, 4)
    flat_back = returned.reshape(expert_count * capacity, mixed_rows.shape[1])
    picked = flat_back[slot_index].astype(jnp.float32).reshape(shard_rows, TOPK, mixed_rows.shape[1])
    routed_sum = jnp.sum(route_weight[:, :, None] * picked, axis=1)
    return (mixed_f + routed_sum).astype(jnp.bfloat16)


def solution(mesh):
    placed = (
        P(("rep", "ctx"), "exp"),
        P(("rep", "ctx"), None),
        P(("rep", "ctx"), None),
        P("rep"),
        P(("rep", "ctx"), "exp"),
        P("exp"),
        P(("rep", "ctx"), None),
        P(("rep", "ctx"), None),
        P("ctx", "exp", None),
        P("ctx", "exp", None),
        P("ctx", None, "exp"),
    )
    return jax.shard_map(
        local, mesh=mesh, in_specs=placed, out_specs=P(("rep", "ctx"), "exp"), check_vma=False
    )
```

```python
import functools
import math

import jax
import jax.numpy as jnp
from jax import lax
from jax.experimental import pallas as pl
from jax.experimental.pallas import tpu as pltpu
from jax.sharding import PartitionSpec as P

D = 4096
QUERY_HEADS = 32
KEY_VALUE_HEADS = 2
HEAD_SIZE = 128
TOPK = 8
EXP_ROW = 2

MASKED_SCORE = -1e30
NORM_EPS = 1e-06
MESH = pl.DeviceIdType.MESH
AHEAD = 2


def exchange_kernel(axis, n, gather, n_in, *refs):
    ins, outs = refs[:n_in], refs[n_in : 2 * n_in]
    send_sem, recv_sem = refs[2 * n_in], refs[2 * n_in + 1]
    me = lax.axis_index(axis)
    barrier = pltpu.get_barrier_semaphore()
    for k in range(1, n):
        pl.semaphore_signal(
            barrier, inc=1, device_id={axis: lax.rem(me + k, n)}, device_id_type=MESH
        )
    pl.semaphore_wait(barrier, n - 1)
    copies = []
    for k in range(1, n):
        peer = lax.rem(me + k, n)
        for i in range(n_in):
            copy = pltpu.make_async_remote_copy(
                src_ref=ins[i] if gather else ins[i].at[peer],
                dst_ref=outs[i].at[me],
                send_sem=send_sem.at[i, k],
                recv_sem=recv_sem.at[i, k],
                device_id={axis: peer},
                device_id_type=MESH,
            )
            copy.start()
            copies.append(copy)
    for i in range(n_in):
        outs[i][me] = ins[i][...] if gather else ins[i][me]
    for copy in copies:
        copy.wait()


def exchange(xs, axis, n, gather, collective_id):
    n_in = len(xs)
    out_shape = [
        jax.ShapeDtypeStruct((n,) + (x.shape if gather else x.shape[1:]), x.dtype) for x in xs
    ]
    nbytes = sum(x.size * x.dtype.itemsize for x in xs) * (n if gather else 1)
    return pl.pallas_call(
        functools.partial(exchange_kernel, axis, n, gather, n_in),
        out_shape=out_shape,
        in_specs=[pl.BlockSpec(memory_space=pltpu.VMEM)] * n_in,
        out_specs=[pl.BlockSpec(memory_space=pltpu.VMEM)] * n_in,
        scratch_shapes=[
            pltpu.SemaphoreType.DMA((n_in, n)),
            pltpu.SemaphoreType.DMA((n_in, n)),
        ],
        compiler_params=pltpu.CompilerParams(collective_id=collective_id, has_side_effects=True),
        cost_estimate=pl.CostEstimate(flops=0, bytes_accessed=2 * nbytes, transcendentals=0),
    )(*xs)


def dispatch_reduce_kernel(n_ctx, n_exp, *refs):
    (mixed, square_block, gain, slot_rows, gate_w, up_w, gate_recv, up_recv, square_all, outgoing, incoming,
     gate_stage, up_stage, q_send, q_recv, d_send, d_recv, r_send, r_recv) = refs
    per_chunk = n_ctx // n_exp
    me_c = lax.axis_index("ctx")
    me_e = lax.axis_index("exp")
    plane = me_c // per_chunk
    barrier = pltpu.get_barrier_semaphore()
    for k in range(1, n_ctx):
        pl.semaphore_signal(
            barrier, inc=1, device_id={"ctx": lax.rem(me_c + k, n_ctx)}, device_id_type=MESH
        )
    for k in range(1, n_exp):
        pl.semaphore_signal(
            barrier, inc=1, device_id={"exp": lax.rem(me_e + k, n_exp)}, device_id_type=MESH
        )
    pl.semaphore_wait(barrier, n_ctx + n_exp - 2)

    def square_copy(r):
        return pltpu.make_async_remote_copy(
            src_ref=square_block,
            dst_ref=square_all.at[me_e],
            send_sem=q_send.at[r],
            recv_sem=q_recv.at[me_e],
            device_id={"exp": r},
            device_id_type=MESH,
        )

    for k in range(1, n_exp):
        square_copy(lax.rem(me_e + k, n_exp)).start()
    pltpu.make_async_copy(square_block, square_all.at[me_e], q_recv.at[me_e]).start()
    for s in range(n_exp):
        pltpu.make_async_copy(square_all.at[s], square_all.at[s], q_recv.at[s]).wait()
    square_sum = square_all[0]
    for s in range(1, n_exp):
        square_sum = square_sum + square_all[s]
    scale = lax.rsqrt(square_sum[:, :1] / D + NORM_EPS)
    normed = (mixed[...].astype(jnp.float32) * scale * gain[...]).astype(jnp.bfloat16)
    filled = jnp.dot(slot_rows[...], normed, preferred_element_type=jnp.float32)
    outgoing[...] = filled.astype(outgoing.dtype).reshape(outgoing.shape)

    def dispatch_copy(p):
        return pltpu.make_async_remote_copy(
            src_ref=outgoing.at[p],
            dst_ref=incoming.at[me_c],
            send_sem=d_send.at[p],
            recv_sem=d_recv.at[me_c],
            device_id={"ctx": p},
            device_id_type=MESH,
        )

    def dispatch_wave(t):
        z_r = lax.rem(plane + 2 * n_exp - me_e - t, n_exp)
        for y in range(per_chunk):
            p = z_r * per_chunk + y

            @pl.when(p != me_c)
            def _():
                dispatch_copy(p).start()

            @pl.when(p == me_c)
            def _():
                pltpu.make_async_copy(outgoing.at[p], incoming.at[p], d_recv.at[p]).start()

    for t in range(AHEAD):
        dispatch_wave(t)

    parts = ((gate_w, gate_stage, gate_recv), (up_w, up_stage, up_recv))

    def reduce_copy(j, which):
        _, stage, recv = parts[which]
        return pltpu.make_async_remote_copy(
            src_ref=stage.at[j],
            dst_ref=recv.at[me_e],
            send_sem=r_send.at[j, which],
            recv_sem=r_recv.at[me_e, which],
            device_id={"exp": j},
            device_id_type=MESH,
        )

    rows = gate_stage.shape[2]
    for t in range(n_exp):
        j = lax.rem(plane + me_e + t, n_exp)
        for y in range(per_chunk):
            s = j * per_chunk + y
            pltpu.make_async_copy(incoming.at[s], incoming.at[s], d_recv.at[s]).wait()
        first = pl.multiple_of(j * per_chunk, per_chunk)
        for k in range(EXP_ROW):
            x = incoming[pl.ds(first, per_chunk), k].reshape(rows, incoming.shape[-1])
            for w, stage, _ in parts:
                stage[j, k] = jnp.dot(x, w[k], preferred_element_type=jnp.float32).astype(
                    stage.dtype
                )

        @pl.when(j != me_e)
        def _():
            for which in range(2):
                reduce_copy(j, which).start()

        @pl.when(j == me_e)
        def _():
            for which, (_, stage, recv) in enumerate(parts):
                pltpu.make_async_copy(stage.at[j], recv.at[j], r_recv.at[j, which]).start()

        if t + AHEAD < n_exp:
            dispatch_wave(t + AHEAD)

    for s in range(n_exp):
        for which, (_, _, recv) in enumerate(parts):
            pltpu.make_async_copy(recv.at[s], recv.at[s], r_recv.at[s, which]).wait()
    for j in range(n_exp):

        @pl.when(j != me_e)
        def _():
            for which in range(2):
                reduce_copy(j, which).wait_send()

    for p in range(n_ctx):

        @pl.when(p != me_c)
        def _():
            dispatch_copy(p).wait_send()
    for r in range(n_exp):

        @pl.when(r != me_e)
        def _():
            square_copy(r).wait_send()


def dispatch_reduce(
    mixed, square_block, gain, slot_rows, out_shape, gate_weight, up_weight, n_ctx, n_exp, collective_id
):
    hid = gate_weight.shape[-1]
    size = math.prod(out_shape)
    slots = out_shape[0] * out_shape[2] // n_exp
    recv_shape = jax.ShapeDtypeStruct((n_exp, EXP_ROW, slots, hid), jnp.bfloat16)
    flops = 2 * 2 * size * hid + 2 * size * mixed.shape[0]
    nbytes = 2 * size * 2 + 4 * gate_weight.size * 2 + 4 * n_exp * EXP_ROW * slots * hid * 2
    return pl.pallas_call(
        functools.partial(dispatch_reduce_kernel, n_ctx, n_exp),
        out_shape=[recv_shape, recv_shape],
        in_specs=[pl.BlockSpec(memory_space=pltpu.VMEM)] * 6,
        out_specs=[pl.BlockSpec(memory_space=pltpu.VMEM)] * 2,
        scratch_shapes=[
            pltpu.VMEM((n_exp,) + square_block.shape, jnp.float32),
            pltpu.VMEM(out_shape, jnp.bfloat16),
            pltpu.VMEM(out_shape, jnp.bfloat16),
            pltpu.VMEM(recv_shape.shape, jnp.bfloat16),
            pltpu.VMEM(recv_shape.shape, jnp.bfloat16),
            pltpu.SemaphoreType.DMA((n_exp,)),
            pltpu.SemaphoreType.DMA((n_exp,)),
            pltpu.SemaphoreType.DMA((n_ctx,)),
            pltpu.SemaphoreType.DMA((n_ctx,)),
            pltpu.SemaphoreType.DMA((n_exp, 2)),
            pltpu.SemaphoreType.DMA((n_exp, 2)),
        ],
        compiler_params=pltpu.CompilerParams(collective_id=collective_id, has_side_effects=True),
        cost_estimate=pl.CostEstimate(flops=flops, bytes_accessed=nbytes, transcendentals=0),
    )(mixed, square_block, gain, slot_rows, gate_weight, up_weight)


def kv_gather_kernel(n_ctx, n_exp, group, *refs):
    block, kv_all, s1_send, s1_recv, s2_send, s2_recv = refs
    per_plane = n_ctx // n_exp
    planes = n_ctx // per_plane
    me_c = lax.axis_index("ctx")
    me_e = lax.axis_index("exp")
    q = lax.rem(me_e, group)
    head_base = me_e - q
    plane = me_c // per_plane
    barrier = pltpu.get_barrier_semaphore()
    for k in range(1, n_ctx):
        pl.semaphore_signal(
            barrier, inc=1, device_id={"ctx": lax.rem(me_c + k, n_ctx)}, device_id_type=MESH
        )
    for k in range(1, group):
        pl.semaphore_signal(
            barrier, inc=1, device_id={"exp": head_base + lax.rem(q + k, group)}, device_id_type=MESH
        )
    pl.semaphore_wait(barrier, n_ctx + group - 2)

    def first_copy(p):
        return pltpu.make_async_remote_copy(
            src_ref=block,
            dst_ref=kv_all.at[me_c],
            send_sem=s1_send.at[p],
            recv_sem=s1_recv.at[me_c],
            device_id={"ctx": p},
            device_id_type=MESH,
        )

    halves = 2
    for h in range(halves):
        z_r = lax.rem(plane + 2 * planes - q - h * (planes // halves), planes)
        for y in range(per_plane):
            p = z_r * per_plane + y

            @pl.when(p != me_c)
            def _():
                first_copy(p).start()

            @pl.when(p == me_c)
            def _():
                pltpu.make_async_copy(block, kv_all.at[p], s1_recv.at[p]).start()

    def second_copy(h, r):
        first = pl.multiple_of(lax.rem(plane + q + h * (planes // halves), planes) * per_plane, per_plane)
        return pltpu.make_async_remote_copy(
            src_ref=kv_all.at[pl.ds(first, per_plane)],
            dst_ref=kv_all.at[pl.ds(first, per_plane)],
            send_sem=s2_send.at[r, h],
            recv_sem=s2_recv.at[r, h],
            device_id={"exp": head_base + lax.rem(q + r, group)},
            device_id_type=MESH,
        )

    for h in range(halves):
        z_s = lax.rem(plane + q + h * (planes // halves), planes)
        for y in range(per_plane):
            s = z_s * per_plane + y
            pltpu.make_async_copy(kv_all.at[s], kv_all.at[s], s1_recv.at[s]).wait()
        for r in range(1, group):
            second_copy(h, r).start()
    for h in range(halves):
        for r in range(1, group):
            second_copy(h, r).wait_recv()
    for h in range(halves):
        for r in range(1, group):
            second_copy(h, r).wait_send()
    for h in range(halves):
        z_r = lax.rem(plane + 2 * planes - q - h * (planes // halves), planes)
        for y in range(per_plane):
            p = z_r * per_plane + y

            @pl.when(p != me_c)
            def _():
                first_copy(p).wait_send()


def kv_gather(block, n_ctx, n_exp, group, collective_id):
    nbytes = block.size * block.dtype.itemsize * n_ctx
    return pl.pallas_call(
        functools.partial(kv_gather_kernel, n_ctx, n_exp, group),
        out_shape=jax.ShapeDtypeStruct((n_ctx,) + block.shape, block.dtype),
        in_specs=[pl.BlockSpec(memory_space=pltpu.VMEM)],
        out_specs=pl.BlockSpec(memory_space=pltpu.VMEM),
        scratch_shapes=[
            pltpu.SemaphoreType.DMA((n_ctx,)),
            pltpu.SemaphoreType.DMA((n_ctx,)),
            pltpu.SemaphoreType.DMA((group, 2)),
            pltpu.SemaphoreType.DMA((group, 2)),
        ],
        compiler_params=pltpu.CompilerParams(collective_id=collective_id, has_side_effects=True),
        cost_estimate=pl.CostEstimate(flops=0, bytes_accessed=2 * nbytes, transcendentals=0),
    )(block)


def gather_return_kernel(n_ctx, n_exp, *refs):
    hidden_mine, down_w, returned, hidden_all, ret_stage, a_send, a_recv, b_send, b_recv = refs
    per_chunk = n_ctx // n_exp
    me_c = lax.axis_index("ctx")
    me_e = lax.axis_index("exp")
    plane = me_c // per_chunk
    barrier = pltpu.get_barrier_semaphore()
    for k in range(1, n_ctx):
        pl.semaphore_signal(
            barrier, inc=1, device_id={"ctx": lax.rem(me_c + k, n_ctx)}, device_id_type=MESH
        )
    for k in range(1, n_exp):
        pl.semaphore_signal(
            barrier, inc=1, device_id={"exp": lax.rem(me_e + k, n_exp)}, device_id_type=MESH
        )
    pl.semaphore_wait(barrier, n_ctx + n_exp - 2)

    def gather_copy(r):
        return pltpu.make_async_remote_copy(
            src_ref=hidden_mine,
            dst_ref=hidden_all.at[me_e],
            send_sem=a_send.at[r],
            recv_sem=a_recv.at[me_e],
            device_id={"exp": r},
            device_id_type=MESH,
        )

    def gather_wave(t):
        r = lax.rem(me_e + 2 * n_exp - plane - t, n_exp)

        @pl.when(r != me_e)
        def _():
            gather_copy(r).start()

        @pl.when(r == me_e)
        def _():
            pltpu.make_async_copy(hidden_mine, hidden_all.at[r], a_recv.at[r]).start()

    for t in range(AHEAD):
        gather_wave(t)

    def return_copy(s):
        return pltpu.make_async_remote_copy(
            src_ref=ret_stage.at[s],
            dst_ref=returned.at[me_c],
            send_sem=b_send.at[s],
            recv_sem=b_recv.at[me_c],
            device_id={"ctx": s},
            device_id_type=MESH,
        )

    rows = hidden_all.shape[2]
    for t in range(n_exp):
        j = lax.rem(me_e + plane + t, n_exp)
        pltpu.make_async_copy(hidden_all.at[j], hidden_all.at[j], a_recv.at[j]).wait()
        first = pl.multiple_of(j * per_chunk, per_chunk)
        for k in range(EXP_ROW):
            out = jnp.dot(hidden_all[j, k], down_w[k], preferred_element_type=jnp.float32)
            ret_stage[pl.ds(first, per_chunk), k] = out.astype(ret_stage.dtype).reshape(
                per_chunk, rows // per_chunk, out.shape[-1]
            )
        for y in range(per_chunk):
            s = j * per_chunk + y

            @pl.when(s != me_c)
            def _():
                return_copy(s).start()

            @pl.when(s == me_c)
            def _():
                pltpu.make_async_copy(ret_stage.at[s], returned.at[s], b_recv.at[s]).start()

        if t + AHEAD < n_exp:
            gather_wave(t + AHEAD)

    for s in range(n_ctx):
        pltpu.make_async_copy(returned.at[s], returned.at[s], b_recv.at[s]).wait()
    for r in range(n_exp):

        @pl.when(r != me_e)
        def _():
            gather_copy(r).wait_send()

    for s in range(n_ctx):

        @pl.when(s != me_c)
        def _():
            return_copy(s).wait_send()


def gather_return(hidden_mine, down_weight, n_ctx, n_exp, collective_id):
    hid, width = down_weight.shape[1:]
    slots = hidden_mine.shape[1]
    ret_shape = (n_ctx, EXP_ROW, slots * n_exp // n_ctx, width)
    flops = 2 * n_exp * hidden_mine.size * width
    nbytes = 2 * n_exp * hidden_mine.size * 2 + down_weight.size * 2 + 4 * n_ctx * EXP_ROW * slots * width * 2 // n_exp
    return pl.pallas_call(
        functools.partial(gather_return_kernel, n_ctx, n_exp),
        out_shape=jax.ShapeDtypeStruct(ret_shape, jnp.bfloat16),
        in_specs=[pl.BlockSpec(memory_space=pltpu.VMEM)] * 2,
        out_specs=pl.BlockSpec(memory_space=pltpu.VMEM),
        scratch_shapes=[
            pltpu.VMEM((n_exp,) + hidden_mine.shape, jnp.bfloat16),
            pltpu.VMEM(ret_shape, jnp.bfloat16),
            pltpu.SemaphoreType.DMA((n_exp,)),
            pltpu.SemaphoreType.DMA((n_exp,)),
            pltpu.SemaphoreType.DMA((n_ctx,)),
            pltpu.SemaphoreType.DMA((n_ctx,)),
        ],
        compiler_params=pltpu.CompilerParams(collective_id=collective_id, has_side_effects=True),
        cost_estimate=pl.CostEstimate(flops=flops, bytes_accessed=nbytes, transcendentals=0),
    )(hidden_mine, down_weight)


def local(
    queries,
    key_rows,
    value_head_rows,
    block_order,
    residual,
    norm_gain,
    expert_ids,
    route_weight,
    gate_weight,
    up_weight,
    down_weight,
):
    shard_rows = queries.shape[0]
    ctx_count = lax.axis_size("ctx")
    exp_count = lax.axis_size("exp")
    local_head = queries.shape[1] // HEAD_SIZE
    expert_index = lax.axis_index("exp")
    ctx_index = lax.axis_index("ctx")
    key_value_head = expert_index * local_head // (QUERY_HEADS // KEY_VALUE_HEADS)
    my_keys = lax.dynamic_slice_in_dim(key_rows, key_value_head * HEAD_SIZE, HEAD_SIZE, 1)
    my_values = lax.dynamic_slice_in_dim(value_head_rows, key_value_head * HEAD_SIZE, HEAD_SIZE, 1)
    block_ids = jnp.arange(ctx_count, dtype=jnp.int32)
    own_block = jnp.sum(jnp.where(block_ids == ctx_index, block_order, 0))
    local_rows = jnp.arange(shard_rows, dtype=jnp.int32)
    query_pos = jnp.tile(own_block * shard_rows + local_rows, local_head)
    query_flat = (
        queries.reshape(shard_rows, local_head, HEAD_SIZE)
        .transpose(1, 0, 2)
        .reshape(local_head * shard_rows, HEAD_SIZE)
    )
    inv_scale = 1.0 / math.sqrt(HEAD_SIZE)
    key_value_all = kv_gather(
        jnp.concatenate([my_keys, my_values], axis=1),
        ctx_count,
        exp_count,
        QUERY_HEADS // KEY_VALUE_HEADS // local_head,
        0,
    )
    key_value_all = key_value_all.reshape(ctx_count * shard_rows, 2 * HEAD_SIZE)
    piece_keys = key_value_all[:, :HEAD_SIZE]
    piece_values = key_value_all[:, HEAD_SIZE:]
    key_index = jnp.arange(piece_keys.shape[0], dtype=jnp.int32)
    owner_shard = key_index // shard_rows
    key_block = jnp.sum(
        jnp.where(owner_shard[:, None] == block_ids[None, :], block_order[None, :], 0), axis=1
    )
    key_pos = key_block * shard_rows + key_index % shard_rows
    visible = key_pos[None, :] <= query_pos[:, None]
    scores = (
        lax.dot_general(
            query_flat, piece_keys, (((1,), (1,)), ((), ())), preferred_element_type=jnp.float32
        )
        * inv_scale
    )
    scores = jnp.where(visible, scores, MASKED_SCORE)
    newest = jnp.max(scores, axis=1)
    weights = jnp.where(visible, jnp.exp(scores - newest[:, None]), 0.0)
    running_sum = jnp.sum(weights, axis=1)
    weighted = jnp.dot(
        weights.astype(jnp.bfloat16), piece_values, preferred_element_type=jnp.float32
    )
    attention = (
        (weighted / running_sum[:, None])
        .reshape(local_head, shard_rows, HEAD_SIZE)
        .transpose(1, 0, 2)
        .reshape(shard_rows, local_head * HEAD_SIZE)
        .astype(jnp.bfloat16)
    )
    mixed_rows = (residual.astype(jnp.float32) + attention.astype(jnp.float32)).astype(jnp.bfloat16)
    mixed_f = mixed_rows.astype(jnp.float32)
    square_part = jnp.sum(mixed_f * mixed_f, axis=1)
    square_block = jnp.broadcast_to(square_part[:, None], (shard_rows, 128))
    expert_count = ctx_count * EXP_ROW
    capacity = 2 * shard_rows * TOPK // expert_count
    flat_ids = expert_ids.reshape(-1)
    onehot = (flat_ids[:, None] == jnp.arange(expert_count, dtype=jnp.int32)[None, :]).astype(
        jnp.int32
    )
    slot_rank = jnp.sum((jnp.cumsum(onehot, axis=0) - onehot) * onehot, axis=1)
    slot_index = flat_ids * capacity + slot_rank
    slot_total = expert_count * capacity
    slot_rows = jnp.any(
        slot_index.reshape(shard_rows, TOPK)[None, :, :]
        == jnp.arange(slot_total, dtype=jnp.int32)[:, None, None],
        axis=2,
    ).astype(jnp.bfloat16)
    gate_recv, up_recv = dispatch_reduce(
        mixed_rows,
        square_block,
        norm_gain.reshape(1, -1),
        slot_rows,
        (ctx_count, EXP_ROW, capacity, mixed_rows.shape[1]),
        gate_weight,
        up_weight,
        ctx_count,
        exp_count,
        2,
    )
    gate_full = jnp.sum(gate_recv.astype(jnp.float32), axis=0)
    up_full = jnp.sum(up_recv.astype(jnp.float32), axis=0)
    hidden_mine = (jax.nn.silu(gate_full) * up_full).astype(jnp.bfloat16)
    returned = gather_return(hidden_mine, down_weight, ctx_count, exp_count, 4)
    flat_back = returned.reshape(expert_count * capacity, mixed_rows.shape[1])
    picked = flat_back[slot_index].astype(jnp.float32).reshape(shard_rows, TOPK, mixed_rows.shape[1])
    routed_sum = jnp.sum(route_weight[:, :, None] * picked, axis=1)
    return (mixed_f + routed_sum).astype(jnp.bfloat16)


def solution(mesh):
    placed = (
        P(("rep", "ctx"), "exp"),
        P(("rep", "ctx"), None),
        P(("rep", "ctx"), None),
        P("rep"),
        P(("rep", "ctx"), "exp"),
        P("exp"),
        P(("rep", "ctx"), None),
        P(("rep", "ctx"), None),
        P("ctx", "exp", None),
        P("ctx", "exp", None),
        P("ctx", None, "exp"),
    )
    return jax.shard_map(
        local, mesh=mesh, in_specs=placed, out_specs=P(("rep", "ctx"), "exp"), check_vma=False
    )
```

```python
import functools
import math

import jax
import jax.numpy as jnp
from jax import lax
from jax.experimental import pallas as pl
from jax.experimental.pallas import tpu as pltpu
from jax.sharding import PartitionSpec as P

D = 4096
QUERY_HEADS = 32
KEY_VALUE_HEADS = 2
HEAD_SIZE = 128
TOPK = 8
EXP_ROW = 2

MASKED_SCORE = -1e30
NORM_EPS = 1e-06
MESH = pl.DeviceIdType.MESH


def exchange_kernel(axis, n, gather, n_in, *refs):
    ins, outs = refs[:n_in], refs[n_in : 2 * n_in]
    send_sem, recv_sem = refs[2 * n_in], refs[2 * n_in + 1]
    me = lax.axis_index(axis)
    barrier = pltpu.get_barrier_semaphore()
    for k in range(1, n):
        pl.semaphore_signal(
            barrier, inc=1, device_id={axis: lax.rem(me + k, n)}, device_id_type=MESH
        )
    pl.semaphore_wait(barrier, n - 1)
    copies = []
    for k in range(1, n):
        peer = lax.rem(me + k, n)
        for i in range(n_in):
            copy = pltpu.make_async_remote_copy(
                src_ref=ins[i] if gather else ins[i].at[peer],
                dst_ref=outs[i].at[me],
                send_sem=send_sem.at[i, k],
                recv_sem=recv_sem.at[i, k],
                device_id={axis: peer},
                device_id_type=MESH,
            )
            copy.start()
            copies.append(copy)
    for i in range(n_in):
        outs[i][me] = ins[i][...] if gather else ins[i][me]
    for copy in copies:
        copy.wait()


def exchange(xs, axis, n, gather, collective_id):
    n_in = len(xs)
    out_shape = [
        jax.ShapeDtypeStruct((n,) + (x.shape if gather else x.shape[1:]), x.dtype) for x in xs
    ]
    nbytes = sum(x.size * x.dtype.itemsize for x in xs) * (n if gather else 1)
    return pl.pallas_call(
        functools.partial(exchange_kernel, axis, n, gather, n_in),
        out_shape=out_shape,
        in_specs=[pl.BlockSpec(memory_space=pltpu.VMEM)] * n_in,
        out_specs=[pl.BlockSpec(memory_space=pltpu.VMEM)] * n_in,
        scratch_shapes=[
            pltpu.SemaphoreType.DMA((n_in, n)),
            pltpu.SemaphoreType.DMA((n_in, n)),
        ],
        compiler_params=pltpu.CompilerParams(collective_id=collective_id, has_side_effects=True),
        cost_estimate=pl.CostEstimate(flops=0, bytes_accessed=2 * nbytes, transcendentals=0),
    )(*xs)


def moe_kernel(n_ctx, n_exp, *refs):
    (mixed, square_block, gain, slot_rows, gate_w, up_w, down_w, w_hi, w_lo, out,
     square_all, outgoing, incoming, gate_stage, up_stage, gate_recv, up_recv, hidden_mine, hidden_all, ret_stage,
     returned, q_send, q_recv, d_send, d_recv, r_send, r_recv, a_send, a_recv, b_send, b_recv) = refs
    per_chunk = n_ctx // n_exp
    me_c = lax.axis_index("ctx")
    me_e = lax.axis_index("exp")
    plane = me_c // per_chunk
    barrier = pltpu.get_barrier_semaphore()
    for k in range(1, n_ctx):
        pl.semaphore_signal(
            barrier, inc=1, device_id={"ctx": lax.rem(me_c + k, n_ctx)}, device_id_type=MESH
        )
    for k in range(1, n_exp):
        pl.semaphore_signal(
            barrier, inc=1, device_id={"exp": lax.rem(me_e + k, n_exp)}, device_id_type=MESH
        )
    pl.semaphore_wait(barrier, n_ctx + n_exp - 2)

    def square_copy(r):
        return pltpu.make_async_remote_copy(
            src_ref=square_block,
            dst_ref=square_all.at[me_e],
            send_sem=q_send.at[r],
            recv_sem=q_recv.at[me_e],
            device_id={"exp": r},
            device_id_type=MESH,
        )

    for k in range(1, n_exp):
        square_copy(lax.rem(me_e + k, n_exp)).start()
    pltpu.make_async_copy(square_block, square_all.at[me_e], q_recv.at[me_e]).start()
    for s in range(n_exp):
        pltpu.make_async_copy(square_all.at[s], square_all.at[s], q_recv.at[s]).wait()
    square_sum = square_all[0]
    for s in range(1, n_exp):
        square_sum = square_sum + square_all[s]
    scale = lax.rsqrt(square_sum[:, :1] / D + NORM_EPS)
    mixed_f = mixed[...].astype(jnp.float32)
    normed = (mixed_f * scale * gain[...]).astype(jnp.bfloat16)
    filled = jnp.dot(slot_rows[...], normed, preferred_element_type=jnp.float32)
    outgoing[...] = filled.astype(outgoing.dtype).reshape(outgoing.shape)

    def dispatch_copy(p):
        return pltpu.make_async_remote_copy(
            src_ref=outgoing.at[p],
            dst_ref=incoming.at[me_c],
            send_sem=d_send.at[p],
            recv_sem=d_recv.at[me_c],
            device_id={"ctx": p},
            device_id_type=MESH,
        )

    for t in range(n_exp):
        z_r = lax.rem(plane + 2 * n_exp - me_e - t, n_exp)
        for y in range(per_chunk):
            p = z_r * per_chunk + y

            @pl.when(p != me_c)
            def _():
                dispatch_copy(p).start()

            @pl.when(p == me_c)
            def _():
                pltpu.make_async_copy(outgoing.at[p], incoming.at[p], d_recv.at[p]).start()

    parts = ((gate_w, gate_stage, gate_recv), (up_w, up_stage, up_recv))

    def reduce_copy(j, which):
        _, stage, recv = parts[which]
        return pltpu.make_async_remote_copy(
            src_ref=stage.at[j],
            dst_ref=recv.at[me_e],
            send_sem=r_send.at[j, which],
            recv_sem=r_recv.at[me_e, which],
            device_id={"exp": j},
            device_id_type=MESH,
        )

    rows = gate_stage.shape[2]
    for t in range(n_exp):
        j = lax.rem(plane + me_e + t, n_exp)
        for y in range(per_chunk):
            s = j * per_chunk + y
            pltpu.make_async_copy(incoming.at[s], incoming.at[s], d_recv.at[s]).wait()
        first = pl.multiple_of(j * per_chunk, per_chunk)
        for k in range(EXP_ROW):
            x = incoming[pl.ds(first, per_chunk), k].reshape(rows, incoming.shape[-1])
            for w, stage, _ in parts:
                stage[j, k] = jnp.dot(x, w[k], preferred_element_type=jnp.float32).astype(
                    stage.dtype
                )

        @pl.when(j != me_e)
        def _():
            for which in range(2):
                reduce_copy(j, which).start()

        @pl.when(j == me_e)
        def _():
            for which, (_, stage, recv) in enumerate(parts):
                pltpu.make_async_copy(stage.at[j], recv.at[j], r_recv.at[j, which]).start()

    for s in range(n_exp):
        for which, (_, _, recv) in enumerate(parts):
            pltpu.make_async_copy(recv.at[s], recv.at[s], r_recv.at[s, which]).wait()
    gate_sum = gate_recv[0].astype(jnp.float32)
    up_sum = up_recv[0].astype(jnp.float32)
    for s in range(1, n_exp):
        gate_sum = gate_sum + gate_recv[s].astype(jnp.float32)
        up_sum = up_sum + up_recv[s].astype(jnp.float32)
    hidden_mine[...] = (gate_sum / (1.0 + jnp.exp(-gate_sum)) * up_sum).astype(hidden_mine.dtype)

    def gather_copy(r):
        return pltpu.make_async_remote_copy(
            src_ref=hidden_mine,
            dst_ref=hidden_all.at[me_e],
            send_sem=a_send.at[r],
            recv_sem=a_recv.at[me_e],
            device_id={"exp": r},
            device_id_type=MESH,
        )

    for t in range(n_exp):
        r = lax.rem(me_e + 2 * n_exp - plane - t, n_exp)

        @pl.when(r != me_e)
        def _():
            gather_copy(r).start()

        @pl.when(r == me_e)
        def _():
            pltpu.make_async_copy(hidden_mine, hidden_all.at[r], a_recv.at[r]).start()

    def return_copy(s):
        return pltpu.make_async_remote_copy(
            src_ref=ret_stage.at[s],
            dst_ref=returned.at[me_c],
            send_sem=b_send.at[s],
            recv_sem=b_recv.at[me_c],
            device_id={"ctx": s},
            device_id_type=MESH,
        )

    for t in range(n_exp):
        j = lax.rem(me_e + plane + t, n_exp)
        pltpu.make_async_copy(hidden_all.at[j], hidden_all.at[j], a_recv.at[j]).wait()
        first = pl.multiple_of(j * per_chunk, per_chunk)
        for k in range(EXP_ROW):
            res = jnp.dot(hidden_all[j, k], down_w[k], preferred_element_type=jnp.float32)
            ret_stage[pl.ds(first, per_chunk), k] = res.astype(ret_stage.dtype).reshape(
                per_chunk, rows // per_chunk, res.shape[-1]
            )
        for y in range(per_chunk):
            s = j * per_chunk + y

            @pl.when(s != me_c)
            def _():
                return_copy(s).start()

            @pl.when(s == me_c)
            def _():
                pltpu.make_async_copy(ret_stage.at[s], returned.at[s], b_recv.at[s]).start()

    for s in range(n_ctx):
        pltpu.make_async_copy(returned.at[s], returned.at[s], b_recv.at[s]).wait()
    back = returned[...].reshape(w_hi.shape[1], returned.shape[-1])
    routed = jnp.dot(w_hi[...], back, preferred_element_type=jnp.float32) + jnp.dot(
        w_lo[...], back, preferred_element_type=jnp.float32
    )
    out[...] = (mixed_f + routed).astype(out.dtype)

    for r in range(n_exp):

        @pl.when(r != me_e)
        def _():
            gather_copy(r).wait_send()
            square_copy(r).wait_send()
            for which in range(2):
                reduce_copy(r, which).wait_send()

    for p in range(n_ctx):

        @pl.when(p != me_c)
        def _():
            dispatch_copy(p).wait_send()
            return_copy(p).wait_send()


def moe(mixed, square_block, gain, slot_rows, out_shape, gate_weight, up_weight, down_weight, w_hi, w_lo,
        n_ctx, n_exp, collective_id):
    hid = gate_weight.shape[-1]
    size = math.prod(out_shape)
    slots = out_shape[0] * out_shape[2] // n_exp
    recv_shape = (n_exp, EXP_ROW, slots, hid)
    flops = 2 * 3 * size * hid + 2 * size * mixed.shape[0] * 3
    nbytes = 4 * size * 2 + 6 * gate_weight.size * 2 + 8 * n_exp * EXP_ROW * slots * hid * 2
    vmem = pltpu.VMEM
    return pl.pallas_call(
        functools.partial(moe_kernel, n_ctx, n_exp),
        out_shape=jax.ShapeDtypeStruct(mixed.shape, jnp.bfloat16),
        in_specs=[pl.BlockSpec(memory_space=pltpu.VMEM)] * 9,
        out_specs=pl.BlockSpec(memory_space=pltpu.VMEM),
        scratch_shapes=[
            vmem((n_exp,) + square_block.shape, jnp.float32),
            vmem(out_shape, jnp.bfloat16),
            vmem(out_shape, jnp.bfloat16),
            vmem(recv_shape, jnp.bfloat16),
            vmem(recv_shape, jnp.bfloat16),
            vmem(recv_shape, jnp.bfloat16),
            vmem(recv_shape, jnp.bfloat16),
            vmem(recv_shape[1:], jnp.bfloat16),
            vmem(recv_shape, jnp.bfloat16),
            vmem(out_shape, jnp.bfloat16),
            vmem(out_shape, jnp.bfloat16),
            pltpu.SemaphoreType.DMA((n_exp,)),
            pltpu.SemaphoreType.DMA((n_exp,)),
            pltpu.SemaphoreType.DMA((n_ctx,)),
            pltpu.SemaphoreType.DMA((n_ctx,)),
            pltpu.SemaphoreType.DMA((n_exp, 2)),
            pltpu.SemaphoreType.DMA((n_exp, 2)),
            pltpu.SemaphoreType.DMA((n_exp,)),
            pltpu.SemaphoreType.DMA((n_exp,)),
            pltpu.SemaphoreType.DMA((n_ctx,)),
            pltpu.SemaphoreType.DMA((n_ctx,)),
        ],
        compiler_params=pltpu.CompilerParams(collective_id=collective_id, has_side_effects=True),
        cost_estimate=pl.CostEstimate(flops=flops, bytes_accessed=nbytes, transcendentals=0),
    )(mixed, square_block, gain, slot_rows, gate_weight, up_weight, down_weight, w_hi, w_lo)

def kv_gather_kernel(n_ctx, n_exp, group, *refs):
    block, kv_all, s1_send, s1_recv, s2_send, s2_recv = refs
    per_plane = n_ctx // n_exp
    planes = n_ctx // per_plane
    me_c = lax.axis_index("ctx")
    me_e = lax.axis_index("exp")
    q = lax.rem(me_e, group)
    head_base = me_e - q
    plane = me_c // per_plane
    barrier = pltpu.get_barrier_semaphore()
    for k in range(1, n_ctx):
        pl.semaphore_signal(
            barrier, inc=1, device_id={"ctx": lax.rem(me_c + k, n_ctx)}, device_id_type=MESH
        )
    for k in range(1, group):
        pl.semaphore_signal(
            barrier, inc=1, device_id={"exp": head_base + lax.rem(q + k, group)}, device_id_type=MESH
        )
    pl.semaphore_wait(barrier, n_ctx + group - 2)

    def first_copy(p):
        return pltpu.make_async_remote_copy(
            src_ref=block,
            dst_ref=kv_all.at[me_c],
            send_sem=s1_send.at[p],
            recv_sem=s1_recv.at[me_c],
            device_id={"ctx": p},
            device_id_type=MESH,
        )

    halves = 2
    for h in range(halves):
        z_r = lax.rem(plane + 2 * planes - q - h * (planes // halves), planes)
        for y in range(per_plane):
            p = z_r * per_plane + y

            @pl.when(p != me_c)
            def _():
                first_copy(p).start()

            @pl.when(p == me_c)
            def _():
                pltpu.make_async_copy(block, kv_all.at[p], s1_recv.at[p]).start()

    def second_copy(h, r):
        first = pl.multiple_of(lax.rem(plane + q + h * (planes // halves), planes) * per_plane, per_plane)
        return pltpu.make_async_remote_copy(
            src_ref=kv_all.at[pl.ds(first, per_plane)],
            dst_ref=kv_all.at[pl.ds(first, per_plane)],
            send_sem=s2_send.at[r, h],
            recv_sem=s2_recv.at[r, h],
            device_id={"exp": head_base + lax.rem(q + r, group)},
            device_id_type=MESH,
        )

    for h in range(halves):
        z_s = lax.rem(plane + q + h * (planes // halves), planes)
        for y in range(per_plane):
            s = z_s * per_plane + y
            pltpu.make_async_copy(kv_all.at[s], kv_all.at[s], s1_recv.at[s]).wait()
        for r in range(1, group):
            second_copy(h, r).start()
    for h in range(halves):
        for r in range(1, group):
            second_copy(h, r).wait_recv()
    for h in range(halves):
        for r in range(1, group):
            second_copy(h, r).wait_send()
    for h in range(halves):
        z_r = lax.rem(plane + 2 * planes - q - h * (planes // halves), planes)
        for y in range(per_plane):
            p = z_r * per_plane + y

            @pl.when(p != me_c)
            def _():
                first_copy(p).wait_send()


def kv_gather(block, n_ctx, n_exp, group, collective_id):
    nbytes = block.size * block.dtype.itemsize * n_ctx
    return pl.pallas_call(
        functools.partial(kv_gather_kernel, n_ctx, n_exp, group),
        out_shape=jax.ShapeDtypeStruct((n_ctx,) + block.shape, block.dtype),
        in_specs=[pl.BlockSpec(memory_space=pltpu.VMEM)],
        out_specs=pl.BlockSpec(memory_space=pltpu.VMEM),
        scratch_shapes=[
            pltpu.SemaphoreType.DMA((n_ctx,)),
            pltpu.SemaphoreType.DMA((n_ctx,)),
            pltpu.SemaphoreType.DMA((group, 2)),
            pltpu.SemaphoreType.DMA((group, 2)),
        ],
        compiler_params=pltpu.CompilerParams(collective_id=collective_id, has_side_effects=True),
        cost_estimate=pl.CostEstimate(flops=0, bytes_accessed=2 * nbytes, transcendentals=0),
    )(block)


def local(
    queries,
    key_rows,
    value_head_rows,
    block_order,
    residual,
    norm_gain,
    expert_ids,
    route_weight,
    gate_weight,
    up_weight,
    down_weight,
):
    shard_rows = queries.shape[0]
    ctx_count = lax.axis_size("ctx")
    exp_count = lax.axis_size("exp")
    local_head = queries.shape[1] // HEAD_SIZE
    expert_index = lax.axis_index("exp")
    ctx_index = lax.axis_index("ctx")
    key_value_head = expert_index * local_head // (QUERY_HEADS // KEY_VALUE_HEADS)
    my_keys = lax.dynamic_slice_in_dim(key_rows, key_value_head * HEAD_SIZE, HEAD_SIZE, 1)
    my_values = lax.dynamic_slice_in_dim(value_head_rows, key_value_head * HEAD_SIZE, HEAD_SIZE, 1)
    block_ids = jnp.arange(ctx_count, dtype=jnp.int32)
    own_block = jnp.sum(jnp.where(block_ids == ctx_index, block_order, 0))
    local_rows = jnp.arange(shard_rows, dtype=jnp.int32)
    query_pos = jnp.tile(own_block * shard_rows + local_rows, local_head)
    query_flat = (
        queries.reshape(shard_rows, local_head, HEAD_SIZE)
        .transpose(1, 0, 2)
        .reshape(local_head * shard_rows, HEAD_SIZE)
    )
    inv_scale = 1.0 / math.sqrt(HEAD_SIZE)
    key_value_all = kv_gather(
        jnp.concatenate([my_keys, my_values], axis=1),
        ctx_count,
        exp_count,
        QUERY_HEADS // KEY_VALUE_HEADS // local_head,
        0,
    )
    key_value_all = key_value_all.reshape(ctx_count * shard_rows, 2 * HEAD_SIZE)
    piece_keys = key_value_all[:, :HEAD_SIZE]
    piece_values = key_value_all[:, HEAD_SIZE:]
    key_index = jnp.arange(piece_keys.shape[0], dtype=jnp.int32)
    owner_shard = key_index // shard_rows
    key_block = jnp.sum(
        jnp.where(owner_shard[:, None] == block_ids[None, :], block_order[None, :], 0), axis=1
    )
    key_pos = key_block * shard_rows + key_index % shard_rows
    visible = key_pos[None, :] <= query_pos[:, None]
    scores = (
        lax.dot_general(
            query_flat, piece_keys, (((1,), (1,)), ((), ())), preferred_element_type=jnp.float32
        )
        * inv_scale
    )
    scores = jnp.where(visible, scores, MASKED_SCORE)
    newest = jnp.max(scores, axis=1)
    weights = jnp.where(visible, jnp.exp(scores - newest[:, None]), 0.0)
    running_sum = jnp.sum(weights, axis=1)
    weighted = jnp.dot(
        weights.astype(jnp.bfloat16), piece_values, preferred_element_type=jnp.float32
    )
    attention = (
        (weighted / running_sum[:, None])
        .reshape(local_head, shard_rows, HEAD_SIZE)
        .transpose(1, 0, 2)
        .reshape(shard_rows, local_head * HEAD_SIZE)
        .astype(jnp.bfloat16)
    )
    mixed_rows = (residual.astype(jnp.float32) + attention.astype(jnp.float32)).astype(jnp.bfloat16)
    mixed_f = mixed_rows.astype(jnp.float32)
    square_part = jnp.sum(mixed_f * mixed_f, axis=1)
    square_block = jnp.broadcast_to(square_part[:, None], (shard_rows, 128))
    expert_count = ctx_count * EXP_ROW
    capacity = 2 * shard_rows * TOPK // expert_count
    flat_ids = expert_ids.reshape(-1)
    onehot = (flat_ids[:, None] == jnp.arange(expert_count, dtype=jnp.int32)[None, :]).astype(
        jnp.int32
    )
    slot_rank = jnp.sum((jnp.cumsum(onehot, axis=0) - onehot) * onehot, axis=1)
    slot_index = flat_ids * capacity + slot_rank
    slot_total = expert_count * capacity
    slot_rows = jnp.any(
        slot_index.reshape(shard_rows, TOPK)[None, :, :]
        == jnp.arange(slot_total, dtype=jnp.int32)[:, None, None],
        axis=2,
    ).astype(jnp.bfloat16)
    slot_weight = jnp.sum(
        jnp.where(
            slot_index.reshape(shard_rows, TOPK)[:, :, None]
            == jnp.arange(slot_total, dtype=jnp.int32)[None, None, :],
            route_weight[:, :, None],
            0.0,
        ),
        axis=1,
    )
    w_hi = slot_weight.astype(jnp.bfloat16)
    w_lo = (slot_weight - w_hi.astype(jnp.float32)).astype(jnp.bfloat16)
    return moe(
        mixed_rows,
        square_block,
        norm_gain.reshape(1, -1),
        slot_rows,
        (ctx_count, EXP_ROW, capacity, mixed_rows.shape[1]),
        gate_weight,
        up_weight,
        down_weight,
        w_hi,
        w_lo,
        ctx_count,
        exp_count,
        2,
    )

def solution(mesh):
    placed = (
        P(("rep", "ctx"), "exp"),
        P(("rep", "ctx"), None),
        P(("rep", "ctx"), None),
        P("rep"),
        P(("rep", "ctx"), "exp"),
        P("exp"),
        P(("rep", "ctx"), None),
        P(("rep", "ctx"), None),
        P("ctx", "exp", None),
        P("ctx", "exp", None),
        P("ctx", None, "exp"),
    )
    return jax.shard_map(
        local, mesh=mesh, in_specs=placed, out_specs=P(("rep", "ctx"), "exp"), check_vma=False
    )
```

```python
import functools
import math

import jax
import jax.numpy as jnp
from jax import lax
from jax.experimental import pallas as pl
from jax.experimental.pallas import tpu as pltpu
from jax.sharding import PartitionSpec as P

D = 4096
QUERY_HEADS = 32
KEY_VALUE_HEADS = 2
HEAD_SIZE = 128
TOPK = 8
EXP_ROW = 2

MASKED_SCORE = -1e30
NORM_EPS = 1e-06
MESH = pl.DeviceIdType.MESH


def exchange_kernel(axis, n, gather, n_in, *refs):
    ins, outs = refs[:n_in], refs[n_in : 2 * n_in]
    send_sem, recv_sem = refs[2 * n_in], refs[2 * n_in + 1]
    me = lax.axis_index(axis)
    barrier = pltpu.get_barrier_semaphore()
    for k in range(1, n):
        pl.semaphore_signal(
            barrier, inc=1, device_id={axis: lax.rem(me + k, n)}, device_id_type=MESH
        )
    pl.semaphore_wait(barrier, n - 1)
    copies = []
    for k in range(1, n):
        peer = lax.rem(me + k, n)
        for i in range(n_in):
            copy = pltpu.make_async_remote_copy(
                src_ref=ins[i] if gather else ins[i].at[peer],
                dst_ref=outs[i].at[me],
                send_sem=send_sem.at[i, k],
                recv_sem=recv_sem.at[i, k],
                device_id={axis: peer},
                device_id_type=MESH,
            )
            copy.start()
            copies.append(copy)
    for i in range(n_in):
        outs[i][me] = ins[i][...] if gather else ins[i][me]
    for copy in copies:
        copy.wait()


def exchange(xs, axis, n, gather, collective_id):
    n_in = len(xs)
    out_shape = [
        jax.ShapeDtypeStruct((n,) + (x.shape if gather else x.shape[1:]), x.dtype) for x in xs
    ]
    nbytes = sum(x.size * x.dtype.itemsize for x in xs) * (n if gather else 1)
    return pl.pallas_call(
        functools.partial(exchange_kernel, axis, n, gather, n_in),
        out_shape=out_shape,
        in_specs=[pl.BlockSpec(memory_space=pltpu.VMEM)] * n_in,
        out_specs=[pl.BlockSpec(memory_space=pltpu.VMEM)] * n_in,
        scratch_shapes=[
            pltpu.SemaphoreType.DMA((n_in, n)),
            pltpu.SemaphoreType.DMA((n_in, n)),
        ],
        compiler_params=pltpu.CompilerParams(collective_id=collective_id, has_side_effects=True),
        cost_estimate=pl.CostEstimate(flops=0, bytes_accessed=2 * nbytes, transcendentals=0),
    )(*xs)


def moe_kernel(n_ctx, n_exp, *refs):
    (queries, kv_block, residual, query_pos, key_pos, gain, slot_rows, gate_w, up_w, down_w, w_hi, w_lo, out,
     kv_all, mixed, square_block, square_all, outgoing, incoming, gate_stage, up_stage, gate_recv, up_recv,
     hidden_mine, hidden_all, ret_stage, returned, s1_send, s1_recv, s2_send, s2_recv, q_send, q_recv, d_send,
     d_recv, r_send, r_recv, a_send, a_recv, b_send, b_recv) = refs
    per_chunk = n_ctx // n_exp
    me_c = lax.axis_index("ctx")
    me_e = lax.axis_index("exp")
    plane = me_c // per_chunk
    barrier = pltpu.get_barrier_semaphore()
    for k in range(1, n_ctx):
        pl.semaphore_signal(
            barrier, inc=1, device_id={"ctx": lax.rem(me_c + k, n_ctx)}, device_id_type=MESH
        )
    for k in range(1, n_exp):
        pl.semaphore_signal(
            barrier, inc=1, device_id={"exp": lax.rem(me_e + k, n_exp)}, device_id_type=MESH
        )
    pl.semaphore_wait(barrier, n_ctx + n_exp - 2)

    group = QUERY_HEADS // KEY_VALUE_HEADS // (queries.shape[1] // HEAD_SIZE)
    q = lax.rem(me_e, group)
    head_base = me_e - q
    planes = n_exp
    halves = 2

    def first_copy(p):
        return pltpu.make_async_remote_copy(
            src_ref=kv_block,
            dst_ref=kv_all.at[me_c],
            send_sem=s1_send.at[p],
            recv_sem=s1_recv.at[me_c],
            device_id={"ctx": p},
            device_id_type=MESH,
        )

    for h in range(halves):
        z_r = lax.rem(plane + 2 * planes - q - h * (planes // halves), planes)
        for y in range(per_chunk):
            p = z_r * per_chunk + y

            @pl.when(p != me_c)
            def _():
                first_copy(p).start()

            @pl.when(p == me_c)
            def _():
                pltpu.make_async_copy(kv_block, kv_all.at[p], s1_recv.at[p]).start()

    def second_copy(h, r):
        first = pl.multiple_of(lax.rem(plane + q + h * (planes // halves), planes) * per_chunk, per_chunk)
        return pltpu.make_async_remote_copy(
            src_ref=kv_all.at[pl.ds(first, per_chunk)],
            dst_ref=kv_all.at[pl.ds(first, per_chunk)],
            send_sem=s2_send.at[r, h],
            recv_sem=s2_recv.at[r, h],
            device_id={"exp": head_base + lax.rem(q + r, group)},
            device_id_type=MESH,
        )

    for h in range(halves):
        z_s = lax.rem(plane + q + h * (planes // halves), planes)
        for y in range(per_chunk):
            s = z_s * per_chunk + y
            pltpu.make_async_copy(kv_all.at[s], kv_all.at[s], s1_recv.at[s]).wait()
        for r in range(1, group):
            second_copy(h, r).start()
    for h in range(halves):
        for r in range(1, group):
            second_copy(h, r).wait_recv()

    total_rows = kv_all.shape[0] * kv_all.shape[1]
    keys = kv_all[:, :, :HEAD_SIZE].reshape(total_rows, HEAD_SIZE)
    values = kv_all[:, :, HEAD_SIZE:].reshape(total_rows, HEAD_SIZE)
    visible = key_pos[...] <= query_pos[...]
    inv_scale = 1.0 / math.sqrt(HEAD_SIZE)
    square_part = jnp.zeros((queries.shape[0], 1), jnp.float32)
    for h in range(queries.shape[1] // HEAD_SIZE):
        cols = slice(h * HEAD_SIZE, (h + 1) * HEAD_SIZE)
        scores = (
            lax.dot_general(
                queries[:, cols], keys, (((1,), (1,)), ((), ())), preferred_element_type=jnp.float32
            )
            * inv_scale
        )
        scores = jnp.where(visible, scores, MASKED_SCORE)
        newest = jnp.max(scores, axis=1, keepdims=True)
        weights = jnp.where(visible, jnp.exp(scores - newest), 0.0)
        weight_sum = jnp.sum(weights, axis=1, keepdims=True)
        weighted = jnp.dot(weights.astype(jnp.bfloat16), values, preferred_element_type=jnp.float32)
        attention = (weighted / weight_sum).astype(jnp.bfloat16)
        mixed_h = (residual[:, cols].astype(jnp.float32) + attention.astype(jnp.float32)).astype(
            jnp.bfloat16
        )
        mixed[:, cols] = mixed_h
        mixed_hf = mixed_h.astype(jnp.float32)
        square_part = square_part + jnp.sum(mixed_hf * mixed_hf, axis=1, keepdims=True)
    square_block[...] = jnp.broadcast_to(square_part, square_block.shape)

    def square_copy(r):
        return pltpu.make_async_remote_copy(
            src_ref=square_block,
            dst_ref=square_all.at[me_e],
            send_sem=q_send.at[r],
            recv_sem=q_recv.at[me_e],
            device_id={"exp": r},
            device_id_type=MESH,
        )

    for k in range(1, n_exp):
        square_copy(lax.rem(me_e + k, n_exp)).start()
    pltpu.make_async_copy(square_block, square_all.at[me_e], q_recv.at[me_e]).start()
    for s in range(n_exp):
        pltpu.make_async_copy(square_all.at[s], square_all.at[s], q_recv.at[s]).wait()
    square_sum = square_all[0]
    for s in range(1, n_exp):
        square_sum = square_sum + square_all[s]
    scale = lax.rsqrt(square_sum[:, :1] / D + NORM_EPS)
    mixed_f = mixed[...].astype(jnp.float32)
    normed = (mixed_f * scale * gain[...]).astype(jnp.bfloat16)
    filled = jnp.dot(slot_rows[...], normed, preferred_element_type=jnp.float32)
    outgoing[...] = filled.astype(outgoing.dtype).reshape(outgoing.shape)

    def dispatch_copy(p):
        return pltpu.make_async_remote_copy(
            src_ref=outgoing.at[p],
            dst_ref=incoming.at[me_c],
            send_sem=d_send.at[p],
            recv_sem=d_recv.at[me_c],
            device_id={"ctx": p},
            device_id_type=MESH,
        )

    for t in range(n_exp):
        z_r = lax.rem(plane + 2 * n_exp - me_e - t, n_exp)
        for y in range(per_chunk):
            p = z_r * per_chunk + y

            @pl.when(p != me_c)
            def _():
                dispatch_copy(p).start()

            @pl.when(p == me_c)
            def _():
                pltpu.make_async_copy(outgoing.at[p], incoming.at[p], d_recv.at[p]).start()

    parts = ((gate_w, gate_stage, gate_recv), (up_w, up_stage, up_recv))

    def reduce_copy(j, which):
        _, stage, recv = parts[which]
        return pltpu.make_async_remote_copy(
            src_ref=stage.at[j],
            dst_ref=recv.at[me_e],
            send_sem=r_send.at[j, which],
            recv_sem=r_recv.at[me_e, which],
            device_id={"exp": j},
            device_id_type=MESH,
        )

    rows = gate_stage.shape[2]
    for t in range(n_exp):
        j = lax.rem(plane + me_e + t, n_exp)
        for y in range(per_chunk):
            s = j * per_chunk + y
            pltpu.make_async_copy(incoming.at[s], incoming.at[s], d_recv.at[s]).wait()
        first = pl.multiple_of(j * per_chunk, per_chunk)
        for k in range(EXP_ROW):
            x = incoming[pl.ds(first, per_chunk), k].reshape(rows, incoming.shape[-1])
            for w, stage, _ in parts:
                stage[j, k] = jnp.dot(x, w[k], preferred_element_type=jnp.float32).astype(
                    stage.dtype
                )

        @pl.when(j != me_e)
        def _():
            for which in range(2):
                reduce_copy(j, which).start()

        @pl.when(j == me_e)
        def _():
            for which, (_, stage, recv) in enumerate(parts):
                pltpu.make_async_copy(stage.at[j], recv.at[j], r_recv.at[j, which]).start()

    for s in range(n_exp):
        for which, (_, _, recv) in enumerate(parts):
            pltpu.make_async_copy(recv.at[s], recv.at[s], r_recv.at[s, which]).wait()
    gate_sum = gate_recv[0].astype(jnp.float32)
    up_sum = up_recv[0].astype(jnp.float32)
    for s in range(1, n_exp):
        gate_sum = gate_sum + gate_recv[s].astype(jnp.float32)
        up_sum = up_sum + up_recv[s].astype(jnp.float32)
    hidden_mine[...] = (gate_sum / (1.0 + jnp.exp(-gate_sum)) * up_sum).astype(hidden_mine.dtype)

    def gather_copy(r):
        return pltpu.make_async_remote_copy(
            src_ref=hidden_mine,
            dst_ref=hidden_all.at[me_e],
            send_sem=a_send.at[r],
            recv_sem=a_recv.at[me_e],
            device_id={"exp": r},
            device_id_type=MESH,
        )

    for t in range(n_exp):
        r = lax.rem(me_e + 2 * n_exp - plane - t, n_exp)

        @pl.when(r != me_e)
        def _():
            gather_copy(r).start()

        @pl.when(r == me_e)
        def _():
            pltpu.make_async_copy(hidden_mine, hidden_all.at[r], a_recv.at[r]).start()

    def return_copy(s):
        return pltpu.make_async_remote_copy(
            src_ref=ret_stage.at[s],
            dst_ref=returned.at[me_c],
            send_sem=b_send.at[s],
            recv_sem=b_recv.at[me_c],
            device_id={"ctx": s},
            device_id_type=MESH,
        )

    for t in range(n_exp):
        j = lax.rem(me_e + plane + t, n_exp)
        pltpu.make_async_copy(hidden_all.at[j], hidden_all.at[j], a_recv.at[j]).wait()
        first = pl.multiple_of(j * per_chunk, per_chunk)
        for k in range(EXP_ROW):
            res = jnp.dot(hidden_all[j, k], down_w[k], preferred_element_type=jnp.float32)
            ret_stage[pl.ds(first, per_chunk), k] = res.astype(ret_stage.dtype).reshape(
                per_chunk, rows // per_chunk, res.shape[-1]
            )
        for y in range(per_chunk):
            s = j * per_chunk + y

            @pl.when(s != me_c)
            def _():
                return_copy(s).start()

            @pl.when(s == me_c)
            def _():
                pltpu.make_async_copy(ret_stage.at[s], returned.at[s], b_recv.at[s]).start()

    for s in range(n_ctx):
        pltpu.make_async_copy(returned.at[s], returned.at[s], b_recv.at[s]).wait()
    back = returned[...].reshape(w_hi.shape[1], returned.shape[-1])
    routed = jnp.dot(w_hi[...], back, preferred_element_type=jnp.float32) + jnp.dot(
        w_lo[...], back, preferred_element_type=jnp.float32
    )
    out[...] = (mixed_f + routed).astype(out.dtype)

    for r in range(n_exp):

        @pl.when(r != me_e)
        def _():
            gather_copy(r).wait_send()
            square_copy(r).wait_send()
            for which in range(2):
                reduce_copy(r, which).wait_send()

    for p in range(n_ctx):

        @pl.when(p != me_c)
        def _():
            dispatch_copy(p).wait_send()
            return_copy(p).wait_send()

    for h in range(halves):
        for r in range(1, group):
            second_copy(h, r).wait_send()
    for h in range(halves):
        z_r = lax.rem(plane + 2 * planes - q - h * (planes // halves), planes)
        for y in range(per_chunk):
            p = z_r * per_chunk + y

            @pl.when(p != me_c)
            def _():
                first_copy(p).wait_send()


def moe(queries, kv_block, residual, query_pos, key_pos, gain, slot_rows, out_shape, gate_weight, up_weight,
        down_weight, w_hi, w_lo, n_ctx, n_exp, collective_id):
    mixed = residual
    square_shape = (residual.shape[0], 128)
    hid = gate_weight.shape[-1]
    size = math.prod(out_shape)
    slots = out_shape[0] * out_shape[2] // n_exp
    recv_shape = (n_exp, EXP_ROW, slots, hid)
    flops = 2 * 3 * size * hid + 2 * size * mixed.shape[0] * 3
    nbytes = 4 * size * 2 + 6 * gate_weight.size * 2 + 8 * n_exp * EXP_ROW * slots * hid * 2
    vmem = pltpu.VMEM
    return pl.pallas_call(
        functools.partial(moe_kernel, n_ctx, n_exp),
        out_shape=jax.ShapeDtypeStruct(mixed.shape, jnp.bfloat16),
        in_specs=[pl.BlockSpec(memory_space=pltpu.VMEM)] * 12,
        out_specs=pl.BlockSpec(memory_space=pltpu.VMEM),
        scratch_shapes=[
            vmem((n_ctx,) + kv_block.shape, jnp.bfloat16),
            vmem(residual.shape, jnp.bfloat16),
            vmem(square_shape, jnp.float32),
            vmem((n_exp,) + square_shape, jnp.float32),
            vmem(out_shape, jnp.bfloat16),
            vmem(out_shape, jnp.bfloat16),
            vmem(recv_shape, jnp.bfloat16),
            vmem(recv_shape, jnp.bfloat16),
            vmem(recv_shape, jnp.bfloat16),
            vmem(recv_shape, jnp.bfloat16),
            vmem(recv_shape[1:], jnp.bfloat16),
            vmem(recv_shape, jnp.bfloat16),
            vmem(out_shape, jnp.bfloat16),
            vmem(out_shape, jnp.bfloat16),
            pltpu.SemaphoreType.DMA((n_ctx,)),
            pltpu.SemaphoreType.DMA((n_ctx,)),
            pltpu.SemaphoreType.DMA((n_exp, 2)),
            pltpu.SemaphoreType.DMA((n_exp, 2)),
            pltpu.SemaphoreType.DMA((n_exp,)),
            pltpu.SemaphoreType.DMA((n_exp,)),
            pltpu.SemaphoreType.DMA((n_ctx,)),
            pltpu.SemaphoreType.DMA((n_ctx,)),
            pltpu.SemaphoreType.DMA((n_exp, 2)),
            pltpu.SemaphoreType.DMA((n_exp, 2)),
            pltpu.SemaphoreType.DMA((n_exp,)),
            pltpu.SemaphoreType.DMA((n_exp,)),
            pltpu.SemaphoreType.DMA((n_ctx,)),
            pltpu.SemaphoreType.DMA((n_ctx,)),
        ],
        compiler_params=pltpu.CompilerParams(collective_id=collective_id, has_side_effects=True),
        cost_estimate=pl.CostEstimate(flops=flops, bytes_accessed=nbytes, transcendentals=0),
    )(queries, kv_block, residual, query_pos, key_pos, gain, slot_rows, gate_weight, up_weight, down_weight,
      w_hi, w_lo)

def kv_gather_kernel(n_ctx, n_exp, group, *refs):
    block, kv_all, s1_send, s1_recv, s2_send, s2_recv = refs
    per_plane = n_ctx // n_exp
    planes = n_ctx // per_plane
    me_c = lax.axis_index("ctx")
    me_e = lax.axis_index("exp")
    q = lax.rem(me_e, group)
    head_base = me_e - q
    plane = me_c // per_plane
    barrier = pltpu.get_barrier_semaphore()
    for k in range(1, n_ctx):
        pl.semaphore_signal(
            barrier, inc=1, device_id={"ctx": lax.rem(me_c + k, n_ctx)}, device_id_type=MESH
        )
    for k in range(1, group):
        pl.semaphore_signal(
            barrier, inc=1, device_id={"exp": head_base + lax.rem(q + k, group)}, device_id_type=MESH
        )
    pl.semaphore_wait(barrier, n_ctx + group - 2)

    def first_copy(p):
        return pltpu.make_async_remote_copy(
            src_ref=block,
            dst_ref=kv_all.at[me_c],
            send_sem=s1_send.at[p],
            recv_sem=s1_recv.at[me_c],
            device_id={"ctx": p},
            device_id_type=MESH,
        )

    halves = 2
    for h in range(halves):
        z_r = lax.rem(plane + 2 * planes - q - h * (planes // halves), planes)
        for y in range(per_plane):
            p = z_r * per_plane + y

            @pl.when(p != me_c)
            def _():
                first_copy(p).start()

            @pl.when(p == me_c)
            def _():
                pltpu.make_async_copy(block, kv_all.at[p], s1_recv.at[p]).start()

    def second_copy(h, r):
        first = pl.multiple_of(lax.rem(plane + q + h * (planes // halves), planes) * per_plane, per_plane)
        return pltpu.make_async_remote_copy(
            src_ref=kv_all.at[pl.ds(first, per_plane)],
            dst_ref=kv_all.at[pl.ds(first, per_plane)],
            send_sem=s2_send.at[r, h],
            recv_sem=s2_recv.at[r, h],
            device_id={"exp": head_base + lax.rem(q + r, group)},
            device_id_type=MESH,
        )

    for h in range(halves):
        z_s = lax.rem(plane + q + h * (planes // halves), planes)
        for y in range(per_plane):
            s = z_s * per_plane + y
            pltpu.make_async_copy(kv_all.at[s], kv_all.at[s], s1_recv.at[s]).wait()
        for r in range(1, group):
            second_copy(h, r).start()
    for h in range(halves):
        for r in range(1, group):
            second_copy(h, r).wait_recv()
    for h in range(halves):
        for r in range(1, group):
            second_copy(h, r).wait_send()
    for h in range(halves):
        z_r = lax.rem(plane + 2 * planes - q - h * (planes // halves), planes)
        for y in range(per_plane):
            p = z_r * per_plane + y

            @pl.when(p != me_c)
            def _():
                first_copy(p).wait_send()


def kv_gather(block, n_ctx, n_exp, group, collective_id):
    nbytes = block.size * block.dtype.itemsize * n_ctx
    return pl.pallas_call(
        functools.partial(kv_gather_kernel, n_ctx, n_exp, group),
        out_shape=jax.ShapeDtypeStruct((n_ctx,) + block.shape, block.dtype),
        in_specs=[pl.BlockSpec(memory_space=pltpu.VMEM)],
        out_specs=pl.BlockSpec(memory_space=pltpu.VMEM),
        scratch_shapes=[
            pltpu.SemaphoreType.DMA((n_ctx,)),
            pltpu.SemaphoreType.DMA((n_ctx,)),
            pltpu.SemaphoreType.DMA((group, 2)),
            pltpu.SemaphoreType.DMA((group, 2)),
        ],
        compiler_params=pltpu.CompilerParams(collective_id=collective_id, has_side_effects=True),
        cost_estimate=pl.CostEstimate(flops=0, bytes_accessed=2 * nbytes, transcendentals=0),
    )(block)


def local(
    queries,
    key_rows,
    value_head_rows,
    block_order,
    residual,
    norm_gain,
    expert_ids,
    route_weight,
    gate_weight,
    up_weight,
    down_weight,
):
    shard_rows = queries.shape[0]
    ctx_count = lax.axis_size("ctx")
    exp_count = lax.axis_size("exp")
    local_head = queries.shape[1] // HEAD_SIZE
    expert_index = lax.axis_index("exp")
    ctx_index = lax.axis_index("ctx")
    key_value_head = expert_index * local_head // (QUERY_HEADS // KEY_VALUE_HEADS)
    my_keys = lax.dynamic_slice_in_dim(key_rows, key_value_head * HEAD_SIZE, HEAD_SIZE, 1)
    my_values = lax.dynamic_slice_in_dim(value_head_rows, key_value_head * HEAD_SIZE, HEAD_SIZE, 1)
    block_ids = jnp.arange(ctx_count, dtype=jnp.int32)
    own_block = jnp.sum(jnp.where(block_ids == ctx_index, block_order, 0))
    local_rows = jnp.arange(shard_rows, dtype=jnp.int32)
    query_pos = (own_block * shard_rows + local_rows).reshape(shard_rows, 1)
    key_index = jnp.arange(ctx_count * shard_rows, dtype=jnp.int32)
    owner_shard = key_index // shard_rows
    key_block = jnp.sum(
        jnp.where(owner_shard[:, None] == block_ids[None, :], block_order[None, :], 0), axis=1
    )
    key_pos = (key_block * shard_rows + key_index % shard_rows).reshape(1, -1)
    kv_block = jnp.concatenate([my_keys, my_values], axis=1)
    expert_count = ctx_count * EXP_ROW
    capacity = 2 * shard_rows * TOPK // expert_count
    flat_ids = expert_ids.reshape(-1)
    onehot = (flat_ids[:, None] == jnp.arange(expert_count, dtype=jnp.int32)[None, :]).astype(
        jnp.int32
    )
    slot_rank = jnp.sum((jnp.cumsum(onehot, axis=0) - onehot) * onehot, axis=1)
    slot_index = flat_ids * capacity + slot_rank
    slot_total = expert_count * capacity
    slot_rows = jnp.any(
        slot_index.reshape(shard_rows, TOPK)[None, :, :]
        == jnp.arange(slot_total, dtype=jnp.int32)[:, None, None],
        axis=2,
    ).astype(jnp.bfloat16)
    slot_weight = jnp.sum(
        jnp.where(
            slot_index.reshape(shard_rows, TOPK)[:, :, None]
            == jnp.arange(slot_total, dtype=jnp.int32)[None, None, :],
            route_weight[:, :, None],
            0.0,
        ),
        axis=1,
    )
    w_hi = slot_weight.astype(jnp.bfloat16)
    w_lo = (slot_weight - w_hi.astype(jnp.float32)).astype(jnp.bfloat16)
    return moe(
        queries,
        kv_block,
        residual,
        query_pos,
        key_pos,
        norm_gain.reshape(1, -1),
        slot_rows,
        (ctx_count, EXP_ROW, capacity, residual.shape[1]),
        gate_weight,
        up_weight,
        down_weight,
        w_hi,
        w_lo,
        ctx_count,
        exp_count,
        2,
    )

def solution(mesh):
    placed = (
        P(("rep", "ctx"), "exp"),
        P(("rep", "ctx"), None),
        P(("rep", "ctx"), None),
        P("rep"),
        P(("rep", "ctx"), "exp"),
        P("exp"),
        P(("rep", "ctx"), None),
        P(("rep", "ctx"), None),
        P("ctx", "exp", None),
        P("ctx", "exp", None),
        P("ctx", None, "exp"),
    )
    return jax.shard_map(
        local, mesh=mesh, in_specs=placed, out_specs=P(("rep", "ctx"), "exp"), check_vma=False
    )
```

```python
import functools
import math

import jax
import jax.numpy as jnp
from jax import lax
from jax.experimental import pallas as pl
from jax.experimental.pallas import tpu as pltpu
from jax.sharding import PartitionSpec as P

D = 4096
QUERY_HEADS = 32
KEY_VALUE_HEADS = 2
HEAD_SIZE = 128
TOPK = 8
EXP_ROW = 2

MASKED_SCORE = -1e30
NORM_EPS = 1e-06
MESH = pl.DeviceIdType.MESH
Y_LO = 2


def exchange_kernel(axis, n, gather, n_in, *refs):
    ins, outs = refs[:n_in], refs[n_in : 2 * n_in]
    send_sem, recv_sem = refs[2 * n_in], refs[2 * n_in + 1]
    me = lax.axis_index(axis)
    barrier = pltpu.get_barrier_semaphore()
    for k in range(1, n):
        pl.semaphore_signal(
            barrier, inc=1, device_id={axis: lax.rem(me + k, n)}, device_id_type=MESH
        )
    pl.semaphore_wait(barrier, n - 1)
    copies = []
    for k in range(1, n):
        peer = lax.rem(me + k, n)
        for i in range(n_in):
            copy = pltpu.make_async_remote_copy(
                src_ref=ins[i] if gather else ins[i].at[peer],
                dst_ref=outs[i].at[me],
                send_sem=send_sem.at[i, k],
                recv_sem=recv_sem.at[i, k],
                device_id={axis: peer},
                device_id_type=MESH,
            )
            copy.start()
            copies.append(copy)
    for i in range(n_in):
        outs[i][me] = ins[i][...] if gather else ins[i][me]
    for copy in copies:
        copy.wait()


def exchange(xs, axis, n, gather, collective_id):
    n_in = len(xs)
    out_shape = [
        jax.ShapeDtypeStruct((n,) + (x.shape if gather else x.shape[1:]), x.dtype) for x in xs
    ]
    nbytes = sum(x.size * x.dtype.itemsize for x in xs) * (n if gather else 1)
    return pl.pallas_call(
        functools.partial(exchange_kernel, axis, n, gather, n_in),
        out_shape=out_shape,
        in_specs=[pl.BlockSpec(memory_space=pltpu.VMEM)] * n_in,
        out_specs=[pl.BlockSpec(memory_space=pltpu.VMEM)] * n_in,
        scratch_shapes=[
            pltpu.SemaphoreType.DMA((n_in, n)),
            pltpu.SemaphoreType.DMA((n_in, n)),
        ],
        compiler_params=pltpu.CompilerParams(collective_id=collective_id, has_side_effects=True),
        cost_estimate=pl.CostEstimate(flops=0, bytes_accessed=2 * nbytes, transcendentals=0),
    )(*xs)


def moe_kernel(n_ctx, n_exp, *refs):
    (queries, kv_block, residual, query_pos, key_pos, gain, slot_rows, gate_w, up_w, down_w, w_hi, w_lo, out,
     kv_all, mixed, square_block, square_all, outgoing, incoming, gate_stage, up_stage, gate_recv, up_recv,
     hidden_mine, hidden_all, ret_stage, returned, column_sum, partner_sum, s1_send, s1_recv, s2_send, s2_recv,
     q_send, q_recv, d_send, d_recv, r_send, r_recv, a_send, a_recv, b_send, b_recv, p_sem) = refs
    per_chunk = n_ctx // n_exp
    me_c = lax.axis_index("ctx")
    me_e = lax.axis_index("exp")
    plane = me_c // per_chunk
    barrier = pltpu.get_barrier_semaphore()
    for k in range(1, n_ctx):
        pl.semaphore_signal(
            barrier, inc=1, device_id={"ctx": lax.rem(me_c + k, n_ctx)}, device_id_type=MESH
        )
    for k in range(1, n_exp):
        pl.semaphore_signal(
            barrier, inc=1, device_id={"exp": lax.rem(me_e + k, n_exp)}, device_id_type=MESH
        )
    pl.semaphore_wait(barrier, n_ctx + n_exp - 2)

    group = QUERY_HEADS // KEY_VALUE_HEADS // (queries.shape[1] // HEAD_SIZE)
    q = lax.rem(me_e, group)
    head_base = me_e - q
    planes = n_exp
    halves = 2

    def first_copy(p):
        return pltpu.make_async_remote_copy(
            src_ref=kv_block,
            dst_ref=kv_all.at[me_c],
            send_sem=s1_send.at[p],
            recv_sem=s1_recv.at[me_c],
            device_id={"ctx": p},
            device_id_type=MESH,
        )

    for h in range(halves):
        z_r = lax.rem(plane + 2 * planes - q - h * (planes // halves), planes)
        for y in range(per_chunk):
            p = z_r * per_chunk + y

            @pl.when(p != me_c)
            def _():
                first_copy(p).start()

            @pl.when(p == me_c)
            def _():
                pltpu.make_async_copy(kv_block, kv_all.at[p], s1_recv.at[p]).start()

    def second_copy(h, r):
        first = pl.multiple_of(lax.rem(plane + q + h * (planes // halves), planes) * per_chunk, per_chunk)
        return pltpu.make_async_remote_copy(
            src_ref=kv_all.at[pl.ds(first, per_chunk)],
            dst_ref=kv_all.at[pl.ds(first, per_chunk)],
            send_sem=s2_send.at[r, h],
            recv_sem=s2_recv.at[r, h],
            device_id={"exp": head_base + lax.rem(q + r, group)},
            device_id_type=MESH,
        )

    for h in range(halves):
        z_s = lax.rem(plane + q + h * (planes // halves), planes)
        for y in range(per_chunk):
            s = z_s * per_chunk + y
            pltpu.make_async_copy(kv_all.at[s], kv_all.at[s], s1_recv.at[s]).wait()
        for r in range(1, group):
            second_copy(h, r).start()
    for h in range(halves):
        for r in range(1, group):
            second_copy(h, r).wait_recv()

    total_rows = kv_all.shape[0] * kv_all.shape[1]
    keys = kv_all[:, :, :HEAD_SIZE].reshape(total_rows, HEAD_SIZE)
    values = kv_all[:, :, HEAD_SIZE:].reshape(total_rows, HEAD_SIZE)
    visible = key_pos[...] <= query_pos[...]
    inv_scale = 1.0 / math.sqrt(HEAD_SIZE)
    square_part = jnp.zeros((queries.shape[0], 1), jnp.float32)
    for h in range(queries.shape[1] // HEAD_SIZE):
        cols = slice(h * HEAD_SIZE, (h + 1) * HEAD_SIZE)
        scores = (
            lax.dot_general(
                queries[:, cols], keys, (((1,), (1,)), ((), ())), preferred_element_type=jnp.float32
            )
            * inv_scale
        )
        scores = jnp.where(visible, scores, MASKED_SCORE)
        newest = jnp.max(scores, axis=1, keepdims=True)
        weights = jnp.where(visible, jnp.exp(scores - newest), 0.0)
        weight_sum = jnp.sum(weights, axis=1, keepdims=True)
        weighted = jnp.dot(weights.astype(jnp.bfloat16), values, preferred_element_type=jnp.float32)
        attention = (weighted / weight_sum).astype(jnp.bfloat16)
        mixed_h = (residual[:, cols].astype(jnp.float32) + attention.astype(jnp.float32)).astype(
            jnp.bfloat16
        )
        mixed[:, cols] = mixed_h
        mixed_hf = mixed_h.astype(jnp.float32)
        square_part = square_part + jnp.sum(mixed_hf * mixed_hf, axis=1, keepdims=True)
    square_block[...] = jnp.broadcast_to(square_part, square_block.shape)

    def square_copy(r):
        return pltpu.make_async_remote_copy(
            src_ref=square_block,
            dst_ref=square_all.at[me_e],
            send_sem=q_send.at[r],
            recv_sem=q_recv.at[me_e],
            device_id={"exp": r},
            device_id_type=MESH,
        )

    for k in range(1, n_exp):
        square_copy(lax.rem(me_e + k, n_exp)).start()
    pltpu.make_async_copy(square_block, square_all.at[me_e], q_recv.at[me_e]).start()
    for s in range(n_exp):
        pltpu.make_async_copy(square_all.at[s], square_all.at[s], q_recv.at[s]).wait()
    square_sum = square_all[0]
    for s in range(1, n_exp):
        square_sum = square_sum + square_all[s]
    scale = lax.rsqrt(square_sum[:, :1] / D + NORM_EPS)
    mixed_f = mixed[...].astype(jnp.float32)
    normed = (mixed_f * scale * gain[...]).astype(jnp.bfloat16)
    filled = jnp.dot(slot_rows[...], normed, preferred_element_type=jnp.float32)
    outgoing[...] = filled.astype(outgoing.dtype).reshape(outgoing.shape)

    def dispatch_copy(p):
        return pltpu.make_async_remote_copy(
            src_ref=outgoing.at[p],
            dst_ref=incoming.at[me_c],
            send_sem=d_send.at[p],
            recv_sem=d_recv.at[me_c],
            device_id={"ctx": p},
            device_id_type=MESH,
        )

    for t in range(n_exp):
        z_r = lax.rem(plane + 2 * n_exp - me_e - t, n_exp)
        for y in range(per_chunk):
            p = z_r * per_chunk + y

            @pl.when(p != me_c)
            def _():
                dispatch_copy(p).start()

            @pl.when(p == me_c)
            def _():
                pltpu.make_async_copy(outgoing.at[p], incoming.at[p], d_recv.at[p]).start()

    parts = ((gate_w, gate_stage, gate_recv), (up_w, up_stage, up_recv))
    mx = me_e // Y_LO
    my = lax.rem(me_e, Y_LO)

    def reduce_copy(j, which):
        _, stage, recv = parts[which]
        return pltpu.make_async_remote_copy(
            src_ref=stage.at[j],
            dst_ref=recv.at[mx, lax.rem(j, Y_LO)],
            send_sem=r_send.at[j // Y_LO, lax.rem(j, Y_LO), which],
            recv_sem=r_recv.at[mx, lax.rem(j, Y_LO), which],
            device_id={"exp": (j // Y_LO) * Y_LO + my},
            device_id_type=MESH,
        )

    rows = gate_stage.shape[2]
    for t in range(n_exp):
        j = lax.rem(plane + me_e + t, n_exp)
        for y in range(per_chunk):
            s = j * per_chunk + y
            pltpu.make_async_copy(incoming.at[s], incoming.at[s], d_recv.at[s]).wait()
        first = pl.multiple_of(j * per_chunk, per_chunk)
        for k in range(EXP_ROW):
            x = incoming[pl.ds(first, per_chunk), k].reshape(rows, incoming.shape[-1])
            for w, stage, _ in parts:
                stage[j, k] = jnp.dot(x, w[k], preferred_element_type=jnp.float32).astype(
                    stage.dtype
                )

        @pl.when(j // Y_LO != mx)
        def _():
            for which in range(2):
                reduce_copy(j, which).start()

        @pl.when(j // Y_LO == mx)
        def _():
            for which, (_, stage, recv) in enumerate(parts):
                pltpu.make_async_copy(
                    stage.at[j], recv.at[mx, lax.rem(j, Y_LO)], r_recv.at[mx, lax.rem(j, Y_LO), which]
                ).start()

    n_x = n_exp // Y_LO
    for sx in range(n_x):
        for cy in range(Y_LO):
            for which, (_, _, recv) in enumerate(parts):
                pltpu.make_async_copy(recv.at[sx, cy], recv.at[sx, cy], r_recv.at[sx, cy, which]).wait()
    for cy in range(Y_LO):
        for which, (_, _, recv) in enumerate(parts):
            total = recv[0, cy].astype(jnp.float32)
            for sx in range(1, n_x):
                total = total + recv[sx, cy].astype(jnp.float32)
            column_sum[cy, which] = total
    partner_copy = pltpu.make_async_remote_copy(
        src_ref=column_sum.at[Y_LO - 1 - my],
        dst_ref=partner_sum,
        send_sem=p_sem.at[0],
        recv_sem=p_sem.at[1],
        device_id={"exp": mx * Y_LO + Y_LO - 1 - my},
        device_id_type=MESH,
    )
    partner_copy.start()
    partner_copy.wait_recv()
    gate_sum = column_sum[my, 0] + partner_sum[0]
    up_sum = column_sum[my, 1] + partner_sum[1]
    hidden_mine[...] = (gate_sum / (1.0 + jnp.exp(-gate_sum)) * up_sum).astype(hidden_mine.dtype)

    def gather_copy(r):
        return pltpu.make_async_remote_copy(
            src_ref=hidden_mine,
            dst_ref=hidden_all.at[me_e],
            send_sem=a_send.at[r],
            recv_sem=a_recv.at[me_e],
            device_id={"exp": r},
            device_id_type=MESH,
        )

    for t in range(n_exp):
        r = lax.rem(me_e + 2 * n_exp - plane - t, n_exp)

        @pl.when(r != me_e)
        def _():
            gather_copy(r).start()

        @pl.when(r == me_e)
        def _():
            pltpu.make_async_copy(hidden_mine, hidden_all.at[r], a_recv.at[r]).start()

    def return_copy(s):
        return pltpu.make_async_remote_copy(
            src_ref=ret_stage.at[s],
            dst_ref=returned.at[me_c],
            send_sem=b_send.at[s],
            recv_sem=b_recv.at[me_c],
            device_id={"ctx": s},
            device_id_type=MESH,
        )

    for t in range(n_exp):
        j = lax.rem(me_e + plane + t, n_exp)
        pltpu.make_async_copy(hidden_all.at[j], hidden_all.at[j], a_recv.at[j]).wait()
        first = pl.multiple_of(j * per_chunk, per_chunk)
        for k in range(EXP_ROW):
            res = jnp.dot(hidden_all[j, k], down_w[k], preferred_element_type=jnp.float32)
            ret_stage[pl.ds(first, per_chunk), k] = res.astype(ret_stage.dtype).reshape(
                per_chunk, rows // per_chunk, res.shape[-1]
            )
        for y in range(per_chunk):
            s = j * per_chunk + y

            @pl.when(s != me_c)
            def _():
                return_copy(s).start()

            @pl.when(s == me_c)
            def _():
                pltpu.make_async_copy(ret_stage.at[s], returned.at[s], b_recv.at[s]).start()

    for s in range(n_ctx):
        pltpu.make_async_copy(returned.at[s], returned.at[s], b_recv.at[s]).wait()
    back = returned[...].reshape(w_hi.shape[1], returned.shape[-1])
    routed = jnp.dot(w_hi[...], back, preferred_element_type=jnp.float32) + jnp.dot(
        w_lo[...], back, preferred_element_type=jnp.float32
    )
    out[...] = (mixed_f + routed).astype(out.dtype)

    for r in range(n_exp):

        @pl.when(r != me_e)
        def _():
            gather_copy(r).wait_send()
            square_copy(r).wait_send()

        @pl.when(r // Y_LO != mx)
        def _():
            for which in range(2):
                reduce_copy(r, which).wait_send()

    partner_copy.wait_send()

    for p in range(n_ctx):

        @pl.when(p != me_c)
        def _():
            dispatch_copy(p).wait_send()
            return_copy(p).wait_send()

    for h in range(halves):
        for r in range(1, group):
            second_copy(h, r).wait_send()
    for h in range(halves):
        z_r = lax.rem(plane + 2 * planes - q - h * (planes // halves), planes)
        for y in range(per_chunk):
            p = z_r * per_chunk + y

            @pl.when(p != me_c)
            def _():
                first_copy(p).wait_send()


def moe(queries, kv_block, residual, query_pos, key_pos, gain, slot_rows, out_shape, gate_weight, up_weight,
        down_weight, w_hi, w_lo, n_ctx, n_exp, collective_id):
    mixed = residual
    square_shape = (residual.shape[0], 128)
    hid = gate_weight.shape[-1]
    size = math.prod(out_shape)
    slots = out_shape[0] * out_shape[2] // n_exp
    recv_shape = (n_exp, EXP_ROW, slots, hid)
    column_shape = (n_exp // Y_LO, Y_LO, EXP_ROW, slots, hid)
    flops = 2 * 3 * size * hid + 2 * size * mixed.shape[0] * 3
    nbytes = 4 * size * 2 + 6 * gate_weight.size * 2 + 8 * n_exp * EXP_ROW * slots * hid * 2
    vmem = pltpu.VMEM
    return pl.pallas_call(
        functools.partial(moe_kernel, n_ctx, n_exp),
        out_shape=jax.ShapeDtypeStruct(mixed.shape, jnp.bfloat16),
        in_specs=[pl.BlockSpec(memory_space=pltpu.VMEM)] * 12,
        out_specs=pl.BlockSpec(memory_space=pltpu.VMEM),
        scratch_shapes=[
            vmem((n_ctx,) + kv_block.shape, jnp.bfloat16),
            vmem(residual.shape, jnp.bfloat16),
            vmem(square_shape, jnp.float32),
            vmem((n_exp,) + square_shape, jnp.float32),
            vmem(out_shape, jnp.bfloat16),
            vmem(out_shape, jnp.bfloat16),
            vmem(recv_shape, jnp.bfloat16),
            vmem(recv_shape, jnp.bfloat16),
            vmem(column_shape, jnp.bfloat16),
            vmem(column_shape, jnp.bfloat16),
            vmem(recv_shape[1:], jnp.bfloat16),
            vmem(recv_shape, jnp.bfloat16),
            vmem(out_shape, jnp.bfloat16),
            vmem(out_shape, jnp.bfloat16),
            vmem((Y_LO, 2) + recv_shape[1:], jnp.float32),
            vmem((2,) + recv_shape[1:], jnp.float32),
            pltpu.SemaphoreType.DMA((n_ctx,)),
            pltpu.SemaphoreType.DMA((n_ctx,)),
            pltpu.SemaphoreType.DMA((n_exp, 2)),
            pltpu.SemaphoreType.DMA((n_exp, 2)),
            pltpu.SemaphoreType.DMA((n_exp,)),
            pltpu.SemaphoreType.DMA((n_exp,)),
            pltpu.SemaphoreType.DMA((n_ctx,)),
            pltpu.SemaphoreType.DMA((n_ctx,)),
            pltpu.SemaphoreType.DMA((n_exp // Y_LO, Y_LO, 2)),
            pltpu.SemaphoreType.DMA((n_exp // Y_LO, Y_LO, 2)),
            pltpu.SemaphoreType.DMA((n_exp,)),
            pltpu.SemaphoreType.DMA((n_exp,)),
            pltpu.SemaphoreType.DMA((n_ctx,)),
            pltpu.SemaphoreType.DMA((n_ctx,)),
            pltpu.SemaphoreType.DMA((2,)),
        ],
        compiler_params=pltpu.CompilerParams(collective_id=collective_id, has_side_effects=True),
        cost_estimate=pl.CostEstimate(flops=flops, bytes_accessed=nbytes, transcendentals=0),
    )(queries, kv_block, residual, query_pos, key_pos, gain, slot_rows, gate_weight, up_weight, down_weight,
      w_hi, w_lo)

def kv_gather_kernel(n_ctx, n_exp, group, *refs):
    block, kv_all, s1_send, s1_recv, s2_send, s2_recv = refs
    per_plane = n_ctx // n_exp
    planes = n_ctx // per_plane
    me_c = lax.axis_index("ctx")
    me_e = lax.axis_index("exp")
    q = lax.rem(me_e, group)
    head_base = me_e - q
    plane = me_c // per_plane
    barrier = pltpu.get_barrier_semaphore()
    for k in range(1, n_ctx):
        pl.semaphore_signal(
            barrier, inc=1, device_id={"ctx": lax.rem(me_c + k, n_ctx)}, device_id_type=MESH
        )
    for k in range(1, group):
        pl.semaphore_signal(
            barrier, inc=1, device_id={"exp": head_base + lax.rem(q + k, group)}, device_id_type=MESH
        )
    pl.semaphore_wait(barrier, n_ctx + group - 2)

    def first_copy(p):
        return pltpu.make_async_remote_copy(
            src_ref=block,
            dst_ref=kv_all.at[me_c],
            send_sem=s1_send.at[p],
            recv_sem=s1_recv.at[me_c],
            device_id={"ctx": p},
            device_id_type=MESH,
        )

    halves = 2
    for h in range(halves):
        z_r = lax.rem(plane + 2 * planes - q - h * (planes // halves), planes)
        for y in range(per_plane):
            p = z_r * per_plane + y

            @pl.when(p != me_c)
            def _():
                first_copy(p).start()

            @pl.when(p == me_c)
            def _():
                pltpu.make_async_copy(block, kv_all.at[p], s1_recv.at[p]).start()

    def second_copy(h, r):
        first = pl.multiple_of(lax.rem(plane + q + h * (planes // halves), planes) * per_plane, per_plane)
        return pltpu.make_async_remote_copy(
            src_ref=kv_all.at[pl.ds(first, per_plane)],
            dst_ref=kv_all.at[pl.ds(first, per_plane)],
            send_sem=s2_send.at[r, h],
            recv_sem=s2_recv.at[r, h],
            device_id={"exp": head_base + lax.rem(q + r, group)},
            device_id_type=MESH,
        )

    for h in range(halves):
        z_s = lax.rem(plane + q + h * (planes // halves), planes)
        for y in range(per_plane):
            s = z_s * per_plane + y
            pltpu.make_async_copy(kv_all.at[s], kv_all.at[s], s1_recv.at[s]).wait()
        for r in range(1, group):
            second_copy(h, r).start()
    for h in range(halves):
        for r in range(1, group):
            second_copy(h, r).wait_recv()
    for h in range(halves):
        for r in range(1, group):
            second_copy(h, r).wait_send()
    for h in range(halves):
        z_r = lax.rem(plane + 2 * planes - q - h * (planes // halves), planes)
        for y in range(per_plane):
            p = z_r * per_plane + y

            @pl.when(p != me_c)
            def _():
                first_copy(p).wait_send()


def kv_gather(block, n_ctx, n_exp, group, collective_id):
    nbytes = block.size * block.dtype.itemsize * n_ctx
    return pl.pallas_call(
        functools.partial(kv_gather_kernel, n_ctx, n_exp, group),
        out_shape=jax.ShapeDtypeStruct((n_ctx,) + block.shape, block.dtype),
        in_specs=[pl.BlockSpec(memory_space=pltpu.VMEM)],
        out_specs=pl.BlockSpec(memory_space=pltpu.VMEM),
        scratch_shapes=[
            pltpu.SemaphoreType.DMA((n_ctx,)),
            pltpu.SemaphoreType.DMA((n_ctx,)),
            pltpu.SemaphoreType.DMA((group, 2)),
            pltpu.SemaphoreType.DMA((group, 2)),
        ],
        compiler_params=pltpu.CompilerParams(collective_id=collective_id, has_side_effects=True),
        cost_estimate=pl.CostEstimate(flops=0, bytes_accessed=2 * nbytes, transcendentals=0),
    )(block)


def local(
    queries,
    key_rows,
    value_head_rows,
    block_order,
    residual,
    norm_gain,
    expert_ids,
    route_weight,
    gate_weight,
    up_weight,
    down_weight,
):
    shard_rows = queries.shape[0]
    ctx_count = lax.axis_size("ctx")
    exp_count = lax.axis_size("exp")
    local_head = queries.shape[1] // HEAD_SIZE
    expert_index = lax.axis_index("exp")
    ctx_index = lax.axis_index("ctx")
    key_value_head = expert_index * local_head // (QUERY_HEADS // KEY_VALUE_HEADS)
    my_keys = lax.dynamic_slice_in_dim(key_rows, key_value_head * HEAD_SIZE, HEAD_SIZE, 1)
    my_values = lax.dynamic_slice_in_dim(value_head_rows, key_value_head * HEAD_SIZE, HEAD_SIZE, 1)
    block_ids = jnp.arange(ctx_count, dtype=jnp.int32)
    own_block = jnp.sum(jnp.where(block_ids == ctx_index, block_order, 0))
    local_rows = jnp.arange(shard_rows, dtype=jnp.int32)
    query_pos = (own_block * shard_rows + local_rows).reshape(shard_rows, 1)
    key_index = jnp.arange(ctx_count * shard_rows, dtype=jnp.int32)
    owner_shard = key_index // shard_rows
    key_block = jnp.sum(
        jnp.where(owner_shard[:, None] == block_ids[None, :], block_order[None, :], 0), axis=1
    )
    key_pos = (key_block * shard_rows + key_index % shard_rows).reshape(1, -1)
    kv_block = jnp.concatenate([my_keys, my_values], axis=1)
    expert_count = ctx_count * EXP_ROW
    capacity = 2 * shard_rows * TOPK // expert_count
    flat_ids = expert_ids.reshape(-1)
    onehot = (flat_ids[:, None] == jnp.arange(expert_count, dtype=jnp.int32)[None, :]).astype(
        jnp.int32
    )
    slot_rank = jnp.sum((jnp.cumsum(onehot, axis=0) - onehot) * onehot, axis=1)
    slot_index = flat_ids * capacity + slot_rank
    slot_total = expert_count * capacity
    slot_rows = jnp.any(
        slot_index.reshape(shard_rows, TOPK)[None, :, :]
        == jnp.arange(slot_total, dtype=jnp.int32)[:, None, None],
        axis=2,
    ).astype(jnp.bfloat16)
    slot_weight = jnp.sum(
        jnp.where(
            slot_index.reshape(shard_rows, TOPK)[:, :, None]
            == jnp.arange(slot_total, dtype=jnp.int32)[None, None, :],
            route_weight[:, :, None],
            0.0,
        ),
        axis=1,
    )
    w_hi = slot_weight.astype(jnp.bfloat16)
    w_lo = (slot_weight - w_hi.astype(jnp.float32)).astype(jnp.bfloat16)
    return moe(
        queries,
        kv_block,
        residual,
        query_pos,
        key_pos,
        norm_gain.reshape(1, -1),
        slot_rows,
        (ctx_count, EXP_ROW, capacity, residual.shape[1]),
        gate_weight,
        up_weight,
        down_weight,
        w_hi,
        w_lo,
        ctx_count,
        exp_count,
        2,
    )

def solution(mesh):
    placed = (
        P(("rep", "ctx"), "exp"),
        P(("rep", "ctx"), None),
        P(("rep", "ctx"), None),
        P("rep"),
        P(("rep", "ctx"), "exp"),
        P("exp"),
        P(("rep", "ctx"), None),
        P(("rep", "ctx"), None),
        P("ctx", "exp", None),
        P("ctx", "exp", None),
        P("ctx", None, "exp"),
    )
    return jax.shard_map(
        local, mesh=mesh, in_specs=placed, out_specs=P(("rep", "ctx"), "exp"), check_vma=False
    )
```

```python
import functools
import math

import jax
import jax.numpy as jnp
from jax import lax
from jax.experimental import pallas as pl
from jax.experimental.pallas import tpu as pltpu
from jax.sharding import PartitionSpec as P

D = 4096
QUERY_HEADS = 32
KEY_VALUE_HEADS = 2
HEAD_SIZE = 128
TOPK = 8
EXP_ROW = 2

MASKED_SCORE = -1e30
NORM_EPS = 1e-06
MESH = pl.DeviceIdType.MESH


def exchange_kernel(axis, n, gather, n_in, *refs):
    ins, outs = refs[:n_in], refs[n_in : 2 * n_in]
    send_sem, recv_sem = refs[2 * n_in], refs[2 * n_in + 1]
    me = lax.axis_index(axis)
    barrier = pltpu.get_barrier_semaphore()
    for k in range(1, n):
        pl.semaphore_signal(
            barrier, inc=1, device_id={axis: lax.rem(me + k, n)}, device_id_type=MESH
        )
    pl.semaphore_wait(barrier, n - 1)
    copies = []
    for k in range(1, n):
        peer = lax.rem(me + k, n)
        for i in range(n_in):
            copy = pltpu.make_async_remote_copy(
                src_ref=ins[i] if gather else ins[i].at[peer],
                dst_ref=outs[i].at[me],
                send_sem=send_sem.at[i, k],
                recv_sem=recv_sem.at[i, k],
                device_id={axis: peer},
                device_id_type=MESH,
            )
            copy.start()
            copies.append(copy)
    for i in range(n_in):
        outs[i][me] = ins[i][...] if gather else ins[i][me]
    for copy in copies:
        copy.wait()


def exchange(xs, axis, n, gather, collective_id):
    n_in = len(xs)
    out_shape = [
        jax.ShapeDtypeStruct((n,) + (x.shape if gather else x.shape[1:]), x.dtype) for x in xs
    ]
    nbytes = sum(x.size * x.dtype.itemsize for x in xs) * (n if gather else 1)
    return pl.pallas_call(
        functools.partial(exchange_kernel, axis, n, gather, n_in),
        out_shape=out_shape,
        in_specs=[pl.BlockSpec(memory_space=pltpu.VMEM)] * n_in,
        out_specs=[pl.BlockSpec(memory_space=pltpu.VMEM)] * n_in,
        scratch_shapes=[
            pltpu.SemaphoreType.DMA((n_in, n)),
            pltpu.SemaphoreType.DMA((n_in, n)),
        ],
        compiler_params=pltpu.CompilerParams(collective_id=collective_id, has_side_effects=True),
        cost_estimate=pl.CostEstimate(flops=0, bytes_accessed=2 * nbytes, transcendentals=0),
    )(*xs)


def moe_kernel(n_ctx, n_exp, *refs):
    (queries, key_rows, value_rows, residual, block_order, gain, slot_rows, gate_w, up_w, down_w, w_hi, w_lo, out,
     kv_block, kv_all, mixed, square_block, square_all, outgoing, incoming, gate_stage, up_stage, gate_recv, up_recv,
     hidden_mine, hidden_all, ret_stage, returned, s1_send, s1_recv, s2_send, s2_recv, q_send, q_recv, d_send,
     d_recv, r_send, r_recv, a_send, a_recv, b_send, b_recv) = refs
    per_chunk = n_ctx // n_exp
    me_c = lax.axis_index("ctx")
    me_e = lax.axis_index("exp")
    plane = me_c // per_chunk
    barrier = pltpu.get_barrier_semaphore()
    for k in range(1, n_ctx):
        pl.semaphore_signal(
            barrier, inc=1, device_id={"ctx": lax.rem(me_c + k, n_ctx)}, device_id_type=MESH
        )
    for k in range(1, n_exp):
        pl.semaphore_signal(
            barrier, inc=1, device_id={"exp": lax.rem(me_e + k, n_exp)}, device_id_type=MESH
        )
    pl.semaphore_wait(barrier, n_ctx + n_exp - 2)

    group = QUERY_HEADS // KEY_VALUE_HEADS // (queries.shape[1] // HEAD_SIZE)
    head_cols = pl.ds(pl.multiple_of((me_e // group) * HEAD_SIZE, HEAD_SIZE), HEAD_SIZE)
    kv_block[:, :HEAD_SIZE] = key_rows[:, head_cols]
    kv_block[:, HEAD_SIZE:] = value_rows[:, head_cols]
    q = lax.rem(me_e, group)
    head_base = me_e - q
    planes = n_exp
    halves = 2

    def first_copy(p):
        return pltpu.make_async_remote_copy(
            src_ref=kv_block,
            dst_ref=kv_all.at[me_c],
            send_sem=s1_send.at[p],
            recv_sem=s1_recv.at[me_c],
            device_id={"ctx": p},
            device_id_type=MESH,
        )

    for h in range(halves):
        z_r = lax.rem(plane + 2 * planes - q - h * (planes // halves), planes)
        for y in range(per_chunk):
            p = z_r * per_chunk + y

            @pl.when(p != me_c)
            def _():
                first_copy(p).start()

            @pl.when(p == me_c)
            def _():
                pltpu.make_async_copy(kv_block, kv_all.at[p], s1_recv.at[p]).start()

    def second_copy(h, r):
        first = pl.multiple_of(lax.rem(plane + q + h * (planes // halves), planes) * per_chunk, per_chunk)
        return pltpu.make_async_remote_copy(
            src_ref=kv_all.at[pl.ds(first, per_chunk)],
            dst_ref=kv_all.at[pl.ds(first, per_chunk)],
            send_sem=s2_send.at[r, h],
            recv_sem=s2_recv.at[r, h],
            device_id={"exp": head_base + lax.rem(q + r, group)},
            device_id_type=MESH,
        )

    for h in range(halves):
        z_s = lax.rem(plane + q + h * (planes // halves), planes)
        for y in range(per_chunk):
            s = z_s * per_chunk + y
            pltpu.make_async_copy(kv_all.at[s], kv_all.at[s], s1_recv.at[s]).wait()
        for r in range(1, group):
            second_copy(h, r).start()
    for h in range(halves):
        for r in range(1, group):
            second_copy(h, r).wait_recv()

    total_rows = kv_all.shape[0] * kv_all.shape[1]
    keys = kv_all[:, :, :HEAD_SIZE].reshape(total_rows, HEAD_SIZE)
    values = kv_all[:, :, HEAD_SIZE:].reshape(total_rows, HEAD_SIZE)
    block_rows = kv_all.shape[1]
    query_pos = block_order[me_c] * block_rows + lax.broadcasted_iota(jnp.int32, (queries.shape[0], 1), 0)
    key_lane = lax.broadcasted_iota(jnp.int32, (1, total_rows), 1)
    key_pos = key_lane % block_rows
    for b in range(kv_all.shape[0]):
        key_pos = jnp.where(key_lane // block_rows == b, key_pos + block_order[b] * block_rows, key_pos)
    visible = key_pos <= query_pos
    inv_scale = 1.0 / math.sqrt(HEAD_SIZE)
    square_part = jnp.zeros((queries.shape[0], 1), jnp.float32)
    for h in range(queries.shape[1] // HEAD_SIZE):
        cols = slice(h * HEAD_SIZE, (h + 1) * HEAD_SIZE)
        scores = (
            lax.dot_general(
                queries[:, cols], keys, (((1,), (1,)), ((), ())), preferred_element_type=jnp.float32
            )
            * inv_scale
        )
        scores = jnp.where(visible, scores, MASKED_SCORE)
        newest = jnp.max(scores, axis=1, keepdims=True)
        weights = jnp.where(visible, jnp.exp(scores - newest), 0.0)
        weight_sum = jnp.sum(weights, axis=1, keepdims=True)
        weighted = jnp.dot(weights.astype(jnp.bfloat16), values, preferred_element_type=jnp.float32)
        attention = (weighted / weight_sum).astype(jnp.bfloat16)
        mixed_h = (residual[:, cols].astype(jnp.float32) + attention.astype(jnp.float32)).astype(
            jnp.bfloat16
        )
        mixed[:, cols] = mixed_h
        mixed_hf = mixed_h.astype(jnp.float32)
        square_part = square_part + jnp.sum(mixed_hf * mixed_hf, axis=1, keepdims=True)
    square_block[...] = jnp.broadcast_to(square_part, square_block.shape)

    def square_copy(r):
        return pltpu.make_async_remote_copy(
            src_ref=square_block,
            dst_ref=square_all.at[me_e],
            send_sem=q_send.at[r],
            recv_sem=q_recv.at[me_e],
            device_id={"exp": r},
            device_id_type=MESH,
        )

    for k in range(1, n_exp):
        square_copy(lax.rem(me_e + k, n_exp)).start()
    pltpu.make_async_copy(square_block, square_all.at[me_e], q_recv.at[me_e]).start()
    for s in range(n_exp):
        pltpu.make_async_copy(square_all.at[s], square_all.at[s], q_recv.at[s]).wait()
    square_sum = square_all[0]
    for s in range(1, n_exp):
        square_sum = square_sum + square_all[s]
    scale = lax.rsqrt(square_sum[:, :1] / D + NORM_EPS)
    mixed_f = mixed[...].astype(jnp.float32)
    normed = (mixed_f * scale * gain[...]).astype(jnp.bfloat16)
    filled = jnp.dot(slot_rows[...], normed, preferred_element_type=jnp.float32)
    outgoing[...] = filled.astype(outgoing.dtype).reshape(outgoing.shape)

    def dispatch_copy(p):
        return pltpu.make_async_remote_copy(
            src_ref=outgoing.at[p],
            dst_ref=incoming.at[me_c],
            send_sem=d_send.at[p],
            recv_sem=d_recv.at[me_c],
            device_id={"ctx": p},
            device_id_type=MESH,
        )

    for t in range(n_exp):
        z_r = lax.rem(plane + 2 * n_exp - me_e - t, n_exp)
        for y in range(per_chunk):
            p = z_r * per_chunk + y

            @pl.when(p != me_c)
            def _():
                dispatch_copy(p).start()

            @pl.when(p == me_c)
            def _():
                pltpu.make_async_copy(outgoing.at[p], incoming.at[p], d_recv.at[p]).start()

    parts = ((gate_w, gate_stage, gate_recv), (up_w, up_stage, up_recv))

    def reduce_copy(j, which):
        _, stage, recv = parts[which]
        return pltpu.make_async_remote_copy(
            src_ref=stage.at[j],
            dst_ref=recv.at[me_e],
            send_sem=r_send.at[j, which],
            recv_sem=r_recv.at[me_e, which],
            device_id={"exp": j},
            device_id_type=MESH,
        )

    rows = gate_stage.shape[2]
    for t in range(n_exp):
        j = lax.rem(plane + me_e + t, n_exp)
        for y in range(per_chunk):
            s = j * per_chunk + y
            pltpu.make_async_copy(incoming.at[s], incoming.at[s], d_recv.at[s]).wait()
        first = pl.multiple_of(j * per_chunk, per_chunk)
        for k in range(EXP_ROW):
            x = incoming[pl.ds(first, per_chunk), k].reshape(rows, incoming.shape[-1])
            for w, stage, _ in parts:
                stage[j, k] = jnp.dot(x, w[k], preferred_element_type=jnp.float32).astype(
                    stage.dtype
                )

        @pl.when(j != me_e)
        def _():
            for which in range(2):
                reduce_copy(j, which).start()

        @pl.when(j == me_e)
        def _():
            for which, (_, stage, recv) in enumerate(parts):
                pltpu.make_async_copy(stage.at[j], recv.at[j], r_recv.at[j, which]).start()

    for s in range(n_exp):
        for which, (_, _, recv) in enumerate(parts):
            pltpu.make_async_copy(recv.at[s], recv.at[s], r_recv.at[s, which]).wait()
    gate_sum = gate_recv[0].astype(jnp.float32)
    up_sum = up_recv[0].astype(jnp.float32)
    for s in range(1, n_exp):
        gate_sum = gate_sum + gate_recv[s].astype(jnp.float32)
        up_sum = up_sum + up_recv[s].astype(jnp.float32)
    hidden_mine[...] = (gate_sum / (1.0 + jnp.exp(-gate_sum)) * up_sum).astype(hidden_mine.dtype)

    def gather_copy(r):
        return pltpu.make_async_remote_copy(
            src_ref=hidden_mine,
            dst_ref=hidden_all.at[me_e],
            send_sem=a_send.at[r],
            recv_sem=a_recv.at[me_e],
            device_id={"exp": r},
            device_id_type=MESH,
        )

    for t in range(n_exp):
        r = lax.rem(me_e + 2 * n_exp - plane - t, n_exp)

        @pl.when(r != me_e)
        def _():
            gather_copy(r).start()

        @pl.when(r == me_e)
        def _():
            pltpu.make_async_copy(hidden_mine, hidden_all.at[r], a_recv.at[r]).start()

    def return_copy(s):
        return pltpu.make_async_remote_copy(
            src_ref=ret_stage.at[s],
            dst_ref=returned.at[me_c],
            send_sem=b_send.at[s],
            recv_sem=b_recv.at[me_c],
            device_id={"ctx": s},
            device_id_type=MESH,
        )

    for t in range(n_exp):
        j = lax.rem(me_e + plane + t, n_exp)
        pltpu.make_async_copy(hidden_all.at[j], hidden_all.at[j], a_recv.at[j]).wait()
        first = pl.multiple_of(j * per_chunk, per_chunk)
        for k in range(EXP_ROW):
            res = jnp.dot(hidden_all[j, k], down_w[k], preferred_element_type=jnp.float32)
            ret_stage[pl.ds(first, per_chunk), k] = res.astype(ret_stage.dtype).reshape(
                per_chunk, rows // per_chunk, res.shape[-1]
            )
        for y in range(per_chunk):
            s = j * per_chunk + y

            @pl.when(s != me_c)
            def _():
                return_copy(s).start()

            @pl.when(s == me_c)
            def _():
                pltpu.make_async_copy(ret_stage.at[s], returned.at[s], b_recv.at[s]).start()

    for s in range(n_ctx):
        pltpu.make_async_copy(returned.at[s], returned.at[s], b_recv.at[s]).wait()
    back = returned[...].reshape(w_hi.shape[1], returned.shape[-1])
    routed = jnp.dot(w_hi[...], back, preferred_element_type=jnp.float32) + jnp.dot(
        w_lo[...], back, preferred_element_type=jnp.float32
    )
    out[...] = (mixed_f + routed).astype(out.dtype)

    for r in range(n_exp):

        @pl.when(r != me_e)
        def _():
            gather_copy(r).wait_send()
            square_copy(r).wait_send()
            for which in range(2):
                reduce_copy(r, which).wait_send()

    for p in range(n_ctx):

        @pl.when(p != me_c)
        def _():
            dispatch_copy(p).wait_send()
            return_copy(p).wait_send()

    for h in range(halves):
        for r in range(1, group):
            second_copy(h, r).wait_send()
    for h in range(halves):
        z_r = lax.rem(plane + 2 * planes - q - h * (planes // halves), planes)
        for y in range(per_chunk):
            p = z_r * per_chunk + y

            @pl.when(p != me_c)
            def _():
                first_copy(p).wait_send()


def moe(queries, key_rows, value_rows, residual, block_order, gain, slot_rows, out_shape, gate_weight, up_weight,
        down_weight, w_hi, w_lo, n_ctx, n_exp, collective_id):
    kv_shape = (residual.shape[0], KEY_VALUE_HEADS * HEAD_SIZE)
    mixed = residual
    square_shape = (residual.shape[0], 128)
    hid = gate_weight.shape[-1]
    size = math.prod(out_shape)
    slots = out_shape[0] * out_shape[2] // n_exp
    recv_shape = (n_exp, EXP_ROW, slots, hid)
    flops = 2 * 3 * size * hid + 2 * size * mixed.shape[0] * 3
    nbytes = 4 * size * 2 + 6 * gate_weight.size * 2 + 8 * n_exp * EXP_ROW * slots * hid * 2
    vmem = pltpu.VMEM
    return pl.pallas_call(
        functools.partial(moe_kernel, n_ctx, n_exp),
        out_shape=jax.ShapeDtypeStruct(mixed.shape, jnp.bfloat16),
        in_specs=[pl.BlockSpec(memory_space=pltpu.VMEM)] * 4
        + [pl.BlockSpec(memory_space=pltpu.SMEM)]
        + [pl.BlockSpec(memory_space=pltpu.VMEM)] * 7,
        out_specs=pl.BlockSpec(memory_space=pltpu.VMEM),
        scratch_shapes=[
            vmem(kv_shape, jnp.bfloat16),
            vmem((n_ctx,) + kv_shape, jnp.bfloat16),
            vmem(residual.shape, jnp.bfloat16),
            vmem(square_shape, jnp.float32),
            vmem((n_exp,) + square_shape, jnp.float32),
            vmem(out_shape, jnp.bfloat16),
            vmem(out_shape, jnp.bfloat16),
            vmem(recv_shape, jnp.bfloat16),
            vmem(recv_shape, jnp.bfloat16),
            vmem(recv_shape, jnp.bfloat16),
            vmem(recv_shape, jnp.bfloat16),
            vmem(recv_shape[1:], jnp.bfloat16),
            vmem(recv_shape, jnp.bfloat16),
            vmem(out_shape, jnp.bfloat16),
            vmem(out_shape, jnp.bfloat16),
            pltpu.SemaphoreType.DMA((n_ctx,)),
            pltpu.SemaphoreType.DMA((n_ctx,)),
            pltpu.SemaphoreType.DMA((n_exp, 2)),
            pltpu.SemaphoreType.DMA((n_exp, 2)),
            pltpu.SemaphoreType.DMA((n_exp,)),
            pltpu.SemaphoreType.DMA((n_exp,)),
            pltpu.SemaphoreType.DMA((n_ctx,)),
            pltpu.SemaphoreType.DMA((n_ctx,)),
            pltpu.SemaphoreType.DMA((n_exp, 2)),
            pltpu.SemaphoreType.DMA((n_exp, 2)),
            pltpu.SemaphoreType.DMA((n_exp,)),
            pltpu.SemaphoreType.DMA((n_exp,)),
            pltpu.SemaphoreType.DMA((n_ctx,)),
            pltpu.SemaphoreType.DMA((n_ctx,)),
        ],
        compiler_params=pltpu.CompilerParams(collective_id=collective_id, has_side_effects=True),
        cost_estimate=pl.CostEstimate(flops=flops, bytes_accessed=nbytes, transcendentals=0),
    )(queries, key_rows, value_rows, residual, block_order, gain, slot_rows, gate_weight, up_weight, down_weight,
      w_hi, w_lo)

def kv_gather_kernel(n_ctx, n_exp, group, *refs):
    block, kv_all, s1_send, s1_recv, s2_send, s2_recv = refs
    per_plane = n_ctx // n_exp
    planes = n_ctx // per_plane
    me_c = lax.axis_index("ctx")
    me_e = lax.axis_index("exp")
    q = lax.rem(me_e, group)
    head_base = me_e - q
    plane = me_c // per_plane
    barrier = pltpu.get_barrier_semaphore()
    for k in range(1, n_ctx):
        pl.semaphore_signal(
            barrier, inc=1, device_id={"ctx": lax.rem(me_c + k, n_ctx)}, device_id_type=MESH
        )
    for k in range(1, group):
        pl.semaphore_signal(
            barrier, inc=1, device_id={"exp": head_base + lax.rem(q + k, group)}, device_id_type=MESH
        )
    pl.semaphore_wait(barrier, n_ctx + group - 2)

    def first_copy(p):
        return pltpu.make_async_remote_copy(
            src_ref=block,
            dst_ref=kv_all.at[me_c],
            send_sem=s1_send.at[p],
            recv_sem=s1_recv.at[me_c],
            device_id={"ctx": p},
            device_id_type=MESH,
        )

    halves = 2
    for h in range(halves):
        z_r = lax.rem(plane + 2 * planes - q - h * (planes // halves), planes)
        for y in range(per_plane):
            p = z_r * per_plane + y

            @pl.when(p != me_c)
            def _():
                first_copy(p).start()

            @pl.when(p == me_c)
            def _():
                pltpu.make_async_copy(block, kv_all.at[p], s1_recv.at[p]).start()

    def second_copy(h, r):
        first = pl.multiple_of(lax.rem(plane + q + h * (planes // halves), planes) * per_plane, per_plane)
        return pltpu.make_async_remote_copy(
            src_ref=kv_all.at[pl.ds(first, per_plane)],
            dst_ref=kv_all.at[pl.ds(first, per_plane)],
            send_sem=s2_send.at[r, h],
            recv_sem=s2_recv.at[r, h],
            device_id={"exp": head_base + lax.rem(q + r, group)},
            device_id_type=MESH,
        )

    for h in range(halves):
        z_s = lax.rem(plane + q + h * (planes // halves), planes)
        for y in range(per_plane):
            s = z_s * per_plane + y
            pltpu.make_async_copy(kv_all.at[s], kv_all.at[s], s1_recv.at[s]).wait()
        for r in range(1, group):
            second_copy(h, r).start()
    for h in range(halves):
        for r in range(1, group):
            second_copy(h, r).wait_recv()
    for h in range(halves):
        for r in range(1, group):
            second_copy(h, r).wait_send()
    for h in range(halves):
        z_r = lax.rem(plane + 2 * planes - q - h * (planes // halves), planes)
        for y in range(per_plane):
            p = z_r * per_plane + y

            @pl.when(p != me_c)
            def _():
                first_copy(p).wait_send()


def kv_gather(block, n_ctx, n_exp, group, collective_id):
    nbytes = block.size * block.dtype.itemsize * n_ctx
    return pl.pallas_call(
        functools.partial(kv_gather_kernel, n_ctx, n_exp, group),
        out_shape=jax.ShapeDtypeStruct((n_ctx,) + block.shape, block.dtype),
        in_specs=[pl.BlockSpec(memory_space=pltpu.VMEM)],
        out_specs=pl.BlockSpec(memory_space=pltpu.VMEM),
        scratch_shapes=[
            pltpu.SemaphoreType.DMA((n_ctx,)),
            pltpu.SemaphoreType.DMA((n_ctx,)),
            pltpu.SemaphoreType.DMA((group, 2)),
            pltpu.SemaphoreType.DMA((group, 2)),
        ],
        compiler_params=pltpu.CompilerParams(collective_id=collective_id, has_side_effects=True),
        cost_estimate=pl.CostEstimate(flops=0, bytes_accessed=2 * nbytes, transcendentals=0),
    )(block)


def local(
    queries,
    key_rows,
    value_head_rows,
    block_order,
    residual,
    norm_gain,
    expert_ids,
    route_weight,
    gate_weight,
    up_weight,
    down_weight,
):
    shard_rows = queries.shape[0]
    ctx_count = lax.axis_size("ctx")
    exp_count = lax.axis_size("exp")
    local_head = queries.shape[1] // HEAD_SIZE
    expert_index = lax.axis_index("exp")
    ctx_index = lax.axis_index("ctx")
    expert_count = ctx_count * EXP_ROW
    capacity = 2 * shard_rows * TOPK // expert_count
    flat_ids = expert_ids.reshape(-1)
    onehot = (flat_ids[:, None] == jnp.arange(expert_count, dtype=jnp.int32)[None, :]).astype(
        jnp.int32
    )
    slot_rank = jnp.sum((jnp.cumsum(onehot, axis=0) - onehot) * onehot, axis=1)
    slot_index = flat_ids * capacity + slot_rank
    slot_total = expert_count * capacity
    slot_rows = jnp.any(
        slot_index.reshape(shard_rows, TOPK)[None, :, :]
        == jnp.arange(slot_total, dtype=jnp.int32)[:, None, None],
        axis=2,
    ).astype(jnp.bfloat16)
    slot_weight = jnp.sum(
        jnp.where(
            slot_index.reshape(shard_rows, TOPK)[:, :, None]
            == jnp.arange(slot_total, dtype=jnp.int32)[None, None, :],
            route_weight[:, :, None],
            0.0,
        ),
        axis=1,
    )
    w_hi = slot_weight.astype(jnp.bfloat16)
    w_lo = (slot_weight - w_hi.astype(jnp.float32)).astype(jnp.bfloat16)
    return moe(
        queries,
        key_rows,
        value_head_rows,
        residual,
        block_order,
        norm_gain.reshape(1, -1),
        slot_rows,
        (ctx_count, EXP_ROW, capacity, residual.shape[1]),
        gate_weight,
        up_weight,
        down_weight,
        w_hi,
        w_lo,
        ctx_count,
        exp_count,
        2,
    )

def solution(mesh):
    placed = (
        P(("rep", "ctx"), "exp"),
        P(("rep", "ctx"), None),
        P(("rep", "ctx"), None),
        P("rep"),
        P(("rep", "ctx"), "exp"),
        P("exp"),
        P(("rep", "ctx"), None),
        P(("rep", "ctx"), None),
        P("ctx", "exp", None),
        P("ctx", "exp", None),
        P("ctx", None, "exp"),
    )
    return jax.shard_map(
        local, mesh=mesh, in_specs=placed, out_specs=P(("rep", "ctx"), "exp"), check_vma=False
    )
```

```python
import functools
import math

import jax
import jax.numpy as jnp
from jax import lax
from jax.experimental import pallas as pl
from jax.experimental.pallas import tpu as pltpu
from jax.sharding import PartitionSpec as P

D = 4096
QUERY_HEADS = 32
KEY_VALUE_HEADS = 2
HEAD_SIZE = 128
TOPK = 8
EXP_ROW = 2

MASKED_SCORE = -1e30
NORM_EPS = 1e-06
MESH = pl.DeviceIdType.MESH


def exchange_kernel(axis, n, gather, n_in, *refs):
    ins, outs = refs[:n_in], refs[n_in : 2 * n_in]
    send_sem, recv_sem = refs[2 * n_in], refs[2 * n_in + 1]
    me = lax.axis_index(axis)
    barrier = pltpu.get_barrier_semaphore()
    for k in range(1, n):
        pl.semaphore_signal(
            barrier, inc=1, device_id={axis: lax.rem(me + k, n)}, device_id_type=MESH
        )
    pl.semaphore_wait(barrier, n - 1)
    copies = []
    for k in range(1, n):
        peer = lax.rem(me + k, n)
        for i in range(n_in):
            copy = pltpu.make_async_remote_copy(
                src_ref=ins[i] if gather else ins[i].at[peer],
                dst_ref=outs[i].at[me],
                send_sem=send_sem.at[i, k],
                recv_sem=recv_sem.at[i, k],
                device_id={axis: peer},
                device_id_type=MESH,
            )
            copy.start()
            copies.append(copy)
    for i in range(n_in):
        outs[i][me] = ins[i][...] if gather else ins[i][me]
    for copy in copies:
        copy.wait()


def exchange(xs, axis, n, gather, collective_id):
    n_in = len(xs)
    out_shape = [
        jax.ShapeDtypeStruct((n,) + (x.shape if gather else x.shape[1:]), x.dtype) for x in xs
    ]
    nbytes = sum(x.size * x.dtype.itemsize for x in xs) * (n if gather else 1)
    return pl.pallas_call(
        functools.partial(exchange_kernel, axis, n, gather, n_in),
        out_shape=out_shape,
        in_specs=[pl.BlockSpec(memory_space=pltpu.VMEM)] * n_in,
        out_specs=[pl.BlockSpec(memory_space=pltpu.VMEM)] * n_in,
        scratch_shapes=[
            pltpu.SemaphoreType.DMA((n_in, n)),
            pltpu.SemaphoreType.DMA((n_in, n)),
        ],
        compiler_params=pltpu.CompilerParams(collective_id=collective_id, has_side_effects=True),
        cost_estimate=pl.CostEstimate(flops=0, bytes_accessed=2 * nbytes, transcendentals=0),
    )(*xs)


def moe_kernel(n_ctx, n_exp, *refs):
    (queries, key_rows, value_rows, residual, block_order, gain, expert_ids, route_weight, gate_w, up_w, down_w, out,
     slot_rows, w_hi, w_lo, kv_block, kv_all, mixed, square_block, square_all, outgoing, incoming, gate_stage, up_stage, gate_recv, up_recv,
     hidden_mine, hidden_all, ret_stage, returned, s1_send, s1_recv, s2_send, s2_recv, q_send, q_recv, d_send,
     d_recv, r_send, r_recv, a_send, a_recv, b_send, b_recv) = refs
    per_chunk = n_ctx // n_exp
    me_c = lax.axis_index("ctx")
    me_e = lax.axis_index("exp")
    plane = me_c // per_chunk
    barrier = pltpu.get_barrier_semaphore()
    for k in range(1, n_ctx):
        pl.semaphore_signal(
            barrier, inc=1, device_id={"ctx": lax.rem(me_c + k, n_ctx)}, device_id_type=MESH
        )
    for k in range(1, n_exp):
        pl.semaphore_signal(
            barrier, inc=1, device_id={"exp": lax.rem(me_e + k, n_exp)}, device_id_type=MESH
        )
    pl.semaphore_wait(barrier, n_ctx + n_exp - 2)

    group = QUERY_HEADS // KEY_VALUE_HEADS // (queries.shape[1] // HEAD_SIZE)
    head_cols = pl.ds(pl.multiple_of((me_e // group) * HEAD_SIZE, HEAD_SIZE), HEAD_SIZE)
    kv_block[:, :HEAD_SIZE] = key_rows[:, head_cols]
    kv_block[:, HEAD_SIZE:] = value_rows[:, head_cols]
    q = lax.rem(me_e, group)
    head_base = me_e - q
    planes = n_exp
    halves = 2

    def first_copy(p):
        return pltpu.make_async_remote_copy(
            src_ref=kv_block,
            dst_ref=kv_all.at[me_c],
            send_sem=s1_send.at[p],
            recv_sem=s1_recv.at[me_c],
            device_id={"ctx": p},
            device_id_type=MESH,
        )

    for h in range(halves):
        z_r = lax.rem(plane + 2 * planes - q - h * (planes // halves), planes)
        for y in range(per_chunk):
            p = z_r * per_chunk + y

            @pl.when(p != me_c)
            def _():
                first_copy(p).start()

            @pl.when(p == me_c)
            def _():
                pltpu.make_async_copy(kv_block, kv_all.at[p], s1_recv.at[p]).start()

    def second_copy(h, r):
        first = pl.multiple_of(lax.rem(plane + q + h * (planes // halves), planes) * per_chunk, per_chunk)
        return pltpu.make_async_remote_copy(
            src_ref=kv_all.at[pl.ds(first, per_chunk)],
            dst_ref=kv_all.at[pl.ds(first, per_chunk)],
            send_sem=s2_send.at[r, h],
            recv_sem=s2_recv.at[r, h],
            device_id={"exp": head_base + lax.rem(q + r, group)},
            device_id_type=MESH,
        )

    rows_here, topk = expert_ids.shape
    slot_total = slot_rows.shape[1]
    capacity = slot_total // (n_ctx * EXP_ROW)
    ids = expert_ids[...]
    expert_lane = lax.broadcasted_iota(jnp.int32, (rows_here, n_ctx * EXP_ROW), 1)
    picks = [(ids[:, i : i + 1] == expert_lane).astype(jnp.float32) for i in range(topk)]
    per_row = picks[0]
    for i in range(1, topk):
        per_row = per_row + picks[i]
    earlier = (
        lax.broadcasted_iota(jnp.int32, (rows_here, rows_here), 1)
        < lax.broadcasted_iota(jnp.int32, (rows_here, rows_here), 0)
    ).astype(jnp.bfloat16)
    before = jnp.dot(earlier, per_row.astype(jnp.bfloat16), preferred_element_type=jnp.float32)
    slot_lane = lax.broadcasted_iota(jnp.int32, (rows_here, slot_total), 1)
    chosen = jnp.zeros((rows_here, slot_total), jnp.float32)
    weight = jnp.zeros((rows_here, slot_total), jnp.float32)
    weights_in = route_weight[...]
    for i in range(topk):
        rank = jnp.sum(picks[i] * before, axis=1, keepdims=True)
        before = before + picks[i]
        slot = ids[:, i : i + 1] * capacity + rank.astype(jnp.int32)
        hit = slot == slot_lane
        chosen = jnp.where(hit, 1.0, chosen)
        weight = jnp.where(hit, weights_in[:, i : i + 1], weight)
    slot_rows[...] = chosen.astype(slot_rows.dtype)
    high = weight.astype(jnp.bfloat16)
    w_hi[...] = high
    w_lo[...] = (weight - high.astype(jnp.float32)).astype(jnp.bfloat16)

    for h in range(halves):
        z_s = lax.rem(plane + q + h * (planes // halves), planes)
        for y in range(per_chunk):
            s = z_s * per_chunk + y
            pltpu.make_async_copy(kv_all.at[s], kv_all.at[s], s1_recv.at[s]).wait()
        for r in range(1, group):
            second_copy(h, r).start()
    for h in range(halves):
        for r in range(1, group):
            second_copy(h, r).wait_recv()

    total_rows = kv_all.shape[0] * kv_all.shape[1]
    keys = kv_all[:, :, :HEAD_SIZE].reshape(total_rows, HEAD_SIZE)
    values = kv_all[:, :, HEAD_SIZE:].reshape(total_rows, HEAD_SIZE)
    block_rows = kv_all.shape[1]
    query_pos = block_order[me_c] * block_rows + lax.broadcasted_iota(jnp.int32, (queries.shape[0], 1), 0)
    key_lane = lax.broadcasted_iota(jnp.int32, (1, total_rows), 1)
    key_pos = key_lane % block_rows
    for b in range(kv_all.shape[0]):
        key_pos = jnp.where(key_lane // block_rows == b, key_pos + block_order[b] * block_rows, key_pos)
    visible = key_pos <= query_pos
    inv_scale = 1.0 / math.sqrt(HEAD_SIZE)
    square_part = jnp.zeros((queries.shape[0], 1), jnp.float32)
    for h in range(queries.shape[1] // HEAD_SIZE):
        cols = slice(h * HEAD_SIZE, (h + 1) * HEAD_SIZE)
        scores = (
            lax.dot_general(
                queries[:, cols], keys, (((1,), (1,)), ((), ())), preferred_element_type=jnp.float32
            )
            * inv_scale
        )
        scores = jnp.where(visible, scores, MASKED_SCORE)
        newest = jnp.max(scores, axis=1, keepdims=True)
        weights = jnp.where(visible, jnp.exp(scores - newest), 0.0)
        weight_sum = jnp.sum(weights, axis=1, keepdims=True)
        weighted = jnp.dot(weights.astype(jnp.bfloat16), values, preferred_element_type=jnp.float32)
        attention = (weighted / weight_sum).astype(jnp.bfloat16)
        mixed_h = (residual[:, cols].astype(jnp.float32) + attention.astype(jnp.float32)).astype(
            jnp.bfloat16
        )
        mixed[:, cols] = mixed_h
        mixed_hf = mixed_h.astype(jnp.float32)
        square_part = square_part + jnp.sum(mixed_hf * mixed_hf, axis=1, keepdims=True)
    square_block[...] = jnp.broadcast_to(square_part, square_block.shape)

    def square_copy(r):
        return pltpu.make_async_remote_copy(
            src_ref=square_block,
            dst_ref=square_all.at[me_e],
            send_sem=q_send.at[r],
            recv_sem=q_recv.at[me_e],
            device_id={"exp": r},
            device_id_type=MESH,
        )

    for k in range(1, n_exp):
        square_copy(lax.rem(me_e + k, n_exp)).start()
    pltpu.make_async_copy(square_block, square_all.at[me_e], q_recv.at[me_e]).start()
    for s in range(n_exp):
        pltpu.make_async_copy(square_all.at[s], square_all.at[s], q_recv.at[s]).wait()
    square_sum = square_all[0]
    for s in range(1, n_exp):
        square_sum = square_sum + square_all[s]
    scale = lax.rsqrt(square_sum[:, :1] / D + NORM_EPS)
    mixed_f = mixed[...].astype(jnp.float32)
    normed = (mixed_f * scale * gain[...]).astype(jnp.bfloat16)
    filled = lax.dot_general(
        slot_rows[...], normed, (((0,), (0,)), ((), ())), preferred_element_type=jnp.float32
    )
    outgoing[...] = filled.astype(outgoing.dtype).reshape(outgoing.shape)

    def dispatch_copy(p):
        return pltpu.make_async_remote_copy(
            src_ref=outgoing.at[p],
            dst_ref=incoming.at[me_c],
            send_sem=d_send.at[p],
            recv_sem=d_recv.at[me_c],
            device_id={"ctx": p},
            device_id_type=MESH,
        )

    for t in range(n_exp):
        z_r = lax.rem(plane + 2 * n_exp - me_e - t, n_exp)
        for y in range(per_chunk):
            p = z_r * per_chunk + y

            @pl.when(p != me_c)
            def _():
                dispatch_copy(p).start()

            @pl.when(p == me_c)
            def _():
                pltpu.make_async_copy(outgoing.at[p], incoming.at[p], d_recv.at[p]).start()

    parts = ((gate_w, gate_stage, gate_recv), (up_w, up_stage, up_recv))

    def reduce_copy(j, which):
        _, stage, recv = parts[which]
        return pltpu.make_async_remote_copy(
            src_ref=stage.at[j],
            dst_ref=recv.at[me_e],
            send_sem=r_send.at[j, which],
            recv_sem=r_recv.at[me_e, which],
            device_id={"exp": j},
            device_id_type=MESH,
        )

    rows = gate_stage.shape[2]
    for t in range(n_exp):
        j = lax.rem(plane + me_e + t, n_exp)
        for y in range(per_chunk):
            s = j * per_chunk + y
            pltpu.make_async_copy(incoming.at[s], incoming.at[s], d_recv.at[s]).wait()
        first = pl.multiple_of(j * per_chunk, per_chunk)
        for k in range(EXP_ROW):
            x = incoming[pl.ds(first, per_chunk), k].reshape(rows, incoming.shape[-1])
            for w, stage, _ in parts:
                stage[j, k] = jnp.dot(x, w[k], preferred_element_type=jnp.float32).astype(
                    stage.dtype
                )

        @pl.when(j != me_e)
        def _():
            for which in range(2):
                reduce_copy(j, which).start()

        @pl.when(j == me_e)
        def _():
            for which, (_, stage, recv) in enumerate(parts):
                pltpu.make_async_copy(stage.at[j], recv.at[j], r_recv.at[j, which]).start()

    for s in range(n_exp):
        for which, (_, _, recv) in enumerate(parts):
            pltpu.make_async_copy(recv.at[s], recv.at[s], r_recv.at[s, which]).wait()
    gate_sum = gate_recv[0].astype(jnp.float32)
    up_sum = up_recv[0].astype(jnp.float32)
    for s in range(1, n_exp):
        gate_sum = gate_sum + gate_recv[s].astype(jnp.float32)
        up_sum = up_sum + up_recv[s].astype(jnp.float32)
    hidden_mine[...] = (gate_sum / (1.0 + jnp.exp(-gate_sum)) * up_sum).astype(hidden_mine.dtype)

    def gather_copy(r):
        return pltpu.make_async_remote_copy(
            src_ref=hidden_mine,
            dst_ref=hidden_all.at[me_e],
            send_sem=a_send.at[r],
            recv_sem=a_recv.at[me_e],
            device_id={"exp": r},
            device_id_type=MESH,
        )

    for t in range(n_exp):
        r = lax.rem(me_e + 2 * n_exp - plane - t, n_exp)

        @pl.when(r != me_e)
        def _():
            gather_copy(r).start()

        @pl.when(r == me_e)
        def _():
            pltpu.make_async_copy(hidden_mine, hidden_all.at[r], a_recv.at[r]).start()

    def return_copy(s):
        return pltpu.make_async_remote_copy(
            src_ref=ret_stage.at[s],
            dst_ref=returned.at[me_c],
            send_sem=b_send.at[s],
            recv_sem=b_recv.at[me_c],
            device_id={"ctx": s},
            device_id_type=MESH,
        )

    for t in range(n_exp):
        j = lax.rem(me_e + plane + t, n_exp)
        pltpu.make_async_copy(hidden_all.at[j], hidden_all.at[j], a_recv.at[j]).wait()
        first = pl.multiple_of(j * per_chunk, per_chunk)
        for k in range(EXP_ROW):
            res = jnp.dot(hidden_all[j, k], down_w[k], preferred_element_type=jnp.float32)
            ret_stage[pl.ds(first, per_chunk), k] = res.astype(ret_stage.dtype).reshape(
                per_chunk, rows // per_chunk, res.shape[-1]
            )
        for y in range(per_chunk):
            s = j * per_chunk + y

            @pl.when(s != me_c)
            def _():
                return_copy(s).start()

            @pl.when(s == me_c)
            def _():
                pltpu.make_async_copy(ret_stage.at[s], returned.at[s], b_recv.at[s]).start()

    for s in range(n_ctx):
        pltpu.make_async_copy(returned.at[s], returned.at[s], b_recv.at[s]).wait()
    back = returned[...].reshape(w_hi.shape[1], returned.shape[-1])
    routed = jnp.dot(w_hi[...], back, preferred_element_type=jnp.float32) + jnp.dot(
        w_lo[...], back, preferred_element_type=jnp.float32
    )
    out[...] = (mixed_f + routed).astype(out.dtype)

    for r in range(n_exp):

        @pl.when(r != me_e)
        def _():
            gather_copy(r).wait_send()
            square_copy(r).wait_send()
            for which in range(2):
                reduce_copy(r, which).wait_send()

    for p in range(n_ctx):

        @pl.when(p != me_c)
        def _():
            dispatch_copy(p).wait_send()
            return_copy(p).wait_send()

    for h in range(halves):
        for r in range(1, group):
            second_copy(h, r).wait_send()
    for h in range(halves):
        z_r = lax.rem(plane + 2 * planes - q - h * (planes // halves), planes)
        for y in range(per_chunk):
            p = z_r * per_chunk + y

            @pl.when(p != me_c)
            def _():
                first_copy(p).wait_send()


def moe(queries, key_rows, value_rows, residual, block_order, gain, expert_ids, route_weight, out_shape, gate_weight,
        up_weight, down_weight, n_ctx, n_exp, collective_id):
    slot_total = out_shape[0] * out_shape[1] * out_shape[2]
    kv_shape = (residual.shape[0], KEY_VALUE_HEADS * HEAD_SIZE)
    mixed = residual
    square_shape = (residual.shape[0], 128)
    hid = gate_weight.shape[-1]
    size = math.prod(out_shape)
    slots = out_shape[0] * out_shape[2] // n_exp
    recv_shape = (n_exp, EXP_ROW, slots, hid)
    flops = 2 * 3 * size * hid + 2 * size * mixed.shape[0] * 3
    nbytes = 4 * size * 2 + 6 * gate_weight.size * 2 + 8 * n_exp * EXP_ROW * slots * hid * 2
    vmem = pltpu.VMEM
    return pl.pallas_call(
        functools.partial(moe_kernel, n_ctx, n_exp),
        out_shape=jax.ShapeDtypeStruct(mixed.shape, jnp.bfloat16),
        in_specs=[pl.BlockSpec(memory_space=pltpu.VMEM)] * 4
        + [pl.BlockSpec(memory_space=pltpu.SMEM)]
        + [pl.BlockSpec(memory_space=pltpu.VMEM)] * 6,
        out_specs=pl.BlockSpec(memory_space=pltpu.VMEM),
        scratch_shapes=[
            vmem((residual.shape[0], slot_total), jnp.bfloat16),
            vmem((residual.shape[0], slot_total), jnp.bfloat16),
            vmem((residual.shape[0], slot_total), jnp.bfloat16),
            vmem(kv_shape, jnp.bfloat16),
            vmem((n_ctx,) + kv_shape, jnp.bfloat16),
            vmem(residual.shape, jnp.bfloat16),
            vmem(square_shape, jnp.float32),
            vmem((n_exp,) + square_shape, jnp.float32),
            vmem(out_shape, jnp.bfloat16),
            vmem(out_shape, jnp.bfloat16),
            vmem(recv_shape, jnp.bfloat16),
            vmem(recv_shape, jnp.bfloat16),
            vmem(recv_shape, jnp.bfloat16),
            vmem(recv_shape, jnp.bfloat16),
            vmem(recv_shape[1:], jnp.bfloat16),
            vmem(recv_shape, jnp.bfloat16),
            vmem(out_shape, jnp.bfloat16),
            vmem(out_shape, jnp.bfloat16),
            pltpu.SemaphoreType.DMA((n_ctx,)),
            pltpu.SemaphoreType.DMA((n_ctx,)),
            pltpu.SemaphoreType.DMA((n_exp, 2)),
            pltpu.SemaphoreType.DMA((n_exp, 2)),
            pltpu.SemaphoreType.DMA((n_exp,)),
            pltpu.SemaphoreType.DMA((n_exp,)),
            pltpu.SemaphoreType.DMA((n_ctx,)),
            pltpu.SemaphoreType.DMA((n_ctx,)),
            pltpu.SemaphoreType.DMA((n_exp, 2)),
            pltpu.SemaphoreType.DMA((n_exp, 2)),
            pltpu.SemaphoreType.DMA((n_exp,)),
            pltpu.SemaphoreType.DMA((n_exp,)),
            pltpu.SemaphoreType.DMA((n_ctx,)),
            pltpu.SemaphoreType.DMA((n_ctx,)),
        ],
        compiler_params=pltpu.CompilerParams(collective_id=collective_id, has_side_effects=True),
        cost_estimate=pl.CostEstimate(flops=flops, bytes_accessed=nbytes, transcendentals=0),
    )(queries, key_rows, value_rows, residual, block_order, gain, expert_ids, route_weight, gate_weight, up_weight,
      down_weight)

def kv_gather_kernel(n_ctx, n_exp, group, *refs):
    block, kv_all, s1_send, s1_recv, s2_send, s2_recv = refs
    per_plane = n_ctx // n_exp
    planes = n_ctx // per_plane
    me_c = lax.axis_index("ctx")
    me_e = lax.axis_index("exp")
    q = lax.rem(me_e, group)
    head_base = me_e - q
    plane = me_c // per_plane
    barrier = pltpu.get_barrier_semaphore()
    for k in range(1, n_ctx):
        pl.semaphore_signal(
            barrier, inc=1, device_id={"ctx": lax.rem(me_c + k, n_ctx)}, device_id_type=MESH
        )
    for k in range(1, group):
        pl.semaphore_signal(
            barrier, inc=1, device_id={"exp": head_base + lax.rem(q + k, group)}, device_id_type=MESH
        )
    pl.semaphore_wait(barrier, n_ctx + group - 2)

    def first_copy(p):
        return pltpu.make_async_remote_copy(
            src_ref=block,
            dst_ref=kv_all.at[me_c],
            send_sem=s1_send.at[p],
            recv_sem=s1_recv.at[me_c],
            device_id={"ctx": p},
            device_id_type=MESH,
        )

    halves = 2
    for h in range(halves):
        z_r = lax.rem(plane + 2 * planes - q - h * (planes // halves), planes)
        for y in range(per_plane):
            p = z_r * per_plane + y

            @pl.when(p != me_c)
            def _():
                first_copy(p).start()

            @pl.when(p == me_c)
            def _():
                pltpu.make_async_copy(block, kv_all.at[p], s1_recv.at[p]).start()

    def second_copy(h, r):
        first = pl.multiple_of(lax.rem(plane + q + h * (planes // halves), planes) * per_plane, per_plane)
        return pltpu.make_async_remote_copy(
            src_ref=kv_all.at[pl.ds(first, per_plane)],
            dst_ref=kv_all.at[pl.ds(first, per_plane)],
            send_sem=s2_send.at[r, h],
            recv_sem=s2_recv.at[r, h],
            device_id={"exp": head_base + lax.rem(q + r, group)},
            device_id_type=MESH,
        )

    for h in range(halves):
        z_s = lax.rem(plane + q + h * (planes // halves), planes)
        for y in range(per_plane):
            s = z_s * per_plane + y
            pltpu.make_async_copy(kv_all.at[s], kv_all.at[s], s1_recv.at[s]).wait()
        for r in range(1, group):
            second_copy(h, r).start()
    for h in range(halves):
        for r in range(1, group):
            second_copy(h, r).wait_recv()
    for h in range(halves):
        for r in range(1, group):
            second_copy(h, r).wait_send()
    for h in range(halves):
        z_r = lax.rem(plane + 2 * planes - q - h * (planes // halves), planes)
        for y in range(per_plane):
            p = z_r * per_plane + y

            @pl.when(p != me_c)
            def _():
                first_copy(p).wait_send()


def kv_gather(block, n_ctx, n_exp, group, collective_id):
    nbytes = block.size * block.dtype.itemsize * n_ctx
    return pl.pallas_call(
        functools.partial(kv_gather_kernel, n_ctx, n_exp, group),
        out_shape=jax.ShapeDtypeStruct((n_ctx,) + block.shape, block.dtype),
        in_specs=[pl.BlockSpec(memory_space=pltpu.VMEM)],
        out_specs=pl.BlockSpec(memory_space=pltpu.VMEM),
        scratch_shapes=[
            pltpu.SemaphoreType.DMA((n_ctx,)),
            pltpu.SemaphoreType.DMA((n_ctx,)),
            pltpu.SemaphoreType.DMA((group, 2)),
            pltpu.SemaphoreType.DMA((group, 2)),
        ],
        compiler_params=pltpu.CompilerParams(collective_id=collective_id, has_side_effects=True),
        cost_estimate=pl.CostEstimate(flops=0, bytes_accessed=2 * nbytes, transcendentals=0),
    )(block)


def local(
    queries,
    key_rows,
    value_head_rows,
    block_order,
    residual,
    norm_gain,
    expert_ids,
    route_weight,
    gate_weight,
    up_weight,
    down_weight,
):
    shard_rows = queries.shape[0]
    ctx_count = lax.axis_size("ctx")
    exp_count = lax.axis_size("exp")
    local_head = queries.shape[1] // HEAD_SIZE
    expert_index = lax.axis_index("exp")
    ctx_index = lax.axis_index("ctx")
    expert_count = ctx_count * EXP_ROW
    capacity = 2 * shard_rows * TOPK // expert_count
    return moe(
        queries,
        key_rows,
        value_head_rows,
        residual,
        block_order,
        norm_gain.reshape(1, -1),
        expert_ids,
        route_weight,
        (ctx_count, EXP_ROW, capacity, residual.shape[1]),
        gate_weight,
        up_weight,
        down_weight,
        ctx_count,
        exp_count,
        2,
    )

def solution(mesh):
    placed = (
        P(("rep", "ctx"), "exp"),
        P(("rep", "ctx"), None),
        P(("rep", "ctx"), None),
        P("rep"),
        P(("rep", "ctx"), "exp"),
        P("exp"),
        P(("rep", "ctx"), None),
        P(("rep", "ctx"), None),
        P("ctx", "exp", None),
        P("ctx", "exp", None),
        P("ctx", None, "exp"),
    )
    return jax.shard_map(
        local, mesh=mesh, in_specs=placed, out_specs=P(("rep", "ctx"), "exp"), check_vma=False
    )
```

```python
import functools
import math

import jax
import jax.numpy as jnp
from jax import lax
from jax.experimental import pallas as pl
from jax.experimental.pallas import tpu as pltpu
from jax.sharding import PartitionSpec as P

D = 4096
QUERY_HEADS = 32
KEY_VALUE_HEADS = 2
HEAD_SIZE = 128
TOPK = 8
EXP_ROW = 2

MASKED_SCORE = -1e30
NORM_EPS = 1e-06
MESH = pl.DeviceIdType.MESH


def exchange_kernel(axis, n, gather, n_in, *refs):
    ins, outs = refs[:n_in], refs[n_in : 2 * n_in]
    send_sem, recv_sem = refs[2 * n_in], refs[2 * n_in + 1]
    me = lax.axis_index(axis)
    barrier = pltpu.get_barrier_semaphore()
    for k in range(1, n):
        pl.semaphore_signal(
            barrier, inc=1, device_id={axis: lax.rem(me + k, n)}, device_id_type=MESH
        )
    pl.semaphore_wait(barrier, n - 1)
    copies = []
    for k in range(1, n):
        peer = lax.rem(me + k, n)
        for i in range(n_in):
            copy = pltpu.make_async_remote_copy(
                src_ref=ins[i] if gather else ins[i].at[peer],
                dst_ref=outs[i].at[me],
                send_sem=send_sem.at[i, k],
                recv_sem=recv_sem.at[i, k],
                device_id={axis: peer},
                device_id_type=MESH,
            )
            copy.start()
            copies.append(copy)
    for i in range(n_in):
        outs[i][me] = ins[i][...] if gather else ins[i][me]
    for copy in copies:
        copy.wait()


def exchange(xs, axis, n, gather, collective_id):
    n_in = len(xs)
    out_shape = [
        jax.ShapeDtypeStruct((n,) + (x.shape if gather else x.shape[1:]), x.dtype) for x in xs
    ]
    nbytes = sum(x.size * x.dtype.itemsize for x in xs) * (n if gather else 1)
    return pl.pallas_call(
        functools.partial(exchange_kernel, axis, n, gather, n_in),
        out_shape=out_shape,
        in_specs=[pl.BlockSpec(memory_space=pltpu.VMEM)] * n_in,
        out_specs=[pl.BlockSpec(memory_space=pltpu.VMEM)] * n_in,
        scratch_shapes=[
            pltpu.SemaphoreType.DMA((n_in, n)),
            pltpu.SemaphoreType.DMA((n_in, n)),
        ],
        compiler_params=pltpu.CompilerParams(collective_id=collective_id, has_side_effects=True),
        cost_estimate=pl.CostEstimate(flops=0, bytes_accessed=2 * nbytes, transcendentals=0),
    )(*xs)


def moe_kernel(n_ctx, n_exp, *refs):
    (queries, key_rows, value_rows, residual, block_order, gain, expert_ids, route_weight, gate_w, up_w, down_w, out,
     slot_rows, w_hi, w_lo, kv_block, kv_all, mixed, square_block, square_all, outgoing, incoming, gate_stage, up_stage, gate_recv, up_recv,
     hidden_mine, hidden_all, ret_stage, returned, s1_send, s1_recv, s2_send, s2_recv, q_send, q_recv, d_send,
     d_recv, r_send, r_recv, a_send, a_recv, b_send, b_recv) = refs
    per_chunk = n_ctx // n_exp
    me_c = lax.axis_index("ctx")
    me_e = lax.axis_index("exp")
    plane = me_c // per_chunk
    barrier = pltpu.get_barrier_semaphore()
    for k in range(1, n_ctx):
        pl.semaphore_signal(
            barrier, inc=1, device_id={"ctx": lax.rem(me_c + k, n_ctx)}, device_id_type=MESH
        )
    for k in range(1, n_exp):
        pl.semaphore_signal(
            barrier, inc=1, device_id={"exp": lax.rem(me_e + k, n_exp)}, device_id_type=MESH
        )
    pl.semaphore_wait(barrier, n_ctx + n_exp - 2)

    group = QUERY_HEADS // KEY_VALUE_HEADS // (queries.shape[1] // HEAD_SIZE)
    head_cols = pl.ds(pl.multiple_of((me_e // group) * HEAD_SIZE, HEAD_SIZE), HEAD_SIZE)
    kv_block[:, :HEAD_SIZE] = key_rows[:, head_cols]
    kv_block[:, HEAD_SIZE:] = value_rows[:, head_cols]
    q = lax.rem(me_e, group)
    head_base = me_e - q
    planes = n_exp
    halves = 2

    def first_copy(p):
        return pltpu.make_async_remote_copy(
            src_ref=kv_block,
            dst_ref=kv_all.at[me_c],
            send_sem=s1_send.at[p],
            recv_sem=s1_recv.at[me_c],
            device_id={"ctx": p},
            device_id_type=MESH,
        )

    for h in range(halves):
        z_r = lax.rem(plane + 2 * planes - q - h * (planes // halves), planes)
        for y in range(per_chunk):
            p = z_r * per_chunk + y

            @pl.when(p != me_c)
            def _():
                first_copy(p).start()

            @pl.when(p == me_c)
            def _():
                pltpu.make_async_copy(kv_block, kv_all.at[p], s1_recv.at[p]).start()

    def second_copy(h, r):
        first = pl.multiple_of(lax.rem(plane + q + h * (planes // halves), planes) * per_chunk, per_chunk)
        return pltpu.make_async_remote_copy(
            src_ref=kv_all.at[pl.ds(first, per_chunk)],
            dst_ref=kv_all.at[pl.ds(first, per_chunk)],
            send_sem=s2_send.at[r, h],
            recv_sem=s2_recv.at[r, h],
            device_id={"exp": head_base + lax.rem(q + r, group)},
            device_id_type=MESH,
        )

    topk, rows_here = expert_ids.shape
    slot_total = slot_rows.shape[0]
    capacity = slot_total // (n_ctx * EXP_ROW)
    ids = expert_ids[...]
    expert_sub = lax.broadcasted_iota(jnp.int32, (n_ctx * EXP_ROW, rows_here), 0)
    picks = [(ids[i : i + 1, :] == expert_sub).astype(jnp.float32) for i in range(topk)]
    per_row = picks[0]
    for i in range(1, topk):
        per_row = per_row + picks[i]
    later = (
        lax.broadcasted_iota(jnp.int32, (rows_here, rows_here), 0)
        < lax.broadcasted_iota(jnp.int32, (rows_here, rows_here), 1)
    ).astype(jnp.bfloat16)
    before = jnp.dot(per_row.astype(jnp.bfloat16), later, preferred_element_type=jnp.float32)
    slot_sub = lax.broadcasted_iota(jnp.int32, (slot_total, rows_here), 0)
    chosen = jnp.zeros((slot_total, rows_here), jnp.float32)
    weight = jnp.zeros((slot_total, rows_here), jnp.float32)
    weights_in = route_weight[...]
    for i in range(topk):
        rank = jnp.sum(picks[i] * before, axis=0, keepdims=True)
        before = before + picks[i]
        slot = ids[i : i + 1, :] * capacity + rank.astype(jnp.int32)
        hit = slot == slot_sub
        chosen = jnp.where(hit, 1.0, chosen)
        weight = jnp.where(hit, weights_in[i : i + 1, :], weight)
    slot_rows[...] = chosen.astype(slot_rows.dtype)
    high = weight.astype(jnp.bfloat16)
    w_hi[...] = high
    w_lo[...] = (weight - high.astype(jnp.float32)).astype(jnp.bfloat16)

    for h in range(halves):
        z_s = lax.rem(plane + q + h * (planes // halves), planes)
        for y in range(per_chunk):
            s = z_s * per_chunk + y
            pltpu.make_async_copy(kv_all.at[s], kv_all.at[s], s1_recv.at[s]).wait()
        for r in range(1, group):
            second_copy(h, r).start()
    for h in range(halves):
        for r in range(1, group):
            second_copy(h, r).wait_recv()

    total_rows = kv_all.shape[0] * kv_all.shape[1]
    keys = kv_all[:, :, :HEAD_SIZE].reshape(total_rows, HEAD_SIZE)
    values = kv_all[:, :, HEAD_SIZE:].reshape(total_rows, HEAD_SIZE)
    block_rows = kv_all.shape[1]
    query_pos = block_order[me_c] * block_rows + lax.broadcasted_iota(jnp.int32, (queries.shape[0], 1), 0)
    key_lane = lax.broadcasted_iota(jnp.int32, (1, total_rows), 1)
    key_pos = key_lane % block_rows
    for b in range(kv_all.shape[0]):
        key_pos = jnp.where(key_lane // block_rows == b, key_pos + block_order[b] * block_rows, key_pos)
    visible = key_pos <= query_pos
    inv_scale = 1.0 / math.sqrt(HEAD_SIZE)
    square_part = jnp.zeros((queries.shape[0], 1), jnp.float32)
    for h in range(queries.shape[1] // HEAD_SIZE):
        cols = slice(h * HEAD_SIZE, (h + 1) * HEAD_SIZE)
        scores = (
            lax.dot_general(
                queries[:, cols], keys, (((1,), (1,)), ((), ())), preferred_element_type=jnp.float32
            )
            * inv_scale
        )
        scores = jnp.where(visible, scores, MASKED_SCORE)
        newest = jnp.max(scores, axis=1, keepdims=True)
        weights = jnp.where(visible, jnp.exp(scores - newest), 0.0)
        weight_sum = jnp.sum(weights, axis=1, keepdims=True)
        weighted = jnp.dot(weights.astype(jnp.bfloat16), values, preferred_element_type=jnp.float32)
        attention = (weighted / weight_sum).astype(jnp.bfloat16)
        mixed_h = (residual[:, cols].astype(jnp.float32) + attention.astype(jnp.float32)).astype(
            jnp.bfloat16
        )
        mixed[:, cols] = mixed_h
        mixed_hf = mixed_h.astype(jnp.float32)
        square_part = square_part + jnp.sum(mixed_hf * mixed_hf, axis=1, keepdims=True)
    square_block[...] = jnp.broadcast_to(square_part, square_block.shape)

    def square_copy(r):
        return pltpu.make_async_remote_copy(
            src_ref=square_block,
            dst_ref=square_all.at[me_e],
            send_sem=q_send.at[r],
            recv_sem=q_recv.at[me_e],
            device_id={"exp": r},
            device_id_type=MESH,
        )

    for k in range(1, n_exp):
        square_copy(lax.rem(me_e + k, n_exp)).start()
    pltpu.make_async_copy(square_block, square_all.at[me_e], q_recv.at[me_e]).start()
    for s in range(n_exp):
        pltpu.make_async_copy(square_all.at[s], square_all.at[s], q_recv.at[s]).wait()
    square_sum = square_all[0]
    for s in range(1, n_exp):
        square_sum = square_sum + square_all[s]
    scale = lax.rsqrt(square_sum[:, :1] / D + NORM_EPS)
    mixed_f = mixed[...].astype(jnp.float32)
    normed = (mixed_f * scale * gain[...]).astype(jnp.bfloat16)
    filled = jnp.dot(slot_rows[...], normed, preferred_element_type=jnp.float32)
    outgoing[...] = filled.astype(outgoing.dtype).reshape(outgoing.shape)

    def dispatch_copy(p):
        return pltpu.make_async_remote_copy(
            src_ref=outgoing.at[p],
            dst_ref=incoming.at[me_c],
            send_sem=d_send.at[p],
            recv_sem=d_recv.at[me_c],
            device_id={"ctx": p},
            device_id_type=MESH,
        )

    for t in range(n_exp):
        z_r = lax.rem(plane + 2 * n_exp - me_e - t, n_exp)
        for y in range(per_chunk):
            p = z_r * per_chunk + y

            @pl.when(p != me_c)
            def _():
                dispatch_copy(p).start()

            @pl.when(p == me_c)
            def _():
                pltpu.make_async_copy(outgoing.at[p], incoming.at[p], d_recv.at[p]).start()

    parts = ((gate_w, gate_stage, gate_recv), (up_w, up_stage, up_recv))

    def reduce_copy(j, which):
        _, stage, recv = parts[which]
        return pltpu.make_async_remote_copy(
            src_ref=stage.at[j],
            dst_ref=recv.at[me_e],
            send_sem=r_send.at[j, which],
            recv_sem=r_recv.at[me_e, which],
            device_id={"exp": j},
            device_id_type=MESH,
        )

    rows = gate_stage.shape[2]
    for t in range(n_exp):
        j = lax.rem(plane + me_e + t, n_exp)
        for y in range(per_chunk):
            s = j * per_chunk + y
            pltpu.make_async_copy(incoming.at[s], incoming.at[s], d_recv.at[s]).wait()
        first = pl.multiple_of(j * per_chunk, per_chunk)
        for k in range(EXP_ROW):
            x = incoming[pl.ds(first, per_chunk), k].reshape(rows, incoming.shape[-1])
            for w, stage, _ in parts:
                stage[j, k] = jnp.dot(x, w[k], preferred_element_type=jnp.float32).astype(
                    stage.dtype
                )

        @pl.when(j != me_e)
        def _():
            for which in range(2):
                reduce_copy(j, which).start()

        @pl.when(j == me_e)
        def _():
            for which, (_, stage, recv) in enumerate(parts):
                pltpu.make_async_copy(stage.at[j], recv.at[j], r_recv.at[j, which]).start()

    for s in range(n_exp):
        for which, (_, _, recv) in enumerate(parts):
            pltpu.make_async_copy(recv.at[s], recv.at[s], r_recv.at[s, which]).wait()
    gate_sum = gate_recv[0].astype(jnp.float32)
    up_sum = up_recv[0].astype(jnp.float32)
    for s in range(1, n_exp):
        gate_sum = gate_sum + gate_recv[s].astype(jnp.float32)
        up_sum = up_sum + up_recv[s].astype(jnp.float32)
    hidden_mine[...] = (gate_sum / (1.0 + jnp.exp(-gate_sum)) * up_sum).astype(hidden_mine.dtype)

    def gather_copy(r):
        return pltpu.make_async_remote_copy(
            src_ref=hidden_mine,
            dst_ref=hidden_all.at[me_e],
            send_sem=a_send.at[r],
            recv_sem=a_recv.at[me_e],
            device_id={"exp": r},
            device_id_type=MESH,
        )

    for t in range(n_exp):
        r = lax.rem(me_e + 2 * n_exp - plane - t, n_exp)

        @pl.when(r != me_e)
        def _():
            gather_copy(r).start()

        @pl.when(r == me_e)
        def _():
            pltpu.make_async_copy(hidden_mine, hidden_all.at[r], a_recv.at[r]).start()

    def return_copy(s):
        return pltpu.make_async_remote_copy(
            src_ref=ret_stage.at[s],
            dst_ref=returned.at[me_c],
            send_sem=b_send.at[s],
            recv_sem=b_recv.at[me_c],
            device_id={"ctx": s},
            device_id_type=MESH,
        )

    for t in range(n_exp):
        j = lax.rem(me_e + plane + t, n_exp)
        pltpu.make_async_copy(hidden_all.at[j], hidden_all.at[j], a_recv.at[j]).wait()
        first = pl.multiple_of(j * per_chunk, per_chunk)
        for k in range(EXP_ROW):
            res = jnp.dot(hidden_all[j, k], down_w[k], preferred_element_type=jnp.float32)
            ret_stage[pl.ds(first, per_chunk), k] = res.astype(ret_stage.dtype).reshape(
                per_chunk, rows // per_chunk, res.shape[-1]
            )
        for y in range(per_chunk):
            s = j * per_chunk + y

            @pl.when(s != me_c)
            def _():
                return_copy(s).start()

            @pl.when(s == me_c)
            def _():
                pltpu.make_async_copy(ret_stage.at[s], returned.at[s], b_recv.at[s]).start()

    for s in range(n_ctx):
        pltpu.make_async_copy(returned.at[s], returned.at[s], b_recv.at[s]).wait()
    back = returned[...].reshape(w_hi.shape[0], returned.shape[-1])
    contract = (((0,), (0,)), ((), ()))
    routed = lax.dot_general(w_hi[...], back, contract, preferred_element_type=jnp.float32) + lax.dot_general(
        w_lo[...], back, contract, preferred_element_type=jnp.float32
    )
    out[...] = (mixed_f + routed).astype(out.dtype)

    for r in range(n_exp):

        @pl.when(r != me_e)
        def _():
            gather_copy(r).wait_send()
            square_copy(r).wait_send()
            for which in range(2):
                reduce_copy(r, which).wait_send()

    for p in range(n_ctx):

        @pl.when(p != me_c)
        def _():
            dispatch_copy(p).wait_send()
            return_copy(p).wait_send()

    for h in range(halves):
        for r in range(1, group):
            second_copy(h, r).wait_send()
    for h in range(halves):
        z_r = lax.rem(plane + 2 * planes - q - h * (planes // halves), planes)
        for y in range(per_chunk):
            p = z_r * per_chunk + y

            @pl.when(p != me_c)
            def _():
                first_copy(p).wait_send()


def moe(queries, key_rows, value_rows, residual, block_order, gain, expert_ids, route_weight, out_shape, gate_weight,
        up_weight, down_weight, n_ctx, n_exp, collective_id):
    slot_total = out_shape[0] * out_shape[1] * out_shape[2]
    kv_shape = (residual.shape[0], KEY_VALUE_HEADS * HEAD_SIZE)
    mixed = residual
    square_shape = (residual.shape[0], 128)
    hid = gate_weight.shape[-1]
    size = math.prod(out_shape)
    slots = out_shape[0] * out_shape[2] // n_exp
    recv_shape = (n_exp, EXP_ROW, slots, hid)
    flops = 2 * 3 * size * hid + 2 * size * mixed.shape[0] * 3
    nbytes = 4 * size * 2 + 6 * gate_weight.size * 2 + 8 * n_exp * EXP_ROW * slots * hid * 2
    vmem = pltpu.VMEM
    return pl.pallas_call(
        functools.partial(moe_kernel, n_ctx, n_exp),
        out_shape=jax.ShapeDtypeStruct(mixed.shape, jnp.bfloat16),
        in_specs=[pl.BlockSpec(memory_space=pltpu.VMEM)] * 4
        + [pl.BlockSpec(memory_space=pltpu.SMEM)]
        + [pl.BlockSpec(memory_space=pltpu.VMEM)] * 6,
        out_specs=pl.BlockSpec(memory_space=pltpu.VMEM),
        scratch_shapes=[
            vmem((slot_total, residual.shape[0]), jnp.bfloat16),
            vmem((slot_total, residual.shape[0]), jnp.bfloat16),
            vmem((slot_total, residual.shape[0]), jnp.bfloat16),
            vmem(kv_shape, jnp.bfloat16),
            vmem((n_ctx,) + kv_shape, jnp.bfloat16),
            vmem(residual.shape, jnp.bfloat16),
            vmem(square_shape, jnp.float32),
            vmem((n_exp,) + square_shape, jnp.float32),
            vmem(out_shape, jnp.bfloat16),
            vmem(out_shape, jnp.bfloat16),
            vmem(recv_shape, jnp.bfloat16),
            vmem(recv_shape, jnp.bfloat16),
            vmem(recv_shape, jnp.bfloat16),
            vmem(recv_shape, jnp.bfloat16),
            vmem(recv_shape[1:], jnp.bfloat16),
            vmem(recv_shape, jnp.bfloat16),
            vmem(out_shape, jnp.bfloat16),
            vmem(out_shape, jnp.bfloat16),
            pltpu.SemaphoreType.DMA((n_ctx,)),
            pltpu.SemaphoreType.DMA((n_ctx,)),
            pltpu.SemaphoreType.DMA((n_exp, 2)),
            pltpu.SemaphoreType.DMA((n_exp, 2)),
            pltpu.SemaphoreType.DMA((n_exp,)),
            pltpu.SemaphoreType.DMA((n_exp,)),
            pltpu.SemaphoreType.DMA((n_ctx,)),
            pltpu.SemaphoreType.DMA((n_ctx,)),
            pltpu.SemaphoreType.DMA((n_exp, 2)),
            pltpu.SemaphoreType.DMA((n_exp, 2)),
            pltpu.SemaphoreType.DMA((n_exp,)),
            pltpu.SemaphoreType.DMA((n_exp,)),
            pltpu.SemaphoreType.DMA((n_ctx,)),
            pltpu.SemaphoreType.DMA((n_ctx,)),
        ],
        compiler_params=pltpu.CompilerParams(collective_id=collective_id, has_side_effects=True),
        cost_estimate=pl.CostEstimate(flops=flops, bytes_accessed=nbytes, transcendentals=0),
    )(queries, key_rows, value_rows, residual, block_order, gain, expert_ids, route_weight, gate_weight, up_weight,
      down_weight)

def kv_gather_kernel(n_ctx, n_exp, group, *refs):
    block, kv_all, s1_send, s1_recv, s2_send, s2_recv = refs
    per_plane = n_ctx // n_exp
    planes = n_ctx // per_plane
    me_c = lax.axis_index("ctx")
    me_e = lax.axis_index("exp")
    q = lax.rem(me_e, group)
    head_base = me_e - q
    plane = me_c // per_plane
    barrier = pltpu.get_barrier_semaphore()
    for k in range(1, n_ctx):
        pl.semaphore_signal(
            barrier, inc=1, device_id={"ctx": lax.rem(me_c + k, n_ctx)}, device_id_type=MESH
        )
    for k in range(1, group):
        pl.semaphore_signal(
            barrier, inc=1, device_id={"exp": head_base + lax.rem(q + k, group)}, device_id_type=MESH
        )
    pl.semaphore_wait(barrier, n_ctx + group - 2)

    def first_copy(p):
        return pltpu.make_async_remote_copy(
            src_ref=block,
            dst_ref=kv_all.at[me_c],
            send_sem=s1_send.at[p],
            recv_sem=s1_recv.at[me_c],
            device_id={"ctx": p},
            device_id_type=MESH,
        )

    halves = 2
    for h in range(halves):
        z_r = lax.rem(plane + 2 * planes - q - h * (planes // halves), planes)
        for y in range(per_plane):
            p = z_r * per_plane + y

            @pl.when(p != me_c)
            def _():
                first_copy(p).start()

            @pl.when(p == me_c)
            def _():
                pltpu.make_async_copy(block, kv_all.at[p], s1_recv.at[p]).start()

    def second_copy(h, r):
        first = pl.multiple_of(lax.rem(plane + q + h * (planes // halves), planes) * per_plane, per_plane)
        return pltpu.make_async_remote_copy(
            src_ref=kv_all.at[pl.ds(first, per_plane)],
            dst_ref=kv_all.at[pl.ds(first, per_plane)],
            send_sem=s2_send.at[r, h],
            recv_sem=s2_recv.at[r, h],
            device_id={"exp": head_base + lax.rem(q + r, group)},
            device_id_type=MESH,
        )

    for h in range(halves):
        z_s = lax.rem(plane + q + h * (planes // halves), planes)
        for y in range(per_plane):
            s = z_s * per_plane + y
            pltpu.make_async_copy(kv_all.at[s], kv_all.at[s], s1_recv.at[s]).wait()
        for r in range(1, group):
            second_copy(h, r).start()
    for h in range(halves):
        for r in range(1, group):
            second_copy(h, r).wait_recv()
    for h in range(halves):
        for r in range(1, group):
            second_copy(h, r).wait_send()
    for h in range(halves):
        z_r = lax.rem(plane + 2 * planes - q - h * (planes // halves), planes)
        for y in range(per_plane):
            p = z_r * per_plane + y

            @pl.when(p != me_c)
            def _():
                first_copy(p).wait_send()


def kv_gather(block, n_ctx, n_exp, group, collective_id):
    nbytes = block.size * block.dtype.itemsize * n_ctx
    return pl.pallas_call(
        functools.partial(kv_gather_kernel, n_ctx, n_exp, group),
        out_shape=jax.ShapeDtypeStruct((n_ctx,) + block.shape, block.dtype),
        in_specs=[pl.BlockSpec(memory_space=pltpu.VMEM)],
        out_specs=pl.BlockSpec(memory_space=pltpu.VMEM),
        scratch_shapes=[
            pltpu.SemaphoreType.DMA((n_ctx,)),
            pltpu.SemaphoreType.DMA((n_ctx,)),
            pltpu.SemaphoreType.DMA((group, 2)),
            pltpu.SemaphoreType.DMA((group, 2)),
        ],
        compiler_params=pltpu.CompilerParams(collective_id=collective_id, has_side_effects=True),
        cost_estimate=pl.CostEstimate(flops=0, bytes_accessed=2 * nbytes, transcendentals=0),
    )(block)


def local(
    queries,
    key_rows,
    value_head_rows,
    block_order,
    residual,
    norm_gain,
    expert_ids,
    route_weight,
    gate_weight,
    up_weight,
    down_weight,
):
    shard_rows = queries.shape[0]
    ctx_count = lax.axis_size("ctx")
    exp_count = lax.axis_size("exp")
    local_head = queries.shape[1] // HEAD_SIZE
    expert_index = lax.axis_index("exp")
    ctx_index = lax.axis_index("ctx")
    expert_count = ctx_count * EXP_ROW
    capacity = 2 * shard_rows * TOPK // expert_count
    return moe(
        queries,
        key_rows,
        value_head_rows,
        residual,
        block_order,
        norm_gain.reshape(1, -1),
        expert_ids.T,
        route_weight.T,
        (ctx_count, EXP_ROW, capacity, residual.shape[1]),
        gate_weight,
        up_weight,
        down_weight,
        ctx_count,
        exp_count,
        2,
    )

def solution(mesh):
    placed = (
        P(("rep", "ctx"), "exp"),
        P(("rep", "ctx"), None),
        P(("rep", "ctx"), None),
        P("rep"),
        P(("rep", "ctx"), "exp"),
        P("exp"),
        P(("rep", "ctx"), None),
        P(("rep", "ctx"), None),
        P("ctx", "exp", None),
        P("ctx", "exp", None),
        P("ctx", None, "exp"),
    )
    return jax.shard_map(
        local, mesh=mesh, in_specs=placed, out_specs=P(("rep", "ctx"), "exp"), check_vma=False
    )
```

```python
import functools
import math

import jax
import jax.numpy as jnp
from jax import lax
from jax.experimental import pallas as pl
from jax.experimental.pallas import tpu as pltpu
from jax.sharding import PartitionSpec as P

D = 4096
QUERY_HEADS = 32
KEY_VALUE_HEADS = 2
HEAD_SIZE = 128
TOPK = 8
EXP_ROW = 2

MASKED_SCORE = -1e30
NORM_EPS = 1e-06
MESH = pl.DeviceIdType.MESH


def exchange_kernel(axis, n, gather, n_in, *refs):
    ins, outs = refs[:n_in], refs[n_in : 2 * n_in]
    send_sem, recv_sem = refs[2 * n_in], refs[2 * n_in + 1]
    me = lax.axis_index(axis)
    barrier = pltpu.get_barrier_semaphore()
    for k in range(1, n):
        pl.semaphore_signal(
            barrier, inc=1, device_id={axis: lax.rem(me + k, n)}, device_id_type=MESH
        )
    pl.semaphore_wait(barrier, n - 1)
    copies = []
    for k in range(1, n):
        peer = lax.rem(me + k, n)
        for i in range(n_in):
            copy = pltpu.make_async_remote_copy(
                src_ref=ins[i] if gather else ins[i].at[peer],
                dst_ref=outs[i].at[me],
                send_sem=send_sem.at[i, k],
                recv_sem=recv_sem.at[i, k],
                device_id={axis: peer},
                device_id_type=MESH,
            )
            copy.start()
            copies.append(copy)
    for i in range(n_in):
        outs[i][me] = ins[i][...] if gather else ins[i][me]
    for copy in copies:
        copy.wait()


def exchange(xs, axis, n, gather, collective_id):
    n_in = len(xs)
    out_shape = [
        jax.ShapeDtypeStruct((n,) + (x.shape if gather else x.shape[1:]), x.dtype) for x in xs
    ]
    nbytes = sum(x.size * x.dtype.itemsize for x in xs) * (n if gather else 1)
    return pl.pallas_call(
        functools.partial(exchange_kernel, axis, n, gather, n_in),
        out_shape=out_shape,
        in_specs=[pl.BlockSpec(memory_space=pltpu.VMEM)] * n_in,
        out_specs=[pl.BlockSpec(memory_space=pltpu.VMEM)] * n_in,
        scratch_shapes=[
            pltpu.SemaphoreType.DMA((n_in, n)),
            pltpu.SemaphoreType.DMA((n_in, n)),
        ],
        compiler_params=pltpu.CompilerParams(collective_id=collective_id, has_side_effects=True),
        cost_estimate=pl.CostEstimate(flops=0, bytes_accessed=2 * nbytes, transcendentals=0),
    )(*xs)


def moe_kernel(n_ctx, n_exp, *refs):
    (queries, key_rows, value_rows, residual, block_order, gain, expert_ids, route_weight, gate_w, up_w, down_w, out,
     slot_rows, w_hi, w_lo, kv_block, kv_all, mixed, square_block, square_all, outgoing, incoming, gate_stage, up_stage, gate_recv, up_recv,
     hidden_mine, hidden_all, ret_stage, returned, s1_send, s1_recv, s2_send, s2_recv, q_send, q_recv, d_send,
     d_recv, r_send, r_recv, a_send, a_recv, b_send, b_recv) = refs
    per_chunk = n_ctx // n_exp
    me_c = lax.axis_index("ctx")
    me_e = lax.axis_index("exp")
    plane = me_c // per_chunk
    barrier = pltpu.get_barrier_semaphore()
    for k in range(1, n_ctx):
        pl.semaphore_signal(
            barrier, inc=1, device_id={"ctx": lax.rem(me_c + k, n_ctx)}, device_id_type=MESH
        )
    for k in range(1, n_exp):
        pl.semaphore_signal(
            barrier, inc=1, device_id={"exp": lax.rem(me_e + k, n_exp)}, device_id_type=MESH
        )
    pl.semaphore_wait(barrier, n_ctx + n_exp - 2)

    group = QUERY_HEADS // KEY_VALUE_HEADS // (queries.shape[1] // HEAD_SIZE)
    head_cols = pl.ds(pl.multiple_of((me_e // group) * HEAD_SIZE, HEAD_SIZE), HEAD_SIZE)
    kv_block[:, :HEAD_SIZE] = key_rows[:, head_cols]
    kv_block[:, HEAD_SIZE:] = value_rows[:, head_cols]
    q = lax.rem(me_e, group)
    head_base = me_e - q
    planes = n_exp
    halves = 2

    def first_copy(p):
        return pltpu.make_async_remote_copy(
            src_ref=kv_block,
            dst_ref=kv_all.at[me_c],
            send_sem=s1_send.at[p],
            recv_sem=s1_recv.at[me_c],
            device_id={"ctx": p},
            device_id_type=MESH,
        )

    for h in range(halves):
        z_r = lax.rem(plane + 2 * planes - q - h * (planes // halves), planes)
        for y in range(per_chunk):
            p = z_r * per_chunk + y

            @pl.when(p != me_c)
            def _():
                first_copy(p).start()

            @pl.when(p == me_c)
            def _():
                pltpu.make_async_copy(kv_block, kv_all.at[p], s1_recv.at[p]).start()

    def second_copy(h, r):
        first = pl.multiple_of(lax.rem(plane + q + h * (planes // halves), planes) * per_chunk, per_chunk)
        return pltpu.make_async_remote_copy(
            src_ref=kv_all.at[pl.ds(first, per_chunk)],
            dst_ref=kv_all.at[pl.ds(first, per_chunk)],
            send_sem=s2_send.at[r, h],
            recv_sem=s2_recv.at[r, h],
            device_id={"exp": head_base + lax.rem(q + r, group)},
            device_id_type=MESH,
        )

    topk, rows_here = expert_ids.shape
    slot_total = slot_rows.shape[0]
    capacity = slot_total // (n_ctx * EXP_ROW)
    ids = expert_ids[...]
    expert_sub = lax.broadcasted_iota(jnp.int32, (n_ctx * EXP_ROW, rows_here), 0)
    picks = [(ids[i : i + 1, :] == expert_sub).astype(jnp.float32) for i in range(topk)]
    per_row = picks[0]
    for i in range(1, topk):
        per_row = per_row + picks[i]
    later = (
        lax.broadcasted_iota(jnp.int32, (rows_here, rows_here), 0)
        < lax.broadcasted_iota(jnp.int32, (rows_here, rows_here), 1)
    ).astype(jnp.bfloat16)
    before = jnp.dot(per_row.astype(jnp.bfloat16), later, preferred_element_type=jnp.float32)
    slot_sub = lax.broadcasted_iota(jnp.int32, (slot_total, rows_here), 0)
    chosen = jnp.zeros((slot_total, rows_here), jnp.float32)
    weight = jnp.zeros((slot_total, rows_here), jnp.float32)
    weights_in = route_weight[...]
    for i in range(topk):
        rank = jnp.sum(picks[i] * before, axis=0, keepdims=True)
        before = before + picks[i]
        slot = ids[i : i + 1, :] * capacity + rank.astype(jnp.int32)
        hit = slot == slot_sub
        chosen = jnp.where(hit, 1.0, chosen)
        weight = jnp.where(hit, weights_in[i : i + 1, :], weight)
    slot_rows[...] = chosen.astype(slot_rows.dtype)
    high = weight.astype(jnp.bfloat16)
    w_hi[...] = high
    w_lo[...] = (weight - high.astype(jnp.float32)).astype(jnp.bfloat16)

    for h in range(halves):
        z_s = lax.rem(plane + q + h * (planes // halves), planes)
        for y in range(per_chunk):
            s = z_s * per_chunk + y
            pltpu.make_async_copy(kv_all.at[s], kv_all.at[s], s1_recv.at[s]).wait()
        for r in range(1, group):
            second_copy(h, r).start()
    for h in range(halves):
        for r in range(1, group):
            second_copy(h, r).wait_recv()

    total_rows = kv_all.shape[0] * kv_all.shape[1]
    keys = kv_all[:, :, :HEAD_SIZE].reshape(total_rows, HEAD_SIZE)
    values = kv_all[:, :, HEAD_SIZE:].reshape(total_rows, HEAD_SIZE)
    block_rows = kv_all.shape[1]
    query_pos = block_order[me_c] * block_rows + lax.broadcasted_iota(jnp.int32, (queries.shape[0], 1), 0)
    key_lane = lax.broadcasted_iota(jnp.int32, (1, total_rows), 1)
    key_pos = key_lane % block_rows
    for b in range(kv_all.shape[0]):
        key_pos = jnp.where(key_lane // block_rows == b, key_pos + block_order[b] * block_rows, key_pos)
    visible = key_pos <= query_pos
    inv_scale = 1.0 / math.sqrt(HEAD_SIZE)
    heads = queries.shape[1] // HEAD_SIZE

    def square_copy(r, h):
        return pltpu.make_async_remote_copy(
            src_ref=square_block.at[h],
            dst_ref=square_all.at[me_e, h],
            send_sem=q_send.at[r, h],
            recv_sem=q_recv.at[me_e, h],
            device_id={"exp": r},
            device_id_type=MESH,
        )

    for h in range(heads):
        cols = slice(h * HEAD_SIZE, (h + 1) * HEAD_SIZE)
        scores = (
            lax.dot_general(
                queries[:, cols], keys, (((1,), (1,)), ((), ())), preferred_element_type=jnp.float32
            )
            * inv_scale
        )
        scores = jnp.where(visible, scores, MASKED_SCORE)
        newest = jnp.max(scores, axis=1, keepdims=True)
        weights = jnp.where(visible, jnp.exp(scores - newest), 0.0)
        weight_sum = jnp.sum(weights, axis=1, keepdims=True)
        weighted = jnp.dot(weights.astype(jnp.bfloat16), values, preferred_element_type=jnp.float32)
        attention = (weighted / weight_sum).astype(jnp.bfloat16)
        mixed_h = (residual[:, cols].astype(jnp.float32) + attention.astype(jnp.float32)).astype(
            jnp.bfloat16
        )
        mixed[:, cols] = mixed_h
        mixed_hf = mixed_h.astype(jnp.float32)
        square_h = jnp.sum(mixed_hf * mixed_hf, axis=1, keepdims=True)
        square_block[h] = jnp.broadcast_to(square_h, square_block.shape[1:])
        for k in range(1, n_exp):
            square_copy(lax.rem(me_e + k, n_exp), h).start()
        pltpu.make_async_copy(square_block.at[h], square_all.at[me_e, h], q_recv.at[me_e, h]).start()

    square_sum = None
    for h in range(heads):
        for s in range(n_exp):
            pltpu.make_async_copy(square_all.at[s, h], square_all.at[s, h], q_recv.at[s, h]).wait()
            term = square_all[s, h]
            square_sum = term if square_sum is None else square_sum + term
    scale = lax.rsqrt(square_sum[:, :1] / D + NORM_EPS)
    mixed_f = mixed[...].astype(jnp.float32)
    normed = (mixed_f * scale * gain[...]).astype(jnp.bfloat16)
    filled = jnp.dot(slot_rows[...], normed, preferred_element_type=jnp.float32)
    outgoing[...] = filled.astype(outgoing.dtype).reshape(outgoing.shape)

    def dispatch_copy(p):
        return pltpu.make_async_remote_copy(
            src_ref=outgoing.at[p],
            dst_ref=incoming.at[me_c],
            send_sem=d_send.at[p],
            recv_sem=d_recv.at[me_c],
            device_id={"ctx": p},
            device_id_type=MESH,
        )

    for t in range(n_exp):
        z_r = lax.rem(plane + 2 * n_exp - me_e - t, n_exp)
        for y in range(per_chunk):
            p = z_r * per_chunk + y

            @pl.when(p != me_c)
            def _():
                dispatch_copy(p).start()

            @pl.when(p == me_c)
            def _():
                pltpu.make_async_copy(outgoing.at[p], incoming.at[p], d_recv.at[p]).start()

    parts = ((gate_w, gate_stage, gate_recv), (up_w, up_stage, up_recv))

    def reduce_copy(j, which):
        _, stage, recv = parts[which]
        return pltpu.make_async_remote_copy(
            src_ref=stage.at[j],
            dst_ref=recv.at[me_e],
            send_sem=r_send.at[j, which],
            recv_sem=r_recv.at[me_e, which],
            device_id={"exp": j},
            device_id_type=MESH,
        )

    rows = gate_stage.shape[2]
    for t in range(n_exp):
        j = lax.rem(plane + me_e + t, n_exp)
        for y in range(per_chunk):
            s = j * per_chunk + y
            pltpu.make_async_copy(incoming.at[s], incoming.at[s], d_recv.at[s]).wait()
        first = pl.multiple_of(j * per_chunk, per_chunk)
        for k in range(EXP_ROW):
            x = incoming[pl.ds(first, per_chunk), k].reshape(rows, incoming.shape[-1])
            for w, stage, _ in parts:
                stage[j, k] = jnp.dot(x, w[k], preferred_element_type=jnp.float32).astype(
                    stage.dtype
                )

        @pl.when(j != me_e)
        def _():
            for which in range(2):
                reduce_copy(j, which).start()

        @pl.when(j == me_e)
        def _():
            for which, (_, stage, recv) in enumerate(parts):
                pltpu.make_async_copy(stage.at[j], recv.at[j], r_recv.at[j, which]).start()

    for s in range(n_exp):
        for which, (_, _, recv) in enumerate(parts):
            pltpu.make_async_copy(recv.at[s], recv.at[s], r_recv.at[s, which]).wait()
    gate_sum = gate_recv[0].astype(jnp.float32)
    up_sum = up_recv[0].astype(jnp.float32)
    for s in range(1, n_exp):
        gate_sum = gate_sum + gate_recv[s].astype(jnp.float32)
        up_sum = up_sum + up_recv[s].astype(jnp.float32)
    hidden_mine[...] = (gate_sum / (1.0 + jnp.exp(-gate_sum)) * up_sum).astype(hidden_mine.dtype)

    def gather_copy(r):
        return pltpu.make_async_remote_copy(
            src_ref=hidden_mine,
            dst_ref=hidden_all.at[me_e],
            send_sem=a_send.at[r],
            recv_sem=a_recv.at[me_e],
            device_id={"exp": r},
            device_id_type=MESH,
        )

    for t in range(n_exp):
        r = lax.rem(me_e + 2 * n_exp - plane - t, n_exp)

        @pl.when(r != me_e)
        def _():
            gather_copy(r).start()

        @pl.when(r == me_e)
        def _():
            pltpu.make_async_copy(hidden_mine, hidden_all.at[r], a_recv.at[r]).start()

    def return_copy(s):
        return pltpu.make_async_remote_copy(
            src_ref=ret_stage.at[s],
            dst_ref=returned.at[me_c],
            send_sem=b_send.at[s],
            recv_sem=b_recv.at[me_c],
            device_id={"ctx": s},
            device_id_type=MESH,
        )

    for t in range(n_exp):
        j = lax.rem(me_e + plane + t, n_exp)
        pltpu.make_async_copy(hidden_all.at[j], hidden_all.at[j], a_recv.at[j]).wait()
        first = pl.multiple_of(j * per_chunk, per_chunk)
        for k in range(EXP_ROW):
            res = jnp.dot(hidden_all[j, k], down_w[k], preferred_element_type=jnp.float32)
            ret_stage[pl.ds(first, per_chunk), k] = res.astype(ret_stage.dtype).reshape(
                per_chunk, rows // per_chunk, res.shape[-1]
            )
        for y in range(per_chunk):
            s = j * per_chunk + y

            @pl.when(s != me_c)
            def _():
                return_copy(s).start()

            @pl.when(s == me_c)
            def _():
                pltpu.make_async_copy(ret_stage.at[s], returned.at[s], b_recv.at[s]).start()

    for s in range(n_ctx):
        pltpu.make_async_copy(returned.at[s], returned.at[s], b_recv.at[s]).wait()
    back = returned[...].reshape(w_hi.shape[0], returned.shape[-1])
    contract = (((0,), (0,)), ((), ()))
    routed = lax.dot_general(w_hi[...], back, contract, preferred_element_type=jnp.float32) + lax.dot_general(
        w_lo[...], back, contract, preferred_element_type=jnp.float32
    )
    out[...] = (mixed_f + routed).astype(out.dtype)

    for r in range(n_exp):

        @pl.when(r != me_e)
        def _():
            gather_copy(r).wait_send()
            for h in range(heads):
                square_copy(r, h).wait_send()
            for which in range(2):
                reduce_copy(r, which).wait_send()

    for p in range(n_ctx):

        @pl.when(p != me_c)
        def _():
            dispatch_copy(p).wait_send()
            return_copy(p).wait_send()

    for h in range(halves):
        for r in range(1, group):
            second_copy(h, r).wait_send()
    for h in range(halves):
        z_r = lax.rem(plane + 2 * planes - q - h * (planes // halves), planes)
        for y in range(per_chunk):
            p = z_r * per_chunk + y

            @pl.when(p != me_c)
            def _():
                first_copy(p).wait_send()


def moe(queries, key_rows, value_rows, residual, block_order, gain, expert_ids, route_weight, out_shape, gate_weight,
        up_weight, down_weight, n_ctx, n_exp, collective_id):
    slot_total = out_shape[0] * out_shape[1] * out_shape[2]
    kv_shape = (residual.shape[0], KEY_VALUE_HEADS * HEAD_SIZE)
    mixed = residual
    square_shape = (residual.shape[0], 128)
    heads = queries.shape[1] // HEAD_SIZE
    hid = gate_weight.shape[-1]
    size = math.prod(out_shape)
    slots = out_shape[0] * out_shape[2] // n_exp
    recv_shape = (n_exp, EXP_ROW, slots, hid)
    flops = 2 * 3 * size * hid + 2 * size * mixed.shape[0] * 3
    nbytes = 4 * size * 2 + 6 * gate_weight.size * 2 + 8 * n_exp * EXP_ROW * slots * hid * 2
    vmem = pltpu.VMEM
    return pl.pallas_call(
        functools.partial(moe_kernel, n_ctx, n_exp),
        out_shape=jax.ShapeDtypeStruct(mixed.shape, jnp.bfloat16),
        in_specs=[pl.BlockSpec(memory_space=pltpu.VMEM)] * 4
        + [pl.BlockSpec(memory_space=pltpu.SMEM)]
        + [pl.BlockSpec(memory_space=pltpu.VMEM)] * 6,
        out_specs=pl.BlockSpec(memory_space=pltpu.VMEM),
        scratch_shapes=[
            vmem((slot_total, residual.shape[0]), jnp.bfloat16),
            vmem((slot_total, residual.shape[0]), jnp.bfloat16),
            vmem((slot_total, residual.shape[0]), jnp.bfloat16),
            vmem(kv_shape, jnp.bfloat16),
            vmem((n_ctx,) + kv_shape, jnp.bfloat16),
            vmem(residual.shape, jnp.bfloat16),
            vmem((heads,) + square_shape, jnp.float32),
            vmem((n_exp, heads) + square_shape, jnp.float32),
            vmem(out_shape, jnp.bfloat16),
            vmem(out_shape, jnp.bfloat16),
            vmem(recv_shape, jnp.bfloat16),
            vmem(recv_shape, jnp.bfloat16),
            vmem(recv_shape, jnp.bfloat16),
            vmem(recv_shape, jnp.bfloat16),
            vmem(recv_shape[1:], jnp.bfloat16),
            vmem(recv_shape, jnp.bfloat16),
            vmem(out_shape, jnp.bfloat16),
            vmem(out_shape, jnp.bfloat16),
            pltpu.SemaphoreType.DMA((n_ctx,)),
            pltpu.SemaphoreType.DMA((n_ctx,)),
            pltpu.SemaphoreType.DMA((n_exp, 2)),
            pltpu.SemaphoreType.DMA((n_exp, 2)),
            pltpu.SemaphoreType.DMA((n_exp, heads)),
            pltpu.SemaphoreType.DMA((n_exp, heads)),
            pltpu.SemaphoreType.DMA((n_ctx,)),
            pltpu.SemaphoreType.DMA((n_ctx,)),
            pltpu.SemaphoreType.DMA((n_exp, 2)),
            pltpu.SemaphoreType.DMA((n_exp, 2)),
            pltpu.SemaphoreType.DMA((n_exp,)),
            pltpu.SemaphoreType.DMA((n_exp,)),
            pltpu.SemaphoreType.DMA((n_ctx,)),
            pltpu.SemaphoreType.DMA((n_ctx,)),
        ],
        compiler_params=pltpu.CompilerParams(collective_id=collective_id, has_side_effects=True),
        cost_estimate=pl.CostEstimate(flops=flops, bytes_accessed=nbytes, transcendentals=0),
    )(queries, key_rows, value_rows, residual, block_order, gain, expert_ids, route_weight, gate_weight, up_weight,
      down_weight)

def kv_gather_kernel(n_ctx, n_exp, group, *refs):
    block, kv_all, s1_send, s1_recv, s2_send, s2_recv = refs
    per_plane = n_ctx // n_exp
    planes = n_ctx // per_plane
    me_c = lax.axis_index("ctx")
    me_e = lax.axis_index("exp")
    q = lax.rem(me_e, group)
    head_base = me_e - q
    plane = me_c // per_plane
    barrier = pltpu.get_barrier_semaphore()
    for k in range(1, n_ctx):
        pl.semaphore_signal(
            barrier, inc=1, device_id={"ctx": lax.rem(me_c + k, n_ctx)}, device_id_type=MESH
        )
    for k in range(1, group):
        pl.semaphore_signal(
            barrier, inc=1, device_id={"exp": head_base + lax.rem(q + k, group)}, device_id_type=MESH
        )
    pl.semaphore_wait(barrier, n_ctx + group - 2)

    def first_copy(p):
        return pltpu.make_async_remote_copy(
            src_ref=block,
            dst_ref=kv_all.at[me_c],
            send_sem=s1_send.at[p],
            recv_sem=s1_recv.at[me_c],
            device_id={"ctx": p},
            device_id_type=MESH,
        )

    halves = 2
    for h in range(halves):
        z_r = lax.rem(plane + 2 * planes - q - h * (planes // halves), planes)
        for y in range(per_plane):
            p = z_r * per_plane + y

            @pl.when(p != me_c)
            def _():
                first_copy(p).start()

            @pl.when(p == me_c)
            def _():
                pltpu.make_async_copy(block, kv_all.at[p], s1_recv.at[p]).start()

    def second_copy(h, r):
        first = pl.multiple_of(lax.rem(plane + q + h * (planes // halves), planes) * per_plane, per_plane)
        return pltpu.make_async_remote_copy(
            src_ref=kv_all.at[pl.ds(first, per_plane)],
            dst_ref=kv_all.at[pl.ds(first, per_plane)],
            send_sem=s2_send.at[r, h],
            recv_sem=s2_recv.at[r, h],
            device_id={"exp": head_base + lax.rem(q + r, group)},
            device_id_type=MESH,
        )

    for h in range(halves):
        z_s = lax.rem(plane + q + h * (planes // halves), planes)
        for y in range(per_plane):
            s = z_s * per_plane + y
            pltpu.make_async_copy(kv_all.at[s], kv_all.at[s], s1_recv.at[s]).wait()
        for r in range(1, group):
            second_copy(h, r).start()
    for h in range(halves):
        for r in range(1, group):
            second_copy(h, r).wait_recv()
    for h in range(halves):
        for r in range(1, group):
            second_copy(h, r).wait_send()
    for h in range(halves):
        z_r = lax.rem(plane + 2 * planes - q - h * (planes // halves), planes)
        for y in range(per_plane):
            p = z_r * per_plane + y

            @pl.when(p != me_c)
            def _():
                first_copy(p).wait_send()


def kv_gather(block, n_ctx, n_exp, group, collective_id):
    nbytes = block.size * block.dtype.itemsize * n_ctx
    return pl.pallas_call(
        functools.partial(kv_gather_kernel, n_ctx, n_exp, group),
        out_shape=jax.ShapeDtypeStruct((n_ctx,) + block.shape, block.dtype),
        in_specs=[pl.BlockSpec(memory_space=pltpu.VMEM)],
        out_specs=pl.BlockSpec(memory_space=pltpu.VMEM),
        scratch_shapes=[
            pltpu.SemaphoreType.DMA((n_ctx,)),
            pltpu.SemaphoreType.DMA((n_ctx,)),
            pltpu.SemaphoreType.DMA((group, 2)),
            pltpu.SemaphoreType.DMA((group, 2)),
        ],
        compiler_params=pltpu.CompilerParams(collective_id=collective_id, has_side_effects=True),
        cost_estimate=pl.CostEstimate(flops=0, bytes_accessed=2 * nbytes, transcendentals=0),
    )(block)


def local(
    queries,
    key_rows,
    value_head_rows,
    block_order,
    residual,
    norm_gain,
    expert_ids,
    route_weight,
    gate_weight,
    up_weight,
    down_weight,
):
    shard_rows = queries.shape[0]
    ctx_count = lax.axis_size("ctx")
    exp_count = lax.axis_size("exp")
    local_head = queries.shape[1] // HEAD_SIZE
    expert_index = lax.axis_index("exp")
    ctx_index = lax.axis_index("ctx")
    expert_count = ctx_count * EXP_ROW
    capacity = 2 * shard_rows * TOPK // expert_count
    return moe(
        queries,
        key_rows,
        value_head_rows,
        residual,
        block_order,
        norm_gain.reshape(1, -1),
        expert_ids.T,
        route_weight.T,
        (ctx_count, EXP_ROW, capacity, residual.shape[1]),
        gate_weight,
        up_weight,
        down_weight,
        ctx_count,
        exp_count,
        2,
    )

def solution(mesh):
    placed = (
        P(("rep", "ctx"), "exp"),
        P(("rep", "ctx"), None),
        P(("rep", "ctx"), None),
        P("rep"),
        P(("rep", "ctx"), "exp"),
        P("exp"),
        P(("rep", "ctx"), None),
        P(("rep", "ctx"), None),
        P("ctx", "exp", None),
        P("ctx", "exp", None),
        P("ctx", None, "exp"),
    )
    return jax.shard_map(
        local, mesh=mesh, in_specs=placed, out_specs=P(("rep", "ctx"), "exp"), check_vma=False
    )
```

```python
import functools
import math

import jax
import jax.numpy as jnp
from jax import lax
from jax.experimental import pallas as pl
from jax.experimental.pallas import tpu as pltpu
from jax.sharding import PartitionSpec as P

D = 4096
QUERY_HEADS = 32
KEY_VALUE_HEADS = 2
HEAD_SIZE = 128
TOPK = 8
EXP_ROW = 2

MASKED_SCORE = -1e30
NORM_EPS = 1e-06
MESH = pl.DeviceIdType.MESH


def exchange_kernel(axis, n, gather, n_in, *refs):
    ins, outs = refs[:n_in], refs[n_in : 2 * n_in]
    send_sem, recv_sem = refs[2 * n_in], refs[2 * n_in + 1]
    me = lax.axis_index(axis)
    barrier = pltpu.get_barrier_semaphore()
    for k in range(1, n):
        pl.semaphore_signal(
            barrier, inc=1, device_id={axis: lax.rem(me + k, n)}, device_id_type=MESH
        )
    pl.semaphore_wait(barrier, n - 1)
    copies = []
    for k in range(1, n):
        peer = lax.rem(me + k, n)
        for i in range(n_in):
            copy = pltpu.make_async_remote_copy(
                src_ref=ins[i] if gather else ins[i].at[peer],
                dst_ref=outs[i].at[me],
                send_sem=send_sem.at[i, k],
                recv_sem=recv_sem.at[i, k],
                device_id={axis: peer},
                device_id_type=MESH,
            )
            copy.start()
            copies.append(copy)
    for i in range(n_in):
        outs[i][me] = ins[i][...] if gather else ins[i][me]
    for copy in copies:
        copy.wait()


def exchange(xs, axis, n, gather, collective_id):
    n_in = len(xs)
    out_shape = [
        jax.ShapeDtypeStruct((n,) + (x.shape if gather else x.shape[1:]), x.dtype) for x in xs
    ]
    nbytes = sum(x.size * x.dtype.itemsize for x in xs) * (n if gather else 1)
    return pl.pallas_call(
        functools.partial(exchange_kernel, axis, n, gather, n_in),
        out_shape=out_shape,
        in_specs=[pl.BlockSpec(memory_space=pltpu.VMEM)] * n_in,
        out_specs=[pl.BlockSpec(memory_space=pltpu.VMEM)] * n_in,
        scratch_shapes=[
            pltpu.SemaphoreType.DMA((n_in, n)),
            pltpu.SemaphoreType.DMA((n_in, n)),
        ],
        compiler_params=pltpu.CompilerParams(collective_id=collective_id, has_side_effects=True),
        cost_estimate=pl.CostEstimate(flops=0, bytes_accessed=2 * nbytes, transcendentals=0),
    )(*xs)


def moe_kernel(n_ctx, n_exp, *refs):
    (queries, key_rows, value_rows, residual, block_order, gain, expert_ids, route_weight, gate_w, up_w, down_w, out,
     slot_rows, w_hi, w_lo, kv_block, kv_all, mixed, square_block, square_all, outgoing, incoming, gate_stage, up_stage, gate_recv, up_recv,
     hidden_mine, hidden_all, ret_stage, returned, s1_send, s1_recv, s2_send, s2_recv, q_send, q_recv, d_send,
     d_recv, r_send, r_recv, a_send, a_recv, b_send, b_recv) = refs
    per_chunk = n_ctx // n_exp
    me_c = lax.axis_index("ctx")
    me_e = lax.axis_index("exp")
    plane = me_c // per_chunk
    barrier = pltpu.get_barrier_semaphore()
    for k in range(1, n_ctx):
        pl.semaphore_signal(
            barrier, inc=1, device_id={"ctx": lax.rem(me_c + k, n_ctx)}, device_id_type=MESH
        )
    for k in range(1, n_exp):
        pl.semaphore_signal(
            barrier, inc=1, device_id={"exp": lax.rem(me_e + k, n_exp)}, device_id_type=MESH
        )
    pl.semaphore_wait(barrier, n_ctx + n_exp - 2)

    group = QUERY_HEADS // KEY_VALUE_HEADS // (queries.shape[1] // HEAD_SIZE)
    head_cols = pl.ds(pl.multiple_of((me_e // group) * HEAD_SIZE, HEAD_SIZE), HEAD_SIZE)
    kv_block[:, :HEAD_SIZE] = key_rows[:, head_cols]
    kv_block[:, HEAD_SIZE:] = value_rows[:, head_cols]
    q = lax.rem(me_e, group)
    head_base = me_e - q
    planes = n_exp
    halves = 2

    def first_copy(p):
        return pltpu.make_async_remote_copy(
            src_ref=kv_block,
            dst_ref=kv_all.at[me_c],
            send_sem=s1_send.at[p],
            recv_sem=s1_recv.at[me_c],
            device_id={"ctx": p},
            device_id_type=MESH,
        )

    for h in range(halves):
        z_r = lax.rem(plane + 2 * planes - q - h * (planes // halves), planes)
        for y in range(per_chunk):
            p = z_r * per_chunk + y

            @pl.when(p != me_c)
            def _():
                first_copy(p).start()

            @pl.when(p == me_c)
            def _():
                pltpu.make_async_copy(kv_block, kv_all.at[p], s1_recv.at[p]).start()

    def second_copy(h, r):
        first = pl.multiple_of(lax.rem(plane + q + h * (planes // halves), planes) * per_chunk, per_chunk)
        return pltpu.make_async_remote_copy(
            src_ref=kv_all.at[pl.ds(first, per_chunk)],
            dst_ref=kv_all.at[pl.ds(first, per_chunk)],
            send_sem=s2_send.at[r, h],
            recv_sem=s2_recv.at[r, h],
            device_id={"exp": head_base + lax.rem(q + r, group)},
            device_id_type=MESH,
        )

    topk, rows_here = expert_ids.shape
    slot_total = slot_rows.shape[0]
    capacity = slot_total // (n_ctx * EXP_ROW)
    ids = expert_ids[...]
    expert_sub = lax.broadcasted_iota(jnp.int32, (n_ctx * EXP_ROW, rows_here), 0)
    picks = [(ids[i : i + 1, :] == expert_sub).astype(jnp.float32) for i in range(topk)]
    per_row = picks[0]
    for i in range(1, topk):
        per_row = per_row + picks[i]
    later = (
        lax.broadcasted_iota(jnp.int32, (rows_here, rows_here), 0)
        < lax.broadcasted_iota(jnp.int32, (rows_here, rows_here), 1)
    ).astype(jnp.bfloat16)
    before = jnp.dot(per_row.astype(jnp.bfloat16), later, preferred_element_type=jnp.float32)
    slot_sub = lax.broadcasted_iota(jnp.int32, (slot_total, rows_here), 0)
    chosen = jnp.zeros((slot_total, rows_here), jnp.float32)
    weight = jnp.zeros((slot_total, rows_here), jnp.float32)
    weights_in = route_weight[...]
    for i in range(topk):
        rank = jnp.sum(picks[i] * before, axis=0, keepdims=True)
        before = before + picks[i]
        slot = ids[i : i + 1, :] * capacity + rank.astype(jnp.int32)
        hit = slot == slot_sub
        chosen = jnp.where(hit, 1.0, chosen)
        weight = jnp.where(hit, weights_in[i : i + 1, :], weight)
    slot_rows[...] = chosen.astype(slot_rows.dtype)
    high = weight.astype(jnp.bfloat16)
    w_hi[...] = high
    w_lo[...] = (weight - high.astype(jnp.float32)).astype(jnp.bfloat16)

    for h in range(halves):
        z_s = lax.rem(plane + q + h * (planes // halves), planes)
        for y in range(per_chunk):
            s = z_s * per_chunk + y
            pltpu.make_async_copy(kv_all.at[s], kv_all.at[s], s1_recv.at[s]).wait()
        for r in range(1, group):
            second_copy(h, r).start()
    for h in range(halves):
        for r in range(1, group):
            second_copy(h, r).wait_recv()

    total_rows = kv_all.shape[0] * kv_all.shape[1]
    keys = kv_all[:, :, :HEAD_SIZE].reshape(total_rows, HEAD_SIZE)
    values = kv_all[:, :, HEAD_SIZE:].reshape(total_rows, HEAD_SIZE)
    block_rows = kv_all.shape[1]
    query_pos = block_order[me_c] * block_rows + lax.broadcasted_iota(jnp.int32, (queries.shape[0], 1), 0)
    key_lane = lax.broadcasted_iota(jnp.int32, (1, total_rows), 1)
    key_pos = key_lane % block_rows
    for b in range(kv_all.shape[0]):
        key_pos = jnp.where(key_lane // block_rows == b, key_pos + block_order[b] * block_rows, key_pos)
    visible = key_pos <= query_pos
    inv_scale = 1.0 / math.sqrt(HEAD_SIZE)
    square_part = jnp.zeros((queries.shape[0], 1), jnp.float32)
    for h in range(queries.shape[1] // HEAD_SIZE):
        cols = slice(h * HEAD_SIZE, (h + 1) * HEAD_SIZE)
        scores = (
            lax.dot_general(
                queries[:, cols], keys, (((1,), (1,)), ((), ())), preferred_element_type=jnp.float32
            )
            * inv_scale
        )
        scores = jnp.where(visible, scores, MASKED_SCORE)
        newest = jnp.max(scores, axis=1, keepdims=True)
        weights = jnp.where(visible, jnp.exp(scores - newest), 0.0)
        weight_sum = jnp.sum(weights, axis=1, keepdims=True)
        weighted = jnp.dot(weights.astype(jnp.bfloat16), values, preferred_element_type=jnp.float32)
        attention = (weighted / weight_sum).astype(jnp.bfloat16)
        mixed_h = (residual[:, cols].astype(jnp.float32) + attention.astype(jnp.float32)).astype(
            jnp.bfloat16
        )
        mixed[:, cols] = mixed_h
        mixed_hf = mixed_h.astype(jnp.float32)
        square_part = square_part + jnp.sum(mixed_hf * mixed_hf, axis=1, keepdims=True)
    square_block[...] = jnp.broadcast_to(square_part, square_block.shape)

    def square_copy(r):
        return pltpu.make_async_remote_copy(
            src_ref=square_block,
            dst_ref=square_all.at[me_e],
            send_sem=q_send.at[r],
            recv_sem=q_recv.at[me_e],
            device_id={"exp": r},
            device_id_type=MESH,
        )

    for k in range(1, n_exp):
        square_copy(lax.rem(me_e + k, n_exp)).start()
    pltpu.make_async_copy(square_block, square_all.at[me_e], q_recv.at[me_e]).start()
    for s in range(n_exp):
        pltpu.make_async_copy(square_all.at[s], square_all.at[s], q_recv.at[s]).wait()
    square_sum = square_all[0]
    for s in range(1, n_exp):
        square_sum = square_sum + square_all[s]
    scale = lax.rsqrt(square_sum[:, :1] / D + NORM_EPS)
    mixed_f = mixed[...].astype(jnp.float32)
    normed = (mixed_f * scale * gain[...]).astype(jnp.bfloat16)
    filled = jnp.dot(slot_rows[...], normed, preferred_element_type=jnp.float32)
    outgoing[...] = filled.astype(outgoing.dtype).reshape(outgoing.shape)

    def dispatch_copy(p):
        return pltpu.make_async_remote_copy(
            src_ref=outgoing.at[p],
            dst_ref=incoming.at[me_c],
            send_sem=d_send.at[p],
            recv_sem=d_recv.at[me_c],
            device_id={"ctx": p},
            device_id_type=MESH,
        )

    for t in range(n_exp):
        z_r = lax.rem(plane + 2 * n_exp - me_e - t, n_exp)
        for y in range(per_chunk):
            p = z_r * per_chunk + y

            @pl.when(p != me_c)
            def _():
                dispatch_copy(p).start()

            @pl.when(p == me_c)
            def _():
                pltpu.make_async_copy(outgoing.at[p], incoming.at[p], d_recv.at[p]).start()

    stage, recv = gate_stage, gate_recv

    def reduce_copy(j):
        return pltpu.make_async_remote_copy(
            src_ref=stage.at[j],
            dst_ref=recv.at[me_e],
            send_sem=r_send.at[j],
            recv_sem=r_recv.at[me_e],
            device_id={"exp": j},
            device_id_type=MESH,
        )

    rows = stage.shape[3]
    for t in range(n_exp):
        j = lax.rem(plane + me_e + t, n_exp)
        for y in range(per_chunk):
            s = j * per_chunk + y
            pltpu.make_async_copy(incoming.at[s], incoming.at[s], d_recv.at[s]).wait()
        first = pl.multiple_of(j * per_chunk, per_chunk)
        for k in range(EXP_ROW):
            x = incoming[pl.ds(first, per_chunk), k].reshape(rows, incoming.shape[-1])
            for which, w in enumerate((gate_w, up_w)):
                stage[j, which, k] = jnp.dot(x, w[k], preferred_element_type=jnp.float32).astype(
                    stage.dtype
                )

        @pl.when(j != me_e)
        def _():
            reduce_copy(j).start()

        @pl.when(j == me_e)
        def _():
            pltpu.make_async_copy(stage.at[j], recv.at[j], r_recv.at[j]).start()

    for s in range(n_exp):
        pltpu.make_async_copy(recv.at[s], recv.at[s], r_recv.at[s]).wait()
    gate_sum = recv[0, 0].astype(jnp.float32)
    up_sum = recv[0, 1].astype(jnp.float32)
    for s in range(1, n_exp):
        gate_sum = gate_sum + recv[s, 0].astype(jnp.float32)
        up_sum = up_sum + recv[s, 1].astype(jnp.float32)
    hidden_mine[...] = (gate_sum / (1.0 + jnp.exp(-gate_sum)) * up_sum).astype(hidden_mine.dtype)

    def gather_copy(r):
        return pltpu.make_async_remote_copy(
            src_ref=hidden_mine,
            dst_ref=hidden_all.at[me_e],
            send_sem=a_send.at[r],
            recv_sem=a_recv.at[me_e],
            device_id={"exp": r},
            device_id_type=MESH,
        )

    for t in range(n_exp):
        r = lax.rem(me_e + 2 * n_exp - plane - t, n_exp)

        @pl.when(r != me_e)
        def _():
            gather_copy(r).start()

        @pl.when(r == me_e)
        def _():
            pltpu.make_async_copy(hidden_mine, hidden_all.at[r], a_recv.at[r]).start()

    def return_copy(s):
        return pltpu.make_async_remote_copy(
            src_ref=ret_stage.at[s],
            dst_ref=returned.at[me_c],
            send_sem=b_send.at[s],
            recv_sem=b_recv.at[me_c],
            device_id={"ctx": s},
            device_id_type=MESH,
        )

    for t in range(n_exp):
        j = lax.rem(me_e + plane + t, n_exp)
        pltpu.make_async_copy(hidden_all.at[j], hidden_all.at[j], a_recv.at[j]).wait()
        first = pl.multiple_of(j * per_chunk, per_chunk)
        for k in range(EXP_ROW):
            res = jnp.dot(hidden_all[j, k], down_w[k], preferred_element_type=jnp.float32)
            ret_stage[pl.ds(first, per_chunk), k] = res.astype(ret_stage.dtype).reshape(
                per_chunk, rows // per_chunk, res.shape[-1]
            )
        for y in range(per_chunk):
            s = j * per_chunk + y

            @pl.when(s != me_c)
            def _():
                return_copy(s).start()

            @pl.when(s == me_c)
            def _():
                pltpu.make_async_copy(ret_stage.at[s], returned.at[s], b_recv.at[s]).start()

    for s in range(n_ctx):
        pltpu.make_async_copy(returned.at[s], returned.at[s], b_recv.at[s]).wait()
    back = returned[...].reshape(w_hi.shape[0], returned.shape[-1])
    contract = (((0,), (0,)), ((), ()))
    routed = lax.dot_general(w_hi[...], back, contract, preferred_element_type=jnp.float32) + lax.dot_general(
        w_lo[...], back, contract, preferred_element_type=jnp.float32
    )
    out[...] = (mixed_f + routed).astype(out.dtype)

    for r in range(n_exp):

        @pl.when(r != me_e)
        def _():
            gather_copy(r).wait_send()
            square_copy(r).wait_send()
            reduce_copy(r).wait_send()

    for p in range(n_ctx):

        @pl.when(p != me_c)
        def _():
            dispatch_copy(p).wait_send()
            return_copy(p).wait_send()

    for h in range(halves):
        for r in range(1, group):
            second_copy(h, r).wait_send()
    for h in range(halves):
        z_r = lax.rem(plane + 2 * planes - q - h * (planes // halves), planes)
        for y in range(per_chunk):
            p = z_r * per_chunk + y

            @pl.when(p != me_c)
            def _():
                first_copy(p).wait_send()


def moe(queries, key_rows, value_rows, residual, block_order, gain, expert_ids, route_weight, out_shape, gate_weight,
        up_weight, down_weight, n_ctx, n_exp, collective_id):
    slot_total = out_shape[0] * out_shape[1] * out_shape[2]
    kv_shape = (residual.shape[0], KEY_VALUE_HEADS * HEAD_SIZE)
    mixed = residual
    square_shape = (residual.shape[0], 128)
    hid = gate_weight.shape[-1]
    size = math.prod(out_shape)
    slots = out_shape[0] * out_shape[2] // n_exp
    recv_shape = (n_exp, EXP_ROW, slots, hid)
    flops = 2 * 3 * size * hid + 2 * size * mixed.shape[0] * 3
    nbytes = 4 * size * 2 + 6 * gate_weight.size * 2 + 8 * n_exp * EXP_ROW * slots * hid * 2
    vmem = pltpu.VMEM
    return pl.pallas_call(
        functools.partial(moe_kernel, n_ctx, n_exp),
        out_shape=jax.ShapeDtypeStruct(mixed.shape, jnp.bfloat16),
        in_specs=[pl.BlockSpec(memory_space=pltpu.VMEM)] * 4
        + [pl.BlockSpec(memory_space=pltpu.SMEM)]
        + [pl.BlockSpec(memory_space=pltpu.VMEM)] * 6,
        out_specs=pl.BlockSpec(memory_space=pltpu.VMEM),
        scratch_shapes=[
            vmem((slot_total, residual.shape[0]), jnp.bfloat16),
            vmem((slot_total, residual.shape[0]), jnp.bfloat16),
            vmem((slot_total, residual.shape[0]), jnp.bfloat16),
            vmem(kv_shape, jnp.bfloat16),
            vmem((n_ctx,) + kv_shape, jnp.bfloat16),
            vmem(residual.shape, jnp.bfloat16),
            vmem(square_shape, jnp.float32),
            vmem((n_exp,) + square_shape, jnp.float32),
            vmem(out_shape, jnp.bfloat16),
            vmem(out_shape, jnp.bfloat16),
            vmem((n_exp, 2) + recv_shape[1:], jnp.bfloat16),
            vmem((8, 128), jnp.bfloat16),
            vmem((n_exp, 2) + recv_shape[1:], jnp.bfloat16),
            vmem((8, 128), jnp.bfloat16),
            vmem(recv_shape[1:], jnp.bfloat16),
            vmem(recv_shape, jnp.bfloat16),
            vmem(out_shape, jnp.bfloat16),
            vmem(out_shape, jnp.bfloat16),
            pltpu.SemaphoreType.DMA((n_ctx,)),
            pltpu.SemaphoreType.DMA((n_ctx,)),
            pltpu.SemaphoreType.DMA((n_exp, 2)),
            pltpu.SemaphoreType.DMA((n_exp, 2)),
            pltpu.SemaphoreType.DMA((n_exp,)),
            pltpu.SemaphoreType.DMA((n_exp,)),
            pltpu.SemaphoreType.DMA((n_ctx,)),
            pltpu.SemaphoreType.DMA((n_ctx,)),
            pltpu.SemaphoreType.DMA((n_exp,)),
            pltpu.SemaphoreType.DMA((n_exp,)),
            pltpu.SemaphoreType.DMA((n_exp,)),
            pltpu.SemaphoreType.DMA((n_exp,)),
            pltpu.SemaphoreType.DMA((n_ctx,)),
            pltpu.SemaphoreType.DMA((n_ctx,)),
        ],
        compiler_params=pltpu.CompilerParams(collective_id=collective_id, has_side_effects=True),
        cost_estimate=pl.CostEstimate(flops=flops, bytes_accessed=nbytes, transcendentals=0),
    )(queries, key_rows, value_rows, residual, block_order, gain, expert_ids, route_weight, gate_weight, up_weight,
      down_weight)

def kv_gather_kernel(n_ctx, n_exp, group, *refs):
    block, kv_all, s1_send, s1_recv, s2_send, s2_recv = refs
    per_plane = n_ctx // n_exp
    planes = n_ctx // per_plane
    me_c = lax.axis_index("ctx")
    me_e = lax.axis_index("exp")
    q = lax.rem(me_e, group)
    head_base = me_e - q
    plane = me_c // per_plane
    barrier = pltpu.get_barrier_semaphore()
    for k in range(1, n_ctx):
        pl.semaphore_signal(
            barrier, inc=1, device_id={"ctx": lax.rem(me_c + k, n_ctx)}, device_id_type=MESH
        )
    for k in range(1, group):
        pl.semaphore_signal(
            barrier, inc=1, device_id={"exp": head_base + lax.rem(q + k, group)}, device_id_type=MESH
        )
    pl.semaphore_wait(barrier, n_ctx + group - 2)

    def first_copy(p):
        return pltpu.make_async_remote_copy(
            src_ref=block,
            dst_ref=kv_all.at[me_c],
            send_sem=s1_send.at[p],
            recv_sem=s1_recv.at[me_c],
            device_id={"ctx": p},
            device_id_type=MESH,
        )

    halves = 2
    for h in range(halves):
        z_r = lax.rem(plane + 2 * planes - q - h * (planes // halves), planes)
        for y in range(per_plane):
            p = z_r * per_plane + y

            @pl.when(p != me_c)
            def _():
                first_copy(p).start()

            @pl.when(p == me_c)
            def _():
                pltpu.make_async_copy(block, kv_all.at[p], s1_recv.at[p]).start()

    def second_copy(h, r):
        first = pl.multiple_of(lax.rem(plane + q + h * (planes // halves), planes) * per_plane, per_plane)
        return pltpu.make_async_remote_copy(
            src_ref=kv_all.at[pl.ds(first, per_plane)],
            dst_ref=kv_all.at[pl.ds(first, per_plane)],
            send_sem=s2_send.at[r, h],
            recv_sem=s2_recv.at[r, h],
            device_id={"exp": head_base + lax.rem(q + r, group)},
            device_id_type=MESH,
        )

    for h in range(halves):
        z_s = lax.rem(plane + q + h * (planes // halves), planes)
        for y in range(per_plane):
            s = z_s * per_plane + y
            pltpu.make_async_copy(kv_all.at[s], kv_all.at[s], s1_recv.at[s]).wait()
        for r in range(1, group):
            second_copy(h, r).start()
    for h in range(halves):
        for r in range(1, group):
            second_copy(h, r).wait_recv()
    for h in range(halves):
        for r in range(1, group):
            second_copy(h, r).wait_send()
    for h in range(halves):
        z_r = lax.rem(plane + 2 * planes - q - h * (planes // halves), planes)
        for y in range(per_plane):
            p = z_r * per_plane + y

            @pl.when(p != me_c)
            def _():
                first_copy(p).wait_send()


def kv_gather(block, n_ctx, n_exp, group, collective_id):
    nbytes = block.size * block.dtype.itemsize * n_ctx
    return pl.pallas_call(
        functools.partial(kv_gather_kernel, n_ctx, n_exp, group),
        out_shape=jax.ShapeDtypeStruct((n_ctx,) + block.shape, block.dtype),
        in_specs=[pl.BlockSpec(memory_space=pltpu.VMEM)],
        out_specs=pl.BlockSpec(memory_space=pltpu.VMEM),
        scratch_shapes=[
            pltpu.SemaphoreType.DMA((n_ctx,)),
            pltpu.SemaphoreType.DMA((n_ctx,)),
            pltpu.SemaphoreType.DMA((group, 2)),
            pltpu.SemaphoreType.DMA((group, 2)),
        ],
        compiler_params=pltpu.CompilerParams(collective_id=collective_id, has_side_effects=True),
        cost_estimate=pl.CostEstimate(flops=0, bytes_accessed=2 * nbytes, transcendentals=0),
    )(block)


def local(
    queries,
    key_rows,
    value_head_rows,
    block_order,
    residual,
    norm_gain,
    expert_ids,
    route_weight,
    gate_weight,
    up_weight,
    down_weight,
):
    shard_rows = queries.shape[0]
    ctx_count = lax.axis_size("ctx")
    exp_count = lax.axis_size("exp")
    local_head = queries.shape[1] // HEAD_SIZE
    expert_index = lax.axis_index("exp")
    ctx_index = lax.axis_index("ctx")
    expert_count = ctx_count * EXP_ROW
    capacity = 2 * shard_rows * TOPK // expert_count
    return moe(
        queries,
        key_rows,
        value_head_rows,
        residual,
        block_order,
        norm_gain.reshape(1, -1),
        expert_ids.T,
        route_weight.T,
        (ctx_count, EXP_ROW, capacity, residual.shape[1]),
        gate_weight,
        up_weight,
        down_weight,
        ctx_count,
        exp_count,
        2,
    )

def solution(mesh):
    placed = (
        P(("rep", "ctx"), "exp"),
        P(("rep", "ctx"), None),
        P(("rep", "ctx"), None),
        P("rep"),
        P(("rep", "ctx"), "exp"),
        P("exp"),
        P(("rep", "ctx"), None),
        P(("rep", "ctx"), None),
        P("ctx", "exp", None),
        P("ctx", "exp", None),
        P("ctx", None, "exp"),
    )
    return jax.shard_map(
        local, mesh=mesh, in_specs=placed, out_specs=P(("rep", "ctx"), "exp"), check_vma=False
    )
```

```python
import functools
import math

import jax
import jax.numpy as jnp
from jax import lax
from jax.experimental import pallas as pl
from jax.experimental.pallas import tpu as pltpu
from jax.sharding import PartitionSpec as P

D = 4096
QUERY_HEADS = 32
KEY_VALUE_HEADS = 2
HEAD_SIZE = 128
TOPK = 8
EXP_ROW = 2

MASKED_SCORE = -1e30
NORM_EPS = 1e-06
MESH = pl.DeviceIdType.MESH


def exchange_kernel(axis, n, gather, n_in, *refs):
    ins, outs = refs[:n_in], refs[n_in : 2 * n_in]
    send_sem, recv_sem = refs[2 * n_in], refs[2 * n_in + 1]
    me = lax.axis_index(axis)
    barrier = pltpu.get_barrier_semaphore()
    for k in range(1, n):
        pl.semaphore_signal(
            barrier, inc=1, device_id={axis: lax.rem(me + k, n)}, device_id_type=MESH
        )
    pl.semaphore_wait(barrier, n - 1)
    copies = []
    for k in range(1, n):
        peer = lax.rem(me + k, n)
        for i in range(n_in):
            copy = pltpu.make_async_remote_copy(
                src_ref=ins[i] if gather else ins[i].at[peer],
                dst_ref=outs[i].at[me],
                send_sem=send_sem.at[i, k],
                recv_sem=recv_sem.at[i, k],
                device_id={axis: peer},
                device_id_type=MESH,
            )
            copy.start()
            copies.append(copy)
    for i in range(n_in):
        outs[i][me] = ins[i][...] if gather else ins[i][me]
    for copy in copies:
        copy.wait()


def exchange(xs, axis, n, gather, collective_id):
    n_in = len(xs)
    out_shape = [
        jax.ShapeDtypeStruct((n,) + (x.shape if gather else x.shape[1:]), x.dtype) for x in xs
    ]
    nbytes = sum(x.size * x.dtype.itemsize for x in xs) * (n if gather else 1)
    return pl.pallas_call(
        functools.partial(exchange_kernel, axis, n, gather, n_in),
        out_shape=out_shape,
        in_specs=[pl.BlockSpec(memory_space=pltpu.VMEM)] * n_in,
        out_specs=[pl.BlockSpec(memory_space=pltpu.VMEM)] * n_in,
        scratch_shapes=[
            pltpu.SemaphoreType.DMA((n_in, n)),
            pltpu.SemaphoreType.DMA((n_in, n)),
        ],
        compiler_params=pltpu.CompilerParams(collective_id=collective_id, has_side_effects=True),
        cost_estimate=pl.CostEstimate(flops=0, bytes_accessed=2 * nbytes, transcendentals=0),
    )(*xs)


def moe_kernel(n_ctx, n_exp, *refs):
    (queries, key_rows, value_rows, residual, block_order, gain, expert_ids, route_weight, gate_w, up_w, down_w, out,
     slot_rows, w_hi, w_lo, kv_block, kv_all, mixed, square_block, square_all, outgoing, incoming, gate_stage, up_stage, gate_recv, up_recv,
     hidden_mine, hidden_all, ret_stage, returned, s1_send, s1_recv, s2_send, s2_recv, q_send, q_recv, d_send,
     d_recv, r_send, r_recv, a_send, a_recv, b_send, b_recv) = refs
    per_chunk = n_ctx // n_exp
    me_c = lax.axis_index("ctx")
    me_e = lax.axis_index("exp")
    plane = me_c // per_chunk
    barrier = pltpu.get_barrier_semaphore()
    for k in range(1, n_ctx):
        pl.semaphore_signal(
            barrier, inc=1, device_id={"ctx": lax.rem(me_c + k, n_ctx)}, device_id_type=MESH
        )
    for k in range(1, n_exp):
        pl.semaphore_signal(
            barrier, inc=1, device_id={"exp": lax.rem(me_e + k, n_exp)}, device_id_type=MESH
        )
    pl.semaphore_wait(barrier, n_ctx + n_exp - 2)

    group = QUERY_HEADS // KEY_VALUE_HEADS // (queries.shape[1] // HEAD_SIZE)
    head_cols = pl.ds(pl.multiple_of((me_e // group) * HEAD_SIZE, HEAD_SIZE), HEAD_SIZE)
    kv_block[:, :HEAD_SIZE] = key_rows[:, head_cols]
    kv_block[:, HEAD_SIZE:] = value_rows[:, head_cols]
    q = lax.rem(me_e, group)
    head_base = me_e - q
    planes = n_exp
    halves = 2

    def first_copy(p):
        return pltpu.make_async_remote_copy(
            src_ref=kv_block,
            dst_ref=kv_all.at[me_c],
            send_sem=s1_send.at[p],
            recv_sem=s1_recv.at[me_c],
            device_id={"ctx": p},
            device_id_type=MESH,
        )

    for h in range(halves):
        z_r = lax.rem(plane + 2 * planes - q - h * (planes // halves), planes)
        for y in range(per_chunk):
            p = z_r * per_chunk + y

            @pl.when(p != me_c)
            def _():
                first_copy(p).start()

            @pl.when(p == me_c)
            def _():
                pltpu.make_async_copy(kv_block, kv_all.at[p], s1_recv.at[p]).start()

    def second_copy(h, r):
        first = pl.multiple_of(lax.rem(plane + q + h * (planes // halves), planes) * per_chunk, per_chunk)
        return pltpu.make_async_remote_copy(
            src_ref=kv_all.at[pl.ds(first, per_chunk)],
            dst_ref=kv_all.at[pl.ds(first, per_chunk)],
            send_sem=s2_send.at[r, h],
            recv_sem=s2_recv.at[r, h],
            device_id={"exp": head_base + lax.rem(q + r, group)},
            device_id_type=MESH,
        )

    topk, rows_here = expert_ids.shape
    slot_total = slot_rows.shape[0]
    capacity = slot_total // (n_ctx * EXP_ROW)
    ids = expert_ids[...]
    expert_sub = lax.broadcasted_iota(jnp.int32, (n_ctx * EXP_ROW, rows_here), 0)
    picks = [(ids[i : i + 1, :] == expert_sub).astype(jnp.float32) for i in range(topk)]
    per_row = picks[0]
    for i in range(1, topk):
        per_row = per_row + picks[i]
    later = (
        lax.broadcasted_iota(jnp.int32, (rows_here, rows_here), 0)
        < lax.broadcasted_iota(jnp.int32, (rows_here, rows_here), 1)
    ).astype(jnp.bfloat16)
    before = jnp.dot(per_row.astype(jnp.bfloat16), later, preferred_element_type=jnp.float32)
    slot_sub = lax.broadcasted_iota(jnp.int32, (slot_total, rows_here), 0)
    chosen = jnp.zeros((slot_total, rows_here), jnp.float32)
    weight = jnp.zeros((slot_total, rows_here), jnp.float32)
    weights_in = route_weight[...]
    for i in range(topk):
        rank = jnp.sum(picks[i] * before, axis=0, keepdims=True)
        before = before + picks[i]
        slot = ids[i : i + 1, :] * capacity + rank.astype(jnp.int32)
        hit = slot == slot_sub
        chosen = jnp.where(hit, 1.0, chosen)
        weight = jnp.where(hit, weights_in[i : i + 1, :], weight)
    slot_rows[...] = chosen.astype(slot_rows.dtype)
    high = weight.astype(jnp.bfloat16)
    w_hi[...] = high
    w_lo[...] = (weight - high.astype(jnp.float32)).astype(jnp.bfloat16)

    for h in range(halves):
        z_s = lax.rem(plane + q + h * (planes // halves), planes)
        for y in range(per_chunk):
            s = z_s * per_chunk + y
            pltpu.make_async_copy(kv_all.at[s], kv_all.at[s], s1_recv.at[s]).wait()
        for r in range(1, group):
            second_copy(h, r).start()
    for h in range(halves):
        for r in range(1, group):
            second_copy(h, r).wait_recv()

    total_rows = kv_all.shape[0] * kv_all.shape[1]
    keys = kv_all[:, :, :HEAD_SIZE].reshape(total_rows, HEAD_SIZE)
    values = kv_all[:, :, HEAD_SIZE:].reshape(total_rows, HEAD_SIZE)
    block_rows = kv_all.shape[1]
    query_pos = block_order[me_c] * block_rows + lax.broadcasted_iota(jnp.int32, (queries.shape[0], 1), 0)
    key_lane = lax.broadcasted_iota(jnp.int32, (1, total_rows), 1)
    key_pos = key_lane % block_rows
    for b in range(kv_all.shape[0]):
        key_pos = jnp.where(key_lane // block_rows == b, key_pos + block_order[b] * block_rows, key_pos)
    visible = key_pos <= query_pos
    inv_scale = 1.0 / math.sqrt(HEAD_SIZE)
    square_part = jnp.zeros((queries.shape[0], 1), jnp.float32)
    for h in range(queries.shape[1] // HEAD_SIZE):
        cols = slice(h * HEAD_SIZE, (h + 1) * HEAD_SIZE)
        scores = (
            lax.dot_general(
                queries[:, cols], keys, (((1,), (1,)), ((), ())), preferred_element_type=jnp.float32
            )
            * inv_scale
        )
        scores = jnp.where(visible, scores, MASKED_SCORE)
        newest = jnp.max(scores, axis=1, keepdims=True)
        weights = jnp.where(visible, jnp.exp(scores - newest), 0.0)
        weight_sum = jnp.sum(weights, axis=1, keepdims=True)
        weighted = jnp.dot(weights.astype(jnp.bfloat16), values, preferred_element_type=jnp.float32)
        attention = (weighted / weight_sum).astype(jnp.bfloat16)
        mixed_h = (residual[:, cols].astype(jnp.float32) + attention.astype(jnp.float32)).astype(
            jnp.bfloat16
        )
        mixed[:, cols] = mixed_h
        mixed_hf = mixed_h.astype(jnp.float32)
        square_part = square_part + jnp.sum(mixed_hf * mixed_hf, axis=1, keepdims=True)
    rows_q = queries.shape[0]
    padded = jnp.concatenate(
        [jnp.broadcast_to(square_part, (rows_q, 128)), jnp.zeros((128 - rows_q, 128), jnp.float32)], axis=0
    )
    square_block[...] = jnp.transpose(padded)[: square_block.shape[0], :]

    def square_copy(r):
        return pltpu.make_async_remote_copy(
            src_ref=square_block,
            dst_ref=square_all.at[me_e],
            send_sem=q_send.at[r],
            recv_sem=q_recv.at[me_e],
            device_id={"exp": r},
            device_id_type=MESH,
        )

    for k in range(1, n_exp):
        square_copy(lax.rem(me_e + k, n_exp)).start()
    pltpu.make_async_copy(square_block, square_all.at[me_e], q_recv.at[me_e]).start()
    for s in range(n_exp):
        pltpu.make_async_copy(square_all.at[s], square_all.at[s], q_recv.at[s]).wait()
    square_sum = square_all[0]
    for s in range(1, n_exp):
        square_sum = square_sum + square_all[s]
    back_rows = jnp.concatenate(
        [square_sum, jnp.zeros((128 - square_sum.shape[0], 128), jnp.float32)], axis=0
    )
    scale = lax.rsqrt(jnp.transpose(back_rows)[: queries.shape[0], :1] / D + NORM_EPS)
    mixed_f = mixed[...].astype(jnp.float32)
    normed = (mixed_f * scale * gain[...]).astype(jnp.bfloat16)
    filled = jnp.dot(slot_rows[...], normed, preferred_element_type=jnp.float32)
    outgoing[...] = filled.astype(outgoing.dtype).reshape(outgoing.shape)

    def dispatch_copy(p):
        return pltpu.make_async_remote_copy(
            src_ref=outgoing.at[p],
            dst_ref=incoming.at[me_c],
            send_sem=d_send.at[p],
            recv_sem=d_recv.at[me_c],
            device_id={"ctx": p},
            device_id_type=MESH,
        )

    for t in range(n_exp):
        z_r = lax.rem(plane + 2 * n_exp - me_e - t, n_exp)
        for y in range(per_chunk):
            p = z_r * per_chunk + y

            @pl.when(p != me_c)
            def _():
                dispatch_copy(p).start()

            @pl.when(p == me_c)
            def _():
                pltpu.make_async_copy(outgoing.at[p], incoming.at[p], d_recv.at[p]).start()

    stage, recv = gate_stage, gate_recv

    def reduce_copy(j):
        return pltpu.make_async_remote_copy(
            src_ref=stage.at[j],
            dst_ref=recv.at[me_e],
            send_sem=r_send.at[j],
            recv_sem=r_recv.at[me_e],
            device_id={"exp": j},
            device_id_type=MESH,
        )

    rows = stage.shape[3]
    for t in range(n_exp):
        j = lax.rem(plane + me_e + t, n_exp)
        for y in range(per_chunk):
            s = j * per_chunk + y
            pltpu.make_async_copy(incoming.at[s], incoming.at[s], d_recv.at[s]).wait()
        first = pl.multiple_of(j * per_chunk, per_chunk)
        for k in range(EXP_ROW):
            x = incoming[pl.ds(first, per_chunk), k].reshape(rows, incoming.shape[-1])
            for which, w in enumerate((gate_w, up_w)):
                stage[j, which, k] = jnp.dot(x, w[k], preferred_element_type=jnp.float32).astype(
                    stage.dtype
                )

        @pl.when(j != me_e)
        def _():
            reduce_copy(j).start()

        @pl.when(j == me_e)
        def _():
            pltpu.make_async_copy(stage.at[j], recv.at[j], r_recv.at[j]).start()

    for s in range(n_exp):
        pltpu.make_async_copy(recv.at[s], recv.at[s], r_recv.at[s]).wait()
    gate_sum = recv[0, 0].astype(jnp.float32)
    up_sum = recv[0, 1].astype(jnp.float32)
    for s in range(1, n_exp):
        gate_sum = gate_sum + recv[s, 0].astype(jnp.float32)
        up_sum = up_sum + recv[s, 1].astype(jnp.float32)
    hidden_mine[...] = (gate_sum / (1.0 + jnp.exp(-gate_sum)) * up_sum).astype(hidden_mine.dtype)

    def gather_copy(r):
        return pltpu.make_async_remote_copy(
            src_ref=hidden_mine,
            dst_ref=hidden_all.at[me_e],
            send_sem=a_send.at[r],
            recv_sem=a_recv.at[me_e],
            device_id={"exp": r},
            device_id_type=MESH,
        )

    for t in range(n_exp):
        r = lax.rem(me_e + 2 * n_exp - plane - t, n_exp)

        @pl.when(r != me_e)
        def _():
            gather_copy(r).start()

        @pl.when(r == me_e)
        def _():
            pltpu.make_async_copy(hidden_mine, hidden_all.at[r], a_recv.at[r]).start()

    def return_copy(s):
        return pltpu.make_async_remote_copy(
            src_ref=ret_stage.at[s],
            dst_ref=returned.at[me_c],
            send_sem=b_send.at[s],
            recv_sem=b_recv.at[me_c],
            device_id={"ctx": s},
            device_id_type=MESH,
        )

    for t in range(n_exp):
        j = lax.rem(me_e + plane + t, n_exp)
        pltpu.make_async_copy(hidden_all.at[j], hidden_all.at[j], a_recv.at[j]).wait()
        first = pl.multiple_of(j * per_chunk, per_chunk)
        for k in range(EXP_ROW):
            res = jnp.dot(hidden_all[j, k], down_w[k], preferred_element_type=jnp.float32)
            ret_stage[pl.ds(first, per_chunk), k] = res.astype(ret_stage.dtype).reshape(
                per_chunk, rows // per_chunk, res.shape[-1]
            )
        for y in range(per_chunk):
            s = j * per_chunk + y

            @pl.when(s != me_c)
            def _():
                return_copy(s).start()

            @pl.when(s == me_c)
            def _():
                pltpu.make_async_copy(ret_stage.at[s], returned.at[s], b_recv.at[s]).start()

    for s in range(n_ctx):
        pltpu.make_async_copy(returned.at[s], returned.at[s], b_recv.at[s]).wait()
    back = returned[...].reshape(w_hi.shape[0], returned.shape[-1])
    contract = (((0,), (0,)), ((), ()))
    routed = lax.dot_general(w_hi[...], back, contract, preferred_element_type=jnp.float32) + lax.dot_general(
        w_lo[...], back, contract, preferred_element_type=jnp.float32
    )
    out[...] = (mixed_f + routed).astype(out.dtype)

    for r in range(n_exp):

        @pl.when(r != me_e)
        def _():
            gather_copy(r).wait_send()
            square_copy(r).wait_send()
            reduce_copy(r).wait_send()

    for p in range(n_ctx):

        @pl.when(p != me_c)
        def _():
            dispatch_copy(p).wait_send()
            return_copy(p).wait_send()

    for h in range(halves):
        for r in range(1, group):
            second_copy(h, r).wait_send()
    for h in range(halves):
        z_r = lax.rem(plane + 2 * planes - q - h * (planes // halves), planes)
        for y in range(per_chunk):
            p = z_r * per_chunk + y

            @pl.when(p != me_c)
            def _():
                first_copy(p).wait_send()


def moe(queries, key_rows, value_rows, residual, block_order, gain, expert_ids, route_weight, out_shape, gate_weight,
        up_weight, down_weight, n_ctx, n_exp, collective_id):
    slot_total = out_shape[0] * out_shape[1] * out_shape[2]
    kv_shape = (residual.shape[0], KEY_VALUE_HEADS * HEAD_SIZE)
    mixed = residual
    square_shape = (8, 128)
    hid = gate_weight.shape[-1]
    size = math.prod(out_shape)
    slots = out_shape[0] * out_shape[2] // n_exp
    recv_shape = (n_exp, EXP_ROW, slots, hid)
    flops = 2 * 3 * size * hid + 2 * size * mixed.shape[0] * 3
    nbytes = 4 * size * 2 + 6 * gate_weight.size * 2 + 8 * n_exp * EXP_ROW * slots * hid * 2
    vmem = pltpu.VMEM
    return pl.pallas_call(
        functools.partial(moe_kernel, n_ctx, n_exp),
        out_shape=jax.ShapeDtypeStruct(mixed.shape, jnp.bfloat16),
        in_specs=[pl.BlockSpec(memory_space=pltpu.VMEM)] * 4
        + [pl.BlockSpec(memory_space=pltpu.SMEM)]
        + [pl.BlockSpec(memory_space=pltpu.VMEM)] * 6,
        out_specs=pl.BlockSpec(memory_space=pltpu.VMEM),
        scratch_shapes=[
            vmem((slot_total, residual.shape[0]), jnp.bfloat16),
            vmem((slot_total, residual.shape[0]), jnp.bfloat16),
            vmem((slot_total, residual.shape[0]), jnp.bfloat16),
            vmem(kv_shape, jnp.bfloat16),
            vmem((n_ctx,) + kv_shape, jnp.bfloat16),
            vmem(residual.shape, jnp.bfloat16),
            vmem(square_shape, jnp.float32),
            vmem((n_exp,) + square_shape, jnp.float32),
            vmem(out_shape, jnp.bfloat16),
            vmem(out_shape, jnp.bfloat16),
            vmem((n_exp, 2) + recv_shape[1:], jnp.bfloat16),
            vmem((8, 128), jnp.bfloat16),
            vmem((n_exp, 2) + recv_shape[1:], jnp.bfloat16),
            vmem((8, 128), jnp.bfloat16),
            vmem(recv_shape[1:], jnp.bfloat16),
            vmem(recv_shape, jnp.bfloat16),
            vmem(out_shape, jnp.bfloat16),
            vmem(out_shape, jnp.bfloat16),
            pltpu.SemaphoreType.DMA((n_ctx,)),
            pltpu.SemaphoreType.DMA((n_ctx,)),
            pltpu.SemaphoreType.DMA((n_exp, 2)),
            pltpu.SemaphoreType.DMA((n_exp, 2)),
            pltpu.SemaphoreType.DMA((n_exp,)),
            pltpu.SemaphoreType.DMA((n_exp,)),
            pltpu.SemaphoreType.DMA((n_ctx,)),
            pltpu.SemaphoreType.DMA((n_ctx,)),
            pltpu.SemaphoreType.DMA((n_exp,)),
            pltpu.SemaphoreType.DMA((n_exp,)),
            pltpu.SemaphoreType.DMA((n_exp,)),
            pltpu.SemaphoreType.DMA((n_exp,)),
            pltpu.SemaphoreType.DMA((n_ctx,)),
            pltpu.SemaphoreType.DMA((n_ctx,)),
        ],
        compiler_params=pltpu.CompilerParams(collective_id=collective_id, has_side_effects=True),
        cost_estimate=pl.CostEstimate(flops=flops, bytes_accessed=nbytes, transcendentals=0),
    )(queries, key_rows, value_rows, residual, block_order, gain, expert_ids, route_weight, gate_weight, up_weight,
      down_weight)

def kv_gather_kernel(n_ctx, n_exp, group, *refs):
    block, kv_all, s1_send, s1_recv, s2_send, s2_recv = refs
    per_plane = n_ctx // n_exp
    planes = n_ctx // per_plane
    me_c = lax.axis_index("ctx")
    me_e = lax.axis_index("exp")
    q = lax.rem(me_e, group)
    head_base = me_e - q
    plane = me_c // per_plane
    barrier = pltpu.get_barrier_semaphore()
    for k in range(1, n_ctx):
        pl.semaphore_signal(
            barrier, inc=1, device_id={"ctx": lax.rem(me_c + k, n_ctx)}, device_id_type=MESH
        )
    for k in range(1, group):
        pl.semaphore_signal(
            barrier, inc=1, device_id={"exp": head_base + lax.rem(q + k, group)}, device_id_type=MESH
        )
    pl.semaphore_wait(barrier, n_ctx + group - 2)

    def first_copy(p):
        return pltpu.make_async_remote_copy(
            src_ref=block,
            dst_ref=kv_all.at[me_c],
            send_sem=s1_send.at[p],
            recv_sem=s1_recv.at[me_c],
            device_id={"ctx": p},
            device_id_type=MESH,
        )

    halves = 2
    for h in range(halves):
        z_r = lax.rem(plane + 2 * planes - q - h * (planes // halves), planes)
        for y in range(per_plane):
            p = z_r * per_plane + y

            @pl.when(p != me_c)
            def _():
                first_copy(p).start()

            @pl.when(p == me_c)
            def _():
                pltpu.make_async_copy(block, kv_all.at[p], s1_recv.at[p]).start()

    def second_copy(h, r):
        first = pl.multiple_of(lax.rem(plane + q + h * (planes // halves), planes) * per_plane, per_plane)
        return pltpu.make_async_remote_copy(
            src_ref=kv_all.at[pl.ds(first, per_plane)],
            dst_ref=kv_all.at[pl.ds(first, per_plane)],
            send_sem=s2_send.at[r, h],
            recv_sem=s2_recv.at[r, h],
            device_id={"exp": head_base + lax.rem(q + r, group)},
            device_id_type=MESH,
        )

    for h in range(halves):
        z_s = lax.rem(plane + q + h * (planes // halves), planes)
        for y in range(per_plane):
            s = z_s * per_plane + y
            pltpu.make_async_copy(kv_all.at[s], kv_all.at[s], s1_recv.at[s]).wait()
        for r in range(1, group):
            second_copy(h, r).start()
    for h in range(halves):
        for r in range(1, group):
            second_copy(h, r).wait_recv()
    for h in range(halves):
        for r in range(1, group):
            second_copy(h, r).wait_send()
    for h in range(halves):
        z_r = lax.rem(plane + 2 * planes - q - h * (planes // halves), planes)
        for y in range(per_plane):
            p = z_r * per_plane + y

            @pl.when(p != me_c)
            def _():
                first_copy(p).wait_send()


def kv_gather(block, n_ctx, n_exp, group, collective_id):
    nbytes = block.size * block.dtype.itemsize * n_ctx
    return pl.pallas_call(
        functools.partial(kv_gather_kernel, n_ctx, n_exp, group),
        out_shape=jax.ShapeDtypeStruct((n_ctx,) + block.shape, block.dtype),
        in_specs=[pl.BlockSpec(memory_space=pltpu.VMEM)],
        out_specs=pl.BlockSpec(memory_space=pltpu.VMEM),
        scratch_shapes=[
            pltpu.SemaphoreType.DMA((n_ctx,)),
            pltpu.SemaphoreType.DMA((n_ctx,)),
            pltpu.SemaphoreType.DMA((group, 2)),
            pltpu.SemaphoreType.DMA((group, 2)),
        ],
        compiler_params=pltpu.CompilerParams(collective_id=collective_id, has_side_effects=True),
        cost_estimate=pl.CostEstimate(flops=0, bytes_accessed=2 * nbytes, transcendentals=0),
    )(block)


def local(
    queries,
    key_rows,
    value_head_rows,
    block_order,
    residual,
    norm_gain,
    expert_ids,
    route_weight,
    gate_weight,
    up_weight,
    down_weight,
):
    shard_rows = queries.shape[0]
    ctx_count = lax.axis_size("ctx")
    exp_count = lax.axis_size("exp")
    local_head = queries.shape[1] // HEAD_SIZE
    expert_index = lax.axis_index("exp")
    ctx_index = lax.axis_index("ctx")
    expert_count = ctx_count * EXP_ROW
    capacity = 2 * shard_rows * TOPK // expert_count
    return moe(
        queries,
        key_rows,
        value_head_rows,
        residual,
        block_order,
        norm_gain.reshape(1, -1),
        expert_ids.T,
        route_weight.T,
        (ctx_count, EXP_ROW, capacity, residual.shape[1]),
        gate_weight,
        up_weight,
        down_weight,
        ctx_count,
        exp_count,
        2,
    )

def solution(mesh):
    placed = (
        P(("rep", "ctx"), "exp"),
        P(("rep", "ctx"), None),
        P(("rep", "ctx"), None),
        P("rep"),
        P(("rep", "ctx"), "exp"),
        P("exp"),
        P(("rep", "ctx"), None),
        P(("rep", "ctx"), None),
        P("ctx", "exp", None),
        P("ctx", "exp", None),
        P("ctx", None, "exp"),
    )
    return jax.shard_map(
        local, mesh=mesh, in_specs=placed, out_specs=P(("rep", "ctx"), "exp"), check_vma=False
    )
```

```python
import functools
import math

import jax
import jax.numpy as jnp
from jax import lax
from jax.experimental import pallas as pl
from jax.experimental.pallas import tpu as pltpu
from jax.sharding import PartitionSpec as P

D = 4096
QUERY_HEADS = 32
KEY_VALUE_HEADS = 2
HEAD_SIZE = 128
TOPK = 8
EXP_ROW = 2

MASKED_SCORE = -1e30
NORM_EPS = 1e-06
MESH = pl.DeviceIdType.MESH


def exchange_kernel(axis, n, gather, n_in, *refs):
    ins, outs = refs[:n_in], refs[n_in : 2 * n_in]
    send_sem, recv_sem = refs[2 * n_in], refs[2 * n_in + 1]
    me = lax.axis_index(axis)
    barrier = pltpu.get_barrier_semaphore()
    for k in range(1, n):
        pl.semaphore_signal(
            barrier, inc=1, device_id={axis: lax.rem(me + k, n)}, device_id_type=MESH
        )
    pl.semaphore_wait(barrier, n - 1)
    copies = []
    for k in range(1, n):
        peer = lax.rem(me + k, n)
        for i in range(n_in):
            copy = pltpu.make_async_remote_copy(
                src_ref=ins[i] if gather else ins[i].at[peer],
                dst_ref=outs[i].at[me],
                send_sem=send_sem.at[i, k],
                recv_sem=recv_sem.at[i, k],
                device_id={axis: peer},
                device_id_type=MESH,
            )
            copy.start()
            copies.append(copy)
    for i in range(n_in):
        outs[i][me] = ins[i][...] if gather else ins[i][me]
    for copy in copies:
        copy.wait()


def exchange(xs, axis, n, gather, collective_id):
    n_in = len(xs)
    out_shape = [
        jax.ShapeDtypeStruct((n,) + (x.shape if gather else x.shape[1:]), x.dtype) for x in xs
    ]
    nbytes = sum(x.size * x.dtype.itemsize for x in xs) * (n if gather else 1)
    return pl.pallas_call(
        functools.partial(exchange_kernel, axis, n, gather, n_in),
        out_shape=out_shape,
        in_specs=[pl.BlockSpec(memory_space=pltpu.VMEM)] * n_in,
        out_specs=[pl.BlockSpec(memory_space=pltpu.VMEM)] * n_in,
        scratch_shapes=[
            pltpu.SemaphoreType.DMA((n_in, n)),
            pltpu.SemaphoreType.DMA((n_in, n)),
        ],
        compiler_params=pltpu.CompilerParams(collective_id=collective_id, has_side_effects=True),
        cost_estimate=pl.CostEstimate(flops=0, bytes_accessed=2 * nbytes, transcendentals=0),
    )(*xs)


def moe_kernel(n_ctx, n_exp, *refs):
    (queries, key_rows, value_rows, residual, block_order, gain, expert_ids, route_weight, gate_w, up_w, down_w, out,
     slot_rows, w_hi, w_lo, kv_block, kv_all, mixed, square_block, square_all, outgoing, incoming, gate_stage, up_stage, gate_recv, up_recv,
     hidden_mine, hidden_all, ret_stage, returned, s1_send, s1_recv, s2_send, s2_recv, q_send, q_recv, d_send,
     d_recv, r_send, r_recv, a_send, a_recv, b_send, b_recv) = refs
    per_chunk = n_ctx // n_exp
    me_c = lax.axis_index("ctx")
    me_e = lax.axis_index("exp")
    plane = me_c // per_chunk
    barrier = pltpu.get_barrier_semaphore()
    for k in range(1, n_ctx):
        pl.semaphore_signal(
            barrier, inc=1, device_id={"ctx": lax.rem(me_c + k, n_ctx)}, device_id_type=MESH
        )
    for k in range(1, n_exp):
        pl.semaphore_signal(
            barrier, inc=1, device_id={"exp": lax.rem(me_e + k, n_exp)}, device_id_type=MESH
        )
    pl.semaphore_wait(barrier, n_ctx + n_exp - 2)

    group = QUERY_HEADS // KEY_VALUE_HEADS // (queries.shape[1] // HEAD_SIZE)
    head_cols = pl.ds(pl.multiple_of((me_e // group) * HEAD_SIZE, HEAD_SIZE), HEAD_SIZE)
    kv_block[:, :HEAD_SIZE] = key_rows[:, head_cols]
    kv_block[:, HEAD_SIZE:] = value_rows[:, head_cols]
    q = lax.rem(me_e, group)
    head_base = me_e - q
    planes = n_exp
    halves = 2

    def first_copy(p):
        return pltpu.make_async_remote_copy(
            src_ref=kv_block,
            dst_ref=kv_all.at[me_c],
            send_sem=s1_send.at[p],
            recv_sem=s1_recv.at[me_c],
            device_id={"ctx": p},
            device_id_type=MESH,
        )

    for h in range(halves):
        z_r = lax.rem(plane + 2 * planes - q - h * (planes // halves), planes)
        for y in range(per_chunk):
            p = z_r * per_chunk + y

            @pl.when(p != me_c)
            def _():
                first_copy(p).start()

            @pl.when(p == me_c)
            def _():
                pltpu.make_async_copy(kv_block, kv_all.at[p], s1_recv.at[p]).start()

    def second_copy(h, r):
        first = pl.multiple_of(lax.rem(plane + q + h * (planes // halves), planes) * per_chunk, per_chunk)
        return pltpu.make_async_remote_copy(
            src_ref=kv_all.at[pl.ds(first, per_chunk)],
            dst_ref=kv_all.at[pl.ds(first, per_chunk)],
            send_sem=s2_send.at[r, h],
            recv_sem=s2_recv.at[r, h],
            device_id={"exp": head_base + lax.rem(q + r, group)},
            device_id_type=MESH,
        )

    topk, rows_here = expert_ids.shape
    slot_total = slot_rows.shape[0]
    capacity = slot_total // (n_ctx * EXP_ROW)
    ids = expert_ids[...]
    expert_sub = lax.broadcasted_iota(jnp.int32, (n_ctx * EXP_ROW, rows_here), 0)
    picks = [(ids[i : i + 1, :] == expert_sub).astype(jnp.float32) for i in range(topk)]
    per_row = picks[0]
    for i in range(1, topk):
        per_row = per_row + picks[i]
    later = (
        lax.broadcasted_iota(jnp.int32, (rows_here, rows_here), 0)
        < lax.broadcasted_iota(jnp.int32, (rows_here, rows_here), 1)
    ).astype(jnp.bfloat16)
    before = jnp.dot(per_row.astype(jnp.bfloat16), later, preferred_element_type=jnp.float32)
    slot_sub = lax.broadcasted_iota(jnp.int32, (slot_total, rows_here), 0)
    chosen = jnp.zeros((slot_total, rows_here), jnp.float32)
    weight = jnp.zeros((slot_total, rows_here), jnp.float32)
    weights_in = route_weight[...]
    for i in range(topk):
        rank = jnp.sum(picks[i] * before, axis=0, keepdims=True)
        before = before + picks[i]
        slot = ids[i : i + 1, :] * capacity + rank.astype(jnp.int32)
        hit = slot == slot_sub
        chosen = jnp.where(hit, 1.0, chosen)
        weight = jnp.where(hit, weights_in[i : i + 1, :], weight)
    slot_rows[...] = chosen.astype(slot_rows.dtype)
    high = weight.astype(jnp.bfloat16)
    w_hi[...] = high
    w_lo[...] = (weight - high.astype(jnp.float32)).astype(jnp.bfloat16)

    total_rows = kv_all.shape[0] * kv_all.shape[1]
    block_rows = kv_all.shape[1]
    query_pos = block_order[me_c] * block_rows + lax.broadcasted_iota(jnp.int32, (queries.shape[0], 1), 0)
    key_lane = lax.broadcasted_iota(jnp.int32, (1, total_rows), 1)
    key_pos = key_lane % block_rows
    for b in range(kv_all.shape[0]):
        key_pos = jnp.where(key_lane // block_rows == b, key_pos + block_order[b] * block_rows, key_pos)
    visible = key_pos <= query_pos

    for h in range(halves):
        z_s = lax.rem(plane + q + h * (planes // halves), planes)
        for y in range(per_chunk):
            s = z_s * per_chunk + y
            pltpu.make_async_copy(kv_all.at[s], kv_all.at[s], s1_recv.at[s]).wait()
        for r in range(1, group):
            second_copy(h, r).start()
    for h in range(halves):
        for r in range(1, group):
            second_copy(h, r).wait_recv()

    total_rows = kv_all.shape[0] * kv_all.shape[1]
    keys = kv_all[:, :, :HEAD_SIZE].reshape(total_rows, HEAD_SIZE)
    values = kv_all[:, :, HEAD_SIZE:].reshape(total_rows, HEAD_SIZE)
    inv_scale = 1.0 / math.sqrt(HEAD_SIZE)
    square_part = jnp.zeros((queries.shape[0], 1), jnp.float32)
    for h in range(queries.shape[1] // HEAD_SIZE):
        cols = slice(h * HEAD_SIZE, (h + 1) * HEAD_SIZE)
        scores = (
            lax.dot_general(
                queries[:, cols], keys, (((1,), (1,)), ((), ())), preferred_element_type=jnp.float32
            )
            * inv_scale
        )
        scores = jnp.where(visible, scores, MASKED_SCORE)
        newest = jnp.max(scores, axis=1, keepdims=True)
        weights = jnp.where(visible, jnp.exp(scores - newest), 0.0)
        weight_sum = jnp.sum(weights, axis=1, keepdims=True)
        weighted = jnp.dot(weights.astype(jnp.bfloat16), values, preferred_element_type=jnp.float32)
        attention = (weighted / weight_sum).astype(jnp.bfloat16)
        mixed_h = (residual[:, cols].astype(jnp.float32) + attention.astype(jnp.float32)).astype(
            jnp.bfloat16
        )
        mixed[:, cols] = mixed_h
        mixed_hf = mixed_h.astype(jnp.float32)
        square_part = square_part + jnp.sum(mixed_hf * mixed_hf, axis=1, keepdims=True)
    rows_q = queries.shape[0]
    padded = jnp.concatenate(
        [jnp.broadcast_to(square_part, (rows_q, 128)), jnp.zeros((128 - rows_q, 128), jnp.float32)], axis=0
    )
    square_block[...] = jnp.transpose(padded)[: square_block.shape[0], :]

    def square_copy(r):
        return pltpu.make_async_remote_copy(
            src_ref=square_block,
            dst_ref=square_all.at[me_e],
            send_sem=q_send.at[r],
            recv_sem=q_recv.at[me_e],
            device_id={"exp": r},
            device_id_type=MESH,
        )

    for k in range(1, n_exp):
        square_copy(lax.rem(me_e + k, n_exp)).start()
    pltpu.make_async_copy(square_block, square_all.at[me_e], q_recv.at[me_e]).start()
    for s in range(n_exp):
        pltpu.make_async_copy(square_all.at[s], square_all.at[s], q_recv.at[s]).wait()
    square_sum = square_all[0]
    for s in range(1, n_exp):
        square_sum = square_sum + square_all[s]
    back_rows = jnp.concatenate(
        [square_sum, jnp.zeros((128 - square_sum.shape[0], 128), jnp.float32)], axis=0
    )
    scale = lax.rsqrt(jnp.transpose(back_rows)[: queries.shape[0], :1] / D + NORM_EPS)
    mixed_f = mixed[...].astype(jnp.float32)
    normed = (mixed_f * scale * gain[...]).astype(jnp.bfloat16)
    filled = jnp.dot(slot_rows[...], normed, preferred_element_type=jnp.float32)
    outgoing[...] = filled.astype(outgoing.dtype).reshape(outgoing.shape)

    def dispatch_copy(p):
        return pltpu.make_async_remote_copy(
            src_ref=outgoing.at[p],
            dst_ref=incoming.at[me_c],
            send_sem=d_send.at[p],
            recv_sem=d_recv.at[me_c],
            device_id={"ctx": p},
            device_id_type=MESH,
        )

    for t in range(n_exp):
        z_r = lax.rem(plane + 2 * n_exp - me_e - t, n_exp)
        for y in range(per_chunk):
            p = z_r * per_chunk + y

            @pl.when(p != me_c)
            def _():
                dispatch_copy(p).start()

            @pl.when(p == me_c)
            def _():
                pltpu.make_async_copy(outgoing.at[p], incoming.at[p], d_recv.at[p]).start()

    stage, recv = gate_stage, gate_recv

    def reduce_copy(j):
        return pltpu.make_async_remote_copy(
            src_ref=stage.at[j],
            dst_ref=recv.at[me_e],
            send_sem=r_send.at[j],
            recv_sem=r_recv.at[me_e],
            device_id={"exp": j},
            device_id_type=MESH,
        )

    rows = stage.shape[3]
    for t in range(n_exp):
        j = lax.rem(plane + me_e + t, n_exp)
        for y in range(per_chunk):
            s = j * per_chunk + y
            pltpu.make_async_copy(incoming.at[s], incoming.at[s], d_recv.at[s]).wait()
        first = pl.multiple_of(j * per_chunk, per_chunk)
        for k in range(EXP_ROW):
            x = incoming[pl.ds(first, per_chunk), k].reshape(rows, incoming.shape[-1])
            for which, w in enumerate((gate_w, up_w)):
                stage[j, which, k] = jnp.dot(x, w[k], preferred_element_type=jnp.float32).astype(
                    stage.dtype
                )

        @pl.when(j != me_e)
        def _():
            reduce_copy(j).start()

        @pl.when(j == me_e)
        def _():
            pltpu.make_async_copy(stage.at[j], recv.at[j], r_recv.at[j]).start()

    for s in range(n_exp):
        pltpu.make_async_copy(recv.at[s], recv.at[s], r_recv.at[s]).wait()
    gate_sum = recv[0, 0].astype(jnp.float32)
    up_sum = recv[0, 1].astype(jnp.float32)
    for s in range(1, n_exp):
        gate_sum = gate_sum + recv[s, 0].astype(jnp.float32)
        up_sum = up_sum + recv[s, 1].astype(jnp.float32)
    hidden_mine[...] = (gate_sum / (1.0 + jnp.exp(-gate_sum)) * up_sum).astype(hidden_mine.dtype)

    def gather_copy(r):
        return pltpu.make_async_remote_copy(
            src_ref=hidden_mine,
            dst_ref=hidden_all.at[me_e],
            send_sem=a_send.at[r],
            recv_sem=a_recv.at[me_e],
            device_id={"exp": r},
            device_id_type=MESH,
        )

    for t in range(n_exp):
        r = lax.rem(me_e + 2 * n_exp - plane - t, n_exp)

        @pl.when(r != me_e)
        def _():
            gather_copy(r).start()

        @pl.when(r == me_e)
        def _():
            pltpu.make_async_copy(hidden_mine, hidden_all.at[r], a_recv.at[r]).start()

    def return_copy(s):
        return pltpu.make_async_remote_copy(
            src_ref=ret_stage.at[s],
            dst_ref=returned.at[me_c],
            send_sem=b_send.at[s],
            recv_sem=b_recv.at[me_c],
            device_id={"ctx": s},
            device_id_type=MESH,
        )

    for t in range(n_exp):
        j = lax.rem(me_e + plane + t, n_exp)
        pltpu.make_async_copy(hidden_all.at[j], hidden_all.at[j], a_recv.at[j]).wait()
        first = pl.multiple_of(j * per_chunk, per_chunk)
        for k in range(EXP_ROW):
            res = jnp.dot(hidden_all[j, k], down_w[k], preferred_element_type=jnp.float32)
            ret_stage[pl.ds(first, per_chunk), k] = res.astype(ret_stage.dtype).reshape(
                per_chunk, rows // per_chunk, res.shape[-1]
            )
        for y in range(per_chunk):
            s = j * per_chunk + y

            @pl.when(s != me_c)
            def _():
                return_copy(s).start()

            @pl.when(s == me_c)
            def _():
                pltpu.make_async_copy(ret_stage.at[s], returned.at[s], b_recv.at[s]).start()

    for s in range(n_ctx):
        pltpu.make_async_copy(returned.at[s], returned.at[s], b_recv.at[s]).wait()
    back = returned[...].reshape(w_hi.shape[0], returned.shape[-1])
    contract = (((0,), (0,)), ((), ()))
    routed = lax.dot_general(w_hi[...], back, contract, preferred_element_type=jnp.float32) + lax.dot_general(
        w_lo[...], back, contract, preferred_element_type=jnp.float32
    )
    out[...] = (mixed_f + routed).astype(out.dtype)

    for r in range(n_exp):

        @pl.when(r != me_e)
        def _():
            gather_copy(r).wait_send()
            square_copy(r).wait_send()
            reduce_copy(r).wait_send()

    for p in range(n_ctx):

        @pl.when(p != me_c)
        def _():
            dispatch_copy(p).wait_send()
            return_copy(p).wait_send()

    for h in range(halves):
        for r in range(1, group):
            second_copy(h, r).wait_send()
    for h in range(halves):
        z_r = lax.rem(plane + 2 * planes - q - h * (planes // halves), planes)
        for y in range(per_chunk):
            p = z_r * per_chunk + y

            @pl.when(p != me_c)
            def _():
                first_copy(p).wait_send()


def moe(queries, key_rows, value_rows, residual, block_order, gain, expert_ids, route_weight, out_shape, gate_weight,
        up_weight, down_weight, n_ctx, n_exp, collective_id):
    slot_total = out_shape[0] * out_shape[1] * out_shape[2]
    kv_shape = (residual.shape[0], KEY_VALUE_HEADS * HEAD_SIZE)
    mixed = residual
    square_shape = (8, 128)
    hid = gate_weight.shape[-1]
    size = math.prod(out_shape)
    slots = out_shape[0] * out_shape[2] // n_exp
    recv_shape = (n_exp, EXP_ROW, slots, hid)
    flops = 2 * 3 * size * hid + 2 * size * mixed.shape[0] * 3
    nbytes = 4 * size * 2 + 6 * gate_weight.size * 2 + 8 * n_exp * EXP_ROW * slots * hid * 2
    vmem = pltpu.VMEM
    return pl.pallas_call(
        functools.partial(moe_kernel, n_ctx, n_exp),
        out_shape=jax.ShapeDtypeStruct(mixed.shape, jnp.bfloat16),
        in_specs=[pl.BlockSpec(memory_space=pltpu.VMEM)] * 4
        + [pl.BlockSpec(memory_space=pltpu.SMEM)]
        + [pl.BlockSpec(memory_space=pltpu.VMEM)] * 6,
        out_specs=pl.BlockSpec(memory_space=pltpu.VMEM),
        scratch_shapes=[
            vmem((slot_total, residual.shape[0]), jnp.bfloat16),
            vmem((slot_total, residual.shape[0]), jnp.bfloat16),
            vmem((slot_total, residual.shape[0]), jnp.bfloat16),
            vmem(kv_shape, jnp.bfloat16),
            vmem((n_ctx,) + kv_shape, jnp.bfloat16),
            vmem(residual.shape, jnp.bfloat16),
            vmem(square_shape, jnp.float32),
            vmem((n_exp,) + square_shape, jnp.float32),
            vmem(out_shape, jnp.bfloat16),
            vmem(out_shape, jnp.bfloat16),
            vmem((n_exp, 2) + recv_shape[1:], jnp.bfloat16),
            vmem((8, 128), jnp.bfloat16),
            vmem((n_exp, 2) + recv_shape[1:], jnp.bfloat16),
            vmem((8, 128), jnp.bfloat16),
            vmem(recv_shape[1:], jnp.bfloat16),
            vmem(recv_shape, jnp.bfloat16),
            vmem(out_shape, jnp.bfloat16),
            vmem(out_shape, jnp.bfloat16),
            pltpu.SemaphoreType.DMA((n_ctx,)),
            pltpu.SemaphoreType.DMA((n_ctx,)),
            pltpu.SemaphoreType.DMA((n_exp, 2)),
            pltpu.SemaphoreType.DMA((n_exp, 2)),
            pltpu.SemaphoreType.DMA((n_exp,)),
            pltpu.SemaphoreType.DMA((n_exp,)),
            pltpu.SemaphoreType.DMA((n_ctx,)),
            pltpu.SemaphoreType.DMA((n_ctx,)),
            pltpu.SemaphoreType.DMA((n_exp,)),
            pltpu.SemaphoreType.DMA((n_exp,)),
            pltpu.SemaphoreType.DMA((n_exp,)),
            pltpu.SemaphoreType.DMA((n_exp,)),
            pltpu.SemaphoreType.DMA((n_ctx,)),
            pltpu.SemaphoreType.DMA((n_ctx,)),
        ],
        compiler_params=pltpu.CompilerParams(collective_id=collective_id, has_side_effects=True),
        cost_estimate=pl.CostEstimate(flops=flops, bytes_accessed=nbytes, transcendentals=0),
    )(queries, key_rows, value_rows, residual, block_order, gain, expert_ids, route_weight, gate_weight, up_weight,
      down_weight)

def kv_gather_kernel(n_ctx, n_exp, group, *refs):
    block, kv_all, s1_send, s1_recv, s2_send, s2_recv = refs
    per_plane = n_ctx // n_exp
    planes = n_ctx // per_plane
    me_c = lax.axis_index("ctx")
    me_e = lax.axis_index("exp")
    q = lax.rem(me_e, group)
    head_base = me_e - q
    plane = me_c // per_plane
    barrier = pltpu.get_barrier_semaphore()
    for k in range(1, n_ctx):
        pl.semaphore_signal(
            barrier, inc=1, device_id={"ctx": lax.rem(me_c + k, n_ctx)}, device_id_type=MESH
        )
    for k in range(1, group):
        pl.semaphore_signal(
            barrier, inc=1, device_id={"exp": head_base + lax.rem(q + k, group)}, device_id_type=MESH
        )
    pl.semaphore_wait(barrier, n_ctx + group - 2)

    def first_copy(p):
        return pltpu.make_async_remote_copy(
            src_ref=block,
            dst_ref=kv_all.at[me_c],
            send_sem=s1_send.at[p],
            recv_sem=s1_recv.at[me_c],
            device_id={"ctx": p},
            device_id_type=MESH,
        )

    halves = 2
    for h in range(halves):
        z_r = lax.rem(plane + 2 * planes - q - h * (planes // halves), planes)
        for y in range(per_plane):
            p = z_r * per_plane + y

            @pl.when(p != me_c)
            def _():
                first_copy(p).start()

            @pl.when(p == me_c)
            def _():
                pltpu.make_async_copy(block, kv_all.at[p], s1_recv.at[p]).start()

    def second_copy(h, r):
        first = pl.multiple_of(lax.rem(plane + q + h * (planes // halves), planes) * per_plane, per_plane)
        return pltpu.make_async_remote_copy(
            src_ref=kv_all.at[pl.ds(first, per_plane)],
            dst_ref=kv_all.at[pl.ds(first, per_plane)],
            send_sem=s2_send.at[r, h],
            recv_sem=s2_recv.at[r, h],
            device_id={"exp": head_base + lax.rem(q + r, group)},
            device_id_type=MESH,
        )

    for h in range(halves):
        z_s = lax.rem(plane + q + h * (planes // halves), planes)
        for y in range(per_plane):
            s = z_s * per_plane + y
            pltpu.make_async_copy(kv_all.at[s], kv_all.at[s], s1_recv.at[s]).wait()
        for r in range(1, group):
            second_copy(h, r).start()
    for h in range(halves):
        for r in range(1, group):
            second_copy(h, r).wait_recv()
    for h in range(halves):
        for r in range(1, group):
            second_copy(h, r).wait_send()
    for h in range(halves):
        z_r = lax.rem(plane + 2 * planes - q - h * (planes // halves), planes)
        for y in range(per_plane):
            p = z_r * per_plane + y

            @pl.when(p != me_c)
            def _():
                first_copy(p).wait_send()


def kv_gather(block, n_ctx, n_exp, group, collective_id):
    nbytes = block.size * block.dtype.itemsize * n_ctx
    return pl.pallas_call(
        functools.partial(kv_gather_kernel, n_ctx, n_exp, group),
        out_shape=jax.ShapeDtypeStruct((n_ctx,) + block.shape, block.dtype),
        in_specs=[pl.BlockSpec(memory_space=pltpu.VMEM)],
        out_specs=pl.BlockSpec(memory_space=pltpu.VMEM),
        scratch_shapes=[
            pltpu.SemaphoreType.DMA((n_ctx,)),
            pltpu.SemaphoreType.DMA((n_ctx,)),
            pltpu.SemaphoreType.DMA((group, 2)),
            pltpu.SemaphoreType.DMA((group, 2)),
        ],
        compiler_params=pltpu.CompilerParams(collective_id=collective_id, has_side_effects=True),
        cost_estimate=pl.CostEstimate(flops=0, bytes_accessed=2 * nbytes, transcendentals=0),
    )(block)


def local(
    queries,
    key_rows,
    value_head_rows,
    block_order,
    residual,
    norm_gain,
    expert_ids,
    route_weight,
    gate_weight,
    up_weight,
    down_weight,
):
    shard_rows = queries.shape[0]
    ctx_count = lax.axis_size("ctx")
    exp_count = lax.axis_size("exp")
    local_head = queries.shape[1] // HEAD_SIZE
    expert_index = lax.axis_index("exp")
    ctx_index = lax.axis_index("ctx")
    expert_count = ctx_count * EXP_ROW
    capacity = 2 * shard_rows * TOPK // expert_count
    return moe(
        queries,
        key_rows,
        value_head_rows,
        residual,
        block_order,
        norm_gain.reshape(1, -1),
        expert_ids.T,
        route_weight.T,
        (ctx_count, EXP_ROW, capacity, residual.shape[1]),
        gate_weight,
        up_weight,
        down_weight,
        ctx_count,
        exp_count,
        2,
    )

def solution(mesh):
    placed = (
        P(("rep", "ctx"), "exp"),
        P(("rep", "ctx"), None),
        P(("rep", "ctx"), None),
        P("rep"),
        P(("rep", "ctx"), "exp"),
        P("exp"),
        P(("rep", "ctx"), None),
        P(("rep", "ctx"), None),
        P("ctx", "exp", None),
        P("ctx", "exp", None),
        P("ctx", None, "exp"),
    )
    return jax.shard_map(
        local, mesh=mesh, in_specs=placed, out_specs=P(("rep", "ctx"), "exp"), check_vma=False
    )
```

```python
import functools
import math

import jax
import jax.numpy as jnp
from jax import lax
from jax.experimental import pallas as pl
from jax.experimental.pallas import tpu as pltpu
from jax.sharding import PartitionSpec as P

D = 4096
QUERY_HEADS = 32
KEY_VALUE_HEADS = 2
HEAD_SIZE = 128
TOPK = 8
EXP_ROW = 2

MASKED_SCORE = -1e30
NORM_EPS = 1e-06
MESH = pl.DeviceIdType.MESH


def exchange_kernel(axis, n, gather, n_in, *refs):
    ins, outs = refs[:n_in], refs[n_in : 2 * n_in]
    send_sem, recv_sem = refs[2 * n_in], refs[2 * n_in + 1]
    me = lax.axis_index(axis)
    barrier = pltpu.get_barrier_semaphore()
    for k in range(1, n):
        pl.semaphore_signal(
            barrier, inc=1, device_id={axis: lax.rem(me + k, n)}, device_id_type=MESH
        )
    pl.semaphore_wait(barrier, n - 1)
    copies = []
    for k in range(1, n):
        peer = lax.rem(me + k, n)
        for i in range(n_in):
            copy = pltpu.make_async_remote_copy(
                src_ref=ins[i] if gather else ins[i].at[peer],
                dst_ref=outs[i].at[me],
                send_sem=send_sem.at[i, k],
                recv_sem=recv_sem.at[i, k],
                device_id={axis: peer},
                device_id_type=MESH,
            )
            copy.start()
            copies.append(copy)
    for i in range(n_in):
        outs[i][me] = ins[i][...] if gather else ins[i][me]
    for copy in copies:
        copy.wait()


def exchange(xs, axis, n, gather, collective_id):
    n_in = len(xs)
    out_shape = [
        jax.ShapeDtypeStruct((n,) + (x.shape if gather else x.shape[1:]), x.dtype) for x in xs
    ]
    nbytes = sum(x.size * x.dtype.itemsize for x in xs) * (n if gather else 1)
    return pl.pallas_call(
        functools.partial(exchange_kernel, axis, n, gather, n_in),
        out_shape=out_shape,
        in_specs=[pl.BlockSpec(memory_space=pltpu.VMEM)] * n_in,
        out_specs=[pl.BlockSpec(memory_space=pltpu.VMEM)] * n_in,
        scratch_shapes=[
            pltpu.SemaphoreType.DMA((n_in, n)),
            pltpu.SemaphoreType.DMA((n_in, n)),
        ],
        compiler_params=pltpu.CompilerParams(collective_id=collective_id, has_side_effects=True),
        cost_estimate=pl.CostEstimate(flops=0, bytes_accessed=2 * nbytes, transcendentals=0),
    )(*xs)


def moe_kernel(n_ctx, n_exp, *refs):
    (queries, key_rows, value_rows, residual, block_order, gain, expert_ids, route_weight, gate_w, up_w, down_w, out,
     slot_rows, w_hi, w_lo, kv_block, kv_all, mixed, square_block, square_all, outgoing, incoming, gate_stage, up_stage, gate_recv, up_recv,
     hidden_mine, hidden_all, ret_stage, returned, s1_send, s1_recv, s2_send, s2_recv, q_send, q_recv, d_send,
     d_recv, r_send, r_recv, a_send, a_recv, b_send, b_recv) = refs
    per_chunk = n_ctx // n_exp
    me_c = lax.axis_index("ctx")
    me_e = lax.axis_index("exp")
    plane = me_c // per_chunk
    barrier = pltpu.get_barrier_semaphore()
    for k in range(1, n_ctx):
        pl.semaphore_signal(
            barrier, inc=1, device_id={"ctx": lax.rem(me_c + k, n_ctx)}, device_id_type=MESH
        )
    for k in range(1, n_exp):
        pl.semaphore_signal(
            barrier, inc=1, device_id={"exp": lax.rem(me_e + k, n_exp)}, device_id_type=MESH
        )
    pl.semaphore_wait(barrier, n_ctx + n_exp - 2)

    group = QUERY_HEADS // KEY_VALUE_HEADS // (queries.shape[1] // HEAD_SIZE)
    head_cols = pl.ds(pl.multiple_of((me_e // group) * HEAD_SIZE, HEAD_SIZE), HEAD_SIZE)
    kv_block[:, :HEAD_SIZE] = key_rows[:, head_cols]
    kv_block[:, HEAD_SIZE:] = value_rows[:, head_cols]
    q = lax.rem(me_e, group)
    head_base = me_e - q
    planes = n_exp
    halves = 2

    def first_copy(p):
        return pltpu.make_async_remote_copy(
            src_ref=kv_block,
            dst_ref=kv_all.at[me_c],
            send_sem=s1_send.at[p],
            recv_sem=s1_recv.at[me_c],
            device_id={"ctx": p},
            device_id_type=MESH,
        )

    for h in range(halves):
        z_r = lax.rem(plane + 2 * planes - q - h * (planes // halves), planes)
        for y in range(per_chunk):
            p = z_r * per_chunk + y

            @pl.when(p != me_c)
            def _():
                first_copy(p).start()

            @pl.when(p == me_c)
            def _():
                pltpu.make_async_copy(kv_block, kv_all.at[p], s1_recv.at[p]).start()

    def second_copy(h, r):
        first = pl.multiple_of(lax.rem(plane + q + h * (planes // halves), planes) * per_chunk, per_chunk)
        return pltpu.make_async_remote_copy(
            src_ref=kv_all.at[pl.ds(first, per_chunk)],
            dst_ref=kv_all.at[pl.ds(first, per_chunk)],
            send_sem=s2_send.at[r, h],
            recv_sem=s2_recv.at[r, h],
            device_id={"exp": head_base + lax.rem(q + r, group)},
            device_id_type=MESH,
        )

    topk, rows_here = expert_ids.shape
    slot_total = slot_rows.shape[0]
    capacity = slot_total // (n_ctx * EXP_ROW)
    ids = expert_ids[...]
    expert_sub = lax.broadcasted_iota(jnp.int32, (n_ctx * EXP_ROW, rows_here), 0)
    picks = [(ids[i : i + 1, :] == expert_sub).astype(jnp.float32) for i in range(topk)]
    per_row = picks[0]
    for i in range(1, topk):
        per_row = per_row + picks[i]
    later = (
        lax.broadcasted_iota(jnp.int32, (rows_here, rows_here), 0)
        < lax.broadcasted_iota(jnp.int32, (rows_here, rows_here), 1)
    ).astype(jnp.bfloat16)
    before = jnp.dot(per_row.astype(jnp.bfloat16), later, preferred_element_type=jnp.float32)
    slot_sub = lax.broadcasted_iota(jnp.int32, (slot_total, rows_here), 0)
    chosen = jnp.zeros((slot_total, rows_here), jnp.float32)
    weight = jnp.zeros((slot_total, rows_here), jnp.float32)
    weights_in = route_weight[...]
    for i in range(topk):
        rank = jnp.sum(picks[i] * before, axis=0, keepdims=True)
        before = before + picks[i]
        slot = ids[i : i + 1, :] * capacity + rank.astype(jnp.int32)
        hit = slot == slot_sub
        chosen = jnp.where(hit, 1.0, chosen)
        weight = jnp.where(hit, weights_in[i : i + 1, :], weight)
    slot_rows[...] = chosen.astype(slot_rows.dtype)
    weight_t = jnp.transpose(weight)
    high = weight_t.astype(jnp.bfloat16)
    w_hi[...] = high
    w_lo[...] = (weight_t - high.astype(jnp.float32)).astype(jnp.bfloat16)

    for h in range(halves):
        z_s = lax.rem(plane + q + h * (planes // halves), planes)
        for y in range(per_chunk):
            s = z_s * per_chunk + y
            pltpu.make_async_copy(kv_all.at[s], kv_all.at[s], s1_recv.at[s]).wait()
        for r in range(1, group):
            second_copy(h, r).start()
    for h in range(halves):
        for r in range(1, group):
            second_copy(h, r).wait_recv()

    total_rows = kv_all.shape[0] * kv_all.shape[1]
    keys = kv_all[:, :, :HEAD_SIZE].reshape(total_rows, HEAD_SIZE)
    values = kv_all[:, :, HEAD_SIZE:].reshape(total_rows, HEAD_SIZE)
    block_rows = kv_all.shape[1]
    query_pos = block_order[me_c] * block_rows + lax.broadcasted_iota(jnp.int32, (queries.shape[0], 1), 0)
    key_lane = lax.broadcasted_iota(jnp.int32, (1, total_rows), 1)
    key_pos = key_lane % block_rows
    for b in range(kv_all.shape[0]):
        key_pos = jnp.where(key_lane // block_rows == b, key_pos + block_order[b] * block_rows, key_pos)
    visible = key_pos <= query_pos
    inv_scale = 1.0 / math.sqrt(HEAD_SIZE)
    square_part = jnp.zeros((queries.shape[0], 1), jnp.float32)
    for h in range(queries.shape[1] // HEAD_SIZE):
        cols = slice(h * HEAD_SIZE, (h + 1) * HEAD_SIZE)
        scores = (
            lax.dot_general(
                queries[:, cols], keys, (((1,), (1,)), ((), ())), preferred_element_type=jnp.float32
            )
            * inv_scale
        )
        scores = jnp.where(visible, scores, MASKED_SCORE)
        newest = jnp.max(scores, axis=1, keepdims=True)
        weights = jnp.where(visible, jnp.exp(scores - newest), 0.0)
        weight_sum = jnp.sum(weights, axis=1, keepdims=True)
        weighted = jnp.dot(weights.astype(jnp.bfloat16), values, preferred_element_type=jnp.float32)
        attention = (weighted / weight_sum).astype(jnp.bfloat16)
        mixed_h = (residual[:, cols].astype(jnp.float32) + attention.astype(jnp.float32)).astype(
            jnp.bfloat16
        )
        mixed[:, cols] = mixed_h
        mixed_hf = mixed_h.astype(jnp.float32)
        square_part = square_part + jnp.sum(mixed_hf * mixed_hf, axis=1, keepdims=True)
    rows_q = queries.shape[0]
    padded = jnp.concatenate(
        [jnp.broadcast_to(square_part, (rows_q, 128)), jnp.zeros((128 - rows_q, 128), jnp.float32)], axis=0
    )
    square_block[...] = jnp.transpose(padded)[: square_block.shape[0], :]

    def square_copy(r):
        return pltpu.make_async_remote_copy(
            src_ref=square_block,
            dst_ref=square_all.at[me_e],
            send_sem=q_send.at[r],
            recv_sem=q_recv.at[me_e],
            device_id={"exp": r},
            device_id_type=MESH,
        )

    for k in range(1, n_exp):
        square_copy(lax.rem(me_e + k, n_exp)).start()
    pltpu.make_async_copy(square_block, square_all.at[me_e], q_recv.at[me_e]).start()
    for s in range(n_exp):
        pltpu.make_async_copy(square_all.at[s], square_all.at[s], q_recv.at[s]).wait()
    square_sum = square_all[0]
    for s in range(1, n_exp):
        square_sum = square_sum + square_all[s]
    back_rows = jnp.concatenate(
        [square_sum, jnp.zeros((128 - square_sum.shape[0], 128), jnp.float32)], axis=0
    )
    scale = lax.rsqrt(jnp.transpose(back_rows)[: queries.shape[0], :1] / D + NORM_EPS)
    mixed_f = mixed[...].astype(jnp.float32)
    normed = (mixed_f * scale * gain[...]).astype(jnp.bfloat16)
    filled = jnp.dot(slot_rows[...], normed, preferred_element_type=jnp.float32)
    outgoing[...] = filled.astype(outgoing.dtype).reshape(outgoing.shape)

    def dispatch_copy(p):
        return pltpu.make_async_remote_copy(
            src_ref=outgoing.at[p],
            dst_ref=incoming.at[me_c],
            send_sem=d_send.at[p],
            recv_sem=d_recv.at[me_c],
            device_id={"ctx": p},
            device_id_type=MESH,
        )

    for t in range(n_exp):
        z_r = lax.rem(plane + 2 * n_exp - me_e - t, n_exp)
        for y in range(per_chunk):
            p = z_r * per_chunk + y

            @pl.when(p != me_c)
            def _():
                dispatch_copy(p).start()

            @pl.when(p == me_c)
            def _():
                pltpu.make_async_copy(outgoing.at[p], incoming.at[p], d_recv.at[p]).start()

    stage, recv = gate_stage, gate_recv

    def reduce_copy(j):
        return pltpu.make_async_remote_copy(
            src_ref=stage.at[j],
            dst_ref=recv.at[me_e],
            send_sem=r_send.at[j],
            recv_sem=r_recv.at[me_e],
            device_id={"exp": j},
            device_id_type=MESH,
        )

    rows = stage.shape[3]
    for t in range(n_exp):
        j = lax.rem(plane + me_e + t, n_exp)
        for y in range(per_chunk):
            s = j * per_chunk + y
            pltpu.make_async_copy(incoming.at[s], incoming.at[s], d_recv.at[s]).wait()
        first = pl.multiple_of(j * per_chunk, per_chunk)
        for k in range(EXP_ROW):
            x = incoming[pl.ds(first, per_chunk), k].reshape(rows, incoming.shape[-1])
            for which, w in enumerate((gate_w, up_w)):
                stage[j, which, k] = jnp.dot(x, w[k], preferred_element_type=jnp.float32).astype(
                    stage.dtype
                )

        @pl.when(j != me_e)
        def _():
            reduce_copy(j).start()

        @pl.when(j == me_e)
        def _():
            pltpu.make_async_copy(stage.at[j], recv.at[j], r_recv.at[j]).start()

    for s in range(n_exp):
        pltpu.make_async_copy(recv.at[s], recv.at[s], r_recv.at[s]).wait()
    gate_sum = recv[0, 0].astype(jnp.float32)
    up_sum = recv[0, 1].astype(jnp.float32)
    for s in range(1, n_exp):
        gate_sum = gate_sum + recv[s, 0].astype(jnp.float32)
        up_sum = up_sum + recv[s, 1].astype(jnp.float32)
    hidden_mine[...] = (gate_sum / (1.0 + jnp.exp(-gate_sum)) * up_sum).astype(hidden_mine.dtype)

    def gather_copy(r):
        return pltpu.make_async_remote_copy(
            src_ref=hidden_mine,
            dst_ref=hidden_all.at[me_e],
            send_sem=a_send.at[r],
            recv_sem=a_recv.at[me_e],
            device_id={"exp": r},
            device_id_type=MESH,
        )

    for t in range(n_exp):
        r = lax.rem(me_e + 2 * n_exp - plane - t, n_exp)

        @pl.when(r != me_e)
        def _():
            gather_copy(r).start()

        @pl.when(r == me_e)
        def _():
            pltpu.make_async_copy(hidden_mine, hidden_all.at[r], a_recv.at[r]).start()

    def return_copy(s):
        return pltpu.make_async_remote_copy(
            src_ref=ret_stage.at[s],
            dst_ref=returned.at[me_c],
            send_sem=b_send.at[s],
            recv_sem=b_recv.at[me_c],
            device_id={"ctx": s},
            device_id_type=MESH,
        )

    for t in range(n_exp):
        j = lax.rem(me_e + plane + t, n_exp)
        pltpu.make_async_copy(hidden_all.at[j], hidden_all.at[j], a_recv.at[j]).wait()
        first = pl.multiple_of(j * per_chunk, per_chunk)
        for k in range(EXP_ROW):
            res = jnp.dot(hidden_all[j, k], down_w[k], preferred_element_type=jnp.float32)
            ret_stage[pl.ds(first, per_chunk), k] = res.astype(ret_stage.dtype).reshape(
                per_chunk, rows // per_chunk, res.shape[-1]
            )
        for y in range(per_chunk):
            s = j * per_chunk + y

            @pl.when(s != me_c)
            def _():
                return_copy(s).start()

            @pl.when(s == me_c)
            def _():
                pltpu.make_async_copy(ret_stage.at[s], returned.at[s], b_recv.at[s]).start()

    for s in range(n_ctx):
        pltpu.make_async_copy(returned.at[s], returned.at[s], b_recv.at[s]).wait()
    back = returned[...].reshape(w_hi.shape[1], returned.shape[-1])
    routed = jnp.dot(w_hi[...], back, preferred_element_type=jnp.float32) + jnp.dot(
        w_lo[...], back, preferred_element_type=jnp.float32
    )
    out[...] = (mixed_f + routed).astype(out.dtype)

    for r in range(n_exp):

        @pl.when(r != me_e)
        def _():
            gather_copy(r).wait_send()
            square_copy(r).wait_send()
            reduce_copy(r).wait_send()

    for p in range(n_ctx):

        @pl.when(p != me_c)
        def _():
            dispatch_copy(p).wait_send()
            return_copy(p).wait_send()

    for h in range(halves):
        for r in range(1, group):
            second_copy(h, r).wait_send()
    for h in range(halves):
        z_r = lax.rem(plane + 2 * planes - q - h * (planes // halves), planes)
        for y in range(per_chunk):
            p = z_r * per_chunk + y

            @pl.when(p != me_c)
            def _():
                first_copy(p).wait_send()


def moe(queries, key_rows, value_rows, residual, block_order, gain, expert_ids, route_weight, out_shape, gate_weight,
        up_weight, down_weight, n_ctx, n_exp, collective_id):
    slot_total = out_shape[0] * out_shape[1] * out_shape[2]
    kv_shape = (residual.shape[0], KEY_VALUE_HEADS * HEAD_SIZE)
    mixed = residual
    square_shape = (8, 128)
    hid = gate_weight.shape[-1]
    size = math.prod(out_shape)
    slots = out_shape[0] * out_shape[2] // n_exp
    recv_shape = (n_exp, EXP_ROW, slots, hid)
    flops = 2 * 3 * size * hid + 2 * size * mixed.shape[0] * 3
    nbytes = 4 * size * 2 + 6 * gate_weight.size * 2 + 8 * n_exp * EXP_ROW * slots * hid * 2
    vmem = pltpu.VMEM
    return pl.pallas_call(
        functools.partial(moe_kernel, n_ctx, n_exp),
        out_shape=jax.ShapeDtypeStruct(mixed.shape, jnp.bfloat16),
        in_specs=[pl.BlockSpec(memory_space=pltpu.VMEM)] * 4
        + [pl.BlockSpec(memory_space=pltpu.SMEM)]
        + [pl.BlockSpec(memory_space=pltpu.VMEM)] * 6,
        out_specs=pl.BlockSpec(memory_space=pltpu.VMEM),
        scratch_shapes=[
            vmem((slot_total, residual.shape[0]), jnp.bfloat16),
            vmem((residual.shape[0], slot_total), jnp.bfloat16),
            vmem((residual.shape[0], slot_total), jnp.bfloat16),
            vmem(kv_shape, jnp.bfloat16),
            vmem((n_ctx,) + kv_shape, jnp.bfloat16),
            vmem(residual.shape, jnp.bfloat16),
            vmem(square_shape, jnp.float32),
            vmem((n_exp,) + square_shape, jnp.float32),
            vmem(out_shape, jnp.bfloat16),
            vmem(out_shape, jnp.bfloat16),
            vmem((n_exp, 2) + recv_shape[1:], jnp.bfloat16),
            vmem((8, 128), jnp.bfloat16),
            vmem((n_exp, 2) + recv_shape[1:], jnp.bfloat16),
            vmem((8, 128), jnp.bfloat16),
            vmem(recv_shape[1:], jnp.bfloat16),
            vmem(recv_shape, jnp.bfloat16),
            vmem(out_shape, jnp.bfloat16),
            vmem(out_shape, jnp.bfloat16),
            pltpu.SemaphoreType.DMA((n_ctx,)),
            pltpu.SemaphoreType.DMA((n_ctx,)),
            pltpu.SemaphoreType.DMA((n_exp, 2)),
            pltpu.SemaphoreType.DMA((n_exp, 2)),
            pltpu.SemaphoreType.DMA((n_exp,)),
            pltpu.SemaphoreType.DMA((n_exp,)),
            pltpu.SemaphoreType.DMA((n_ctx,)),
            pltpu.SemaphoreType.DMA((n_ctx,)),
            pltpu.SemaphoreType.DMA((n_exp,)),
            pltpu.SemaphoreType.DMA((n_exp,)),
            pltpu.SemaphoreType.DMA((n_exp,)),
            pltpu.SemaphoreType.DMA((n_exp,)),
            pltpu.SemaphoreType.DMA((n_ctx,)),
            pltpu.SemaphoreType.DMA((n_ctx,)),
        ],
        compiler_params=pltpu.CompilerParams(collective_id=collective_id, has_side_effects=True),
        cost_estimate=pl.CostEstimate(flops=flops, bytes_accessed=nbytes, transcendentals=0),
    )(queries, key_rows, value_rows, residual, block_order, gain, expert_ids, route_weight, gate_weight, up_weight,
      down_weight)

def kv_gather_kernel(n_ctx, n_exp, group, *refs):
    block, kv_all, s1_send, s1_recv, s2_send, s2_recv = refs
    per_plane = n_ctx // n_exp
    planes = n_ctx // per_plane
    me_c = lax.axis_index("ctx")
    me_e = lax.axis_index("exp")
    q = lax.rem(me_e, group)
    head_base = me_e - q
    plane = me_c // per_plane
    barrier = pltpu.get_barrier_semaphore()
    for k in range(1, n_ctx):
        pl.semaphore_signal(
            barrier, inc=1, device_id={"ctx": lax.rem(me_c + k, n_ctx)}, device_id_type=MESH
        )
    for k in range(1, group):
        pl.semaphore_signal(
            barrier, inc=1, device_id={"exp": head_base + lax.rem(q + k, group)}, device_id_type=MESH
        )
    pl.semaphore_wait(barrier, n_ctx + group - 2)

    def first_copy(p):
        return pltpu.make_async_remote_copy(
            src_ref=block,
            dst_ref=kv_all.at[me_c],
            send_sem=s1_send.at[p],
            recv_sem=s1_recv.at[me_c],
            device_id={"ctx": p},
            device_id_type=MESH,
        )

    halves = 2
    for h in range(halves):
        z_r = lax.rem(plane + 2 * planes - q - h * (planes // halves), planes)
        for y in range(per_plane):
            p = z_r * per_plane + y

            @pl.when(p != me_c)
            def _():
                first_copy(p).start()

            @pl.when(p == me_c)
            def _():
                pltpu.make_async_copy(block, kv_all.at[p], s1_recv.at[p]).start()

    def second_copy(h, r):
        first = pl.multiple_of(lax.rem(plane + q + h * (planes // halves), planes) * per_plane, per_plane)
        return pltpu.make_async_remote_copy(
            src_ref=kv_all.at[pl.ds(first, per_plane)],
            dst_ref=kv_all.at[pl.ds(first, per_plane)],
            send_sem=s2_send.at[r, h],
            recv_sem=s2_recv.at[r, h],
            device_id={"exp": head_base + lax.rem(q + r, group)},
            device_id_type=MESH,
        )

    for h in range(halves):
        z_s = lax.rem(plane + q + h * (planes // halves), planes)
        for y in range(per_plane):
            s = z_s * per_plane + y
            pltpu.make_async_copy(kv_all.at[s], kv_all.at[s], s1_recv.at[s]).wait()
        for r in range(1, group):
            second_copy(h, r).start()
    for h in range(halves):
        for r in range(1, group):
            second_copy(h, r).wait_recv()
    for h in range(halves):
        for r in range(1, group):
            second_copy(h, r).wait_send()
    for h in range(halves):
        z_r = lax.rem(plane + 2 * planes - q - h * (planes // halves), planes)
        for y in range(per_plane):
            p = z_r * per_plane + y

            @pl.when(p != me_c)
            def _():
                first_copy(p).wait_send()


def kv_gather(block, n_ctx, n_exp, group, collective_id):
    nbytes = block.size * block.dtype.itemsize * n_ctx
    return pl.pallas_call(
        functools.partial(kv_gather_kernel, n_ctx, n_exp, group),
        out_shape=jax.ShapeDtypeStruct((n_ctx,) + block.shape, block.dtype),
        in_specs=[pl.BlockSpec(memory_space=pltpu.VMEM)],
        out_specs=pl.BlockSpec(memory_space=pltpu.VMEM),
        scratch_shapes=[
            pltpu.SemaphoreType.DMA((n_ctx,)),
            pltpu.SemaphoreType.DMA((n_ctx,)),
            pltpu.SemaphoreType.DMA((group, 2)),
            pltpu.SemaphoreType.DMA((group, 2)),
        ],
        compiler_params=pltpu.CompilerParams(collective_id=collective_id, has_side_effects=True),
        cost_estimate=pl.CostEstimate(flops=0, bytes_accessed=2 * nbytes, transcendentals=0),
    )(block)


def local(
    queries,
    key_rows,
    value_head_rows,
    block_order,
    residual,
    norm_gain,
    expert_ids,
    route_weight,
    gate_weight,
    up_weight,
    down_weight,
):
    shard_rows = queries.shape[0]
    ctx_count = lax.axis_size("ctx")
    exp_count = lax.axis_size("exp")
    local_head = queries.shape[1] // HEAD_SIZE
    expert_index = lax.axis_index("exp")
    ctx_index = lax.axis_index("ctx")
    expert_count = ctx_count * EXP_ROW
    capacity = 2 * shard_rows * TOPK // expert_count
    return moe(
        queries,
        key_rows,
        value_head_rows,
        residual,
        block_order,
        norm_gain.reshape(1, -1),
        expert_ids.T,
        route_weight.T,
        (ctx_count, EXP_ROW, capacity, residual.shape[1]),
        gate_weight,
        up_weight,
        down_weight,
        ctx_count,
        exp_count,
        2,
    )

def solution(mesh):
    placed = (
        P(("rep", "ctx"), "exp"),
        P(("rep", "ctx"), None),
        P(("rep", "ctx"), None),
        P("rep"),
        P(("rep", "ctx"), "exp"),
        P("exp"),
        P(("rep", "ctx"), None),
        P(("rep", "ctx"), None),
        P("ctx", "exp", None),
        P("ctx", "exp", None),
        P("ctx", None, "exp"),
    )
    return jax.shard_map(
        local, mesh=mesh, in_specs=placed, out_specs=P(("rep", "ctx"), "exp"), check_vma=False
    )
```
